32 devices in a mesh: dp: 8 (over y, x, core), tensor: 4 (over z).
Axes of the slice: x: 2, y: 2, z: 4, core: 2. Of those that a mesh axis runs over, the one named last changes fastest.
Arguments:
- tokens: bfloat16 [8, 1024, 768], P('dp', 'tensor'), may hold values from -6 to 6
- segments: int32 [8, 1024], P('dp'), may hold values from 0 to 2, as said below
- row_order: int32 [8], replicated, may hold values from 0 to 7, each once
- first_gain: float32 [768], P('dp'), may hold values from 0.5 to 1.5
- first_shift: float32 [768], P('dp'), may hold values from -1.5 to 1.5
- triple_weight: float32 [768, 3, 768], P('dp', None, 'tensor'), may hold values from -0.21875 to 0.21875
- triple_bias: float32 [3, 4, 192], P(None, 'tensor', 'dp'), may hold values from -1.5 to 1.5
- shift_taps: float32 [768, 64], P('tensor', 'dp'), may hold values from -0.75 to 0.75
- kernel_modes: float32 [12, 128], P('tensor', 'dp')
- out_weight: float32 [768, 768], P('tensor', 'dp'), may hold values from -0.21875 to 0.21875
- out_bias: float32 [768], P('dp'), may hold values from -1.5 to 1.5
- second_gain: float32 [768], P('dp'), may hold values from 0.5 to 1.5
- second_shift: float32 [768], P('dp'), may hold values from -1.5 to 1.5
- up_weight: float32 [768, 3072], P('dp', 'tensor'), may hold values from -0.21875 to 0.21875
- up_bias: float32 [4, 768], P('tensor', 'dp'), may hold values from -1.5 to 1.5
- down_weight: float32 [3072, 768], P('tensor', 'dp'), may hold values from -0.109375 to 0.109375
- down_bias: float32 [768], P('dp'), may hold values from -1.5 to 1.5
- cotangent: bfloat16 [8, 1024, 768], P('dp', 'tensor'), may hold values from -6 to 6
Outputs:
- output: bfloat16 [8, 1024, 768], P('dp', 'tensor')
- input_grad: bfloat16 [8, 1024, 768], P('dp', 'tensor')
- first_gain_grad: float32 [768], P('dp')
- first_shift_grad: float32 [768], P('dp')
- triple_weight_grad: float32 [768, 3, 768], P('dp', None, 'tensor')
- triple_bias_grad: float32 [3, 4, 192], P(None, 'tensor', 'dp')
- shift_taps_grad: float32 [768, 64], P('tensor', 'dp')
- kernel_modes_grad: float32 [12, 128], P('tensor', 'dp')
- out_weight_grad: float32 [768, 768], P('tensor', 'dp')
- out_bias_grad: float32 [768], P('dp')
- second_gain_grad: float32 [768], P('dp')
- second_shift_grad: float32 [768], P('dp')
- up_weight_grad: float32 [768, 3072], P('dp', 'tensor')
- up_bias_grad: float32 [4, 768], P('tensor', 'dp')
- down_weight_grad: float32 [3072, 768], P('tensor', 'dp')
- down_bias_grad: float32 [768], P('dp')
The draws below stay inside these ranges and needn't reach their ends.
Inputs may be any that keep to these rules, and one draw needn't show every extreme that they name: `segments`: each row of 1024 positions holds 3 sequences whose ids rise from 0 to 2 along the row, each of 128 to 512 positions; in some row one sequence has exactly 512. `row_order`: each of 0 to 7 appears exactly once.
All inputs are finite; a program needn't handle non-finite values.
Results may differ from the reference program's by a relative error of at most 0.018.
The reference program's roundings to bfloat16 on the way count: a program that leaves them out, or rounds other values in their place, can miss the bound.
Values may be sent and summed in bfloat16 or wider, within the bound.
No kernel may reach another device: no remote copies, remote signals or barrier semaphores. Data moves between devices by JAX's collectives and lax.ppermute only.
A program may use at most 192 MiB of HBM per device.

```python
import math
from functools import partial
import jax
import jax.numpy as jnp
from jax import lax

MODEL_WIDTH = 768
HEADS = 12
HD = 64
FF = 3072
TAPS = 64
MODES = 32
SEGS = 3
ROW_LENGTH = 1024
PACKED_ROWS = 8
N_TENSOR = 4


def draw_segments(key, part):
    shorter_length = ROW_LENGTH // 8
    longer_length = ROW_LENGTH // 2
    first_key, second_key, pick_key = jax.random.split(key, 3)
    leading_length = jax.random.randint(first_key, (PACKED_ROWS,), shorter_length, longer_length + 1)
    chosen = jax.random.randint(pick_key, (), 0, PACKED_ROWS)
    leading_length = jnp.where(jnp.arange(PACKED_ROWS, dtype=jnp.int32) == chosen, longer_length, leading_length)
    lower_limit = jnp.maximum(shorter_length, ROW_LENGTH - longer_length - leading_length)
    upper_limit = jnp.minimum(longer_length, ROW_LENGTH - shorter_length - leading_length)
    spread_draw = jax.random.randint(second_key, (PACKED_ROWS,), 0, 1 << 20)
    second_len = lower_limit + spread_draw % (upper_limit - lower_limit + 1)
    position_index = jnp.arange(ROW_LENGTH, dtype=jnp.int32)[None, :]
    first_part = (position_index >= leading_length[:, None]).astype(jnp.int32)
    second_part = (position_index >= (leading_length + second_len)[:, None]).astype(jnp.int32)
    return first_part + second_part


def draw_kernel_modes(key, part):
    rate_key, freq_key, weight_key = jax.random.split(key, 3)
    table_shape = (HEADS, MODES)
    longest_timing = math.log(1.0 / ROW_LENGTH)
    quickest_timing = math.log(1.0 / 30.0)
    log_rates = jax.random.uniform(rate_key, table_shape, jnp.float32, longest_timing, quickest_timing)
    frequency = jax.random.uniform(freq_key, table_shape, jnp.float32, 0.0, 0.25)
    mode_weights = jax.random.normal(weight_key, (HEADS, 2 * MODES), jnp.float32) * (0.012 / math.sqrt(MODES))
    return jnp.concatenate([log_rates, frequency, mode_weights], axis=1)


def levels(stream_key, dims, shards, least, high):
    factor_of, own = 1.0, jax.random.fold_in(stream_key, 6)
    for axis_at, shards_of in shards:
        heights = jnp.exp(jax.random.uniform(jax.random.fold_in(own, axis_at), (shards_of,), jnp.float32, least / len(shards), high / len(shards)))
        factor_of = factor_of * jnp.repeat(heights, dims[axis_at] // shards_of).reshape([-1 if axis == axis_at else 1 for axis in range(len(dims))])
    return factor_of


def gaussian(rng, shape, spread, reach, cuts=(), kind=jnp.bfloat16):
    entries = jax.random.normal(rng, shape, jnp.float32) * spread
    if len(cuts) > 0:
        entries = levels(rng, shape, cuts, -0.22, 0.18) * entries
    return jnp.clip(entries, min=-reach, max=reach).astype(kind)


def setup_inputs(seed: int = 0) -> dict:
    key_of = jax.random.split(jax.random.key(seed), 19)
    return {
        "tokens": gaussian(key_of[0], (PACKED_ROWS, ROW_LENGTH, MODEL_WIDTH), 1.0, 6.0, ((0, 8), (1, 4))),
        "segments": draw_segments(jax.random.fold_in(key_of[18], 71), 0),
        "row_order": jax.random.permutation(key_of[2], PACKED_ROWS).astype(jnp.int32),
        "first_gain": jnp.clip(1.0 + 0.1 * jax.random.normal(key_of[3], (MODEL_WIDTH,), jnp.float32), 0.5, 1.5),
        "first_shift": gaussian(key_of[4], (MODEL_WIDTH,), 0.3, 1.5, ((0, 8),), jnp.float32),
        "triple_weight": gaussian(key_of[5], (MODEL_WIDTH, 3, MODEL_WIDTH), MODEL_WIDTH ** -0.5, 0.21875, ((0, 8), (2, 4)), jnp.float32),
        "triple_bias": gaussian(key_of[6], (3, N_TENSOR, MODEL_WIDTH // N_TENSOR), 0.3, 1.5, ((1, 4), (2, 8)), jnp.float32),
        "shift_taps": gaussian(key_of[7], (MODEL_WIDTH, TAPS), TAPS ** -0.5, 0.75, ((0, 4), (1, 8)), jnp.float32),
        "kernel_modes": draw_kernel_modes(jax.random.fold_in(key_of[18], 71), 0),
        "out_weight": gaussian(key_of[9], (MODEL_WIDTH, MODEL_WIDTH), MODEL_WIDTH ** -0.5, 0.21875, ((0, 4), (1, 8)), jnp.float32),
        "out_bias": gaussian(key_of[10], (MODEL_WIDTH,), 0.3, 1.5, ((0, 8),), jnp.float32),
        "second_gain": jnp.clip(1.0 + 0.1 * jax.random.normal(key_of[11], (MODEL_WIDTH,), jnp.float32), 0.5, 1.5),
        "second_shift": gaussian(key_of[12], (MODEL_WIDTH,), 0.3, 1.5, ((0, 8),), jnp.float32),
        "up_weight": gaussian(key_of[13], (MODEL_WIDTH, FF), MODEL_WIDTH ** -0.5, 0.21875, ((0, 8), (1, 4)), jnp.float32),
        "up_bias": gaussian(key_of[14], (N_TENSOR, FF // N_TENSOR), 0.3, 1.5, ((0, 4), (1, 8)), jnp.float32),
        "down_weight": gaussian(key_of[15], (FF, MODEL_WIDTH), FF ** -0.5, 0.109375, ((0, 4), (1, 8)), jnp.float32),
        "down_bias": gaussian(key_of[16], (MODEL_WIDTH,), 0.3, 1.5, ((0, 8),), jnp.float32),
        "cotangent": gaussian(key_of[17], (PACKED_ROWS, ROW_LENGTH, MODEL_WIDTH), 1.0, 6.0, ((0, 8), (1, 4))),
    }


EPS = 1e-05
HIGH = lax.Precision.HIGHEST

@jax.custom_vjp
def low(v):
    return lax.optimization_barrier(v.astype(jnp.bfloat16)).astype(jnp.float32)

@jax.custom_vjp
def low_back(v):
    return v

def low_keep(v):
    return (low(v), None)

def low_pass(kept, grad):
    return (grad,)

def back_keep(v):
    return (v, None)

def back_low(kept, grad):
    return (low(grad),)
low.defvjp(low_keep, low_pass)
low_back.defvjp(back_keep, back_low)

def normalize(values_in, gains, shifts):
    row_mean = lax.optimization_barrier(jnp.mean(values_in, axis=-1, keepdims=True))
    centred = values_in - row_mean
    variance = lax.optimization_barrier(jnp.mean(centred * centred, axis=-1, keepdims=True))
    return centred * lax.rsqrt(variance + EPS) * gains + shifts

def shift_conv(seg_row, key_rows, tap_table):
    length, channels = key_rows.shape
    tap_count = tap_table.shape[1]
    blocks = length // tap_count
    lag_index = jnp.arange(tap_count, dtype=jnp.int32)[:, None] + tap_count - jnp.arange(2 * tap_count, dtype=jnp.int32)[None, :]
    one_hot = (lag_index[:, :, None] == jnp.arange(tap_count, dtype=jnp.int32)[None, None, :]).astype(jnp.float32)
    band_taps = jnp.einsum('cm,ism->cis', tap_table, one_hot, precision=HIGH)
    summed = jnp.zeros((blocks, tap_count, channels), jnp.float32)
    for segment in range(SEGS):
        inside = (seg_row == segment).astype(jnp.float32)[:, None]
        masked = key_rows * inside
        earlier = jnp.pad(masked, ((tap_count, 0), (0, 0)))[:length]
        window = jnp.concatenate([earlier.reshape(blocks, tap_count, channels), masked.reshape(blocks, tap_count, channels)], axis=1)
        convolved = jnp.einsum('cis,bsc->bic', band_taps, window, precision=HIGH)
        summed = summed + convolved * inside.reshape(blocks, tap_count, 1)
    return summed.reshape(length, channels)

def mode_kernel(mode_table, length):
    mode_count = mode_table.shape[1] // 4
    decay_rate = jnp.exp(mode_table[:, :mode_count])[:, :, None]
    frequency = mode_table[:, mode_count:2 * mode_count][:, :, None]
    cosine_weight = mode_table[:, 2 * mode_count:3 * mode_count][:, :, None]
    sine_weight = mode_table[:, 3 * mode_count:][:, :, None]
    offsets = jnp.arange(length, dtype=jnp.int32).astype(jnp.float32)[None, None, :]
    phases = frequency * offsets
    return lax.optimization_barrier(jnp.sum(jnp.exp(-decay_rate * offsets) * (cosine_weight * jnp.cos(phases) + sine_weight * jnp.sin(phases)), axis=1))

def by_heads(table, length):
    return table.reshape(length, HEADS, HD).transpose(1, 0, 2)

def layer_forward(seg_row, row_data, params):
    first_gain, first_shift, triple_weight, triple_bias, shift_taps, kernel_modes, out_weight, out_bias, second_gain, second_shift, up_weight, up_bias, down_weight, down_bias = [low(entry) for entry in params]
    length = row_data.shape[0]
    first_normed = low(normalize(row_data, first_gain, first_shift))
    projected = low_back(jnp.dot(first_normed, triple_weight.reshape(MODEL_WIDTH, 3 * MODEL_WIDTH), precision=HIGH) + triple_bias.reshape(3 * MODEL_WIDTH))
    queries = low(projected[:, :MODEL_WIDTH])
    key_rows = low(shift_conv(seg_row, projected[:, MODEL_WIDTH:2 * MODEL_WIDTH], shift_taps))
    values = low(projected[:, 2 * MODEL_WIDTH:])
    kernel = mode_kernel(kernel_modes, length)
    position_index = jnp.arange(length, dtype=jnp.int32)
    live_mask = ((position_index[:, None] >= position_index[None, :]) & (seg_row[:, None] == seg_row[None, :])).astype(jnp.float32)
    lag_table = jnp.maximum(position_index[:, None] - position_index[None, :], 0)

    def one_head(head_item):
        head_query, head_key, head_value, head_kernel = head_item
        scores = low_back(jnp.dot(head_query, head_key.T, precision=HIGH))
        weights = low(head_kernel[lag_table] * live_mask * scores)
        return jnp.dot(weights, head_value, precision=HIGH)
    mixed = lax.map(jax.checkpoint(one_head), (by_heads(queries, length), by_heads(key_rows, length), by_heads(values, length), kernel))
    mixed_low = low(low_back(mixed.transpose(1, 0, 2).reshape(length, MODEL_WIDTH)))
    middle = row_data + low_back(jnp.dot(mixed_low, out_weight, precision=HIGH)) + out_bias
    second_normed = low(normalize(middle, second_gain, second_shift))
    pre_act = low_back(jnp.dot(second_normed, up_weight, precision=HIGH) + up_bias.reshape(FF))
    activated = low(jax.nn.gelu(pre_act, approximate=False))
    return middle + jnp.dot(activated, down_weight, precision=HIGH) + down_bias

def reference(tokens, segments, row_order, first_gain, first_shift, triple_weight, triple_bias, shift_taps, kernel_modes, out_weight, out_bias, second_gain, second_shift, up_weight, up_bias, down_weight, down_bias, cotangent):
    params = (first_gain, first_shift, triple_weight, triple_bias, shift_taps, kernel_modes, out_weight, out_bias, second_gain, second_shift, up_weight, up_bias, down_weight, down_bias)
    order = row_order.astype(jnp.int32)
    routed_tokens = tokens[order]
    routed_cot = cotangent[order]

    def one_row(totals, row_item):
        row_data, seg_row, row_cot = row_item
        result, back_fn = jax.vjp(partial(layer_forward, seg_row), row_data.astype(jnp.float32), params)
        row_grad, param_grads = back_fn(row_cot.astype(jnp.float32))
        totals = jax.tree.map(lambda running, fresh: running + fresh, totals, param_grads)
        return (totals, (result.astype(jnp.bfloat16), row_grad.astype(jnp.bfloat16)))
    start = jax.tree.map(jnp.zeros_like, params)
    totals, (outputs, input_grads) = lax.scan(one_row, start, (routed_tokens, segments, routed_cot))
    outputs = jnp.zeros_like(outputs).at[order].set(outputs)
    input_grads = jnp.zeros_like(input_grads).at[order].set(input_grads)
    return (outputs, input_grads) + tuple(totals)
```

```python
from functools import partial

import jax
import jax.numpy as jnp
from jax import lax
from jax.experimental import pallas as pl
from jax.experimental.pallas import tpu as pltpu
from jax.sharding import Mesh
from jax.sharding import PartitionSpec as P

EPS = 1e-05
BF = jnp.bfloat16
F32 = jnp.float32
TILE = 128
BLOCK = 256
LAGS = 5
REACH = 3
LIMIT = 512
SEQUENCES = 3
GAP = 64
SMALL = 16
AXES = ("g", "c", "h", "b")
VMEM_BYTES = 56 * 1024 * 1024


def vm():
    return pl.BlockSpec(memory_space=pltpu.VMEM)


def sm():
    return pl.BlockSpec(memory_space=pltpu.SMEM)


def dot(a, b):
    return jnp.dot(a, b, preferred_element_type=F32)


def dot_nt(a, b):
    return lax.dot_general(a, b, (((1,), (1,)), ((), ())), preferred_element_type=F32)


def dot_tn(a, b):
    return lax.dot_general(a, b, (((0,), (0,)), ((), ())), preferred_element_type=F32)


def call(kernel, n_smem, args, outs, scratch=(), name=None, flops=0, nbytes=0, trans=0):
    return pl.pallas_call(
        kernel,
        out_shape=tuple(jax.ShapeDtypeStruct(s, d) for s, d in outs),
        in_specs=[sm()] * n_smem + [vm()] * (len(args) - n_smem),
        out_specs=tuple(vm() for _ in outs),
        scratch_shapes=[pltpu.VMEM(s, d) for s, d in scratch],
        compiler_params=pltpu.CompilerParams(vmem_limit_bytes=VMEM_BYTES),
        cost_estimate=pl.CostEstimate(
            flops=int(flops), bytes_accessed=int(nbytes), transcendentals=int(trans)
        ),
        name=name,
    )(*args)


def norm_rows(values):
    mean = jnp.mean(values, axis=-1, keepdims=True)
    centred = values - mean
    variance = jnp.mean(centred * centred, axis=-1, keepdims=True)
    inv = lax.rsqrt(variance + EPS)
    return centred * inv, inv


def project_kernel(pieces, meta, *refs):
    x_refs = refs[:4]
    a_refs = refs[4 : 4 + pieces]
    vec, bias, first_o, q_o, k_o, v_o = refs[4 + pieces : 10 + pieces]
    local = q_o.shape[1]
    if pieces > 1:
        out_o, w_ref = refs[10 + pieces :]
        g, c = meta[1], meta[2]
        rows = a_refs[0].shape[1] - SMALL
        for k in range(pieces):
            for j in range(2):
                at = pl.multiple_of((2 * (g ^ k) + (c ^ j)) * rows, rows)
                w_ref[pl.ds(at, rows), :] = a_refs[k][j, :rows, : 3 * local]
                out_o[pl.ds(at, rows), :] = a_refs[k][j, :rows, 3 * local :]
    else:
        w_ref = a_refs[0]
    quarter = x_refs[0].shape[0]
    gain, shift = vec[0:1, :], vec[1:2, :]
    step = 32
    for k in range(4):
        base = pl.multiple_of((meta[0] ^ k) * quarter, quarter)

        def chunk(i, _, k=k, base=base):
            at = pl.multiple_of(i * step, step)
            normed, _inv = norm_rows(x_refs[k][pl.ds(at, step), :].astype(F32))
            first_o[pl.ds(pl.multiple_of(base + at, step), step), :] = (
                normed * gain + shift
            ).astype(BF)
            return 0

        lax.fori_loop(0, quarter // step, chunk, 0)
        made = dot(first_o[pl.ds(base, quarter), :], w_ref[...]) + bias[0:1, :]
        q_o[pl.ds(base, quarter), :] = made[:, :local].astype(BF)
        k_o[pl.ds(base, quarter), :] = made[:, local : 2 * local]
        v_o[pl.ds(base, quarter), :] = made[:, 2 * local :].astype(BF)


def sequence_of(rows, start, stop):
    return (rows >= start).astype(jnp.int32) + (rows >= stop).astype(jnp.int32)


def spread_rows(source, target, meta, length, channels):
    for i in range(target.shape[0] // GAP):
        total = jnp.zeros((GAP, channels), F32)
        for s in range(SEQUENCES):
            j = i - s - 1
            if 0 <= j < length // GAP:
                rows = lax.broadcasted_iota(jnp.int32, (GAP, channels), 0) + j * GAP
                hit = sequence_of(rows, meta[4], meta[5]) == s
                total = total + jnp.where(hit, source[j * GAP : (j + 1) * GAP, :], 0.0)
        target[i * GAP : (i + 1) * GAP, :] = total


def gather_rows(source, target, meta, length, channels):
    for j in range(length // GAP):
        rows = lax.broadcasted_iota(jnp.int32, (GAP, channels), 0) + j * GAP
        ids = sequence_of(rows, meta[4], meta[5])
        total = jnp.zeros((GAP, channels), F32)
        for s in range(SEQUENCES):
            i = j + s + 1
            total = jnp.where(ids == s, source[i * GAP : (i + 1) * GAP, :], total)
        target[j * GAP : (j + 1) * GAP, :] = total.astype(target.dtype)


def shifted_copies(source, target, sign):
    total = source.shape[0]
    target[0, :, :] = source[...]
    for r in range(1, 8):
        if sign > 0:
            target[r, 8:total, :] = source[8 - r : total - r, :]
            target[r, 0:8, :] = jnp.zeros((8, source.shape[1]), F32)
        else:
            target[r, 0 : total - 8, :] = source[r : total - 8 + r, :]
            target[r, total - 8 : total, :] = jnp.zeros((8, source.shape[1]), F32)


def taps_sum(copies, taps, target, sign, blocks):
    channels = target.shape[1]
    n_taps = taps.shape[0]

    def block(i, _):
        at = pl.multiple_of((i + 1) * GAP, GAP)
        total = jnp.zeros((GAP, channels), F32)
        for r in range(8):
            if sign > 0:
                window = copies[r, pl.ds(pl.multiple_of(at - n_taps + 8, 8), GAP + n_taps - 8), :]
            else:
                window = copies[r, pl.ds(at, GAP + n_taps - 8), :]
            for m in range(n_taps // 8):
                low = n_taps - 8 - 8 * m if sign > 0 else 8 * m
                total = total + window[low : low + GAP] * taps[8 * m + r : 8 * m + r + 1, :]
        target[pl.ds(at, GAP), :] = total
        return 0

    lax.fori_loop(0, blocks, block, 0)


def conv_kernel(meta, k_ref, taps, kb_o, copies_o, pad, made):
    length, channels = k_ref.shape
    spread_rows(k_ref, pad, meta, length, channels)
    shifted_copies(pad, copies_o, 1)
    taps_sum(copies_o, taps, made, 1, length // GAP + SEQUENCES - 1)
    gather_rows(made, kb_o, meta, length, channels)


def conv_back_kernel(meta, gk_ref, taps, copies, graw_o, gtaps_o, pad, back, made):
    length, channels = gk_ref.shape
    n_taps = taps.shape[0]
    spread_rows(gk_ref, pad, meta, length, channels)
    shifted_copies(pad, back, -1)
    taps_sum(back, taps, made, -1, length // GAP + SEQUENCES - 1)
    gather_rows(made, graw_o, meta, length, channels)
    blocks = length // GAP + SEQUENCES - 1
    half = GAP // 2
    for m in range(n_taps // 8):

        def block(i, totals, m=m):
            at = pl.multiple_of(GAP + i * half, half)
            grad = pad[pl.ds(at, half), :]
            fresh = []
            for r in range(8):
                prod = grad * copies[r, pl.ds(pl.multiple_of(at - 8 * m, 8), half), :]
                part = prod[0:8]
                for k in range(1, half // 8):
                    part = part + prod[8 * k : 8 * k + 8]
                fresh.append(totals[r] + part)
            return tuple(fresh)

        totals = lax.fori_loop(
            0, 2 * blocks, block, tuple(jnp.zeros((8, channels), F32) for _ in range(8))
        )
        gtaps_o[8 * m : 8 * m + 8, :] = jnp.concatenate(
            [jnp.sum(t, axis=0, keepdims=True) for t in totals], axis=0
        )


def make_tiles(lags_ref, tiles, heads):
    for h in range(heads):
        for d in range(LAGS):
            at = TILE * (LAGS - 1 - d)
            row = jnp.broadcast_to(lags_ref[h : h + 1, at : at + 2 * TILE], (TILE, 2 * TILE))
            turned = pltpu.roll(row, TILE + 1, 1, stride=1, stride_axis=0)
            tiles[h, d, :, :] = turned[:, :TILE]


def head_masked(source, target, heads):
    length, channels = source.shape
    size = channels // heads
    for h in range(heads):
        lane = lax.broadcasted_iota(jnp.int32, (BLOCK, channels), 1)
        hit = (lane >= h * size) & (lane < (h + 1) * size)
        for a in range(length // BLOCK):
            part = source[a * BLOCK : (a + 1) * BLOCK, :]
            target[h, a, :, :] = jnp.where(hit, part, jnp.zeros_like(part))


def starts_of(meta, target):
    rows = lax.broadcasted_iota(jnp.int32, target.shape, 0)
    first = jnp.where(rows >= meta[4], meta[4], 0)
    target[...] = jnp.where(rows >= meta[5], meta[5], first)


def live_of(starts, t_at, u_at):
    lane = lax.broadcasted_iota(jnp.int32, (TILE, TILE), 1) + u_at
    return lane >= starts[t_at : t_at + TILE, :]


def mix_kernel(meta, q_ref, k_ref, v_ref, lags_ref, mixed_o, tiles_o, qm, vmask, starts, weights):
    length, local = q_ref.shape
    heads = qm.shape[0]
    make_tiles(lags_ref, tiles_o, heads)
    head_masked(q_ref, qm, heads)
    starts_of(meta, starts)
    size = local // heads
    lane = lax.broadcasted_iota(jnp.int32, (BLOCK, local), 1)
    for a in range(length // BLOCK):
        part = v_ref[a * BLOCK : (a + 1) * BLOCK, :]
        for h in range(heads):
            hit = (lane >= h * size) & (lane < (h + 1) * size)
            at = (a * heads + h) * BLOCK
            vmask[at : at + BLOCK, :] = jnp.where(hit, part, jnp.zeros_like(part))
    for a in range(length // BLOCK):
        least = max(0, a - REACH + 1)
        for s in range(least, a + 1):
            keys = k_ref[s * BLOCK : (s + 1) * BLOCK, :]
            lives = {}
            for i in range(2):
                for j in range(2):
                    d = 2 * (a - s) + i - j
                    if 0 <= d < LAGS:
                        lives[i, j] = live_of(
                            starts, a * BLOCK + i * TILE, s * BLOCK + j * TILE
                        )

            def head(h, _, a=a, s=s, keys=keys, lives=lives, least=least):
                scores = dot_nt(qm[h, a], keys)
                at = pl.multiple_of(((s - least) * heads + h) * BLOCK, BLOCK)
                for i in range(2):
                    for j in range(2):
                        where = (
                            pl.ds(i * TILE, TILE),
                            pl.ds(pl.multiple_of(at + j * TILE, TILE), TILE),
                        )
                        if (i, j) in lives:
                            factor = jnp.where(
                                lives[i, j], tiles_o[h, 2 * (a - s) + i - j], 0.0
                            )
                            piece = scores[
                                i * TILE : (i + 1) * TILE, j * TILE : (j + 1) * TILE
                            ]
                            weights[where] = (factor * piece).astype(BF)
                        else:
                            weights[where] = jnp.zeros((TILE, TILE), BF)
                return 0

            lax.fori_loop(0, heads, head, 0)
        wide = (a - least + 1) * heads * BLOCK
        mixed_o[a * BLOCK : (a + 1) * BLOCK, :] = dot(
            weights[:, :wide], vmask[least * heads * BLOCK : (a + 1) * heads * BLOCK, :]
        ).astype(BF)


def mix_back_kernel(
    meta, q_ref, k_ref, v_ref, gm0, gm1, gm2, gm3, out_ref, tiles, gq_o, gk_o, gv_o, glag_o,
    gmix, qm, gmask, kmask, qt, gt, starts, grads, gkt, gvt, diag
):
    length, local = q_ref.shape
    heads = qm.shape[0]
    size = local // heads
    quarter = gm0.shape[0]
    for k, part in enumerate((gm0, gm1, gm2, gm3)):
        base = pl.multiple_of((meta[0] ^ k) * quarter, quarter)
        gmix[pl.ds(base, quarter), :] = dot(part[...], out_ref[...]).astype(BF)
    head_masked(q_ref, qm, heads)
    head_masked(gmix, gmask, heads)
    starts_of(meta, starts)
    lane = lax.broadcasted_iota(jnp.int32, (BLOCK, local), 1)
    for a in range(length // BLOCK):
        part = k_ref[a * BLOCK : (a + 1) * BLOCK, :]
        for h in range(heads):
            hit = (lane >= h * size) & (lane < (h + 1) * size)
            at = (a * heads + h) * BLOCK
            kmask[at : at + BLOCK, :] = jnp.where(hit, part, jnp.zeros_like(part))
    qt[...] = q_ref[...].astype(F32).T.astype(BF)
    gt[...] = gmix[...].astype(F32).T.astype(BF)
    gkt[...] = jnp.zeros_like(gkt)
    gvt[...] = jnp.zeros_like(gvt)
    diag[...] = jnp.zeros_like(diag)
    for a in range(length // BLOCK):
        least = max(0, a - REACH + 1)
        for s in range(least, a + 1):
            keys = k_ref[s * BLOCK : (s + 1) * BLOCK, :]
            vals = v_ref[s * BLOCK : (s + 1) * BLOCK, :]
            lives = {}
            for i in range(2):
                for j in range(2):
                    d = 2 * (a - s) + i - j
                    if 0 <= d < LAGS:
                        lives[i, j] = live_of(
                            starts, a * BLOCK + i * TILE, s * BLOCK + j * TILE
                        )

            def head(h, _, a=a, s=s, keys=keys, vals=vals, lives=lives, least=least):
                scores = dot_nt(qm[h, a], keys)
                wgrad = dot_nt(gmask[h, a], vals)
                at = pl.multiple_of(((s - least) * heads + h) * BLOCK, BLOCK)
                rows_w, rows_g = [], []
                for i in range(2):
                    line_w, line_g = [], []
                    for j in range(2):
                        if (i, j) in lives:
                            d = 2 * (a - s) + i - j
                            spot = (
                                slice(i * TILE, (i + 1) * TILE),
                                slice(j * TILE, (j + 1) * TILE),
                            )
                            factor = jnp.where(lives[i, j], tiles[h, d], 0.0)
                            line_w.append((factor * scores[spot]).astype(BF))
                            line_g.append((wgrad[spot] * factor).astype(BF))
                            diag[h, d] += jnp.where(
                                lives[i, j], wgrad[spot] * scores[spot], 0.0
                            )
                        else:
                            line_w.append(jnp.zeros((TILE, TILE), BF))
                            line_g.append(jnp.zeros((TILE, TILE), BF))
                    rows_w.append(jnp.concatenate(line_w, axis=1))
                    rows_g.append(jnp.concatenate(line_g, axis=1))
                w = jnp.concatenate(rows_w, axis=0)
                g = jnp.concatenate(rows_g, axis=0)
                grads[:, pl.ds(at, BLOCK)] = g
                band = pl.ds(pl.multiple_of(h * size, size), size)
                cols = slice(s * BLOCK, (s + 1) * BLOCK)
                gvt[band, cols] += dot(gt[band, a * BLOCK : (a + 1) * BLOCK], w)
                gkt[band, cols] += dot(qt[band, a * BLOCK : (a + 1) * BLOCK], g)
                return 0

            lax.fori_loop(0, heads, head, 0)
        wide = (a - least + 1) * heads * BLOCK
        gq_o[a * BLOCK : (a + 1) * BLOCK, :] = dot(
            grads[:, :wide], kmask[least * heads * BLOCK : (a + 1) * heads * BLOCK, :]
        ).astype(BF)
    gk_o[...] = gkt[...].T
    gv_o[...] = gvt[...].T.astype(BF)
    glag_o[...] = jnp.zeros_like(glag_o)
    for h in range(heads):
        for d in range(LAGS):
            total = jnp.concatenate([diag[h, d], jnp.zeros((TILE, TILE), F32)], axis=1)
            rows = TILE
            while rows > 1:
                rows //= 2
                total = pltpu.roll(total[:rows], rows, 1) + total[rows : 2 * rows]
            at = TILE * (LAGS - 1 - d)
            glag_o[h : h + 1, at : at + 2 * TILE] += total


ROOT_HALF = 0.7071067811865476
PHI_SCALE = 0.3989422804014327


def mlp_kernel(ks, keep, meta, *refs):
    x_refs, g_refs = refs[0:2], refs[2:4]
    mixed, outs = refs[4:8], refs[8:12]
    vec, up_bias, both = refs[12:15]
    second_o, act_o, gpre_o, ga_o, gb_o, ubias_o = refs[15:21]
    rest = refs[21:]
    if keep:
        middle_o, rest = rest[0], rest[1:]
    pre, agrad, mid = rest
    quarter, width = x_refs[0].shape
    hidden = both.shape[1] // 2
    step = 32
    ubias_o[...] = jnp.zeros_like(ubias_o)
    for n, k in enumerate(ks):
        base = pl.multiple_of((meta[0] ^ k) * quarter, quarter)
        total = x_refs[n][...].astype(F32) + vec[2:3, :]
        for m, o in zip(mixed, outs):
            total = total + dot_nt(m[pl.ds(base, quarter), :], o[...])
        mid[...] = total
        if keep and n == 0:
            middle_o[...] = total

        def normed_chunk(i, _, n=n):
            at = pl.multiple_of(i * step, step)
            normed, _inv = norm_rows(mid[pl.ds(at, step), :])
            second_o[pl.ds(pl.multiple_of(n * quarter + at, step), step), :] = (
                normed * vec[3:4, :] + vec[4:5, :]
            ).astype(BF)
            return 0

        lax.fori_loop(0, quarter // step, normed_chunk, 0)
        pre[...] = dot(second_o[n * quarter : (n + 1) * quarter, :], both[:, :hidden])
        agrad[...] = dot(g_refs[n][...], both[:, hidden:])

        def act_chunk(i, total, n=n):
            at = pl.multiple_of(i * 16, 16)
            to = pl.multiple_of(n * quarter + at, 16)
            v = pre[pl.ds(at, 16), :] + up_bias[0:1, :]
            cdf = 0.5 + 0.5 * lax.erf(v * ROOT_HALF)
            act_o[pl.ds(to, 16), :] = (v * cdf).astype(BF)
            slope = cdf + v * (PHI_SCALE * jnp.exp(-0.5 * v * v))
            grad = (slope * agrad[pl.ds(at, 16), :]).astype(BF)
            gpre_o[pl.ds(to, 16), :] = grad
            wide = grad.astype(F32)
            return total + wide[0:8] + wide[8:16]

        total = lax.fori_loop(0, quarter // 16, act_chunk, jnp.zeros((8, hidden), F32))
        ubias_o[...] += total
        part = dot_nt(gpre_o[n * quarter : (n + 1) * quarter, :], both[:, :hidden])
        target = (ga_o, gb_o)[n]
        target[...] = part.astype(target.dtype)


def middle_back_kernel(part, near, far, cot, middle, vec, gmid_o, gmb_o, sums_o):
    rows, width = middle.shape
    step = 16

    def chunk(i, totals):
        at = pl.multiple_of(i * step, step)
        spot = pl.ds(at, step)
        up = part[spot, :] + near[spot, :].astype(F32) + far[spot, :].astype(F32)
        normed, inv = norm_rows(middle[spot, :])
        cotangent = cot[spot, :].astype(F32)
        e = up * vec[3:4, :]
        mean_e = jnp.mean(e, axis=-1, keepdims=True)
        mean_x = jnp.mean(e * normed, axis=-1, keepdims=True)
        grad = cotangent + inv * (e - mean_e - normed * mean_x)
        gmid_o[spot, :] = grad
        gmb_o[spot, :] = grad.astype(BF)
        terms = (grad, up * normed, up, cotangent)
        return tuple(t + x[0:8] + x[8:16] for t, x in zip(totals, terms))

    totals = lax.fori_loop(
        0, rows // step, chunk, tuple(jnp.zeros((8, width), F32) for _ in range(4))
    )
    sums_o[...] = jnp.zeros_like(sums_o)
    for i, t in enumerate(totals):
        sums_o[2 + i : 3 + i, :] = jnp.sum(t, axis=0, keepdims=True)


def first_back_kernel(part, near, far, tokens, gmid, vec, grad_o, sums_o):
    rows, width = tokens.shape
    step = 16

    def chunk(i, totals):
        at = pl.multiple_of(i * step, step)
        spot = pl.ds(at, step)
        up = part[spot, :] + near[spot, :].astype(F32) + far[spot, :].astype(F32)
        normed, inv = norm_rows(tokens[spot, :].astype(F32))
        e = up * vec[0:1, :]
        mean_e = jnp.mean(e, axis=-1, keepdims=True)
        mean_x = jnp.mean(e * normed, axis=-1, keepdims=True)
        grad_o[spot, :] = (gmid[spot, :] + inv * (e - mean_e - normed * mean_x)).astype(BF)
        terms = (up * normed, up)
        return tuple(t + x[0:8] + x[8:16] for t, x in zip(totals, terms))

    totals = lax.fori_loop(
        0, rows // step, chunk, tuple(jnp.zeros((8, width), F32) for _ in range(2))
    )
    sums_o[...] = jnp.zeros_like(sums_o)
    for i, t in enumerate(totals):
        sums_o[i : i + 1, :] = jnp.sum(t, axis=0, keepdims=True)


def first_grad_kernel(meta, gq, gk, gv, w_ref, p0, p1, p2, p3, tri_o, bias_o):
    length, local = gq.shape
    quarter = length // 4
    total = jnp.zeros((8, 3 * local), F32)
    for k, target in enumerate((p0, p1, p2, p3)):
        base = pl.multiple_of((meta[0] ^ k) * quarter, quarter)
        made = jnp.concatenate(
            [r[pl.ds(base, quarter), :] for r in (gq, gk, gv)], axis=1
        )
        tri_o[pl.ds(base, quarter), :] = made
        target[...] = dot_nt(made, w_ref[...]).astype(target.dtype)
        wide = made.astype(F32)
        for i in range(quarter // 8):
            total = total + wide[8 * i : 8 * i + 8]
    bias_o[...] = total


def permute(value, groups, target_of):
    pairs = []
    for g in range(groups):
        for c in range(2):
            for z in range(4):
                to = target_of(g, c, z)
                if to is not None:
                    pairs.append((g * 8 + c * 4 + z, to[0] * 8 + to[1] * 4 + to[2]))
    return lax.ppermute(value, AXES, pairs)


def swap_quarters(value, groups):
    return permute(
        value, groups, lambda g, c, z: (g, c, z) if c == z // 2 else (g, 1 - c, z ^ 2)
    )


def to_core(value, groups):
    return permute(value, groups, lambda g, c, z: (g, 1 - c, z))


def to_chip(value, groups):
    return permute(value, groups, lambda g, c, z: (g, c, z ^ 1))


def gather_group(value, groups):
    chip = to_chip(value, groups)
    core = to_core(value, groups)
    both = to_core(chip, groups)
    return value, chip, core, both


def spread_pieces(piece, groups, same):
    near = permute(
        piece, groups, lambda g, c, z: (g, c, z ^ 2) if c == z // 2 else (g, 1 - c, z)
    )
    far = permute(piece, groups, lambda g, c, z: None if c == z // 2 else (g, 1 - c, z ^ 2))
    return jnp.where(same, piece, near), jnp.where(same, near, far)


def return_pieces(pieces, half, groups, same):
    kept = lax.dynamic_index_in_dim(pieces, half, 0, False)
    sent = lax.dynamic_index_in_dim(pieces, 1 - half, 0, False)
    near = permute(
        sent, groups, lambda g, c, z: (g, 1 - c, z) if c == z // 2 else (g, c, z ^ 2)
    )
    far = permute(kept, groups, lambda g, c, z: None if c == z // 2 else (g, 1 - c, z ^ 2))
    return near.astype(F32) + jnp.where(same, kept, far).astype(F32)


def pad_to(value, rows, lanes):
    return jnp.pad(value, ((0, rows - value.shape[0]), (0, lanes - value.shape[1])))


def on_device(
    groups,
    tokens,
    segments,
    row_order,
    first_gain,
    first_shift,
    triple_weight,
    triple_bias,
    shift_taps,
    kernel_modes,
    out_weight,
    out_bias,
    second_gain,
    second_shift,
    up_weight,
    up_bias,
    down_weight,
    down_bias,
    cotangent,
):
    g = lax.axis_index("g")
    c = lax.axis_index("c")
    h = lax.axis_index("h")
    b = lax.axis_index("b")
    same = c == h
    n_pieces = 2 * groups
    quarter, width = tokens.shape[1:]
    length = 4 * quarter
    rows, _, local = triple_weight.shape
    heads = kernel_modes.shape[0]
    n_modes = kernel_modes.shape[1] * n_pieces // 4
    taps_rows = shift_taps.shape[1]
    mode_cols = kernel_modes.shape[1]
    bias_cols = triple_bias.shape[2]
    hidden = up_weight.shape[1]

    own_x = swap_quarters(tokens[0], groups)
    x = gather_group(own_x, groups)
    seg = segments[0]
    first_end = jnp.sum((seg < 1).astype(jnp.int32))
    second_end = jnp.sum((seg < 2).astype(jnp.int32))
    ends = jnp.stack(
        [first_end // 32, first_end % 32, second_end // 32, second_end % 32]
    ).astype(BF)
    vectors = jnp.stack([first_gain, first_shift, out_bias, second_gain, second_shift, down_bias])
    small = jnp.concatenate(
        [
            pad_to(shift_taps.astype(BF).T, SMALL, local),
            pad_to(vectors.astype(BF), SMALL, TILE),
            pad_to(triple_bias[:, 0, :].astype(BF), SMALL, TILE),
            pad_to(kernel_modes.astype(BF), SMALL, TILE),
            pad_to(up_bias.astype(BF), SMALL, TILE),
            pad_to(ends[None], SMALL, width - local - 4 * TILE),
        ],
        axis=1,
    )
    first_piece = jnp.concatenate(
        [
            jnp.concatenate(
                [triple_weight.astype(BF).reshape(rows, 3 * local), out_weight.astype(BF).T], axis=1
            ),
            small,
        ],
        axis=0,
    )
    a_pair = jnp.stack(spread_pieces(first_piece, groups, same))
    if groups == 4:
        a_all = [a_pair] + [
            permute(a_pair, groups, lambda g, c, z, k=k: (g ^ k, c, z)) for k in (1, 2, 3)
        ]
        small_rel = jnp.stack([a[:, rows:, :] for a in a_all])
        order = jnp.arange(groups, dtype=jnp.int32) ^ g
        small_all = sum(
            jnp.where((order == k)[:, None, None, None], small_rel[k][None], 0)
            for k in range(groups)
        )
    else:
        a_all = lax.all_gather(a_pair, "g", axis=0, tiled=False)
        small_all = a_all[:, :, rows:, :]
    small_all = jnp.where(c == 0, small_all, small_all[:, ::-1])
    small_all = small_all.reshape(n_pieces, SMALL, width)

    def part(n_rows, at, n_cols):
        return small_all[:, :n_rows, at : at + n_cols]

    taps = part(taps_rows, 0, local).reshape(n_pieces * taps_rows, local).astype(F32)
    vec = part(6, local, rows).transpose(1, 0, 2).reshape(6, width).astype(F32)
    vec = pad_to(vec, 8, width)
    bias = part(3, local + TILE, bias_cols).transpose(1, 0, 2).reshape(1, 3 * local).astype(F32)
    modes = part(heads, local + 2 * TILE, mode_cols).transpose(1, 0, 2)
    modes = modes.reshape(heads, 4 * n_modes).astype(F32)
    up_bias_all = part(1, local + 3 * TILE, rows).reshape(1, hidden).astype(F32)
    ends_all = part(1, local + 4 * TILE, 4).reshape(n_pieces, 4).astype(jnp.int32)
    mine = (row_order == 2 * g + h)[:, None]
    ends_own = jnp.sum(jnp.where(mine, ends_all, 0), axis=0)
    q_at = 2 * c + b
    meta = jnp.stack(
        [q_at, g, c, h, 32 * ends_own[0] + ends_own[1], 32 * ends_own[2] + ends_own[3], g, g]
    ).astype(jnp.int32)

    second_piece = jnp.concatenate([up_weight.astype(BF), down_weight.astype(BF).T], axis=1)
    lo, hi = spread_pieces(second_piece, groups, same)
    b_pair = jnp.concatenate([jnp.where(c == 0, lo, hi), jnp.where(c == 0, hi, lo)], axis=0)
    both = lax.all_gather(b_pair, "g", axis=0, tiled=True)

    own_cot = swap_quarters(cotangent[0], groups)
    cot = gather_group(own_cot, groups)

    wide = [((length, width), BF), ((length, local), BF), ((length, local), F32)]
    wide += [((length, local), BF)]
    proj_cost = dict(flops=2 * length * width * 3 * local, nbytes=6 * length * width)
    if groups == 4:
        first, queries, raw_keys, values, out_own, triple = call(
            partial(project_kernel, 4), 1, (meta, *x, *a_all, vec, bias),
            wide + [((width, local), BF), ((width, 3 * local), BF)], name="project", **proj_cost,
        )
    else:
        turned = jnp.where(c == 0, a_all, a_all[:, ::-1])[:, :, :rows, :].reshape(width, 4 * local)
        triple, out_own = turned[:, : 3 * local], turned[:, 3 * local :]
        first, queries, raw_keys, values = call(
            partial(project_kernel, 1), 1, (meta, *x, triple, vec, bias), wide,
            name="project", **proj_cost,
        )
    outs = gather_group(out_own, groups)

    lag = LIMIT + TILE - 1 - jnp.arange(6 * TILE, dtype=jnp.int32)
    held = ((lag >= 0) & (lag < LIMIT)).astype(F32)[None, None, :]
    place = jnp.clip(lag, 0, LIMIT - 1).astype(F32)[None, None, :]
    rate = jnp.exp(modes[:, :n_modes])[:, :, None]
    phase = modes[:, n_modes : 2 * n_modes][:, :, None] * place
    decay = jnp.exp(-rate * place) * held
    wave_c, wave_s = decay * jnp.cos(phase), decay * jnp.sin(phase)
    weight_c = modes[:, 2 * n_modes : 3 * n_modes][:, :, None]
    weight_s = modes[:, 3 * n_modes :][:, :, None]
    lags = jnp.sum(weight_c * wave_c + weight_s * wave_s, axis=1)
    lags = pad_to(lags, 8, 6 * TILE)

    padded = length + (SEQUENCES + 1) * GAP
    n_blocks = length // BLOCK
    keys, copies = call(
        conv_kernel, 1, (meta, raw_keys, taps),
        [((length, local), BF), ((8, padded, local), F32)],
        [((padded, local), F32), ((padded, local), F32)],
        name="conv", flops=2 * length * local * 64, nbytes=4 * 10 * padded * local,
    )
    per_head = (heads, n_blocks, BLOCK, local)
    stacked = (n_blocks * heads * BLOCK, local)
    mixed, tiles = call(
        mix_kernel, 1, (meta, queries, keys, values, lags),
        [((length, local), BF), ((heads, LAGS, TILE, TILE), F32)],
        [
            (per_head, BF), (stacked, BF), ((length, TILE), jnp.int32),
            ((BLOCK, REACH * heads * BLOCK), BF),
        ],
        name="mix", flops=heads * 9 * BLOCK * BLOCK * 64 * 16, nbytes=8 * length * local,
    )
    mixes = gather_group(mixed, groups)

    half_out = [((2 * quarter, width), BF), ((2 * quarter, hidden), BF), ((2 * quarter, hidden), BF)]
    scratch = [((quarter, hidden), F32), ((quarter, hidden), F32), ((quarter, width), F32)]
    mlp_cost = dict(
        flops=2 * 2 * quarter * width * (width + 3 * hidden), nbytes=2 * width * (8 * quarter + 3 * width),
        trans=4 * quarter * hidden,
    )
    shared = (*mixes, *outs, vec, up_bias_all, both)
    second_b, act_b, gpre_b, gsec_c, gsec_d, ubias_b = call(
        partial(mlp_kernel, (2, 3), False), 1, (meta, x[2], x[3], cot[2], cot[3], *shared),
        half_out + [((quarter, width), BF), ((quarter, width), BF), ((8, hidden), F32)],
        scratch, name="mlp_far", **mlp_cost,
    )
    near_own = to_core(gsec_c, groups)
    near_chip = to_core(gsec_d, groups)
    second_a, act_a, gpre_a, gsec_a, gsec_b, ubias_a, middle = call(
        partial(mlp_kernel, (0, 1), True), 1, (meta, x[0], x[1], cot[0], cot[1], *shared),
        half_out
        + [((quarter, width), F32), ((quarter, width), F32), ((8, hidden), F32)]
        + [((quarter, width), F32)],
        scratch, name="mlp_near", **mlp_cost,
    )
    far_own = to_chip((gsec_b + near_chip.astype(F32)).astype(BF), groups)
    gmid, gmb_own, sums_two = call(
        middle_back_kernel, 0, (gsec_a, near_own, far_own, own_cot, middle, vec),
        [((quarter, width), F32), ((quarter, width), BF), ((8, width), F32)],
        name="middle_back", flops=20 * quarter * width, nbytes=20 * quarter * width,
    )
    gmb = gather_group(gmb_own, groups)

    act = jnp.concatenate([act_a, act_b], axis=0)
    gpre = jnp.concatenate([gpre_a, gpre_b], axis=0)
    second = jnp.concatenate([second_a, second_b], axis=0)
    cot_all = jnp.concatenate(cot, axis=0)
    down_part = both[:, hidden:]
    share_far = dot_nt(act_b, down_part).astype(BF)
    share = dot_nt(act_a, down_part)
    share_near = to_core(share_far, groups).astype(F32)
    share_chip = to_chip((share[quarter:] + share_near[quarter:]).astype(BF), groups)
    result = (
        middle + share[:quarter] + share_near[:quarter] + share_chip.astype(F32) + vec[5:6, :]
    ).astype(BF)
    result = swap_quarters(result, groups)
    up_grad = dot_tn(second, gpre)
    down_grad = dot_tn(cot_all, act)
    b_grad = jnp.concatenate([up_grad.astype(BF), down_grad.astype(BF)], axis=1)
    b_grad = lax.psum_scatter(b_grad, "g", scatter_dimension=0, tiled=True)
    b_out = return_pieces(b_grad.reshape(2, rows, 2 * hidden), h, groups, same)

    gq, gk, gv, glag = call(
        mix_back_kernel, 1, (meta, queries, keys, values, *gmb, out_own, tiles),
        [
            ((length, local), BF), ((length, local), F32), ((length, local), BF),
            ((8, 6 * TILE), F32),
        ],
        [
            ((length, local), BF), (per_head, BF), (per_head, BF), (stacked, BF),
            ((local, length), BF), ((local, length), BF), ((length, TILE), jnp.int32),
            ((BLOCK, REACH * heads * BLOCK), BF), ((local, length), F32), ((local, length), F32),
            ((heads, LAGS, TILE, TILE), F32),
        ],
        name="mix_back", flops=heads * 9 * BLOCK * BLOCK * 64 * 30, nbytes=16 * length * local,
    )
    graw, gtaps = call(
        conv_back_kernel, 1, (meta, gk, taps, copies),
        [((length, local), BF), ((taps.shape[0], local), F32)],
        [((padded, local), F32), ((8, padded, local), F32), ((padded, local), F32)],
        name="conv_back", flops=4 * length * local * 64, nbytes=4 * 10 * padded * local,
    )
    p0, p1, p2, p3, gproj, gbias = call(
        first_grad_kernel, 1, (meta, gq, graw, gv, triple),
        [((quarter, width), F32), ((quarter, width), F32), ((quarter, width), BF)]
        + [((quarter, width), BF), ((length, 3 * local), BF), ((8, 3 * local), F32)],
        name="first_grad", flops=2 * length * width * 3 * local, nbytes=6 * length * width,
    )
    near_own1 = to_core(p2, groups)
    near_chip1 = to_core(p3, groups)
    far_own1 = to_chip((p1 + near_chip1.astype(F32)).astype(BF), groups)
    input_grad, sums_one = call(
        first_back_kernel, 0, (p0, near_own1, far_own1, own_x, gmid, vec),
        [((quarter, width), BF), ((8, width), F32)],
        name="first_back", flops=20 * quarter * width, nbytes=20 * quarter * width,
    )
    input_grad = swap_quarters(input_grad, groups)

    glags = glag[:heads][:, None, :]
    grad_c = jnp.sum(glags * wave_c, axis=-1)
    grad_s = jnp.sum(glags * wave_s, axis=-1)
    both_waves = weight_c * wave_c + weight_s * wave_s
    turned_waves = weight_s * wave_c - weight_c * wave_s
    grad_rate = -jnp.sum(glags * place * both_waves, axis=-1) * rate[:, :, 0]
    grad_freq = jnp.sum(glags * place * turned_waves, axis=-1)
    modes_grad = jnp.concatenate([grad_rate, grad_freq, grad_c, grad_s], axis=1)

    mixed_rel = jnp.concatenate(
        [
            lax.dynamic_slice_in_dim(mixed, (q_at ^ k) * quarter, quarter, 0)
            for k in range(4)
        ],
        axis=0,
    )
    out_grad = dot_tn(jnp.concatenate(gmb, axis=0), mixed_rel)
    triple_grad = dot_tn(first, gproj)
    a_grad = jnp.concatenate([triple_grad.astype(BF), out_grad.astype(BF)], axis=1)
    vec_grad = (sums_one + sums_two)[:6]
    bias_grad = jnp.sum(gbias, axis=0).reshape(3, n_pieces, bias_cols)
    ubias_grad = jnp.sum(ubias_a + ubias_b, axis=0).reshape(n_pieces, 1, rows)

    def block_of(value, lanes):
        return jnp.pad(
            value,
            ((0, 0), (0, SMALL - value.shape[1]), (0, lanes - value.shape[2])),
        )

    small_grad = jnp.concatenate(
        [
            block_of(gtaps.reshape(n_pieces, taps_rows, local), local),
            block_of(vec_grad.reshape(6, n_pieces, rows).transpose(1, 0, 2), TILE),
            block_of(bias_grad.transpose(1, 0, 2), TILE),
            block_of(modes_grad.reshape(heads, n_pieces, mode_cols).transpose(1, 0, 2), TILE),
            block_of(ubias_grad, width - local - 3 * TILE),
        ],
        axis=2,
    )
    a_grad = jnp.concatenate(
        [a_grad.reshape(n_pieces, rows, width), small_grad.astype(BF)], axis=1
    )
    if groups == 4:
        a_grad = a_grad.reshape(groups, 2, rows + SMALL, width)
        a_sum = lax.dynamic_index_in_dim(a_grad, g, 0, False).astype(F32)
        for k in (1, 2, 3):
            sent = lax.dynamic_index_in_dim(a_grad, g ^ k, 0, False)
            a_sum = a_sum + permute(
                sent, groups, lambda g, c, z, k=k: (g ^ k, c, z)
            ).astype(F32)
        a_sum = a_sum.astype(BF)
    else:
        a_sum = lax.psum_scatter(
            a_grad.reshape(n_pieces * (rows + SMALL), width), "g", scatter_dimension=0, tiled=True
        ).reshape(2, rows + SMALL, width)
    a_out = return_pieces(a_sum, h, groups, same)
    main, tail = a_out[:rows], a_out[rows:]
    vec_out = tail[:6, local : local + rows]
    vec_out = vec_out + permute(vec_out, groups, lambda g, c, z: (g, c, z ^ 1))
    vec_out = vec_out + permute(vec_out, groups, lambda g, c, z: (g, c, z ^ 2))
    at = local + TILE
    return (
        result[None],
        input_grad[None],
        vec_out[0],
        vec_out[1],
        main[:, : 3 * local].reshape(rows, 3, local),
        tail[:3, at : at + bias_cols][:, None, :],
        tail[:taps_rows, :local].T,
        tail[:heads, at + TILE : at + TILE + mode_cols],
        main[:, 3 * local :].T,
        vec_out[2],
        vec_out[3],
        vec_out[4],
        b_out[:, :hidden],
        tail[:1, at + 2 * TILE : at + 2 * TILE + rows],
        b_out[:, hidden:].T,
        vec_out[5],
    )


def solution(mesh):
    n_data, _ = mesh.devices.shape
    groups = n_data // 2
    fine = Mesh(mesh.devices.reshape(groups, 2, 2, 2), AXES)
    dp, tensor = ("g", "c"), ("h", "b")
    return jax.shard_map(
        partial(on_device, groups),
        mesh=fine,
        in_specs=(
            P(dp, tensor, None),
            P(dp, None),
            P(),
            P(dp),
            P(dp),
            P(dp, None, tensor),
            P(None, tensor, dp),
            P(tensor, dp),
            P(tensor, dp),
            P(tensor, dp),
            P(dp),
            P(dp),
            P(dp),
            P(dp, tensor),
            P(tensor, dp),
            P(tensor, dp),
            P(dp),
            P(dp, tensor, None),
        ),
        out_specs=(
            P(dp, tensor, None),
            P(dp, tensor, None),
            P(dp),
            P(dp),
            P(dp, None, tensor),
            P(None, tensor, dp),
            P(tensor, dp),
            P(tensor, dp),
            P(tensor, dp),
            P(dp),
            P(dp),
            P(dp),
            P(dp, tensor),
            P(tensor, dp),
            P(tensor, dp),
            P(dp),
        ),
        check_vma=False,
    )
```

```python
from functools import partial

import jax
import jax.numpy as jnp
from jax import lax
from jax.experimental import pallas as pl
from jax.experimental.pallas import tpu as pltpu
from jax.sharding import Mesh
from jax.sharding import PartitionSpec as P

EPS = 1e-05
BF = jnp.bfloat16
F32 = jnp.float32
TILE = 128
BLOCK = 256
LAGS = 5
REACH = 3
LIMIT = 512
SEQUENCES = 3
GAP = 64
SMALL = 16
AXES = ("g", "c", "h", "b")
VMEM_BYTES = 56 * 1024 * 1024


def vm():
    return pl.BlockSpec(memory_space=pltpu.VMEM)


def sm():
    return pl.BlockSpec(memory_space=pltpu.SMEM)


def dot(a, b):
    return jnp.dot(a, b, preferred_element_type=F32)


def dot_nt(a, b):
    return lax.dot_general(a, b, (((1,), (1,)), ((), ())), preferred_element_type=F32)


def dot_tn(a, b):
    return lax.dot_general(a, b, (((0,), (0,)), ((), ())), preferred_element_type=F32)


FLOPS_PER_US = 1_150_000_000


def call(kernel, n_smem, args, outs, scratch=(), name=None, us=1.0):
    return pl.pallas_call(
        kernel,
        out_shape=tuple(jax.ShapeDtypeStruct(s, d) for s, d in outs),
        in_specs=[sm()] * n_smem + [vm()] * (len(args) - n_smem),
        out_specs=tuple(sm() if s == (2,) else vm() for s, _ in outs),
        scratch_shapes=[pltpu.VMEM(s, d) for s, d in scratch],
        compiler_params=pltpu.CompilerParams(vmem_limit_bytes=VMEM_BYTES),
        cost_estimate=pl.CostEstimate(
            flops=int(us * FLOPS_PER_US), bytes_accessed=0, transcendentals=0
        ),
        name=name,
    )(*args)


def norm_rows(values):
    mean = jnp.mean(values, axis=-1, keepdims=True)
    centred = values - mean
    variance = jnp.mean(centred * centred, axis=-1, keepdims=True)
    inv = lax.rsqrt(variance + EPS)
    return centred * inv, inv


def eye(n):
    rows = lax.broadcasted_iota(jnp.int32, (n, n), 0)
    return jnp.where(rows == lax.broadcasted_iota(jnp.int32, (n, n), 1), 1.0, 0.0)


def turned(values):
    return dot_nt(eye(values.shape[1]).astype(BF), values.astype(BF))


def pack_kernel(triple, out_w, up, down, taps, modes, tbias, ubias, *refs):
    vectors, (seg, a_o, b_o, box) = refs[:6], refs[6:]
    _, rows, local = triple.shape
    hidden = up.shape[1]
    for i in range(3):
        a_o[:rows, i * local : (i + 1) * local] = triple[i].astype(BF)
    box[...] = jnp.zeros_like(box)
    box[0 : taps.shape[0], 0:local] = taps[...]
    for i, vector in enumerate(vectors):
        box[8 + i : 9 + i, 0:rows] = vector[...]
    box[14:15, 0:rows] = ubias[...]
    for i in range(3):
        box[8 + i : 9 + i, 2 * TILE : 2 * TILE + tbias.shape[2]] = tbias[i]
    box[8 : 8 + modes.shape[0], 3 * TILE : 3 * TILE + modes.shape[1]] = modes[...]
    lane = lax.broadcasted_iota(jnp.int32, (1, TILE), 1)
    line = jnp.zeros((1, TILE), F32)
    for i in range(2):
        count = jnp.sum((seg[...] < i + 1).astype(F32), axis=1, keepdims=True)
        high = jnp.floor(count * (1.0 / 32))
        line = line + jnp.where(lane == 2 * i, high, 0.0)
        line = line + jnp.where(lane == 2 * i + 1, count - 32 * high, 0.0)
    box[15:16, 0:TILE] = line
    a_o[rows:, :] = box[...].astype(BF)
    b_o[:, :hidden] = up[...].astype(BF)
    b_o[:, hidden : 2 * hidden] = down[...].astype(BF)
    b_o[:, 2 * hidden :] = turned(out_w[...]).astype(BF)


def unpack(meta, order, a_refs, weights, taps_o, vec_o, modes_o, ends_o):
    g, c, h = meta[1], meta[2], meta[3]
    rows = a_refs[0].shape[1] - SMALL
    local = weights[0].shape[1]
    width = weights[0].shape[0]
    n_pieces = 2 * len(a_refs)
    bias_cols, mode_cols = local // n_pieces, TILE // n_pieces

    def spot(n_cols, wide, at):
        i = lax.broadcasted_iota(jnp.int32, (TILE, wide), 0)
        n = lax.broadcasted_iota(jnp.int32, (TILE, wide), 1)
        return jnp.where((n == i + at) & (i < n_cols), 1.0, 0.0).astype(BF)

    vec = jnp.zeros((8, width), F32)
    bias = jnp.zeros((8, local), F32)
    modes = jnp.zeros((8, TILE), F32)
    for k, ref in enumerate(a_refs):
        for j in range(2):
            d = 2 * (g ^ k) + (c ^ j)
            at = pl.multiple_of(d * rows, rows)
            for i, target in enumerate(weights):
                target[pl.ds(at, rows), :] = ref[j, :rows, i * local : (i + 1) * local]
            box = ref[j, rows:, :]
            taps_o[pl.ds(pl.multiple_of(d * 8, 8), 8), :] = box[:, :local].astype(F32)[0:8]
            low = box.astype(F32)[8:16].astype(BF)
            vec = vec + dot(low[:, :TILE], spot(rows, width, d * rows))
            bias = bias + dot(low[:, 2 * TILE : 3 * TILE], spot(bias_cols, local, d * bias_cols))
            modes = modes + dot(low[:, 3 * TILE : 4 * TILE], spot(mode_cols, TILE, d * mode_cols))
    vec_o[...] = vec
    modes_o[...] = modes
    own = 0
    for d in range(n_pieces):
        own = own + jnp.where(order[d] == 2 * g + h, d, 0)
    lane = lax.broadcasted_iota(jnp.int32, (1, width), 1)
    for i in range(2):
        scale = jnp.where(lane == own * rows + 2 * i, 32.0, 0.0)
        scale = scale + jnp.where(lane == own * rows + 2 * i + 1, 1.0, 0.0)
        ends_o[i] = jnp.sum(vec[7:8, :] * scale).astype(jnp.int32)
    return bias


def project_kernel(pieces, meta, *refs):
    if pieces > 1:
        order, refs = refs[0], refs[1:]
    x_refs, refs = refs[:4], refs[4:]
    if pieces > 1:
        a_refs, refs = refs[:pieces], refs[pieces:]
        first_o, q_o, k_o, v_o, mean_o, inv_o = refs[:6]
        weights, (taps_o, vec_ref, modes_o, ends_o) = refs[6:9], refs[9:13]
        bias = unpack(meta, order, a_refs, weights, taps_o, vec_ref, modes_o, ends_o)
        biases = [bias[i : i + 1, :] for i in range(3)]
    else:
        weights, (bias_ref, vec_ref) = refs[:3], refs[3:5]
        first_o, q_o, k_o, v_o, mean_o, inv_o = refs[5:]
        local = weights[0].shape[1]
        biases = [bias_ref[i : i + 1, :] for i in range(3)]
    quarter = x_refs[0].shape[0]
    gain, shift = vec_ref[0:1, :], vec_ref[1:2, :]
    step = 64
    for k in range(4):
        base = pl.multiple_of((meta[0] ^ k) * quarter, quarter)

        def chunk(i, _, k=k, base=base):
            at = pl.multiple_of(i * step, step)
            to = pl.ds(pl.multiple_of(base + at, step), step)
            values = x_refs[k][pl.ds(at, step), :].astype(F32)
            mean = jnp.mean(values, axis=-1, keepdims=True)
            centred = values - mean
            inv = lax.rsqrt(jnp.mean(centred * centred, axis=-1, keepdims=True) + EPS)
            mean_o[to, :] = mean
            inv_o[to, :] = inv
            first_o[to, :] = (centred * inv * gain + shift).astype(BF)
            return 0

        lax.fori_loop(0, quarter // step, chunk, 0)
        rows = first_o[pl.ds(base, quarter), :]
        for target, weight, bias in zip((q_o, k_o, v_o), weights, biases):
            target[pl.ds(base, quarter), :] = (dot(rows, weight[...]) + bias).astype(target.dtype)


def sequence_of(rows, start, stop):
    return (rows >= start).astype(jnp.int32) + (rows >= stop).astype(jnp.int32)


def spread_rows(source, target, ends, length, channels):
    for i in range(target.shape[0] // GAP):
        total = jnp.zeros((GAP, channels), F32)
        for s in range(SEQUENCES):
            j = i - s - 1
            if 0 <= j < length // GAP:
                rows = lax.broadcasted_iota(jnp.int32, (GAP, channels), 0) + j * GAP
                hit = sequence_of(rows, ends[0], ends[1]) == s
                total = total + jnp.where(hit, source[j * GAP : (j + 1) * GAP, :], 0.0)
        target[i * GAP : (i + 1) * GAP, :] = total


def gather_rows(source, target, ends, length, channels):
    for j in range(length // GAP):
        rows = lax.broadcasted_iota(jnp.int32, (GAP, channels), 0) + j * GAP
        ids = sequence_of(rows, ends[0], ends[1])
        total = jnp.zeros((GAP, channels), F32)
        for s in range(SEQUENCES):
            i = j + s + 1
            total = jnp.where(ids == s, source[i * GAP : (i + 1) * GAP, :], total)
        target[j * GAP : (j + 1) * GAP, :] = total.astype(target.dtype)


def taps_sum(pad, taps, target, sign, blocks):
    channels = target.shape[1]
    n_taps = taps.shape[0]
    reach = n_taps - 8

    def block(i, edges):
        at = pl.multiple_of((i + 1 if sign > 0 else blocks - i) * GAP, GAP)
        if sign > 0:
            window = pad[pl.ds(pl.multiple_of(at - reach, 8), GAP + reach), :]
        else:
            window = pad[pl.ds(at, GAP + reach), :]
        total, fresh = None, []
        for r in range(8):
            part = None
            for m in range(n_taps // 8):
                low = reach - 8 * m if sign > 0 else 8 * m
                term = window[low : low + GAP] * taps[8 * m + r : 8 * m + r + 1, :]
                part = term if part is None else part + term
            if r == 0:
                total = part
            elif sign > 0:
                total = total + jnp.concatenate([edges[r - 1], part], axis=0)[8 - r : 8 - r + GAP]
                fresh.append(part[GAP - 8 :])
            else:
                total = total + jnp.concatenate([part, edges[r - 1]], axis=0)[r : r + GAP]
                fresh.append(part[:8])
        target[pl.ds(at, GAP), :] = total
        return tuple(fresh)

    lax.fori_loop(0, blocks, block, tuple(jnp.zeros((8, channels), F32) for _ in range(7)))


def conv_kernel(ends, k_ref, taps, kb_o, pad_o, made):
    length, channels = k_ref.shape
    spread_rows(k_ref, pad_o, ends, length, channels)
    taps_sum(pad_o, taps, made, 1, length // GAP + SEQUENCES - 1)
    gather_rows(made, kb_o, ends, length, channels)


def conv_back_kernel(ends, gk_ref, taps, graw_o, pad_o, made):
    length, channels = gk_ref.shape
    spread_rows(gk_ref, pad_o, ends, length, channels)
    taps_sum(pad_o, taps, made, -1, length // GAP + SEQUENCES - 1)
    gather_rows(made, graw_o, ends, length, channels)


def taps_grad_kernel(grad, keys, gtaps_o):
    channels = grad.shape[1]
    n_taps = gtaps_o.shape[0]
    reach = n_taps - 8
    blocks = grad.shape[0] // GAP - 2
    for r in range(8):

        def block(i, totals, r=r):
            at = pl.multiple_of((i + 1) * GAP, GAP)
            rows = grad[pl.ds(at, GAP + 8), :][r : r + GAP]
            window = keys[pl.ds(pl.multiple_of(at - reach, 8), GAP + reach), :]
            out = []
            for m in range(n_taps // 8):
                prod = rows * window[reach - 8 * m : reach - 8 * m + GAP]
                part = prod[0:8]
                for k in range(1, GAP // 8):
                    part = part + prod[8 * k : 8 * k + 8]
                out.append(totals[m] + part)
            return tuple(out)

        zero = tuple(jnp.zeros((8, channels), F32) for _ in range(n_taps // 8))
        totals = lax.fori_loop(0, blocks, block, zero, unroll=3)
        for m in range(n_taps // 8):
            gtaps_o[8 * m + r : 8 * m + r + 1, :] = jnp.sum(totals[m], axis=0, keepdims=True)


def make_tiles(lags_ref, tiles, heads):
    for h in range(heads):
        for d in range(LAGS):
            at = TILE * (LAGS - 1 - d)
            row = jnp.broadcast_to(lags_ref[h : h + 1, at : at + 2 * TILE], (TILE, 2 * TILE))
            turned = pltpu.roll(row, TILE + 1, 1, stride=1, stride_axis=0)
            tiles[h, d, :, :] = turned[:, :TILE]


def head_masked(source, target, heads):
    length, channels = source.shape
    size = channels // heads
    for h in range(heads):
        lane = lax.broadcasted_iota(jnp.int32, (BLOCK, channels), 1)
        hit = (lane >= h * size) & (lane < (h + 1) * size)
        for a in range(length // BLOCK):
            part = source[a * BLOCK : (a + 1) * BLOCK, :]
            target[h, a, :, :] = jnp.where(hit, part, jnp.zeros_like(part))


def starts_of(ends, target):
    rows = lax.broadcasted_iota(jnp.int32, target.shape, 0)
    first = jnp.where(rows >= ends[0], ends[0], 0)
    target[...] = jnp.where(rows >= ends[1], ends[1], first)


def live_of(starts, t_at, u_at):
    lane = lax.broadcasted_iota(jnp.int32, (TILE, TILE), 1) + u_at
    return lane >= starts[t_at : t_at + TILE, :]


def mix_kernel(ends, q_ref, k_ref, v_ref, lags_ref, mixed_o, tiles_o, qm, vmask, starts, weights):
    length, local = q_ref.shape
    heads = qm.shape[0]
    make_tiles(lags_ref, tiles_o, heads)
    head_masked(q_ref, qm, heads)
    starts_of(ends, starts)
    size = local // heads
    lane = lax.broadcasted_iota(jnp.int32, (BLOCK, local), 1)
    for a in range(length // BLOCK):
        part = v_ref[a * BLOCK : (a + 1) * BLOCK, :]
        for h in range(heads):
            hit = (lane >= h * size) & (lane < (h + 1) * size)
            at = (a * heads + h) * BLOCK
            vmask[at : at + BLOCK, :] = jnp.where(hit, part, jnp.zeros_like(part))
    for a in range(length // BLOCK):
        least = max(0, a - REACH + 1)
        for s in range(least, a + 1):
            keys = k_ref[s * BLOCK : (s + 1) * BLOCK, :]
            lives = {}
            for i in range(2):
                for j in range(2):
                    d = 2 * (a - s) + i - j
                    if 0 <= d < LAGS:
                        lives[i, j] = live_of(
                            starts, a * BLOCK + i * TILE, s * BLOCK + j * TILE
                        )

            def head(h, _, a=a, s=s, keys=keys, lives=lives, least=least):
                scores = dot_nt(qm[h, a], keys)
                at = pl.multiple_of(((s - least) * heads + h) * BLOCK, BLOCK)
                for i in range(2):
                    for j in range(2):
                        where = (
                            pl.ds(i * TILE, TILE),
                            pl.ds(pl.multiple_of(at + j * TILE, TILE), TILE),
                        )
                        if (i, j) in lives:
                            factor = jnp.where(
                                lives[i, j], tiles_o[h, 2 * (a - s) + i - j], 0.0
                            )
                            piece = scores[
                                i * TILE : (i + 1) * TILE, j * TILE : (j + 1) * TILE
                            ]
                            weights[where] = (factor * piece).astype(BF)
                        else:
                            weights[where] = jnp.zeros((TILE, TILE), BF)
                return 0

            lax.fori_loop(0, heads, head, 0)
        wide = (a - least + 1) * heads * BLOCK
        mixed_o[a * BLOCK : (a + 1) * BLOCK, :] = dot(
            weights[:, :wide], vmask[least * heads * BLOCK : (a + 1) * heads * BLOCK, :]
        ).astype(BF)


def mix_back_kernel(
    meta, ends, q_ref, k_ref, v_ref, gm0, gm1, gm2, gm3, out_ref, tiles, gq_o, gk_o, gv_o, glag_o,
    gmix, qm, gmask, kmask, qt, gt, starts, grads, gkt, gvt, diag
):
    length, local = q_ref.shape
    heads = qm.shape[0]
    size = local // heads
    quarter = gm0.shape[0]
    for k, part in enumerate((gm0, gm1, gm2, gm3)):
        base = pl.multiple_of((meta[0] ^ k) * quarter, quarter)
        gmix[pl.ds(base, quarter), :] = dot(part[...], out_ref[0]).astype(BF)
    head_masked(q_ref, qm, heads)
    head_masked(gmix, gmask, heads)
    starts_of(ends, starts)
    lane = lax.broadcasted_iota(jnp.int32, (BLOCK, local), 1)
    for a in range(length // BLOCK):
        part = k_ref[a * BLOCK : (a + 1) * BLOCK, :]
        for h in range(heads):
            hit = (lane >= h * size) & (lane < (h + 1) * size)
            at = (a * heads + h) * BLOCK
            kmask[at : at + BLOCK, :] = jnp.where(hit, part, jnp.zeros_like(part))
    qt[...] = q_ref[...].astype(F32).T.astype(BF)
    gt[...] = gmix[...].astype(F32).T.astype(BF)
    gkt[...] = jnp.zeros_like(gkt)
    gvt[...] = jnp.zeros_like(gvt)
    diag[...] = jnp.zeros_like(diag)
    for a in range(length // BLOCK):
        least = max(0, a - REACH + 1)
        for s in range(least, a + 1):
            keys = k_ref[s * BLOCK : (s + 1) * BLOCK, :]
            vals = v_ref[s * BLOCK : (s + 1) * BLOCK, :]
            lives = {}
            for i in range(2):
                for j in range(2):
                    d = 2 * (a - s) + i - j
                    if 0 <= d < LAGS:
                        lives[i, j] = live_of(
                            starts, a * BLOCK + i * TILE, s * BLOCK + j * TILE
                        )

            def head(h, _, a=a, s=s, keys=keys, vals=vals, lives=lives, least=least):
                scores = dot_nt(qm[h, a], keys)
                wgrad = dot_nt(gmask[h, a], vals)
                at = pl.multiple_of(((s - least) * heads + h) * BLOCK, BLOCK)
                rows_w, rows_g = [], []
                for i in range(2):
                    line_w, line_g = [], []
                    for j in range(2):
                        if (i, j) in lives:
                            d = 2 * (a - s) + i - j
                            spot = (
                                slice(i * TILE, (i + 1) * TILE),
                                slice(j * TILE, (j + 1) * TILE),
                            )
                            factor = jnp.where(lives[i, j], tiles[h, d], 0.0)
                            line_w.append((factor * scores[spot]).astype(BF))
                            line_g.append((wgrad[spot] * factor).astype(BF))
                            diag[h, d] += jnp.where(
                                lives[i, j], wgrad[spot] * scores[spot], 0.0
                            )
                        else:
                            line_w.append(jnp.zeros((TILE, TILE), BF))
                            line_g.append(jnp.zeros((TILE, TILE), BF))
                    rows_w.append(jnp.concatenate(line_w, axis=1))
                    rows_g.append(jnp.concatenate(line_g, axis=1))
                w = jnp.concatenate(rows_w, axis=0)
                g = jnp.concatenate(rows_g, axis=0)
                grads[:, pl.ds(at, BLOCK)] = g
                band = pl.ds(pl.multiple_of(h * size, size), size)
                cols = slice(s * BLOCK, (s + 1) * BLOCK)
                gvt[band, cols] += dot(gt[band, a * BLOCK : (a + 1) * BLOCK], w)
                gkt[band, cols] += dot(qt[band, a * BLOCK : (a + 1) * BLOCK], g)
                return 0

            lax.fori_loop(0, heads, head, 0)
        wide = (a - least + 1) * heads * BLOCK
        gq_o[a * BLOCK : (a + 1) * BLOCK, :] = dot(
            grads[:, :wide], kmask[least * heads * BLOCK : (a + 1) * heads * BLOCK, :]
        ).astype(BF)
    gk_o[...] = gkt[...].T
    gv_o[...] = gvt[...].T.astype(BF)
    glag_o[...] = jnp.zeros_like(glag_o)
    for h in range(heads):
        for d in range(LAGS):
            total = jnp.concatenate([diag[h, d], jnp.zeros((TILE, TILE), F32)], axis=1)
            rows = TILE
            while rows > 1:
                rows //= 2
                total = pltpu.roll(total[:rows], rows, 1) + total[rows : 2 * rows]
            at = TILE * (LAGS - 1 - d)
            glag_o[h : h + 1, at : at + 2 * TILE] += total


ROOT_HALF = 0.7071067811865476
PHI_SCALE = 0.3989422804014327


def mlp_kernel(ks, keep, meta, *refs):
    x_refs, g_refs, mixed = refs[0:2], refs[2:4], refs[4:8]
    vec, both = refs[8:10]
    ins = refs[10:-10]
    second_o, act_o, gpre_o, ga_o, gb_o, ubias_o, extra_o, pre, agrad, mid = refs[-10:]
    out_ref = ins[0] if keep else extra_o
    if not keep and len(ins) == 1:
        out_ref[...] = ins[0][...]
    elif not keep:
        g = meta[1]
        rows = ins[0].shape[2]
        for k, ref in enumerate(ins):
            for j in range(2):
                at = pl.multiple_of((2 * (g ^ k) + j) * rows, rows)
                for i in range(4):
                    out_ref[i, pl.ds(at, rows), :] = ref[i, j]
    quarter, width = x_refs[0].shape
    hidden = both.shape[1] // 2
    step = 64
    ubias_o[...] = jnp.zeros_like(ubias_o)
    for n, k in enumerate(ks):
        base = pl.multiple_of((meta[0] ^ k) * quarter, quarter)
        total = x_refs[n][...].astype(F32) + vec[2:3, :]
        for i, m in enumerate(mixed):
            total = total + dot_nt(m[pl.ds(base, quarter), :], out_ref[i])
        mid[...] = total
        if keep and n == 0:
            extra_o[...] = total

        def normed_chunk(i, _, n=n):
            at = pl.multiple_of(i * step, step)
            normed, _inv = norm_rows(mid[pl.ds(at, step), :])
            second_o[pl.ds(pl.multiple_of(n * quarter + at, step), step), :] = (
                normed * vec[3:4, :] + vec[4:5, :]
            ).astype(BF)
            return 0

        lax.fori_loop(0, quarter // step, normed_chunk, 0)
        pre[...] = dot(second_o[n * quarter : (n + 1) * quarter, :], both[:, :hidden])
        agrad[...] = dot(g_refs[n][...], both[:, hidden:])

        def act_chunk(i, total, n=n):
            at = pl.multiple_of(i * 32, 32)
            to = pl.multiple_of(n * quarter + at, 32)
            v = pre[pl.ds(at, 32), :] + vec[6:7, :]
            cdf = 0.5 + 0.5 * lax.erf(v * ROOT_HALF)
            act_o[pl.ds(to, 32), :] = (v * cdf).astype(BF)
            slope = cdf + v * (PHI_SCALE * jnp.exp(-0.5 * v * v))
            grad = (slope * agrad[pl.ds(at, 32), :]).astype(BF)
            gpre_o[pl.ds(to, 32), :] = grad
            wide = grad.astype(F32)
            return total + ((wide[0:8] + wide[8:16]) + (wide[16:24] + wide[24:32]))

        total = lax.fori_loop(0, quarter // 32, act_chunk, jnp.zeros((8, hidden), F32))
        ubias_o[...] += total
        part = dot_nt(gpre_o[n * quarter : (n + 1) * quarter, :], both[:, :hidden])
        target = (ga_o, gb_o)[n]
        target[...] = part.astype(target.dtype)


def folded(values):
    parts = [values[i : i + 8] for i in range(0, values.shape[0], 8)]
    while len(parts) > 1:
        parts = [sum(parts[i : i + 2]) for i in range(0, len(parts), 2)]
    return parts[0]


def middle_back_kernel(part, near, far, cot, middle, vec, gmid_o, gmb_o, sums_o):
    rows, width = middle.shape
    step = 64

    def chunk(i, totals):
        at = pl.multiple_of(i * step, step)
        spot = pl.ds(at, step)
        up = part[spot, :] + near[spot, :].astype(F32) + far[spot, :].astype(F32)
        normed, inv = norm_rows(middle[spot, :])
        cotangent = cot[spot, :].astype(F32)
        e = up * vec[3:4, :]
        mean_e = jnp.mean(e, axis=-1, keepdims=True)
        mean_x = jnp.mean(e * normed, axis=-1, keepdims=True)
        grad = cotangent + inv * (e - mean_e - normed * mean_x)
        gmid_o[spot, :] = grad
        gmb_o[spot, :] = grad.astype(BF)
        terms = (grad, up * normed, up, cotangent)
        return tuple(t + folded(x) for t, x in zip(totals, terms))

    totals = lax.fori_loop(
        0, rows // step, chunk, tuple(jnp.zeros((8, width), F32) for _ in range(4))
    )
    sums_o[...] = jnp.zeros_like(sums_o)
    for i, t in enumerate(totals):
        sums_o[2 + i : 3 + i, :] = jnp.sum(t, axis=0, keepdims=True)


def first_back_kernel(meta, part, near, far, tokens, gmid, vec, mean_ref, inv_ref, grad_o):
    rows, width = tokens.shape
    step = 64
    base = pl.multiple_of(meta[0] * rows, rows)

    def chunk(i, _):
        at = pl.multiple_of(i * step, step)
        spot = pl.ds(at, step)
        stat = pl.ds(pl.multiple_of(base + at, step), step)
        up = part[spot, :] + near[spot, :].astype(F32) + far[spot, :].astype(F32)
        inv = inv_ref[stat, :]
        normed = (tokens[spot, :].astype(F32) - mean_ref[stat, :]) * inv
        e = up * vec[0:1, :]
        mean_e = jnp.mean(e, axis=-1, keepdims=True)
        mean_x = jnp.mean(e * normed, axis=-1, keepdims=True)
        grad_o[spot, :] = (gmid[spot, :] + inv * (e - mean_e - normed * mean_x)).astype(BF)
        return 0

    lax.fori_loop(0, rows // step, chunk, 0)


def first_grad_kernel(
    meta, gq, gk, gv, wq, wk, wv, x0, x1, x2, x3, mean_ref, inv_ref, sums_two, *outs
):
    parts, (bias_o, made) = outs[:4], outs[4:]
    length, local = gq.shape
    quarter = length // 4
    width = wq.shape[0]
    step = 64
    for i, ref in enumerate((gq, gk, gv)):
        total = jnp.zeros((8, local), F32)
        for j in range(length // 64):
            total = total + folded(ref[64 * j : 64 * j + 64, :].astype(F32))
        bias_o[i, :, :] = total
    gains = jnp.zeros((8, width), F32)
    shifts = jnp.zeros((8, width), F32)
    for k, (target, x_ref) in enumerate(zip(parts, (x0, x1, x2, x3))):
        base = pl.multiple_of((meta[0] ^ k) * quarter, quarter)
        total = None
        for ref, weight in ((gq, wq), (gk, wk), (gv, wv)):
            term = dot_nt(ref[pl.ds(base, quarter), :], weight[...])
            total = term if total is None else total + term
        made[...] = total
        target[:quarter, :] = total.astype(target.dtype)

        def chunk(i, sums, base=base, x_ref=x_ref):
            at = pl.multiple_of(i * step, step)
            stat = pl.ds(pl.multiple_of(base + at, step), step)
            up = made[pl.ds(at, step), :]
            normed = (x_ref[pl.ds(at, step), :].astype(F32) - mean_ref[stat, :]) * inv_ref[stat, :]
            return sums[0] + folded(up * normed), sums[1] + folded(up)

        gains, shifts = lax.fori_loop(0, quarter // step, chunk, (gains, shifts))
    sums = jnp.concatenate(
        [
            jnp.sum(gains, axis=0, keepdims=True),
            jnp.sum(shifts, axis=0, keepdims=True),
            sums_two[2:8, :],
            jnp.zeros((8, width), F32),
        ],
        axis=0,
    )
    for target in (parts[1], parts[3]):
        target[quarter:, :] = sums.astype(target.dtype)


def permute(value, groups, target_of):
    pairs = []
    for g in range(groups):
        for c in range(2):
            for z in range(4):
                to = target_of(g, c, z)
                if to is not None:
                    pairs.append((g * 8 + c * 4 + z, to[0] * 8 + to[1] * 4 + to[2]))
    return lax.ppermute(value, AXES, pairs)


def swap_quarters(value, groups):
    return permute(
        value, groups, lambda g, c, z: (g, c, z) if c == z // 2 else (g, 1 - c, z ^ 2)
    )


def to_core(value, groups):
    return permute(value, groups, lambda g, c, z: (g, 1 - c, z))


def to_chip(value, groups):
    return permute(value, groups, lambda g, c, z: (g, c, z ^ 1))


def gather_group(value, groups):
    chip = to_chip(value, groups)
    core = to_core(value, groups)
    both = to_core(chip, groups)
    return value, chip, core, both


def spread_pieces(piece, groups, same):
    near = permute(
        piece, groups, lambda g, c, z: (g, c, z ^ 2) if c == z // 2 else (g, 1 - c, z)
    )
    far = permute(piece, groups, lambda g, c, z: None if c == z // 2 else (g, 1 - c, z ^ 2))
    return jnp.where(same, piece, near), jnp.where(same, near, far)


def return_pieces(pieces, half, groups, same):
    kept = lax.dynamic_index_in_dim(pieces, half, 0, False)
    sent = lax.dynamic_index_in_dim(pieces, 1 - half, 0, False)
    near = permute(
        sent, groups, lambda g, c, z: (g, 1 - c, z) if c == z // 2 else (g, c, z ^ 2)
    )
    far = permute(kept, groups, lambda g, c, z: None if c == z // 2 else (g, 1 - c, z ^ 2))
    return near.astype(F32) + jnp.where(same, kept, far).astype(F32)


def after(value, *others):
    return lax.optimization_barrier((value, *others))[0]


def pad_to(value, rows, lanes):
    return jnp.pad(value, ((0, rows - value.shape[0]), (0, lanes - value.shape[1])))


def shift_groups(value, groups, k):
    return permute(value, groups, lambda g, c, z: (g ^ k, c, z))


def send_to_groups(pieces, groups, g):
    if groups != 4:
        shape = pieces.shape
        flat = pieces.reshape(groups * 2 * shape[2], shape[3])
        total = lax.psum_scatter(flat, "g", scatter_dimension=0, tiled=True)
        return (total.reshape(shape[1:]),), ()
    sent = [lax.dynamic_index_in_dim(pieces, g ^ k, 0, False) for k in range(groups)]
    return sent, [shift_groups(sent[k], groups, k) for k in (1, 2, 3)]


def sum_of(sent, came):
    total = sent[0].astype(F32)
    for value in came:
        total = total + value.astype(F32)
    return total.astype(BF)


def plain_pack(triple, out_w, up, down, taps, modes, tbias, ubias, *rest):
    vectors, seg = rest[:6], rest[6]
    _, rows, local = triple.shape
    first_end = jnp.sum((seg[0] < 1).astype(jnp.int32))
    second_end = jnp.sum((seg[0] < 2).astype(jnp.int32))
    ends = jnp.stack([first_end // 32, first_end % 32, second_end // 32, second_end % 32])
    left = jnp.concatenate(
        [
            pad_to(taps, 8, local),
            pad_to(jnp.concatenate(vectors, axis=0), 6, local),
            pad_to(ubias, 1, local),
            pad_to(ends.astype(F32)[None], 1, local),
        ],
        axis=0,
    )
    low = jnp.concatenate([pad_to(tbias[:, 0, :], 8, TILE), pad_to(modes, 8, TILE)], axis=1)
    right = jnp.concatenate([jnp.zeros_like(low), low], axis=0)
    small = jnp.concatenate([left, jnp.zeros((SMALL, 2 * TILE - local), F32), right], axis=1)
    small = pad_to(small, SMALL, 3 * local)
    main = triple.transpose(1, 0, 2).reshape(rows, 3 * local)
    return (
        jnp.concatenate([main, small], axis=0).astype(BF),
        jnp.concatenate([up, down, out_w.T], axis=1).astype(BF),
    )


def on_device(
    groups,
    tokens,
    segments,
    row_order,
    first_gain,
    first_shift,
    triple_weight,
    triple_bias,
    shift_taps,
    kernel_modes,
    out_weight,
    out_bias,
    second_gain,
    second_shift,
    up_weight,
    up_bias,
    down_weight,
    down_bias,
    cotangent,
):
    g = lax.axis_index("g")
    c = lax.axis_index("c")
    h = lax.axis_index("h")
    b = lax.axis_index("b")
    same = c == h
    n_pieces = 2 * groups
    quarter, width = tokens.shape[1:]
    length = 4 * quarter
    rows, _, local = triple_weight.shape
    heads = kernel_modes.shape[0]
    n_modes = kernel_modes.shape[1] * n_pieces // 4
    taps_rows = shift_taps.shape[1]
    n_taps = taps_rows * n_pieces
    mode_cols = kernel_modes.shape[1]
    bias_cols = triple_bias.shape[2]
    hidden = up_weight.shape[1]
    q_at = 2 * c + b
    meta = jnp.stack([q_at, g, c, h]).astype(jnp.int32)

    own_x = swap_quarters(tokens[0], groups)
    vectors = (first_gain, first_shift, out_bias, second_gain, second_shift, down_bias)
    raw = (
        triple_weight.transpose(1, 0, 2), out_weight, up_weight, down_weight.T, shift_taps.T,
        kernel_modes, triple_bias, up_bias, *(v[None] for v in vectors), segments,
    )
    if groups == 4:
        a_piece, b_piece = call(
            pack_kernel, 0, raw,
            [((rows + SMALL, 3 * local), BF), ((rows, 2 * hidden + width // 4), BF)],
            [((SMALL, 3 * local), F32)], name="pack", us=2.2,
        )
    else:
        a_piece, b_piece = plain_pack(*raw)
    a_near, a_other = spread_pieces(after(a_piece, own_x), groups, same)
    a_pair = jnp.stack([a_near, a_other])
    x = gather_group(after(own_x, a_near), groups)
    if groups == 4:
        a_all = [a_pair] + [shift_groups(a_pair, groups, k) for k in (1, 2, 3)]
    else:
        a_all = lax.all_gather(a_pair, "g", axis=0, tiled=False)
        a_all = jnp.where(c == 0, a_all, a_all[:, ::-1]).reshape(n_pieces, rows + SMALL, 3 * local)

    lo, hi = spread_pieces(after(b_piece, x[1], x[2]), groups, same)
    first_b, second_b = jnp.where(c == 0, lo, hi), jnp.where(c == 0, hi, lo)
    b_pair = jnp.concatenate([first_b[:, : 2 * hidden], second_b[:, : 2 * hidden]], axis=0)
    both = lax.all_gather(b_pair, "g", axis=0, tiled=True)
    out_pair = jnp.stack([first_b[:, 2 * hidden :], second_b[:, 2 * hidden :]])
    out_quad = gather_group(out_pair, groups)
    out_quad = jnp.stack(out_quad)
    if groups == 4:
        out_all = [out_quad] + [shift_groups(out_quad, groups, k) for k in (1, 2, 3)]
    else:
        out_all = lax.all_gather(out_quad, "g", axis=0, tiled=False)
        out_all = [out_all.transpose(1, 0, 2, 3, 4).reshape(4, width, local)]

    own_cot = swap_quarters(after(cotangent[0], first_b), groups)
    cot = gather_group(own_cot, groups)

    made = [((length, width), BF), ((length, local), BF), ((length, local), F32)]
    made += [((length, local), BF), ((length, 1), F32), ((length, 1), F32)]
    if groups == 4:
        unpacked = [((width, local), BF)] * 3
        unpacked += [((n_taps, local), F32), ((8, width), F32), ((8, TILE), F32), ((2,), jnp.int32)]
        first, queries, raw_keys, values, mean, inv, wq, wk, wv, taps, vec, modes, ends = call(
            partial(project_kernel, 4), 2, (meta, row_order, *x, *a_all), made + unpacked,
            name="project", us=9.8,
        )
    else:
        weights = a_all[:, :rows, :].reshape(width, 3 * local)
        wq, wk, wv = (weights[:, i * local : (i + 1) * local] for i in range(3))
        small = a_all[:, rows:, :].astype(F32)
        taps = small[:, :taps_rows, :local].reshape(n_taps, local)
        vec = small[:, 8:16, :rows].transpose(1, 0, 2).reshape(8, width)
        bias = small[:, 8:16, 2 * TILE : 2 * TILE + bias_cols].transpose(1, 0, 2).reshape(8, local)
        modes = small[:, 8:16, 3 * TILE : 3 * TILE + mode_cols].transpose(1, 0, 2).reshape(8, TILE)
        mine = (row_order == 2 * g + h)[:, None]
        found = jnp.sum(jnp.where(mine, small[:, 15, :4], 0), axis=0)
        ends = jnp.stack([32 * found[0] + found[1], 32 * found[2] + found[3]]).astype(jnp.int32)
        first, queries, raw_keys, values, mean, inv = call(
            partial(project_kernel, 1), 1, (meta, *x, wq, wk, wv, bias, vec), made,
            name="project", us=9.8,
        )

    modes = modes[:heads]
    lag = LIMIT + TILE - 1 - jnp.arange(6 * TILE, dtype=jnp.int32)
    held = ((lag >= 0) & (lag < LIMIT)).astype(F32)[None, None, :]
    place = jnp.clip(lag, 0, LIMIT - 1).astype(F32)[None, None, :]
    rate = jnp.exp(modes[:, :n_modes])[:, :, None]
    phase = modes[:, n_modes : 2 * n_modes][:, :, None] * place
    decay = jnp.exp(-rate * place) * held
    wave_c, wave_s = decay * jnp.cos(phase), decay * jnp.sin(phase)
    weight_c = modes[:, 2 * n_modes : 3 * n_modes][:, :, None]
    weight_s = modes[:, 3 * n_modes :][:, :, None]
    lags = jnp.sum(weight_c * wave_c + weight_s * wave_s, axis=1)

    padded = length + (SEQUENCES + 1) * GAP
    n_blocks = length // BLOCK
    keys, key_rows = call(
        conv_kernel, 1, (ends, after(raw_keys, own_cot, out_quad), taps),
        [((length, local), BF), ((padded, local), F32)], [((padded, local), F32)],
        name="conv", us=9,
    )
    per_head = (heads, n_blocks, BLOCK, local)
    stacked = (n_blocks * heads * BLOCK, local)
    mixed, tiles = call(
        mix_kernel, 1, (ends, queries, after(keys, cot[1], *out_all[1:]), values, lags),
        [((length, local), BF), ((heads, LAGS, TILE, TILE), F32)],
        [
            (per_head, BF), (stacked, BF), ((length, TILE), jnp.int32),
            ((BLOCK, REACH * heads * BLOCK), BF),
        ],
        name="mix", us=11.6,
    )
    mixes = gather_group(mixed, groups)

    half_out = [((2 * quarter, width), BF), ((2 * quarter, hidden), BF), ((2 * quarter, hidden), BF)]
    scratch = [((quarter, hidden), F32), ((quarter, hidden), F32), ((quarter, width), F32)]
    shared = (*mixes, vec, both)
    second_b, act_b, gpre_b, gsec_c, gsec_d, ubias_b, outs = call(
        partial(mlp_kernel, (2, 3), False), 1,
        (meta, x[2], x[3], cot[2], cot[3], *shared, *out_all),
        half_out + [((quarter, width), BF), ((quarter, width), BF), ((8, hidden), F32)]
        + [((4, width, local), BF)],
        scratch, name="mlp_far", us=11.6,
    )
    near_own = to_core(gsec_c, groups)
    near_chip = to_core(gsec_d, groups)
    second_a, act_a, gpre_a, gsec_a, gsec_b, ubias_a, middle = call(
        partial(mlp_kernel, (0, 1), True), 1, (meta, x[0], x[1], cot[0], cot[1], *shared, outs),
        half_out
        + [((quarter, width), F32), ((quarter, width), F32), ((8, hidden), F32)]
        + [((quarter, width), F32)],
        scratch, name="mlp_near", us=12,
    )
    far_own = to_chip((gsec_b + near_chip.astype(F32)).astype(BF), groups)
    gmid, gmb_own, sums_two = call(
        middle_back_kernel, 0, (gsec_a, near_own, far_own, own_cot, middle, vec),
        [((quarter, width), F32), ((quarter, width), BF), ((8, width), F32)],
        name="middle_back", us=4,
    )
    gmb = gather_group(gmb_own, groups)

    act = jnp.concatenate([act_a, act_b], axis=0)
    gpre = jnp.concatenate([gpre_a, gpre_b], axis=0)
    second = jnp.concatenate([second_a, second_b], axis=0)
    cot_all = jnp.concatenate(cot, axis=0)
    down_part = both[:, hidden:]
    up_grad = dot_tn(second, gpre)
    down_grad = dot_tn(cot_all, act)
    b_shape = (groups, 1, 2 * rows, hidden)
    b_grad = jnp.concatenate(
        [up_grad.astype(BF).reshape(b_shape), down_grad.astype(BF).reshape(b_shape)], axis=1
    ).reshape(groups * 4 * rows, hidden)
    share_far = dot_nt(after(act_b, b_grad), down_part).astype(BF)
    b_sum = lax.psum_scatter(b_grad, "g", scatter_dimension=0, tiled=True)
    b_sum = b_sum.reshape(2, 2, rows, hidden).transpose(1, 0, 2, 3)
    share = dot_nt(act_a, down_part)
    share_near = to_core(share_far, groups).astype(F32)
    share_chip = to_chip((share[quarter:] + share_near[quarter:]).astype(BF), groups)
    result = (
        middle + share[:quarter] + share_near[:quarter] + share_chip.astype(F32) + vec[5:6, :]
    ).astype(BF)

    gq, gk, gv, glag = call(
        mix_back_kernel, 2,
        (meta, ends, after(queries, b_grad, share_far, share), keys, values, *gmb, outs, tiles),
        [
            ((length, local), BF), ((length, local), F32), ((length, local), BF),
            ((8, 6 * TILE), F32),
        ],
        [
            ((length, local), BF), (per_head, BF), (per_head, BF), (stacked, BF),
            ((local, length), BF), ((local, length), BF), ((length, TILE), jnp.int32),
            ((BLOCK, REACH * heads * BLOCK), BF), ((local, length), F32), ((local, length), F32),
            ((heads, LAGS, TILE, TILE), F32),
        ],
        name="mix_back", us=21,
    )

    mixed_rel = jnp.concatenate(
        [lax.dynamic_slice_in_dim(mixed, (q_at ^ k) * quarter, quarter, 0) for k in range(4)],
        axis=0,
    )
    out_grad = dot_tn(jnp.concatenate(gmb, axis=0), mixed_rel)
    early = jnp.concatenate(
        [dot_tn(first, gq).astype(BF), dot_tn(first, gv).astype(BF), out_grad.astype(BF)], axis=1
    )

    graw, grad_rows = call(
        conv_back_kernel, 1, (ends, after(gk, result, early), taps),
        [((length, local), BF), ((padded, local), F32)], [((padded, local), F32)],
        name="conv_back", us=8.7,
    )
    early = lax.psum_scatter(after(early, b_sum), "g", scatter_dimension=0, tiled=True)
    result = swap_quarters(result, groups)
    p0, p1, p2, p3, gbias = call(
        first_grad_kernel, 1,
        (meta, gq, after(graw, result), gv, wq, wk, wv, *x, mean, inv, sums_two),
        [((quarter, width), F32), ((quarter + SMALL, width), F32), ((quarter, width), BF)]
        + [((quarter + SMALL, width), BF), ((3, 8, local), F32)],
        [((quarter, width), F32)],
        name="first_grad", us=8.8,
    )
    near_chip1 = to_core(p3, groups)
    near_own1 = to_core(p2, groups)
    far_share = p1 + near_chip1.astype(F32)
    far_sent = far_share.astype(BF)
    far_own1 = to_chip(far_sent, groups)
    b_out = return_pieces(after(b_sum, far_sent), h, groups, same)
    (gtaps,) = call(
        taps_grad_kernel, 0, (grad_rows, after(key_rows, far_sent)), [((n_taps, local), F32)],
        name="taps_grad", us=11.8,
    )
    key_grad = dot_tn(first, after(graw, far_sent)).astype(BF)
    (input_grad,) = call(
        first_back_kernel, 1,
        (meta, after(p0, gtaps, key_grad, b_out), near_own1, far_own1, own_x, gmid, vec, mean, inv),
        [((quarter, width), BF)], name="first_back", us=3.6,
    )
    vec_grad = far_share[quarter : quarter + 6] + far_own1[quarter : quarter + 6].astype(F32)
    vec_grad = after(vec_grad, input_grad)
    input_grad = swap_quarters(input_grad, groups)

    glags = glag[:heads][:, None, :]
    grad_c = jnp.sum(glags * wave_c, axis=-1)
    grad_s = jnp.sum(glags * wave_s, axis=-1)
    both_waves = weight_c * wave_c + weight_s * wave_s
    turned_waves = weight_s * wave_c - weight_c * wave_s
    grad_rate = -jnp.sum(glags * place * both_waves, axis=-1) * rate[:, :, 0]
    grad_freq = jnp.sum(glags * place * turned_waves, axis=-1)
    modes_grad = jnp.concatenate([grad_rate, grad_freq, grad_c, grad_s], axis=1)

    key_grad = key_grad.reshape(n_pieces, rows, local)
    vec_grad = vec_grad.reshape(6, n_pieces, rows).transpose(1, 0, 2)
    ubias_grad = jnp.sum(ubias_a + ubias_b, axis=0).reshape(n_pieces, 1, rows)
    modes_grad = modes_grad.reshape(heads, n_pieces, mode_cols).transpose(1, 0, 2)
    bias_grad = jnp.sum(gbias, axis=1).reshape(3, n_pieces, bias_cols).transpose(1, 0, 2)

    def block_of(value, n_rows, lanes):
        shape = value.shape
        return jnp.pad(value, ((0, 0), (0, n_rows - shape[1]), (0, lanes - shape[2])))

    low_left = block_of(jnp.concatenate([vec_grad, ubias_grad], axis=1), 8, TILE)
    low_right = block_of(bias_grad, 4, local - TILE) + jnp.pad(
        modes_grad, ((0, 0), (0, 4 - heads), (local - TILE - mode_cols, 0))
    )
    low = jnp.concatenate([low_left, block_of(low_right, 8, local - TILE)], axis=2)
    small_grad = jnp.concatenate(
        [block_of(gtaps.reshape(n_pieces, taps_rows, local), 8, local), low], axis=1
    )
    late = jnp.concatenate([key_grad, small_grad.astype(BF)], axis=1)
    late = sum_of(*send_to_groups(late.reshape(groups, 2, rows + SMALL, local), groups, g))
    early = jnp.pad(early.reshape(2, rows, 3 * local), ((0, 0), (0, SMALL), (0, 0)))
    a_out = return_pieces(jnp.concatenate([early, late], axis=2), h, groups, same)
    main, tail = a_out[:rows], a_out[rows:, 3 * local :]
    return (
        result[None],
        input_grad[None],
        tail[8, :rows],
        tail[9, :rows],
        jnp.stack(
            [main[:, :local], main[:, 3 * local :], main[:, local : 2 * local]], axis=0
        ).transpose(1, 0, 2),
        tail[8:11, TILE : TILE + bias_cols][:, None, :],
        tail[:taps_rows].T,
        tail[8 : 8 + heads, local - mode_cols :],
        main[:, 2 * local : 3 * local].T,
        tail[10, :rows],
        tail[11, :rows],
        tail[12, :rows],
        b_out[0],
        tail[14:15, :rows],
        b_out[1].T,
        tail[13, :rows],
    )


def solution(mesh):
    n_data, _ = mesh.devices.shape
    groups = n_data // 2
    fine = Mesh(mesh.devices.reshape(groups, 2, 2, 2), AXES)
    dp, tensor = ("g", "c"), ("h", "b")
    return jax.shard_map(
        partial(on_device, groups),
        mesh=fine,
        in_specs=(
            P(dp, tensor, None),
            P(dp, None),
            P(),
            P(dp),
            P(dp),
            P(dp, None, tensor),
            P(None, tensor, dp),
            P(tensor, dp),
            P(tensor, dp),
            P(tensor, dp),
            P(dp),
            P(dp),
            P(dp),
            P(dp, tensor),
            P(tensor, dp),
            P(tensor, dp),
            P(dp),
            P(dp, tensor, None),
        ),
        out_specs=(
            P(dp, tensor, None),
            P(dp, tensor, None),
            P(dp),
            P(dp),
            P(dp, None, tensor),
            P(None, tensor, dp),
            P(tensor, dp),
            P(tensor, dp),
            P(tensor, dp),
            P(dp),
            P(dp),
            P(dp),
            P(dp, tensor),
            P(tensor, dp),
            P(tensor, dp),
            P(dp),
        ),
        check_vma=False,
    )
```

```python
from functools import partial

import jax
import jax.numpy as jnp
from jax import lax
from jax.experimental import pallas as pl
from jax.experimental.pallas import tpu as pltpu
from jax.sharding import Mesh
from jax.sharding import PartitionSpec as P

EPS = 1e-05
BF = jnp.bfloat16
F32 = jnp.float32
TILE = 128
BLOCK = 256
LAGS = 5
REACH = 3
LIMIT = 512
SEQUENCES = 3
GAP = 64
SMALL = 16
AXES = ("g", "c", "h", "b")
VMEM_BYTES = 56 * 1024 * 1024


def vm():
    return pl.BlockSpec(memory_space=pltpu.VMEM)


def sm():
    return pl.BlockSpec(memory_space=pltpu.SMEM)


def dot(a, b):
    return jnp.dot(a, b, preferred_element_type=F32)


def dot_nt(a, b):
    return lax.dot_general(a, b, (((1,), (1,)), ((), ())), preferred_element_type=F32)


def dot_tn(a, b):
    return lax.dot_general(a, b, (((0,), (0,)), ((), ())), preferred_element_type=F32)


FLOPS_PER_US = 1_150_000_000


def call(kernel, n_smem, args, outs, scratch=(), name=None, us=1.0):
    return pl.pallas_call(
        kernel,
        out_shape=tuple(jax.ShapeDtypeStruct(s, d) for s, d in outs),
        in_specs=[sm()] * n_smem + [vm()] * (len(args) - n_smem),
        out_specs=tuple(sm() if s == (2,) else vm() for s, _ in outs),
        scratch_shapes=[pltpu.VMEM(s, d) for s, d in scratch],
        compiler_params=pltpu.CompilerParams(vmem_limit_bytes=VMEM_BYTES),
        cost_estimate=pl.CostEstimate(
            flops=int(us * FLOPS_PER_US), bytes_accessed=0, transcendentals=0
        ),
        name=name,
    )(*args)


def norm_rows(values):
    mean = jnp.mean(values, axis=-1, keepdims=True)
    centred = values - mean
    variance = jnp.mean(centred * centred, axis=-1, keepdims=True)
    inv = lax.rsqrt(variance + EPS)
    return centred * inv, inv


def folded(values):
    parts = [values[i : i + 8] for i in range(0, values.shape[0], 8)]
    while len(parts) > 1:
        parts = [sum(parts[i : i + 2]) for i in range(0, len(parts), 2)]
    return parts[0]


def eye(n):
    rows = lax.broadcasted_iota(jnp.int32, (n, n), 0)
    return jnp.where(rows == lax.broadcasted_iota(jnp.int32, (n, n), 1), 1.0, 0.0)


def turned(values):
    return dot_nt(eye(values.shape[1]).astype(BF), values.astype(BF))


def pack_kernel(triple, out_w, up, down, taps, modes, tbias, ubias, *refs):
    vectors, (seg, a_o, b_o, box) = refs[:6], refs[6:]
    _, rows, local = triple.shape
    hidden = up.shape[1]
    for i in range(3):
        a_o[:rows, i * local : (i + 1) * local] = triple[i].astype(BF)
    box[...] = jnp.zeros_like(box)
    box[0 : taps.shape[0], 0:local] = taps[...]
    for i, vector in enumerate(vectors):
        box[8 + i : 9 + i, 0:rows] = vector[...]
    box[14:15, 0:rows] = ubias[...]
    for i in range(3):
        box[8 + i : 9 + i, 2 * TILE : 2 * TILE + tbias.shape[2]] = tbias[i]
    box[8 : 8 + modes.shape[0], 3 * TILE : 3 * TILE + modes.shape[1]] = modes[...]
    lane = lax.broadcasted_iota(jnp.int32, (1, TILE), 1)
    line = jnp.zeros((1, TILE), F32)
    for i in range(2):
        count = jnp.sum((seg[...] < i + 1).astype(F32), axis=1, keepdims=True)
        high = jnp.floor(count * (1.0 / 32))
        line = line + jnp.where(lane == 2 * i, high, 0.0)
        line = line + jnp.where(lane == 2 * i + 1, count - 32 * high, 0.0)
    box[15:16, 0:TILE] = line
    a_o[rows:, :] = box[...].astype(BF)
    b_o[:, :hidden] = up[...].astype(BF)
    b_o[:, hidden : 2 * hidden] = down[...].astype(BF)
    b_o[:, 2 * hidden :] = turned(out_w[...]).astype(BF)


def unpack(meta, order, a_refs, weights, taps_o, vec_o, modes_o, ends_o):
    g, c, h = meta[1], meta[2], meta[3]
    rows = a_refs[0].shape[1] - SMALL
    local = weights[0].shape[1]
    width = weights[0].shape[0]
    n_pieces = 2 * len(a_refs)
    bias_cols, mode_cols = local // n_pieces, TILE // n_pieces

    def spot(n_cols, wide, at):
        i = lax.broadcasted_iota(jnp.int32, (TILE, wide), 0)
        n = lax.broadcasted_iota(jnp.int32, (TILE, wide), 1)
        return jnp.where((n == i + at) & (i < n_cols), 1.0, 0.0).astype(BF)

    vec = jnp.zeros((8, width), F32)
    bias = jnp.zeros((8, local), F32)
    modes = jnp.zeros((8, TILE), F32)
    for k, ref in enumerate(a_refs):
        for j in range(2):
            d = 2 * (g ^ k) + (c ^ j)
            at = pl.multiple_of(d * rows, rows)
            for i, target in enumerate(weights):
                target[pl.ds(at, rows), :] = ref[j, :rows, i * local : (i + 1) * local]
            box = ref[j, rows:, :]
            taps_o[pl.ds(pl.multiple_of(d * 8, 8), 8), :] = box[:, :local].astype(F32)[0:8]
            low = box.astype(F32)[8:16].astype(BF)
            vec = vec + dot(low[:, :TILE], spot(rows, width, d * rows))
            bias = bias + dot(low[:, 2 * TILE : 3 * TILE], spot(bias_cols, local, d * bias_cols))
            modes = modes + dot(low[:, 3 * TILE : 4 * TILE], spot(mode_cols, TILE, d * mode_cols))
    vec_o[...] = vec
    modes_o[...] = modes
    own = 0
    for d in range(n_pieces):
        own = own + jnp.where(order[d] == 2 * g + h, d, 0)
    lane = lax.broadcasted_iota(jnp.int32, (1, width), 1)
    for i in range(2):
        scale = jnp.where(lane == own * rows + 2 * i, 32.0, 0.0)
        scale = scale + jnp.where(lane == own * rows + 2 * i + 1, 1.0, 0.0)
        ends_o[i] = jnp.sum(vec[7:8, :] * scale).astype(jnp.int32)
    return bias


def project_kernel(pieces, meta, *refs):
    if pieces > 1:
        order, refs = refs[0], refs[1:]
    x_refs, refs = refs[:4], refs[4:]
    if pieces > 1:
        a_refs, refs = refs[:pieces], refs[pieces:]
        first_o, q_o, k_o, v_o, mean_o, inv_o = refs[:6]
        weights, (taps_o, vec_ref, modes_o, ends_o) = refs[6:9], refs[9:13]
        bias = unpack(meta, order, a_refs, weights, taps_o, vec_ref, modes_o, ends_o)
        biases = [bias[i : i + 1, :] for i in range(3)]
    else:
        weights, (bias_ref, vec_ref) = refs[:3], refs[3:5]
        first_o, q_o, k_o, v_o, mean_o, inv_o = refs[5:]
        local = weights[0].shape[1]
        biases = [bias_ref[i : i + 1, :] for i in range(3)]
    quarter = x_refs[0].shape[0]
    gain, shift = vec_ref[0:1, :], vec_ref[1:2, :]
    step = 64
    for k in range(4):
        base = pl.multiple_of((meta[0] ^ k) * quarter, quarter)

        def chunk(i, _, k=k, base=base):
            at = pl.multiple_of(i * step, step)
            to = pl.ds(pl.multiple_of(base + at, step), step)
            values = x_refs[k][pl.ds(at, step), :].astype(F32)
            mean = jnp.mean(values, axis=-1, keepdims=True)
            centred = values - mean
            inv = lax.rsqrt(jnp.mean(centred * centred, axis=-1, keepdims=True) + EPS)
            mean_o[to, :] = mean
            inv_o[to, :] = inv
            first_o[to, :] = (centred * inv * gain + shift).astype(BF)
            return 0

        lax.fori_loop(0, quarter // step, chunk, 0, unroll=True)
        rows = first_o[pl.ds(base, quarter), :]
        for target, weight, bias in zip((q_o, k_o, v_o), weights, biases):
            target[pl.ds(base, quarter), :] = (dot(rows, weight[...]) + bias).astype(target.dtype)


def sequence_of(rows, start, stop):
    return (rows >= start).astype(jnp.int32) + (rows >= stop).astype(jnp.int32)


def spread_rows(source, target, ends, length, channels):
    for i in range(target.shape[0] // GAP):
        total = jnp.zeros((GAP, channels), F32)
        for s in range(SEQUENCES):
            j = i - s - 1
            if 0 <= j < length // GAP:
                rows = lax.broadcasted_iota(jnp.int32, (GAP, channels), 0) + j * GAP
                hit = sequence_of(rows, ends[0], ends[1]) == s
                total = total + jnp.where(hit, source[j * GAP : (j + 1) * GAP, :], 0.0)
        target[i * GAP : (i + 1) * GAP, :] = total


def gather_rows(source, target, ends, length, channels):
    for j in range(length // GAP):
        rows = lax.broadcasted_iota(jnp.int32, (GAP, channels), 0) + j * GAP
        ids = sequence_of(rows, ends[0], ends[1])
        total = jnp.zeros((GAP, channels), F32)
        for s in range(SEQUENCES):
            i = j + s + 1
            total = jnp.where(ids == s, source[i * GAP : (i + 1) * GAP, :], total)
        target[j * GAP : (j + 1) * GAP, :] = total.astype(target.dtype)


def taps_sum(pad, taps, target, sign, blocks):
    channels = target.shape[1]
    n_taps = taps.shape[0]
    reach = n_taps - 8

    def block(i, edges):
        at = pl.multiple_of((i + 1 if sign > 0 else blocks - i) * GAP, GAP)
        if sign > 0:
            window = pad[pl.ds(pl.multiple_of(at - reach, 8), GAP + reach), :]
        else:
            window = pad[pl.ds(at, GAP + reach), :]
        total, fresh = None, []
        for r in range(8):
            part = None
            for m in range(n_taps // 8):
                low = reach - 8 * m if sign > 0 else 8 * m
                term = window[low : low + GAP] * taps[8 * m + r : 8 * m + r + 1, :]
                part = term if part is None else part + term
            if r == 0:
                total = part
            elif sign > 0:
                total = total + jnp.concatenate([edges[r - 1], part], axis=0)[8 - r : 8 - r + GAP]
                fresh.append(part[GAP - 8 :])
            else:
                total = total + jnp.concatenate([part, edges[r - 1]], axis=0)[r : r + GAP]
                fresh.append(part[:8])
        target[pl.ds(at, GAP), :] = total
        return tuple(fresh)

    lax.fori_loop(0, blocks, block, tuple(jnp.zeros((8, channels), F32) for _ in range(7)), unroll=2)


def conv_kernel(ends, k_ref, taps, kb_o, pad_o, made):
    length, channels = k_ref.shape
    spread_rows(k_ref, pad_o, ends, length, channels)
    taps_sum(pad_o, taps, made, 1, length // GAP + SEQUENCES - 1)
    gather_rows(made, kb_o, ends, length, channels)


def conv_back_kernel(ends, gk_ref, taps, graw_o, pad_o, made):
    length, channels = gk_ref.shape
    spread_rows(gk_ref, pad_o, ends, length, channels)
    taps_sum(pad_o, taps, made, -1, length // GAP + SEQUENCES - 1)
    gather_rows(made, graw_o, ends, length, channels)


def taps_grad_kernel(grad, keys, gtaps_o, sums):
    n_taps = gtaps_o.shape[0]
    reach = n_taps - 8
    sums[...] = jnp.zeros_like(sums)

    def block(i, _):
        at = pl.multiple_of((i + 1) * GAP, GAP)
        window = keys[pl.ds(pl.multiple_of(at - reach, 8), GAP + reach), :]
        rows = grad[pl.ds(at, GAP + 8), :]
        for r in range(8):
            turned_rows = pltpu.roll(rows, (GAP + 8 - r) % (GAP + 8), 0)[:GAP]
            for m in range(n_taps // 8):
                low = reach - 8 * m
                sums[8 * m + r, :, :] += folded(turned_rows * window[low : low + GAP])
        return 0

    lax.fori_loop(0, grad.shape[0] // GAP - 2, block, 0, unroll=2)
    gtaps_o[...] = jnp.sum(sums[...], axis=1)


def make_tiles(lags_ref, tiles, heads):
    for h in range(heads):
        for d in range(LAGS):
            at = TILE * (LAGS - 1 - d)
            row = jnp.broadcast_to(lags_ref[h : h + 1, at : at + 2 * TILE], (TILE, 2 * TILE))
            turned = pltpu.roll(row, TILE + 1, 1, stride=1, stride_axis=0)
            tiles[h, d, :, :] = turned[:, :TILE]


def head_masked(source, target, heads):
    length, channels = source.shape
    size = channels // heads
    for h in range(heads):
        lane = lax.broadcasted_iota(jnp.int32, (BLOCK, channels), 1)
        hit = (lane >= h * size) & (lane < (h + 1) * size)
        for a in range(length // BLOCK):
            part = source[a * BLOCK : (a + 1) * BLOCK, :]
            target[h, a, :, :] = jnp.where(hit, part, jnp.zeros_like(part))


def starts_of(ends, target):
    rows = lax.broadcasted_iota(jnp.int32, target.shape, 0)
    first = jnp.where(rows >= ends[0], ends[0], 0)
    target[...] = jnp.where(rows >= ends[1], ends[1], first)


def live_of(starts, t_at, u_at):
    lane = lax.broadcasted_iota(jnp.int32, (TILE, TILE), 1) + u_at
    return lane >= starts[t_at : t_at + TILE, :]


def mix_kernel(ends, q_ref, k_ref, v_ref, lags_ref, mixed_o, tiles_o, qm, vmask, starts, weights):
    length, local = q_ref.shape
    heads = qm.shape[0]
    make_tiles(lags_ref, tiles_o, heads)
    head_masked(q_ref, qm, heads)
    starts_of(ends, starts)
    size = local // heads
    lane = lax.broadcasted_iota(jnp.int32, (BLOCK, local), 1)
    for a in range(length // BLOCK):
        part = v_ref[a * BLOCK : (a + 1) * BLOCK, :]
        for h in range(heads):
            hit = (lane >= h * size) & (lane < (h + 1) * size)
            at = (a * heads + h) * BLOCK
            vmask[at : at + BLOCK, :] = jnp.where(hit, part, jnp.zeros_like(part))
    for a in range(length // BLOCK):
        least = max(0, a - REACH + 1)
        for s in range(least, a + 1):
            keys = k_ref[s * BLOCK : (s + 1) * BLOCK, :]
            lives = {}
            for i in range(2):
                for j in range(2):
                    d = 2 * (a - s) + i - j
                    if 0 <= d < LAGS:
                        lives[i, j] = live_of(
                            starts, a * BLOCK + i * TILE, s * BLOCK + j * TILE
                        )

            def head(h, _, a=a, s=s, keys=keys, lives=lives, least=least):
                scores = dot_nt(qm[h, a], keys)
                at = pl.multiple_of(((s - least) * heads + h) * BLOCK, BLOCK)
                for i in range(2):
                    for j in range(2):
                        where = (
                            pl.ds(i * TILE, TILE),
                            pl.ds(pl.multiple_of(at + j * TILE, TILE), TILE),
                        )
                        if (i, j) in lives:
                            factor = jnp.where(
                                lives[i, j], tiles_o[h, 2 * (a - s) + i - j], 0.0
                            )
                            piece = scores[
                                i * TILE : (i + 1) * TILE, j * TILE : (j + 1) * TILE
                            ]
                            weights[where] = (factor * piece).astype(BF)
                        else:
                            weights[where] = jnp.zeros((TILE, TILE), BF)
                return 0

            lax.fori_loop(0, heads, head, 0, unroll=True)
        wide = (a - least + 1) * heads * BLOCK
        mixed_o[a * BLOCK : (a + 1) * BLOCK, :] = dot(
            weights[:, :wide], vmask[least * heads * BLOCK : (a + 1) * heads * BLOCK, :]
        ).astype(BF)


def mix_back_kernel(
    meta, ends, q_ref, k_ref, v_ref, gm0, gm1, gm2, gm3, out_ref, tiles, gq_o, gk_o, gv_o, glag_o,
    gmix, qm, gmask, kmask, qt, gt, starts, grads, gkt, gvt, diag
):
    length, local = q_ref.shape
    heads = qm.shape[0]
    size = local // heads
    quarter = gm0.shape[0]
    for k, part in enumerate((gm0, gm1, gm2, gm3)):
        base = pl.multiple_of((meta[0] ^ k) * quarter, quarter)
        gmix[pl.ds(base, quarter), :] = dot(part[...], out_ref[0]).astype(BF)
    head_masked(q_ref, qm, heads)
    head_masked(gmix, gmask, heads)
    starts_of(ends, starts)
    lane = lax.broadcasted_iota(jnp.int32, (BLOCK, local), 1)
    for a in range(length // BLOCK):
        part = k_ref[a * BLOCK : (a + 1) * BLOCK, :]
        for h in range(heads):
            hit = (lane >= h * size) & (lane < (h + 1) * size)
            at = (a * heads + h) * BLOCK
            kmask[at : at + BLOCK, :] = jnp.where(hit, part, jnp.zeros_like(part))
    qt[...] = q_ref[...].astype(F32).T.astype(BF)
    gt[...] = gmix[...].astype(F32).T.astype(BF)
    gkt[...] = jnp.zeros_like(gkt)
    gvt[...] = jnp.zeros_like(gvt)
    diag[...] = jnp.zeros_like(diag)
    for a in range(length // BLOCK):
        least = max(0, a - REACH + 1)
        for s in range(least, a + 1):
            keys = k_ref[s * BLOCK : (s + 1) * BLOCK, :]
            vals = v_ref[s * BLOCK : (s + 1) * BLOCK, :]
            lives = {}
            for i in range(2):
                for j in range(2):
                    d = 2 * (a - s) + i - j
                    if 0 <= d < LAGS:
                        lives[i, j] = live_of(
                            starts, a * BLOCK + i * TILE, s * BLOCK + j * TILE
                        )

            def head(h, _, a=a, s=s, keys=keys, vals=vals, lives=lives, least=least):
                scores = dot_nt(qm[h, a], keys)
                wgrad = dot_nt(gmask[h, a], vals)
                at = pl.multiple_of(((s - least) * heads + h) * BLOCK, BLOCK)
                rows_w, rows_g = [], []
                for i in range(2):
                    line_w, line_g = [], []
                    for j in range(2):
                        if (i, j) in lives:
                            d = 2 * (a - s) + i - j
                            spot = (
                                slice(i * TILE, (i + 1) * TILE),
                                slice(j * TILE, (j + 1) * TILE),
                            )
                            factor = jnp.where(lives[i, j], tiles[h, d], 0.0)
                            line_w.append((factor * scores[spot]).astype(BF))
                            line_g.append((wgrad[spot] * factor).astype(BF))
                            diag[h, d] += jnp.where(
                                lives[i, j], wgrad[spot] * scores[spot], 0.0
                            )
                        else:
                            line_w.append(jnp.zeros((TILE, TILE), BF))
                            line_g.append(jnp.zeros((TILE, TILE), BF))
                    rows_w.append(jnp.concatenate(line_w, axis=1))
                    rows_g.append(jnp.concatenate(line_g, axis=1))
                w = jnp.concatenate(rows_w, axis=0)
                g = jnp.concatenate(rows_g, axis=0)
                grads[:, pl.ds(at, BLOCK)] = g
                band = pl.ds(pl.multiple_of(h * size, size), size)
                cols = slice(s * BLOCK, (s + 1) * BLOCK)
                gvt[band, cols] += dot(gt[band, a * BLOCK : (a + 1) * BLOCK], w)
                gkt[band, cols] += dot(qt[band, a * BLOCK : (a + 1) * BLOCK], g)
                return 0

            lax.fori_loop(0, heads, head, 0, unroll=True)
        wide = (a - least + 1) * heads * BLOCK
        gq_o[a * BLOCK : (a + 1) * BLOCK, :] = dot(
            grads[:, :wide], kmask[least * heads * BLOCK : (a + 1) * heads * BLOCK, :]
        ).astype(BF)
    gk_o[...] = gkt[...].T
    gv_o[...] = gvt[...].T.astype(BF)
    glag_o[...] = jnp.zeros_like(glag_o)
    for h in range(heads):
        for d in range(LAGS):
            total = jnp.concatenate([diag[h, d], jnp.zeros((TILE, TILE), F32)], axis=1)
            rows = TILE
            while rows > 1:
                rows //= 2
                total = pltpu.roll(total[:rows], rows, 1) + total[rows : 2 * rows]
            at = TILE * (LAGS - 1 - d)
            glag_o[h : h + 1, at : at + 2 * TILE] += total


ROOT_HALF = 0.7071067811865476
PHI_SCALE = 0.3989422804014327


def mlp_kernel(ks, keep, meta, *refs):
    x_refs, g_refs, mixed = refs[0:2], refs[2:4], refs[4:8]
    vec, both = refs[8:10]
    ins = refs[10:-10]
    second_o, act_o, gpre_o, ga_o, gb_o, ubias_o, extra_o, pre, agrad, mid = refs[-10:]
    out_ref = ins[0] if keep else extra_o
    if not keep and len(ins) == 1:
        out_ref[...] = ins[0][...]
    elif not keep:
        g = meta[1]
        rows = ins[0].shape[2]
        for k, ref in enumerate(ins):
            for j in range(2):
                at = pl.multiple_of((2 * (g ^ k) + j) * rows, rows)
                for i in range(4):
                    out_ref[i, pl.ds(at, rows), :] = ref[i, j]
    quarter, width = x_refs[0].shape
    hidden = both.shape[1] // 2
    step = 64
    ubias_o[...] = jnp.zeros_like(ubias_o)
    for n, k in enumerate(ks):
        base = pl.multiple_of((meta[0] ^ k) * quarter, quarter)
        total = x_refs[n][...].astype(F32) + vec[2:3, :]
        for i, m in enumerate(mixed):
            total = total + dot_nt(m[pl.ds(base, quarter), :], out_ref[i])
        mid[...] = total
        if keep and n == 0:
            extra_o[...] = total

        def normed_chunk(i, _, n=n):
            at = pl.multiple_of(i * step, step)
            normed, _inv = norm_rows(mid[pl.ds(at, step), :])
            second_o[pl.ds(pl.multiple_of(n * quarter + at, step), step), :] = (
                normed * vec[3:4, :] + vec[4:5, :]
            ).astype(BF)
            return 0

        lax.fori_loop(0, quarter // step, normed_chunk, 0, unroll=True)
        pre[...] = dot(second_o[n * quarter : (n + 1) * quarter, :], both[:, :hidden])
        agrad[...] = dot(g_refs[n][...], both[:, hidden:])

        def act_chunk(i, total, n=n):
            at = pl.multiple_of(i * 32, 32)
            to = pl.multiple_of(n * quarter + at, 32)
            v = pre[pl.ds(at, 32), :] + vec[6:7, :]
            cdf = 0.5 + 0.5 * lax.erf(v * ROOT_HALF)
            act_o[pl.ds(to, 32), :] = (v * cdf).astype(BF)
            slope = cdf + v * (PHI_SCALE * jnp.exp(-0.5 * v * v))
            grad = (slope * agrad[pl.ds(at, 32), :]).astype(BF)
            gpre_o[pl.ds(to, 32), :] = grad
            wide = grad.astype(F32)
            return total + ((wide[0:8] + wide[8:16]) + (wide[16:24] + wide[24:32]))

        total = lax.fori_loop(0, quarter // 32, act_chunk, jnp.zeros((8, hidden), F32), unroll=True)
        ubias_o[...] += total
        part = dot_nt(gpre_o[n * quarter : (n + 1) * quarter, :], both[:, :hidden])
        target = (ga_o, gb_o)[n]
        target[...] = part.astype(target.dtype)


def middle_back_kernel(part, near, far, cot, middle, vec, gmid_o, gmb_o, sums_o):
    rows, width = middle.shape
    step = 64

    def chunk(i, totals):
        at = pl.multiple_of(i * step, step)
        spot = pl.ds(at, step)
        up = part[spot, :] + near[spot, :].astype(F32) + far[spot, :].astype(F32)
        normed, inv = norm_rows(middle[spot, :])
        cotangent = cot[spot, :].astype(F32)
        e = up * vec[3:4, :]
        mean_e = jnp.mean(e, axis=-1, keepdims=True)
        mean_x = jnp.mean(e * normed, axis=-1, keepdims=True)
        grad = cotangent + inv * (e - mean_e - normed * mean_x)
        gmid_o[spot, :] = grad
        gmb_o[spot, :] = grad.astype(BF)
        terms = (grad, up * normed, up, cotangent)
        return tuple(t + folded(x) for t, x in zip(totals, terms))

    totals = lax.fori_loop(
        0, rows // step, chunk, tuple(jnp.zeros((8, width), F32) for _ in range(4)), unroll=True
    )
    sums_o[...] = jnp.zeros_like(sums_o)
    for i, t in enumerate(totals):
        sums_o[2 + i : 3 + i, :] = jnp.sum(t, axis=0, keepdims=True)


def first_back_kernel(meta, part, near, far, tokens, gmid, vec, mean_ref, inv_ref, grad_o):
    rows, width = tokens.shape
    step = 64
    base = pl.multiple_of(meta[0] * rows, rows)

    def chunk(i, _):
        at = pl.multiple_of(i * step, step)
        spot = pl.ds(at, step)
        stat = pl.ds(pl.multiple_of(base + at, step), step)
        up = part[spot, :] + near[spot, :].astype(F32) + far[spot, :].astype(F32)
        inv = inv_ref[stat, :]
        normed = (tokens[spot, :].astype(F32) - mean_ref[stat, :]) * inv
        e = up * vec[0:1, :]
        mean_e = jnp.mean(e, axis=-1, keepdims=True)
        mean_x = jnp.mean(e * normed, axis=-1, keepdims=True)
        grad_o[spot, :] = (gmid[spot, :] + inv * (e - mean_e - normed * mean_x)).astype(BF)
        return 0

    lax.fori_loop(0, rows // step, chunk, 0, unroll=True)


def first_grad_kernel(
    meta, gq, gk, gv, wq, wk, wv, x0, x1, x2, x3, mean_ref, inv_ref, sums_two, *outs
):
    parts, (bias_o, made) = outs[:4], outs[4:]
    length, local = gq.shape
    quarter = length // 4
    width = wq.shape[0]
    step = 64
    for i, ref in enumerate((gq, gk, gv)):
        total = jnp.zeros((8, local), F32)
        for j in range(length // 64):
            total = total + folded(ref[64 * j : 64 * j + 64, :].astype(F32))
        bias_o[i, :, :] = total
    gains = jnp.zeros((8, width), F32)
    shifts = jnp.zeros((8, width), F32)
    for k, (target, x_ref) in enumerate(zip(parts, (x0, x1, x2, x3))):
        base = pl.multiple_of((meta[0] ^ k) * quarter, quarter)
        total = None
        for ref, weight in ((gq, wq), (gk, wk), (gv, wv)):
            term = dot_nt(ref[pl.ds(base, quarter), :], weight[...])
            total = term if total is None else total + term
        made[...] = total
        target[:quarter, :] = total.astype(target.dtype)

        def chunk(i, sums, base=base, x_ref=x_ref):
            at = pl.multiple_of(i * step, step)
            stat = pl.ds(pl.multiple_of(base + at, step), step)
            up = made[pl.ds(at, step), :]
            normed = (x_ref[pl.ds(at, step), :].astype(F32) - mean_ref[stat, :]) * inv_ref[stat, :]
            return sums[0] + folded(up * normed), sums[1] + folded(up)

        gains, shifts = lax.fori_loop(0, quarter // step, chunk, (gains, shifts), unroll=True)
    sums = jnp.concatenate(
        [
            jnp.sum(gains, axis=0, keepdims=True),
            jnp.sum(shifts, axis=0, keepdims=True),
            sums_two[2:8, :],
            jnp.zeros((8, width), F32),
        ],
        axis=0,
    )
    for target in (parts[1], parts[3]):
        target[quarter:, :] = sums.astype(target.dtype)


def permute(value, groups, target_of):
    pairs = []
    for g in range(groups):
        for c in range(2):
            for z in range(4):
                to = target_of(g, c, z)
                if to is not None:
                    pairs.append((g * 8 + c * 4 + z, to[0] * 8 + to[1] * 4 + to[2]))
    return lax.ppermute(value, AXES, pairs)


def swap_quarters(value, groups):
    return permute(
        value, groups, lambda g, c, z: (g, c, z) if c == z // 2 else (g, 1 - c, z ^ 2)
    )


def to_core(value, groups):
    return permute(value, groups, lambda g, c, z: (g, 1 - c, z))


def to_chip(value, groups):
    return permute(value, groups, lambda g, c, z: (g, c, z ^ 1))


def gather_group(value, groups):
    chip = to_chip(value, groups)
    core = to_core(value, groups)
    both = to_core(chip, groups)
    return value, chip, core, both


def spread_pieces(piece, groups, same):
    near = permute(
        piece, groups, lambda g, c, z: (g, c, z ^ 2) if c == z // 2 else (g, 1 - c, z)
    )
    far = permute(piece, groups, lambda g, c, z: None if c == z // 2 else (g, 1 - c, z ^ 2))
    return jnp.where(same, piece, near), jnp.where(same, near, far)


def halves_of(pieces, half):
    return tuple(lax.dynamic_index_in_dim(pieces, i, 0, False) for i in (half, 1 - half))


def return_pieces(kept, sent, groups, same):
    near = permute(
        sent, groups, lambda g, c, z: (g, 1 - c, z) if c == z // 2 else (g, c, z ^ 2)
    )
    far = permute(kept, groups, lambda g, c, z: None if c == z // 2 else (g, 1 - c, z ^ 2))
    return near.astype(F32) + jnp.where(same, kept, far).astype(F32)


def after(value, *others):
    return lax.optimization_barrier((value, *others))[0]


def pad_to(value, rows, lanes):
    return jnp.pad(value, ((0, rows - value.shape[0]), (0, lanes - value.shape[1])))


def shift_groups(value, groups, k):
    return permute(value, groups, lambda g, c, z: (g ^ k, c, z))


def send_to_groups(pieces, groups, g):
    if groups != 4:
        shape = pieces.shape
        flat = pieces.reshape(groups * 2 * shape[2], shape[3])
        total = lax.psum_scatter(flat, "g", scatter_dimension=0, tiled=True)
        return (total.reshape(shape[1:]),), ()
    sent = [lax.dynamic_index_in_dim(pieces, g ^ k, 0, False) for k in range(groups)]
    return sent, [shift_groups(sent[k], groups, k) for k in (1, 2, 3)]


def sum_of(sent, came):
    total = sent[0].astype(F32)
    for value in came:
        total = total + value.astype(F32)
    return total.astype(BF)


def plain_pack(triple, out_w, up, down, taps, modes, tbias, ubias, *rest):
    vectors, seg = rest[:6], rest[6]
    _, rows, local = triple.shape
    first_end = jnp.sum((seg[0] < 1).astype(jnp.int32))
    second_end = jnp.sum((seg[0] < 2).astype(jnp.int32))
    ends = jnp.stack([first_end // 32, first_end % 32, second_end // 32, second_end % 32])
    left = jnp.concatenate(
        [
            pad_to(taps, 8, local),
            pad_to(jnp.concatenate(vectors, axis=0), 6, local),
            pad_to(ubias, 1, local),
            pad_to(ends.astype(F32)[None], 1, local),
        ],
        axis=0,
    )
    low = jnp.concatenate([pad_to(tbias[:, 0, :], 8, TILE), pad_to(modes, 8, TILE)], axis=1)
    right = jnp.concatenate([jnp.zeros_like(low), low], axis=0)
    small = jnp.concatenate([left, jnp.zeros((SMALL, 2 * TILE - local), F32), right], axis=1)
    small = pad_to(small, SMALL, 3 * local)
    main = triple.transpose(1, 0, 2).reshape(rows, 3 * local)
    return (
        jnp.concatenate([main, small], axis=0).astype(BF),
        jnp.concatenate([up, down, out_w.T], axis=1).astype(BF),
    )


def on_device(
    groups,
    tokens,
    segments,
    row_order,
    first_gain,
    first_shift,
    triple_weight,
    triple_bias,
    shift_taps,
    kernel_modes,
    out_weight,
    out_bias,
    second_gain,
    second_shift,
    up_weight,
    up_bias,
    down_weight,
    down_bias,
    cotangent,
):
    g = lax.axis_index("g")
    c = lax.axis_index("c")
    h = lax.axis_index("h")
    b = lax.axis_index("b")
    same = c == h
    n_pieces = 2 * groups
    quarter, width = tokens.shape[1:]
    length = 4 * quarter
    rows, _, local = triple_weight.shape
    heads = kernel_modes.shape[0]
    n_modes = kernel_modes.shape[1] * n_pieces // 4
    taps_rows = shift_taps.shape[1]
    n_taps = taps_rows * n_pieces
    mode_cols = kernel_modes.shape[1]
    bias_cols = triple_bias.shape[2]
    hidden = up_weight.shape[1]
    q_at = 2 * c + b
    meta = jnp.stack([q_at, g, c, h]).astype(jnp.int32)

    own_x = swap_quarters(tokens[0], groups)
    vectors = (first_gain, first_shift, out_bias, second_gain, second_shift, down_bias)
    raw = (
        triple_weight.transpose(1, 0, 2), out_weight, up_weight, down_weight.T, shift_taps.T,
        kernel_modes, triple_bias, up_bias, *(v[None] for v in vectors), segments,
    )
    if groups == 4:
        a_piece, b_piece = call(
            pack_kernel, 0, raw,
            [((rows + SMALL, 3 * local), BF), ((rows, 2 * hidden + width // 4), BF)],
            [((SMALL, 3 * local), F32)], name="pack", us=2.2,
        )
    else:
        a_piece, b_piece = plain_pack(*raw)
    a_near, a_other = spread_pieces(after(a_piece, own_x), groups, same)
    a_pair = jnp.stack([a_near, a_other])
    x = gather_group(after(own_x, a_near), groups)
    if groups == 4:
        a_all = [a_pair] + [shift_groups(a_pair, groups, k) for k in (1, 2, 3)]
    else:
        a_all = lax.all_gather(a_pair, "g", axis=0, tiled=False)
        a_all = jnp.where(c == 0, a_all, a_all[:, ::-1]).reshape(n_pieces, rows + SMALL, 3 * local)

    lo, hi = spread_pieces(after(b_piece, a_near), groups, same)
    first_b, second_b = jnp.where(c == 0, lo, hi), jnp.where(c == 0, hi, lo)
    b_pair = jnp.concatenate([first_b[:, : 2 * hidden], second_b[:, : 2 * hidden]], axis=0)
    both = lax.all_gather(b_pair, "g", axis=0, tiled=True)
    out_pair = jnp.stack([first_b[:, 2 * hidden :], second_b[:, 2 * hidden :]])
    out_quad = gather_group(out_pair, groups)
    out_quad = jnp.stack(out_quad)
    if groups == 4:
        out_all = [out_quad] + [shift_groups(out_quad, groups, k) for k in (1, 2, 3)]
    else:
        out_all = lax.all_gather(out_quad, "g", axis=0, tiled=False)
        out_all = [out_all.transpose(1, 0, 2, 3, 4).reshape(4, width, local)]

    own_cot = swap_quarters(after(cotangent[0], first_b, x[1], *a_all[1:]), groups)
    cot = gather_group(own_cot, groups)

    made = [((length, width), BF), ((length, local), BF), ((length, local), F32)]
    made += [((length, local), BF), ((length, 1), F32), ((length, 1), F32)]
    if groups == 4:
        unpacked = [((width, local), BF)] * 3
        unpacked += [((n_taps, local), F32), ((8, width), F32), ((8, TILE), F32), ((2,), jnp.int32)]
        first, queries, raw_keys, values, mean, inv, wq, wk, wv, taps, vec, modes, ends = call(
            partial(project_kernel, 4), 2, (meta, row_order, *x, *a_all), made + unpacked,
            name="project", us=6.8,
        )
    else:
        weights = a_all[:, :rows, :].reshape(width, 3 * local)
        wq, wk, wv = (weights[:, i * local : (i + 1) * local] for i in range(3))
        small = a_all[:, rows:, :].astype(F32)
        taps = small[:, :taps_rows, :local].reshape(n_taps, local)
        vec = small[:, 8:16, :rows].transpose(1, 0, 2).reshape(8, width)
        bias = small[:, 8:16, 2 * TILE : 2 * TILE + bias_cols].transpose(1, 0, 2).reshape(8, local)
        modes = small[:, 8:16, 3 * TILE : 3 * TILE + mode_cols].transpose(1, 0, 2).reshape(8, TILE)
        mine = (row_order == 2 * g + h)[:, None]
        found = jnp.sum(jnp.where(mine, small[:, 15, :4], 0), axis=0)
        ends = jnp.stack([32 * found[0] + found[1], 32 * found[2] + found[3]]).astype(jnp.int32)
        first, queries, raw_keys, values, mean, inv = call(
            partial(project_kernel, 1), 1, (meta, *x, wq, wk, wv, bias, vec), made,
            name="project", us=6.8,
        )

    modes = modes[:heads]
    lag = LIMIT + TILE - 1 - jnp.arange(6 * TILE, dtype=jnp.int32)
    held = ((lag >= 0) & (lag < LIMIT)).astype(F32)[None, None, :]
    place = jnp.clip(lag, 0, LIMIT - 1).astype(F32)[None, None, :]
    rate = jnp.exp(modes[:, :n_modes])[:, :, None]
    phase = modes[:, n_modes : 2 * n_modes][:, :, None] * place
    decay = jnp.exp(-rate * place) * held
    wave_c, wave_s = decay * jnp.cos(phase), decay * jnp.sin(phase)
    weight_c = modes[:, 2 * n_modes : 3 * n_modes][:, :, None]
    weight_s = modes[:, 3 * n_modes :][:, :, None]
    lags = jnp.sum(weight_c * wave_c + weight_s * wave_s, axis=1)

    padded = length + (SEQUENCES + 1) * GAP
    n_blocks = length // BLOCK
    keys, key_rows = call(
        conv_kernel, 1, (ends, after(raw_keys, own_cot, out_quad), taps),
        [((length, local), BF), ((padded, local), F32)], [((padded, local), F32)],
        name="conv", us=8.5,
    )
    per_head = (heads, n_blocks, BLOCK, local)
    stacked = (n_blocks * heads * BLOCK, local)
    mixed, tiles = call(
        mix_kernel, 1, (ends, queries, after(keys, cot[1]), values, lags),
        [((length, local), BF), ((heads, LAGS, TILE, TILE), F32)],
        [
            (per_head, BF), (stacked, BF), ((length, TILE), jnp.int32),
            ((BLOCK, REACH * heads * BLOCK), BF),
        ],
        name="mix", us=4.8,
    )
    mixed = after(mixed, *out_all[1:])
    mixes = gather_group(mixed, groups)

    half_out = [((2 * quarter, width), BF), ((2 * quarter, hidden), BF), ((2 * quarter, hidden), BF)]
    scratch = [((quarter, hidden), F32), ((quarter, hidden), F32), ((quarter, width), F32)]
    shared = (*mixes, vec, both)
    second_b, act_b, gpre_b, gsec_c, gsec_d, ubias_b, outs = call(
        partial(mlp_kernel, (2, 3), False), 1,
        (meta, x[2], x[3], cot[2], cot[3], *shared, *out_all),
        half_out + [((quarter, width), BF), ((quarter, width), BF), ((8, hidden), F32)]
        + [((4, width, local), BF)],
        scratch, name="mlp_far", us=8.9,
    )
    near_own = to_core(gsec_c, groups)
    near_chip = to_core(gsec_d, groups)
    second_a, act_a, gpre_a, gsec_a, gsec_b, ubias_a, middle = call(
        partial(mlp_kernel, (0, 1), True), 1, (meta, x[0], x[1], cot[0], cot[1], *shared, outs),
        half_out
        + [((quarter, width), F32), ((quarter, width), F32), ((8, hidden), F32)]
        + [((quarter, width), F32)],
        scratch, name="mlp_near", us=8.8,
    )
    mid_sent = (gsec_b + near_chip.astype(F32)).astype(BF)
    far_own = to_chip(mid_sent, groups)
    gmid, gmb_own, sums_two = call(
        middle_back_kernel, 0, (gsec_a, near_own, far_own, own_cot, middle, vec),
        [((quarter, width), F32), ((quarter, width), BF), ((8, width), F32)],
        name="middle_back", us=3.5,
    )
    gmb = gather_group(gmb_own, groups)

    act = jnp.concatenate([after(act_a, mid_sent), act_b], axis=0)
    gpre = jnp.concatenate([gpre_a, gpre_b], axis=0)
    second = jnp.concatenate([after(second_a, mid_sent), second_b], axis=0)
    cot_all = jnp.concatenate(cot, axis=0)
    down_part = both[:, hidden:]
    up_grad = dot_tn(second, gpre)
    down_grad = dot_tn(cot_all, act)
    b_shape = (groups, 1, 2 * rows, hidden)
    b_grad = jnp.concatenate(
        [up_grad.astype(BF).reshape(b_shape), down_grad.astype(BF).reshape(b_shape)], axis=1
    ).reshape(groups * 4 * rows, hidden)
    share_far = dot_nt(after(act_b, b_grad), down_part).astype(BF)
    b_sum = lax.psum_scatter(b_grad, "g", scatter_dimension=0, tiled=True)
    b_sum = b_sum.reshape(2, 2, rows, hidden).transpose(1, 0, 2, 3)
    share = dot_nt(act_a, down_part)
    share_near = to_core(share_far, groups).astype(F32)
    share_chip = to_chip((share[quarter:] + share_near[quarter:]).astype(BF), groups)
    result = (
        middle + share[:quarter] + share_near[:quarter] + share_chip.astype(F32) + vec[5:6, :]
    ).astype(BF)

    gq, gk, gv, glag = call(
        mix_back_kernel, 2,
        (meta, ends, after(queries, b_grad, share_far, share), keys, values, *gmb, outs, tiles),
        [
            ((length, local), BF), ((length, local), F32), ((length, local), BF),
            ((8, 6 * TILE), F32),
        ],
        [
            ((length, local), BF), (per_head, BF), (per_head, BF), (stacked, BF),
            ((local, length), BF), ((local, length), BF), ((length, TILE), jnp.int32),
            ((BLOCK, REACH * heads * BLOCK), BF), ((local, length), F32), ((local, length), F32),
            ((heads, LAGS, TILE, TILE), F32),
        ],
        name="mix_back", us=12.3,
    )

    mixed_rel = jnp.concatenate(
        [lax.dynamic_slice_in_dim(mixed, (q_at ^ k) * quarter, quarter, 0) for k in range(4)],
        axis=0,
    )
    out_grad = dot_tn(jnp.concatenate(gmb, axis=0), mixed_rel)
    early = jnp.concatenate(
        [dot_tn(first, gq).astype(BF), dot_tn(first, gv).astype(BF), out_grad.astype(BF)], axis=1
    )
    early = after(early, b_sum)
    graw, grad_rows = call(
        conv_back_kernel, 1, (ends, after(gk, result, early), taps),
        [((length, local), BF), ((padded, local), F32)], [((padded, local), F32)],
        name="conv_back", us=8.2,
    )
    early = lax.psum_scatter(early, "g", scatter_dimension=0, tiled=True)
    result = swap_quarters(result, groups)
    p0, p1, p2, p3, gbias = call(
        first_grad_kernel, 1,
        (meta, gq, after(graw, result), gv, wq, wk, wv, *x, mean, inv, sums_two),
        [((quarter, width), F32), ((quarter + SMALL, width), F32), ((quarter, width), BF)]
        + [((quarter + SMALL, width), BF), ((3, 8, local), F32)],
        [((quarter, width), F32)],
        name="first_grad", us=5.3,
    )
    near_chip1 = to_core(p3, groups)
    near_own1 = to_core(p2, groups)
    far_share = p1 + near_chip1.astype(F32)
    far_sent = far_share.astype(BF)
    far_own1 = to_chip(far_sent, groups)
    b_kept, b_sent = halves_of(after(b_sum, far_sent), h)
    b_out = return_pieces(b_kept, b_sent, groups, same)
    (gtaps,) = call(
        taps_grad_kernel, 0, (grad_rows, after(key_rows, far_sent, b_kept, b_sent)), [((n_taps, local), F32)],
        [((n_taps, 8, local), F32)], name="taps_grad", us=8.2,
    )
    key_grad = dot_tn(first, after(graw, far_sent)).astype(BF)
    (input_grad,) = call(
        first_back_kernel, 1,
        (meta, after(p0, gtaps, key_grad, b_out), near_own1, far_own1, own_x, gmid, vec, mean, inv),
        [((quarter, width), BF)], name="first_back", us=3.4,
    )
    vec_grad = far_share[quarter : quarter + 6] + far_own1[quarter : quarter + 6].astype(F32)
    vec_grad = after(vec_grad, input_grad)
    input_grad = swap_quarters(input_grad, groups)

    glags = glag[:heads][:, None, :]
    grad_c = jnp.sum(glags * wave_c, axis=-1)
    grad_s = jnp.sum(glags * wave_s, axis=-1)
    both_waves = weight_c * wave_c + weight_s * wave_s
    turned_waves = weight_s * wave_c - weight_c * wave_s
    grad_rate = -jnp.sum(glags * place * both_waves, axis=-1) * rate[:, :, 0]
    grad_freq = jnp.sum(glags * place * turned_waves, axis=-1)
    modes_grad = jnp.concatenate([grad_rate, grad_freq, grad_c, grad_s], axis=1)

    key_grad = key_grad.reshape(n_pieces, rows, local)
    vec_grad = vec_grad.reshape(6, n_pieces, rows).transpose(1, 0, 2)
    ubias_grad = jnp.sum(ubias_a + ubias_b, axis=0).reshape(n_pieces, 1, rows)
    modes_grad = modes_grad.reshape(heads, n_pieces, mode_cols).transpose(1, 0, 2)
    bias_grad = jnp.sum(gbias, axis=1).reshape(3, n_pieces, bias_cols).transpose(1, 0, 2)

    def block_of(value, n_rows, lanes):
        shape = value.shape
        return jnp.pad(value, ((0, 0), (0, n_rows - shape[1]), (0, lanes - shape[2])))

    low_left = block_of(jnp.concatenate([vec_grad, ubias_grad], axis=1), 8, TILE)
    low_right = block_of(bias_grad, 4, local - TILE) + jnp.pad(
        modes_grad, ((0, 0), (0, 4 - heads), (local - TILE - mode_cols, 0))
    )
    low = jnp.concatenate([low_left, block_of(low_right, 8, local - TILE)], axis=2)
    small_grad = jnp.concatenate(
        [block_of(gtaps.reshape(n_pieces, taps_rows, local), 8, local), low], axis=1
    )
    late = jnp.concatenate([key_grad, small_grad.astype(BF)], axis=1)
    late = sum_of(*send_to_groups(late.reshape(groups, 2, rows + SMALL, local), groups, g))
    early = jnp.pad(early.reshape(2, rows, 3 * local), ((0, 0), (0, SMALL), (0, 0)))
    kept, sent = halves_of(jnp.concatenate([early, late], axis=2), h)
    a_out = return_pieces(kept, sent, groups, same)
    main, tail = a_out[:rows], a_out[rows:, 3 * local :]
    return (
        result[None],
        input_grad[None],
        tail[8, :rows],
        tail[9, :rows],
        jnp.stack(
            [main[:, :local], main[:, 3 * local :], main[:, local : 2 * local]], axis=0
        ).transpose(1, 0, 2),
        tail[8:11, TILE : TILE + bias_cols][:, None, :],
        tail[:taps_rows].T,
        tail[8 : 8 + heads, local - mode_cols :],
        main[:, 2 * local : 3 * local].T,
        tail[10, :rows],
        tail[11, :rows],
        tail[12, :rows],
        b_out[0],
        tail[14:15, :rows],
        b_out[1].T,
        tail[13, :rows],
    )


def solution(mesh):
    n_data, _ = mesh.devices.shape
    groups = n_data // 2
    fine = Mesh(mesh.devices.reshape(groups, 2, 2, 2), AXES)
    dp, tensor = ("g", "c"), ("h", "b")
    return jax.shard_map(
        partial(on_device, groups),
        mesh=fine,
        in_specs=(
            P(dp, tensor, None),
            P(dp, None),
            P(),
            P(dp),
            P(dp),
            P(dp, None, tensor),
            P(None, tensor, dp),
            P(tensor, dp),
            P(tensor, dp),
            P(tensor, dp),
            P(dp),
            P(dp),
            P(dp),
            P(dp, tensor),
            P(tensor, dp),
            P(tensor, dp),
            P(dp),
            P(dp, tensor, None),
        ),
        out_specs=(
            P(dp, tensor, None),
            P(dp, tensor, None),
            P(dp),
            P(dp),
            P(dp, None, tensor),
            P(None, tensor, dp),
            P(tensor, dp),
            P(tensor, dp),
            P(tensor, dp),
            P(dp),
            P(dp),
            P(dp),
            P(dp, tensor),
            P(tensor, dp),
            P(tensor, dp),
            P(dp),
        ),
        check_vma=False,
    )
```

```python
from functools import partial

import jax
import jax.numpy as jnp
from jax import lax
from jax.experimental import pallas as pl
from jax.experimental.pallas import tpu as pltpu
from jax.sharding import Mesh
from jax.sharding import PartitionSpec as P

EPS = 1e-05
BF = jnp.bfloat16
F32 = jnp.float32
TILE = 128
BLOCK = 256
LAGS = 5
REACH = 3
LIMIT = 512
SEQUENCES = 3
GAP = 64
SMALL = 16
AXES = ("g", "c", "h", "b")
VMEM_BYTES = 56 * 1024 * 1024


def vm():
    return pl.BlockSpec(memory_space=pltpu.VMEM)


def sm():
    return pl.BlockSpec(memory_space=pltpu.SMEM)


def mult(value, factor):
    return value if isinstance(value, int) else pl.multiple_of(value, factor)


def dot(a, b):
    return jnp.dot(a, b, preferred_element_type=F32)


def dot_nt(a, b):
    return lax.dot_general(a, b, (((1,), (1,)), ((), ())), preferred_element_type=F32)


def dot_tn(a, b):
    return lax.dot_general(a, b, (((0,), (0,)), ((), ())), preferred_element_type=F32)


FLOPS_PER_US = 1_150_000_000


def call(kernel, n_smem, args, outs, scratch=(), name=None, us=1.0):
    return pl.pallas_call(
        kernel,
        out_shape=tuple(jax.ShapeDtypeStruct(s, d) for s, d in outs),
        in_specs=[sm()] * n_smem + [vm()] * (len(args) - n_smem),
        out_specs=tuple(sm() if s == (2,) else vm() for s, _ in outs),
        scratch_shapes=[pltpu.VMEM(s, d) for s, d in scratch],
        compiler_params=pltpu.CompilerParams(vmem_limit_bytes=VMEM_BYTES),
        cost_estimate=pl.CostEstimate(
            flops=int(us * FLOPS_PER_US), bytes_accessed=0, transcendentals=0
        ),
        name=name,
    )(*args)


def norm_rows(values):
    mean = jnp.mean(values, axis=-1, keepdims=True)
    centred = values - mean
    variance = jnp.mean(centred * centred, axis=-1, keepdims=True)
    inv = lax.rsqrt(variance + EPS)
    return centred * inv, inv


def folded(values):
    parts = [values[i : i + 8] for i in range(0, values.shape[0], 8)]
    while len(parts) > 1:
        parts = [sum(parts[i : i + 2]) for i in range(0, len(parts), 2)]
    return parts[0]


def eye(n):
    rows = lax.broadcasted_iota(jnp.int32, (n, n), 0)
    return jnp.where(rows == lax.broadcasted_iota(jnp.int32, (n, n), 1), 1.0, 0.0)


def turned(values):
    return dot_nt(eye(values.shape[1]).astype(BF), values.astype(BF))


def pack_kernel(triple, out_w, up, down, taps, modes, tbias, ubias, *refs):
    vectors, (seg, a_o, b_o, box) = refs[:6], refs[6:]
    _, rows, local = triple.shape
    hidden = up.shape[1]
    for i in range(3):
        a_o[:rows, i * local : (i + 1) * local] = triple[i].astype(BF)
    box[...] = jnp.zeros_like(box)
    box[0 : taps.shape[0], 0:local] = taps[...]
    for i, vector in enumerate(vectors):
        box[8 + i : 9 + i, 0:rows] = vector[...]
    box[14:15, 0:rows] = ubias[...]
    for i in range(3):
        box[8 + i : 9 + i, 2 * TILE : 2 * TILE + tbias.shape[2]] = tbias[i]
    box[8 : 8 + modes.shape[0], 3 * TILE : 3 * TILE + modes.shape[1]] = modes[...]
    lane = lax.broadcasted_iota(jnp.int32, (1, TILE), 1)
    line = jnp.zeros((1, TILE), F32)
    for i in range(2):
        count = jnp.sum((seg[...] < i + 1).astype(F32), axis=1, keepdims=True)
        high = jnp.floor(count * (1.0 / 32))
        line = line + jnp.where(lane == 2 * i, high, 0.0)
        line = line + jnp.where(lane == 2 * i + 1, count - 32 * high, 0.0)
    box[15:16, 0:TILE] = line
    a_o[rows:, :] = box[...].astype(BF)
    b_o[:, :hidden] = up[...].astype(BF)
    b_o[:, hidden : 2 * hidden] = down[...].astype(BF)
    b_o[:, 2 * hidden :] = turned(out_w[...]).astype(BF)


def unpack(meta, order, a_refs, weights, taps_o, vec_o, modes_o, ends_o):
    g, c, h = meta[1], meta[2], meta[3]
    rows = a_refs[0].shape[1] - SMALL
    local = weights[0].shape[1]
    width = weights[0].shape[0]
    n_pieces = 2 * len(a_refs)
    bias_cols, mode_cols = local // n_pieces, TILE // n_pieces

    def spot(n_cols, wide, at):
        i = lax.broadcasted_iota(jnp.int32, (TILE, wide), 0)
        n = lax.broadcasted_iota(jnp.int32, (TILE, wide), 1)
        return jnp.where((n == i + at) & (i < n_cols), 1.0, 0.0).astype(BF)

    vec = jnp.zeros((8, width), F32)
    bias = jnp.zeros((8, local), F32)
    modes = jnp.zeros((8, TILE), F32)
    for k, ref in enumerate(a_refs):
        for j in range(2):
            d = 2 * (g ^ k) + (c ^ j)
            at = pl.multiple_of(d * rows, rows)
            for i, target in enumerate(weights):
                target[pl.ds(at, rows), :] = ref[j, :rows, i * local : (i + 1) * local]
            box = ref[j, rows:, :]
            taps_o[pl.ds(pl.multiple_of(d * 8, 8), 8), :] = box[:, :local].astype(F32)[0:8]
            low = box.astype(F32)[8:16].astype(BF)
            vec = vec + dot(low[:, :TILE], spot(rows, width, d * rows))
            bias = bias + dot(low[:, 2 * TILE : 3 * TILE], spot(bias_cols, local, d * bias_cols))
            modes = modes + dot(low[:, 3 * TILE : 4 * TILE], spot(mode_cols, TILE, d * mode_cols))
    vec_o[...] = vec
    modes_o[...] = modes
    own = 0
    for d in range(n_pieces):
        own = own + jnp.where(order[d] == 2 * g + h, d, 0)
    lane = lax.broadcasted_iota(jnp.int32, (1, width), 1)
    for i in range(2):
        scale = jnp.where(lane == own * rows + 2 * i, 32.0, 0.0)
        scale = scale + jnp.where(lane == own * rows + 2 * i + 1, 1.0, 0.0)
        ends_o[i] = jnp.sum(vec[7:8, :] * scale).astype(jnp.int32)
    return bias


def project_kernel(pieces, meta, *refs):
    if pieces > 1:
        order, refs = refs[0], refs[1:]
    x_refs, refs = refs[:4], refs[4:]
    if pieces > 1:
        a_refs, refs = refs[:pieces], refs[pieces:]
        first_o, q_o, k_o, v_o, mean_o, inv_o = refs[:6]
        weights, (taps_o, vec_ref, modes_o, ends_o) = refs[6:9], refs[9:13]
        bias = unpack(meta, order, a_refs, weights, taps_o, vec_ref, modes_o, ends_o)
        biases = [bias[i : i + 1, :] for i in range(3)]
    else:
        weights, (bias_ref, vec_ref) = refs[:3], refs[3:5]
        first_o, q_o, k_o, v_o, mean_o, inv_o = refs[5:]
        local = weights[0].shape[1]
        biases = [bias_ref[i : i + 1, :] for i in range(3)]
    quarter = x_refs[0].shape[0]
    gain, shift = vec_ref[0:1, :], vec_ref[1:2, :]
    step = 64
    for k, ref in enumerate(x_refs):
        first_o[pl.ds(pl.multiple_of((meta[0] ^ k) * quarter, quarter), quarter), :] = ref[...]

    for k in range(4):
        base = k * quarter
        for i in range(quarter // step):
            to = pl.ds(base + i * step, step)
            values = first_o[to, :].astype(F32)
            mean = jnp.mean(values, axis=-1, keepdims=True)
            centred = values - mean
            inv = lax.rsqrt(jnp.mean(centred * centred, axis=-1, keepdims=True) + EPS)
            mean_o[to, :] = mean
            inv_o[to, :] = inv
            first_o[to, :] = (centred * inv * gain + shift).astype(BF)
        rows = first_o[pl.ds(base, quarter), :]
        for target, weight, bias in zip((q_o, k_o, v_o), weights, biases):
            target[pl.ds(base, quarter), :] = (dot(rows, weight[...]) + bias).astype(target.dtype)


def sequence_of(rows, start, stop):
    return (rows >= start).astype(jnp.int32) + (rows >= stop).astype(jnp.int32)


def spread_rows(source, target, ends, length, channels):
    for i in range(target.shape[0] // GAP):
        total = jnp.zeros((GAP, channels), F32)
        for s in range(SEQUENCES):
            j = i - s - 1
            if 0 <= j < length // GAP:
                rows = lax.broadcasted_iota(jnp.int32, (GAP, channels), 0) + j * GAP
                hit = sequence_of(rows, ends[0], ends[1]) == s
                total = total + jnp.where(hit, source[j * GAP : (j + 1) * GAP, :], 0.0)
        target[i * GAP : (i + 1) * GAP, :] = total


def gather_rows(source, target, ends, length, channels):
    for j in range(length // GAP):
        rows = lax.broadcasted_iota(jnp.int32, (GAP, channels), 0) + j * GAP
        ids = sequence_of(rows, ends[0], ends[1])
        total = jnp.zeros((GAP, channels), F32)
        for s in range(SEQUENCES):
            i = j + s + 1
            total = jnp.where(ids == s, source[i * GAP : (i + 1) * GAP, :], total)
        target[j * GAP : (j + 1) * GAP, :] = total.astype(target.dtype)


def taps_sum(pad, taps, target, sign, blocks):
    channels = target.shape[1]
    n_taps = taps.shape[0]
    reach = n_taps - 8

    def block(i, edges):
        at = pl.multiple_of((i + 1 if sign > 0 else blocks - i) * GAP, GAP)
        if sign > 0:
            window = pad[pl.ds(pl.multiple_of(at - reach, 8), GAP + reach), :]
        else:
            window = pad[pl.ds(at, GAP + reach), :]
        total, fresh = None, []
        for r in range(8):
            part = None
            for m in range(n_taps // 8):
                low = reach - 8 * m if sign > 0 else 8 * m
                term = window[low : low + GAP] * taps[8 * m + r : 8 * m + r + 1, :]
                part = term if part is None else part + term
            if r == 0:
                total = part
            elif sign > 0:
                total = total + jnp.concatenate([edges[r - 1], part], axis=0)[8 - r : 8 - r + GAP]
                fresh.append(part[GAP - 8 :])
            else:
                total = total + jnp.concatenate([part, edges[r - 1]], axis=0)[r : r + GAP]
                fresh.append(part[:8])
        target[pl.ds(at, GAP), :] = total
        return tuple(fresh)

    lax.fori_loop(0, blocks, block, tuple(jnp.zeros((8, channels), F32) for _ in range(7)), unroll=2)


def conv_kernel(ends, k_ref, taps, kb_o, pad_o, made):
    length, channels = k_ref.shape
    spread_rows(k_ref, pad_o, ends, length, channels)
    taps_sum(pad_o, taps, made, 1, length // GAP + SEQUENCES - 1)
    gather_rows(made, kb_o, ends, length, channels)


def conv_back_kernel(ends, gk_ref, taps, graw_o, pad_o, made):
    length, channels = gk_ref.shape
    spread_rows(gk_ref, pad_o, ends, length, channels)
    taps_sum(pad_o, taps, made, -1, length // GAP + SEQUENCES - 1)
    gather_rows(made, graw_o, ends, length, channels)


def taps_grad_kernel(grad, keys, gtaps_o, sums):
    n_taps = gtaps_o.shape[0]
    reach = n_taps - 8
    sums[...] = jnp.zeros_like(sums)

    def block(i, _):
        at = pl.multiple_of((i + 1) * GAP, GAP)
        window = keys[pl.ds(pl.multiple_of(at - reach, 8), GAP + reach), :]
        rows = grad[pl.ds(at, GAP + 8), :]
        for r in range(8):
            turned_rows = pltpu.roll(rows, (GAP + 8 - r) % (GAP + 8), 0)[:GAP]
            for m in range(n_taps // 8):
                low = reach - 8 * m
                sums[8 * m + r, :, :] += folded(turned_rows * window[low : low + GAP])
        return 0

    lax.fori_loop(0, grad.shape[0] // GAP - 2, block, 0, unroll=2)
    gtaps_o[...] = jnp.sum(sums[...], axis=1)


def make_tiles(lags_ref, tiles, heads):
    for h in range(heads):
        for d in range(LAGS):
            at = TILE * (LAGS - 1 - d)
            row = jnp.broadcast_to(lags_ref[h : h + 1, at : at + 2 * TILE], (TILE, 2 * TILE))
            turned = pltpu.roll(row, TILE + 1, 1, stride=1, stride_axis=0)
            tiles[h, d, :, :] = turned[:, :TILE]


def head_lanes(h, heads, channels):
    size = channels // heads
    lane = lax.broadcasted_iota(jnp.int32, (BLOCK, channels), 1)
    return (lane >= h * size) & (lane < (h + 1) * size)


def head_masked(source, target, heads):
    length, channels = source.shape

    for a in range(length // BLOCK):
        part = source[a * BLOCK : (a + 1) * BLOCK, :]
        for h in range(heads):
            target[a, h * BLOCK : (h + 1) * BLOCK, :] = jnp.where(
                head_lanes(h, heads, channels), part, jnp.zeros_like(part)
            )


def starts_of(ends, target):
    rows = lax.broadcasted_iota(jnp.int32, target.shape, 0)
    first = jnp.where(rows >= ends[0], ends[0], 0)
    target[...] = jnp.where(rows >= ends[1], ends[1], first)


def lives_of(starts, a, lag):
    lives = {}
    for i in range(2):
        for j in range(2):
            if 0 <= 2 * lag + i - j < LAGS:
                lane = lax.broadcasted_iota(jnp.int32, (TILE, TILE), 1)
                lane = lane + ((a - lag) * BLOCK + j * TILE)
                lives[i, j] = lane >= starts[pl.ds(a * BLOCK + i * TILE, TILE), :]
    return lives


def mix_kernel(ends, q_ref, k_ref, v_ref, lags_ref, mixed_o, tiles_o, qm, vmask, starts, weights):
    length, local = q_ref.shape
    heads = tiles_o.shape[0]
    make_tiles(lags_ref, tiles_o, heads)
    head_masked(q_ref, qm, heads)
    head_masked(v_ref, vmask, heads)
    starts_of(ends, starts)
    for a in range(length // BLOCK):
        least = max(0, a - REACH + 1)
        for s in range(least, a + 1):
            lag = a - s
            keys = k_ref[s * BLOCK : (s + 1) * BLOCK, :]
            lives = lives_of(starts, a, lag)
            for h in range(heads):
                scores = dot_nt(qm[a, h * BLOCK : (h + 1) * BLOCK, :], keys)
                at = ((s - least) * heads + h) * BLOCK
                for i in range(2):
                    for j in range(2):
                        spot = (slice(i * TILE, (i + 1) * TILE), slice(j * TILE, (j + 1) * TILE))
                        where = (spot[0], slice(at + j * TILE, at + (j + 1) * TILE))
                        if (i, j) in lives:
                            factor = jnp.where(lives[i, j], tiles_o[h, 2 * lag + i - j], 0.0)
                            weights[where] = (factor * scores[spot]).astype(BF)
                        else:
                            weights[where] = jnp.zeros((TILE, TILE), BF)
        wide = (a - least + 1) * heads * BLOCK
        stack = vmask[least : a + 1].reshape(wide, local)
        mixed_o[a * BLOCK : (a + 1) * BLOCK, :] = dot(weights[:, :wide], stack).astype(BF)


def mix_back_kernel(
    meta, ends, q_ref, k_ref, v_ref, gm0, gm1, gm2, gm3, out_ref, tiles, gq_o, gk_o, gv_o, glag_o,
    gmix, qm, gmask, kmask, qt, gt, starts, grads, gkt, gvt, diag
):
    length, local = q_ref.shape
    heads = tiles.shape[0]
    size = local // heads
    quarter = gm0.shape[0]
    blocks = length // BLOCK
    for k, part in enumerate((gm0, gm1, gm2, gm3)):
        base = pl.multiple_of((meta[0] ^ k) * quarter, quarter)
        gmix[pl.ds(base, quarter), :] = dot(part[...], out_ref[0]).astype(BF)
    head_masked(q_ref, qm, heads)
    head_masked(gmix, gmask, heads)
    head_masked(k_ref, kmask, heads)
    starts_of(ends, starts)

    for a in range(blocks):
        spot = slice(a * BLOCK, (a + 1) * BLOCK)
        qt[a, :, :] = q_ref[spot, :].astype(F32).T.astype(BF)
        gt[a, :, :] = gmix[spot, :].astype(F32).T.astype(BF)
    gkt[...] = jnp.zeros_like(gkt)
    gvt[...] = jnp.zeros_like(gvt)
    diag[...] = jnp.zeros_like(diag)
    for a in range(blocks):
        least = max(0, a - REACH + 1)
        for s in range(least, a + 1):
            lag = a - s
            source = slice(s * BLOCK, (s + 1) * BLOCK)
            keys, vals = k_ref[source, :], v_ref[source, :]
            lives = lives_of(starts, a, lag)
            for h in range(heads):
                own = slice(h * BLOCK, (h + 1) * BLOCK)
                scores = dot_nt(qm[a, own, :], keys)
                wgrad = dot_nt(gmask[a, own, :], vals)
                rows_w, rows_g = [], []
                for i in range(2):
                    line_w, line_g = [], []
                    for j in range(2):
                        if (i, j) in lives:
                            d = 2 * lag + i - j
                            spot = (
                                slice(i * TILE, (i + 1) * TILE),
                                slice(j * TILE, (j + 1) * TILE),
                            )
                            factor = jnp.where(lives[i, j], tiles[h, d], 0.0)
                            line_w.append((factor * scores[spot]).astype(BF))
                            line_g.append((wgrad[spot] * factor).astype(BF))
                            diag[h, d] += jnp.where(lives[i, j], wgrad[spot] * scores[spot], 0.0)
                        else:
                            line_w.append(jnp.zeros((TILE, TILE), BF))
                            line_g.append(jnp.zeros((TILE, TILE), BF))
                    rows_w.append(jnp.concatenate(line_w, axis=1))
                    rows_g.append(jnp.concatenate(line_g, axis=1))
                w = jnp.concatenate(rows_w, axis=0)
                g = jnp.concatenate(rows_g, axis=0)
                at = ((s - least) * heads + h) * BLOCK
                grads[:, at : at + BLOCK] = g
                band = slice(h * size, (h + 1) * size)
                gvt[s, band, :] += dot(gt[a, band, :], w)
                gkt[s, band, :] += dot(qt[a, band, :], g)
        wide = (a - least + 1) * heads * BLOCK
        stack = kmask[least : a + 1].reshape(wide, local)
        gq_o[a * BLOCK : (a + 1) * BLOCK, :] = dot(grads[:, :wide], stack).astype(BF)
    for a in range(blocks):
        gk_o[a * BLOCK : (a + 1) * BLOCK, :] = gkt[a].T
        gv_o[a * BLOCK : (a + 1) * BLOCK, :] = gvt[a].T.astype(BF)
    glag_o[...] = jnp.zeros_like(glag_o)
    for h in range(heads):
        for d in range(LAGS):
            line = jnp.concatenate([diag[h, d], jnp.zeros((TILE, TILE), F32)], axis=1)
            rows = TILE
            while rows > 1:
                rows //= 2
                line = pltpu.roll(line[:rows], rows, 1) + line[rows : 2 * rows]
            at = TILE * (LAGS - 1 - d)
            glag_o[h : h + 1, at : at + 2 * TILE] += line


ROOT_HALF = 0.7071067811865476
PHI_SCALE = 0.3989422804014327


def mlp_kernel(near, meta, x_ref, g_ref, m0, m1, m2, m3, vec, *refs):
    n_out = 9 if near else 10
    ins, refs = refs[:-n_out], refs[-n_out:]
    second_o, act_o, gpre_o, gsec_o, ubias_o = refs[:5]
    pre, agrad, mid = refs[-3:]
    if near:
        out_ref, both = ins
        middle_o = refs[5]
    else:
        out_ref, both = refs[5:7]
        count = len(ins) // 2
        if count == 1:
            out_ref[...] = ins[0][...]
            both[...] = ins[1][...]
        else:
            rows = ins[0].shape[2]
            for k in range(count):
                for j in range(2):
                    to = pl.ds(pl.multiple_of((2 * (meta[1] ^ k) + j) * rows, rows), rows)
                    for i in range(4):
                        out_ref[i, to, :] = ins[k][i, j]
                    both[to, :] = ins[count + k][j]
    quarter = pre.shape[0]
    hidden = both.shape[1] // 2
    step = 64
    ubias_o[...] = jnp.zeros_like(ubias_o)

    for n in range(2):
        k = n if near else n + 2
        base = pl.multiple_of((meta[0] ^ k) * quarter, quarter)
        here = k * quarter
        row = n * quarter
        total = x_ref[pl.ds(here, quarter), :].astype(F32) + vec[2:3, :]
        for i, m in enumerate((m0, m1, m2, m3)):
            total = total + dot_nt(m[pl.ds(base, quarter), :], out_ref[i])
        mid[...] = total
        if near:
            middle_o[pl.ds(row, quarter), :] = total
        for i in range(quarter // step):
            normed, _inv = norm_rows(mid[i * step : (i + 1) * step, :])
            second_o[pl.ds(row + i * step, step), :] = (
                normed * vec[3:4, :] + vec[4:5, :]
            ).astype(BF)
        pre[...] = dot(second_o[pl.ds(row, quarter), :], both[:, :hidden])
        agrad[...] = dot(g_ref[pl.ds(here, quarter), :], both[:, hidden:])
        sums = None
        for i in range(quarter // 32):
            to = pl.ds(row + i * 32, 32)
            v = pre[i * 32 : (i + 1) * 32, :] + vec[6:7, :]
            cdf = 0.5 + 0.5 * lax.erf(v * ROOT_HALF)
            act_o[to, :] = (v * cdf).astype(BF)
            slope = cdf + v * (PHI_SCALE * jnp.exp(-0.5 * v * v))
            grad = (slope * agrad[i * 32 : (i + 1) * 32, :]).astype(BF)
            gpre_o[to, :] = grad
            part = folded(grad.astype(F32))
            sums = part if sums is None else sums + part
        ubias_o[...] += sums
        part = dot_nt(gpre_o[pl.ds(row, quarter), :], both[:, :hidden])
        gsec_o[pl.ds(row, quarter), :] = part.astype(gsec_o.dtype)


def ff_grad_kernel(meta, second_a, second_b, gpre_a, gpre_b, cot, act_a, act_b, *refs):
    targets, made = refs[:-1], refs[-1]
    half = second_a.shape[0]
    made[0, :, :] = dot_tn(second_a[...], gpre_a[...]) + dot_tn(second_b[...], gpre_b[...])
    made[1, :, :] = dot_tn(cot[:half, :], act_a[...]) + dot_tn(cot[half:, :], act_b[...])
    rows = targets[0].shape[2]
    for k, target in enumerate(targets):
        for j in range(2):
            spot = pl.ds(pl.multiple_of((2 * (meta[1] ^ k) + j) * rows, rows), rows)
            for i in range(2):
                target[j, i, :, :] = made[i, spot, :].astype(BF)


def early_grad_kernel(meta, first, gq, gv, gm0, gm1, gm2, gm3, mixed, *refs):
    targets, made = refs[:-1], refs[-1]
    quarter = gm0.shape[0]
    made[0, :, :] = dot_tn(first[...], gq[...])
    made[1, :, :] = dot_tn(first[...], gv[...])
    total = None
    for k, ref in enumerate((gm0, gm1, gm2, gm3)):
        base = pl.multiple_of((meta[0] ^ k) * quarter, quarter)
        part = dot_tn(ref[...], mixed[pl.ds(base, quarter), :])
        total = part if total is None else total + part
    made[2, :, :] = total
    rows = targets[0].shape[2]
    for k, target in enumerate(targets):
        for j in range(2):
            spot = pl.ds(pl.multiple_of((2 * (meta[1] ^ k) + j) * rows, rows), rows)
            for i in range(3):
                target[j, i, :, :] = made[i, spot, :].astype(BF)


def middle_back_kernel(part, near, far, cot, middle, vec, gmid_o, gmb_o, sums_o):
    rows, width = far.shape
    step = 64

    def chunk(i, totals):
        at = pl.multiple_of(i * step, step)
        spot = pl.ds(at, step)
        up = part[spot, :] + near[spot, :].astype(F32) + far[spot, :].astype(F32)
        normed, inv = norm_rows(middle[spot, :])
        cotangent = cot[spot, :].astype(F32)
        e = up * vec[3:4, :]
        mean_e = jnp.mean(e, axis=-1, keepdims=True)
        mean_x = jnp.mean(e * normed, axis=-1, keepdims=True)
        grad = cotangent + inv * (e - mean_e - normed * mean_x)
        gmid_o[spot, :] = grad
        gmb_o[spot, :] = grad.astype(BF)
        terms = (grad, up * normed, up, cotangent)
        return tuple(t + folded(x) for t, x in zip(totals, terms))

    totals = lax.fori_loop(
        0, rows // step, chunk, tuple(jnp.zeros((8, width), F32) for _ in range(4)), unroll=True
    )
    sums_o[...] = jnp.zeros_like(sums_o)
    for i, t in enumerate(totals):
        sums_o[2 + i : 3 + i, :] = jnp.sum(t, axis=0, keepdims=True)


def first_back_kernel(meta, part, near, far, tokens, gmid, vec, mean_ref, inv_ref, grad_o):
    rows, width = tokens.shape
    step = 64
    base = pl.multiple_of(meta[0] * rows, rows)

    def chunk(i, _):
        at = pl.multiple_of(i * step, step)
        spot = pl.ds(at, step)
        stat = pl.ds(pl.multiple_of(base + at, step), step)
        up = part[spot, :] + near[spot, :].astype(F32) + far[spot, :].astype(F32)
        inv = inv_ref[stat, :]
        normed = (tokens[spot, :].astype(F32) - mean_ref[stat, :]) * inv
        e = up * vec[0:1, :]
        mean_e = jnp.mean(e, axis=-1, keepdims=True)
        mean_x = jnp.mean(e * normed, axis=-1, keepdims=True)
        grad_o[spot, :] = (gmid[spot, :] + inv * (e - mean_e - normed * mean_x)).astype(BF)
        return 0

    lax.fori_loop(0, rows // step, chunk, 0, unroll=True)


def first_grad_kernel(
    meta, gq, gk, gv, wq, wk, wv, x_ref, mean_ref, inv_ref, sums_two, near_o, far_o, bias_o, made, sums
):
    length, local = gq.shape
    quarter = length // 4
    step = 64
    for i, ref in enumerate((gq, gk, gv)):
        total = jnp.zeros((8, local), F32)
        for j in range(length // 256):
            total = total + folded(ref[256 * j : 256 * j + 256, :].astype(F32))
        bias_o[i, :, :] = total
    sums[...] = jnp.zeros_like(sums)
    for first, target in ((0, near_o), (2, far_o)):

        for n in range(2):
            base = pl.multiple_of((meta[0] ^ (first + n)) * quarter, quarter)
            here = (first + n) * quarter
            total = None
            for ref, weight in ((gq, wq), (gk, wk), (gv, wv)):
                term = dot_nt(ref[pl.ds(base, quarter), :], weight[...])
                total = term if total is None else total + term
            made[...] = total
            row = n * quarter
            target[pl.ds(row, quarter), :] = total.astype(target.dtype)
            for i in range(quarter // step):
                stat = pl.ds(pl.multiple_of(base + i * step, step), step)
                up = made[i * step : (i + 1) * step, :]
                values = x_ref[pl.ds(here + i * step, step), :].astype(F32)
                normed = (values - mean_ref[stat, :]) * inv_ref[stat, :]
                sums[0, :, :] += folded(up * normed)
                sums[1, :, :] += folded(up)
    ends = jnp.concatenate(
        [
            jnp.sum(sums[0], axis=0, keepdims=True),
            jnp.sum(sums[1], axis=0, keepdims=True),
            sums_two[2:8, :],
            jnp.zeros_like(sums_two),
        ],
        axis=0,
    )
    near_o[2 * quarter :, :] = ends
    far_o[2 * quarter :, :] = ends.astype(BF)


def permute(value, groups, target_of):
    pairs = []
    for g in range(groups):
        for c in range(2):
            for z in range(4):
                to = target_of(g, c, z)
                if to is not None:
                    pairs.append((g * 8 + c * 4 + z, to[0] * 8 + to[1] * 4 + to[2]))
    return lax.ppermute(value, AXES, pairs)


def swap_quarters(value, groups):
    return permute(
        value, groups, lambda g, c, z: (g, c, z) if c == z // 2 else (g, 1 - c, z ^ 2)
    )


def to_core(value, groups):
    return permute(value, groups, lambda g, c, z: (g, 1 - c, z))


def to_chip(value, groups):
    return permute(value, groups, lambda g, c, z: (g, c, z ^ 1))


def gather_group(value, groups):
    chip = to_chip(value, groups)
    core = to_core(value, groups)
    both = to_core(chip, groups)
    return value, chip, core, both


def spread_pieces(piece, groups, same):
    near = permute(
        piece, groups, lambda g, c, z: (g, c, z ^ 2) if c == z // 2 else (g, 1 - c, z)
    )
    far = permute(piece, groups, lambda g, c, z: None if c == z // 2 else (g, 1 - c, z ^ 2))
    return jnp.where(same, piece, near), jnp.where(same, near, far)


def halves_of(pieces, half):
    return tuple(lax.dynamic_index_in_dim(pieces, i, 0, False) for i in (half, 1 - half))


def return_pieces(kept, sent, groups, same):
    near = permute(
        sent, groups, lambda g, c, z: (g, 1 - c, z) if c == z // 2 else (g, c, z ^ 2)
    )
    far = permute(kept, groups, lambda g, c, z: None if c == z // 2 else (g, 1 - c, z ^ 2))
    return near.astype(F32) + jnp.where(same, kept, far).astype(F32)


def after(value, *others):
    return lax.optimization_barrier((value, *others))[0]


def pad_to(value, rows, lanes):
    return jnp.pad(value, ((0, rows - value.shape[0]), (0, lanes - value.shape[1])))


def shift_groups(value, groups, k):
    return permute(value, groups, lambda g, c, z: (g ^ k, c, z))


def send_to_groups(pieces, groups, g):
    if groups != 4:
        shape = pieces.shape
        flat = pieces.reshape(groups * 2 * shape[2], shape[3])
        total = lax.psum_scatter(flat, "g", scatter_dimension=0, tiled=True)
        return (total.reshape(shape[1:]),), ()
    sent = [lax.dynamic_index_in_dim(pieces, g ^ k, 0, False) for k in range(groups)]
    return sent, [shift_groups(sent[k], groups, k) for k in (1, 2, 3)]


def grouped(values, groups):
    n, width, columns = values.shape
    pieces = values.reshape(n, groups, 2, width // groups // 2, columns).transpose(1, 2, 0, 3, 4)
    shape = pieces.shape[1:]
    total = lax.psum_scatter(
        pieces.reshape(-1, columns), "g", scatter_dimension=0, tiled=True
    )
    return total.reshape(shape)


def sum_of(sent, came):
    total = sent[0].astype(F32)
    for value in came:
        total = total + value.astype(F32)
    return total.astype(BF)


def plain_pack(triple, out_w, up, down, taps, modes, tbias, ubias, *rest):
    vectors, seg = rest[:6], rest[6]
    _, rows, local = triple.shape
    first_end = jnp.sum((seg[0] < 1).astype(jnp.int32))
    second_end = jnp.sum((seg[0] < 2).astype(jnp.int32))
    ends = jnp.stack([first_end // 32, first_end % 32, second_end // 32, second_end % 32])
    left = jnp.concatenate(
        [
            pad_to(taps, 8, local),
            pad_to(jnp.concatenate(vectors, axis=0), 6, local),
            pad_to(ubias, 1, local),
            pad_to(ends.astype(F32)[None], 1, local),
        ],
        axis=0,
    )
    low = jnp.concatenate([pad_to(tbias[:, 0, :], 8, TILE), pad_to(modes, 8, TILE)], axis=1)
    right = jnp.concatenate([jnp.zeros_like(low), low], axis=0)
    small = jnp.concatenate([left, jnp.zeros((SMALL, 2 * TILE - local), F32), right], axis=1)
    small = pad_to(small, SMALL, 3 * local)
    main = triple.transpose(1, 0, 2).reshape(rows, 3 * local)
    return (
        jnp.concatenate([main, small], axis=0).astype(BF),
        jnp.concatenate([up, down, out_w.T], axis=1).astype(BF),
    )


def on_device(
    groups,
    tokens,
    segments,
    row_order,
    first_gain,
    first_shift,
    triple_weight,
    triple_bias,
    shift_taps,
    kernel_modes,
    out_weight,
    out_bias,
    second_gain,
    second_shift,
    up_weight,
    up_bias,
    down_weight,
    down_bias,
    cotangent,
):
    g = lax.axis_index("g")
    c = lax.axis_index("c")
    h = lax.axis_index("h")
    b = lax.axis_index("b")
    same = c == h
    n_pieces = 2 * groups
    quarter, width = tokens.shape[1:]
    length = 4 * quarter
    rows, _, local = triple_weight.shape
    heads = kernel_modes.shape[0]
    n_modes = kernel_modes.shape[1] * n_pieces // 4
    taps_rows = shift_taps.shape[1]
    n_taps = taps_rows * n_pieces
    mode_cols = kernel_modes.shape[1]
    bias_cols = triple_bias.shape[2]
    hidden = up_weight.shape[1]
    q_at = 2 * c + b
    meta = jnp.stack([q_at, g, c, h]).astype(jnp.int32)

    own_x = swap_quarters(tokens[0], groups)
    vectors = (first_gain, first_shift, out_bias, second_gain, second_shift, down_bias)
    raw = (
        triple_weight.transpose(1, 0, 2), out_weight, up_weight, down_weight.T, shift_taps.T,
        kernel_modes, triple_bias, up_bias, *(v[None] for v in vectors), segments,
    )
    if groups == 4:
        a_piece, b_piece = call(
            pack_kernel, 0, raw,
            [((rows + SMALL, 3 * local), BF), ((rows, 2 * hidden + width // 4), BF)],
            [((SMALL, 3 * local), F32)], name="pack", us=2.2,
        )
    else:
        a_piece, b_piece = plain_pack(*raw)
    a_near, a_other = spread_pieces(a_piece, groups, same)
    a_pair = jnp.stack([a_near, a_other])
    x = gather_group(after(own_x, a_piece), groups)
    if groups == 4:
        a_all = [a_pair] + [shift_groups(a_pair, groups, k) for k in (1, 2, 3)]
    else:
        a_all = lax.all_gather(a_pair, "g", axis=0, tiled=False)
        a_all = jnp.where(c == 0, a_all, a_all[:, ::-1]).reshape(n_pieces, rows + SMALL, 3 * local)

    lo, hi = spread_pieces(after(b_piece, x[1]), groups, same)
    first_b, second_b = jnp.where(c == 0, lo, hi), jnp.where(c == 0, hi, lo)
    b_pair = jnp.stack([first_b[:, : 2 * hidden], second_b[:, : 2 * hidden]])
    out_quad = jnp.stack(gather_group(jnp.stack([first_b, second_b])[:, :, 2 * hidden :], groups))
    if groups == 4:
        b_side, b_next = (shift_groups(b_pair, groups, k) for k in (1, 2))
        b_all = [b_pair, b_side, b_next, shift_groups(b_side, groups, 2)]
        out_all = [out_quad] + [shift_groups(out_quad, groups, k) for k in (1, 2, 3)]
    else:
        b_all = [lax.all_gather(b_pair, "g", axis=0, tiled=False).reshape(width, 2 * hidden)]
        out_all = lax.all_gather(out_quad, "g", axis=0, tiled=False)
        out_all = [out_all.transpose(1, 0, 2, 3, 4).reshape(4, width, local)]

    own_cot = swap_quarters(after(cotangent[0], x[1]), groups)
    cot = gather_group(own_cot, groups)

    made = [((length, width), BF), ((length, local), BF), ((length, local), F32)]
    made += [((length, local), BF), ((length, 1), F32), ((length, 1), F32)]
    if groups == 4:
        unpacked = [((width, local), BF)] * 3
        unpacked += [((n_taps, local), F32), ((8, width), F32), ((8, TILE), F32), ((2,), jnp.int32)]
        first, queries, raw_keys, values, mean, inv, wq, wk, wv, taps, vec, modes, ends = call(
            partial(project_kernel, 4), 2, (meta, row_order, *x, *a_all), made + unpacked,
            name="project", us=6.8,
        )
    else:
        weights = a_all[:, :rows, :].reshape(width, 3 * local)
        wq, wk, wv = (weights[:, i * local : (i + 1) * local] for i in range(3))
        small = a_all[:, rows:, :].astype(F32)
        taps = small[:, :taps_rows, :local].reshape(n_taps, local)
        vec = small[:, 8:16, :rows].transpose(1, 0, 2).reshape(8, width)
        bias = small[:, 8:16, 2 * TILE : 2 * TILE + bias_cols].transpose(1, 0, 2).reshape(8, local)
        modes = small[:, 8:16, 3 * TILE : 3 * TILE + mode_cols].transpose(1, 0, 2).reshape(8, TILE)
        mine = (row_order == 2 * g + h)[:, None]
        found = jnp.sum(jnp.where(mine, small[:, 15, :4], 0), axis=0)
        ends = jnp.stack([32 * found[0] + found[1], 32 * found[2] + found[3]]).astype(jnp.int32)
        first, queries, raw_keys, values, mean, inv = call(
            partial(project_kernel, 1), 1, (meta, *x, wq, wk, wv, bias, vec), made,
            name="project", us=6.8,
        )

    modes = modes[:heads]
    lag = LIMIT + TILE - 1 - jnp.arange(6 * TILE, dtype=jnp.int32)
    held = ((lag >= 0) & (lag < LIMIT)).astype(F32)[None, None, :]
    place = jnp.clip(lag, 0, LIMIT - 1).astype(F32)[None, None, :]
    rate = jnp.exp(modes[:, :n_modes])[:, :, None]
    phase = modes[:, n_modes : 2 * n_modes][:, :, None] * place
    decay = jnp.exp(-rate * place) * held
    wave_c, wave_s = decay * jnp.cos(phase), decay * jnp.sin(phase)
    weight_c = modes[:, 2 * n_modes : 3 * n_modes][:, :, None]
    weight_s = modes[:, 3 * n_modes :][:, :, None]
    lags = jnp.sum(weight_c * wave_c + weight_s * wave_s, axis=1)

    padded = length + (SEQUENCES + 1) * GAP
    n_blocks = length // BLOCK
    keys, key_rows = call(
        conv_kernel, 1, (ends, after(raw_keys, own_cot, b_all[1 % len(b_all)]), taps),
        [((length, local), BF), ((padded, local), F32)], [((padded, local), F32)],
        name="conv", us=8.5,
    )
    per_block = (n_blocks, heads * BLOCK, local)
    mixed, tiles = call(
        mix_kernel, 1, (ends, queries, after(keys, cot[1]), values, lags),
        [((length, local), BF), ((heads, LAGS, TILE, TILE), F32)],
        [
            (per_block, BF), (per_block, BF), ((length, TILE), jnp.int32),
            ((BLOCK, REACH * heads * BLOCK), BF),
        ],
        name="mix", us=4.9,
    )
    mixed = after(mixed, *b_all[1:3], *out_all[1:])
    mixes = gather_group(mixed, groups)

    x_all = jnp.concatenate(x, axis=0)
    cot_all = jnp.concatenate(cot, axis=0)
    half = [((2 * quarter, width), BF), ((2 * quarter, hidden), BF), ((2 * quarter, hidden), BF)]
    scratch = [((quarter, hidden), F32), ((quarter, hidden), F32), ((quarter, width), F32)]
    shared = (meta, x_all, cot_all, *mixes, vec)
    second_b, act_b, gpre_b, gsec_b, ubias_b, outs, both = call(
        partial(mlp_kernel, False), 1, (*shared, *out_all, *b_all),
        half
        + [((2 * quarter, width), BF), ((8, hidden), F32), ((4, width, local), BF)]
        + [((width, 2 * hidden), BF)],
        scratch, name="mlp_far", us=8.9,
    )
    came = to_core(gsec_b, groups)
    second_a, act_a, gpre_a, gsec_a, ubias_a, middle = call(
        partial(mlp_kernel, True), 1, (*shared, outs, both),
        half + [((2 * quarter, width), F32), ((8, hidden), F32), ((2 * quarter, width), F32)],
        scratch, name="mlp_near", us=8.8,
    )
    mid_sent = (gsec_a[quarter:] + came[quarter:].astype(F32)).astype(BF)
    far_own = to_chip(mid_sent, groups)

    if groups == 4:
        b_sent = call(
            ff_grad_kernel, 1,
            (meta, after(second_a, mid_sent), second_b, gpre_a, gpre_b, cot_all, act_a, act_b),
            [((2, 2, rows, hidden), BF)] * 4, [((2, width, hidden), F32)], name="ff_grad", us=5.3,
        )
        b_came = [shift_groups(b_sent[k], groups, k) for k in (1, 2, 3)]
    else:
        up_grad = dot_tn(
            jnp.concatenate([second_a, second_b], axis=0), jnp.concatenate([gpre_a, gpre_b], axis=0)
        )
        down_grad = dot_tn(cot_all, jnp.concatenate([act_a, act_b], axis=0))
        b_sent = [grouped(jnp.stack([up_grad, down_grad]).astype(BF), groups)]
        b_came = []
    gmid, gmb_own, sums_two = call(
        middle_back_kernel, 0, (after(gsec_a, *b_sent), came, far_own, own_cot, middle, vec),
        [((quarter, width), F32), ((quarter, width), BF), ((8, width), F32)],
        name="middle_back", us=3.5,
    )
    gmb = gather_group(gmb_own, groups)

    down_part = both[:, hidden:]
    share_far = dot_nt(after(act_b, gmb_own), down_part).astype(BF)
    share = dot_nt(after(act_a, gmb_own), down_part)
    share_near = to_core(share_far, groups).astype(F32)
    share_chip = to_chip((share[quarter:] + share_near[quarter:]).astype(BF), groups)
    result = (
        middle[:quarter] + share[:quarter] + share_near[:quarter] + share_chip.astype(F32) + vec[5:6, :]
    ).astype(BF)

    gq, gk, gv, glag = call(
        mix_back_kernel, 2,
        (meta, ends, after(queries, share_far, share), keys, values, *gmb, outs, tiles),
        [
            ((length, local), BF), ((length, local), F32), ((length, local), BF),
            ((8, 6 * TILE), F32),
        ],
        [
            ((length, local), BF), (per_block, BF), (per_block, BF), (per_block, BF),
            ((n_blocks, local, BLOCK), BF), ((n_blocks, local, BLOCK), BF),
            ((length, TILE), jnp.int32), ((BLOCK, REACH * heads * BLOCK), BF),
            ((n_blocks, local, BLOCK), F32), ((n_blocks, local, BLOCK), F32),
            ((heads, LAGS, TILE, TILE), F32),
        ],
        name="mix_back", us=12.3,
    )

    if groups == 4:
        early_sent = call(
            early_grad_kernel, 1, (meta, first, gq, gv, *gmb, mixed),
            [((2, 3, rows, local), BF)] * 4, [((3, width, local), F32)], name="early_grad", us=3.0,
        )
        early_came = [shift_groups(early_sent[k], groups, k) for k in (1, 2, 3)]
    else:
        mixed_rel = jnp.concatenate(
            [lax.dynamic_slice_in_dim(mixed, (q_at ^ k) * quarter, quarter, 0) for k in range(4)],
            axis=0,
        )
        out_grad = dot_tn(jnp.concatenate(gmb, axis=0), mixed_rel)
        early = jnp.stack([dot_tn(first, gq), dot_tn(first, gv), out_grad])
        early_sent, early_came = [grouped(early.astype(BF), groups)], []

    b_kept, b_away = halves_of(sum_of(b_sent, [after(v, gk) for v in b_came]), h)
    b_out = return_pieces(b_kept, b_away, groups, same)
    graw, grad_rows = call(
        conv_back_kernel, 1, (ends, after(gk, result, *early_sent, b_kept, b_away), taps),
        [((length, local), BF), ((padded, local), F32)], [((padded, local), F32)],
        name="conv_back", us=8.2,
    )
    result = swap_quarters(result, groups)
    share_rows = 2 * quarter + SMALL
    near_part, far_part, gbias = call(
        first_grad_kernel, 1,
        (meta, gq, after(graw, result, b_out), gv, wq, wk, wv, x_all, mean, inv, sums_two),
        [((share_rows, width), F32), ((share_rows, width), BF), ((3, 8, local), F32)],
        [((quarter, width), F32), ((2, 8, width), F32)],
        name="first_grad", us=5.3,
    )
    came1 = to_core(far_part, groups)
    far_share = near_part[quarter:] + came1[quarter:].astype(F32)
    far_sent = far_share.astype(BF)
    far_own1 = to_chip(far_sent, groups)
    e_sum = sum_of(early_sent, [after(v, far_sent) for v in early_came])
    e_kept, e_away = halves_of(e_sum, h)
    e_out = return_pieces(e_kept, e_away, groups, same)
    (gtaps,) = call(
        taps_grad_kernel, 0, (grad_rows, after(key_rows, far_sent, e_kept, e_away)), [((n_taps, local), F32)],
        [((n_taps, 8, local), F32)], name="taps_grad", us=8.2,
    )
    key_grad = dot_tn(first, after(graw, far_sent)).astype(BF)
    (input_grad,) = call(
        first_back_kernel, 1,
        (meta, after(near_part, gtaps, key_grad, e_out), came1, far_own1, own_x, gmid, vec, mean, inv),
        [((quarter, width), BF)], name="first_back", us=3.4,
    )
    vec_grad = far_share[quarter : quarter + 6] + far_own1[quarter : quarter + 6].astype(F32)
    vec_grad = after(vec_grad, input_grad)
    input_grad = swap_quarters(input_grad, groups)

    glags = glag[:heads][:, None, :]
    grad_c = jnp.sum(glags * wave_c, axis=-1)
    grad_s = jnp.sum(glags * wave_s, axis=-1)
    both_waves = weight_c * wave_c + weight_s * wave_s
    turned_waves = weight_s * wave_c - weight_c * wave_s
    grad_rate = -jnp.sum(glags * place * both_waves, axis=-1) * rate[:, :, 0]
    grad_freq = jnp.sum(glags * place * turned_waves, axis=-1)
    modes_grad = jnp.concatenate([grad_rate, grad_freq, grad_c, grad_s], axis=1)

    key_grad = key_grad.reshape(n_pieces, rows, local)
    vec_grad = vec_grad.reshape(6, n_pieces, rows).transpose(1, 0, 2)
    ubias_grad = jnp.sum(ubias_a + ubias_b, axis=0).reshape(n_pieces, 1, rows)
    modes_grad = modes_grad.reshape(heads, n_pieces, mode_cols).transpose(1, 0, 2)
    bias_grad = jnp.sum(gbias, axis=1).reshape(3, n_pieces, bias_cols).transpose(1, 0, 2)

    def block_of(value, n_rows, lanes):
        shape = value.shape
        return jnp.pad(value, ((0, 0), (0, n_rows - shape[1]), (0, lanes - shape[2])))

    low_left = block_of(jnp.concatenate([vec_grad, ubias_grad], axis=1), 8, TILE)
    low_right = block_of(bias_grad, 4, local - TILE) + jnp.pad(
        modes_grad, ((0, 0), (0, 4 - heads), (local - TILE - mode_cols, 0))
    )
    low = jnp.concatenate([low_left, block_of(low_right, 8, local - TILE)], axis=2)
    small_grad = jnp.concatenate(
        [block_of(gtaps.reshape(n_pieces, taps_rows, local), 8, local), low], axis=1
    )
    late = jnp.concatenate([key_grad, small_grad.astype(BF)], axis=1)
    late = sum_of(*send_to_groups(late.reshape(groups, 2, rows + SMALL, local), groups, g))
    kept, sent = halves_of(late, h)
    late_out = return_pieces(kept, sent, groups, same)
    tail = late_out[rows:]
    return (
        result[None],
        input_grad[None],
        tail[8, :rows],
        tail[9, :rows],
        jnp.stack([e_out[0], late_out[:rows], e_out[1]]).transpose(1, 0, 2),
        tail[8:11, TILE : TILE + bias_cols][:, None, :],
        tail[:taps_rows].T,
        tail[8 : 8 + heads, local - mode_cols :],
        e_out[2].T,
        tail[10, :rows],
        tail[11, :rows],
        tail[12, :rows],
        b_out[0],
        tail[14:15, :rows],
        b_out[1].T,
        tail[13, :rows],
    )


def solution(mesh):
    n_data, _ = mesh.devices.shape
    groups = n_data // 2
    fine = Mesh(mesh.devices.reshape(groups, 2, 2, 2), AXES)
    dp, tensor = ("g", "c"), ("h", "b")
    return jax.shard_map(
        partial(on_device, groups),
        mesh=fine,
        in_specs=(
            P(dp, tensor, None),
            P(dp, None),
            P(),
            P(dp),
            P(dp),
            P(dp, None, tensor),
            P(None, tensor, dp),
            P(tensor, dp),
            P(tensor, dp),
            P(tensor, dp),
            P(dp),
            P(dp),
            P(dp),
            P(dp, tensor),
            P(tensor, dp),
            P(tensor, dp),
            P(dp),
            P(dp, tensor, None),
        ),
        out_specs=(
            P(dp, tensor, None),
            P(dp, tensor, None),
            P(dp),
            P(dp),
            P(dp, None, tensor),
            P(None, tensor, dp),
            P(tensor, dp),
            P(tensor, dp),
            P(tensor, dp),
            P(dp),
            P(dp),
            P(dp),
            P(dp, tensor),
            P(tensor, dp),
            P(tensor, dp),
            P(dp),
        ),
        check_vma=False,
    )
```

```python
from functools import partial

import jax
import jax.numpy as jnp
from jax import lax
from jax.experimental import pallas as pl
from jax.experimental.pallas import tpu as pltpu
from jax.sharding import Mesh
from jax.sharding import PartitionSpec as P

EPS = 1e-05
BF = jnp.bfloat16
F32 = jnp.float32
TILE = 128
BLOCK = 256
LAGS = 5
REACH = 3
LIMIT = 512
SEQUENCES = 3
GAP = 64
SMALL = 16
AXES = ("g", "c", "h", "b")
VMEM_BYTES = 56 * 1024 * 1024


def vm():
    return pl.BlockSpec(memory_space=pltpu.VMEM)


def sm():
    return pl.BlockSpec(memory_space=pltpu.SMEM)


def mult(value, factor):
    return value if isinstance(value, int) else pl.multiple_of(value, factor)


def dot(a, b):
    return jnp.dot(a, b, preferred_element_type=F32)


def dot_nt(a, b):
    return lax.dot_general(a, b, (((1,), (1,)), ((), ())), preferred_element_type=F32)


def dot_tn(a, b):
    return lax.dot_general(a, b, (((0,), (0,)), ((), ())), preferred_element_type=F32)


FLOPS_PER_US = 1_150_000_000


def call(kernel, n_smem, args, outs, scratch=(), name=None, us=1.0):
    return pl.pallas_call(
        kernel,
        out_shape=tuple(jax.ShapeDtypeStruct(s, d) for s, d in outs),
        in_specs=[sm()] * n_smem + [vm()] * (len(args) - n_smem),
        out_specs=tuple(sm() if s == (2,) else vm() for s, _ in outs),
        scratch_shapes=[pltpu.VMEM(s, d) for s, d in scratch],
        compiler_params=pltpu.CompilerParams(vmem_limit_bytes=VMEM_BYTES),
        cost_estimate=pl.CostEstimate(
            flops=int(us * FLOPS_PER_US), bytes_accessed=0, transcendentals=0
        ),
        name=name,
    )(*args)


def norm_rows(values):
    mean = jnp.mean(values, axis=-1, keepdims=True)
    centred = values - mean
    variance = jnp.mean(centred * centred, axis=-1, keepdims=True)
    inv = lax.rsqrt(variance + EPS)
    return centred * inv, inv


def folded(values):
    parts = [values[i : i + 8] for i in range(0, values.shape[0], 8)]
    while len(parts) > 1:
        parts = [sum(parts[i : i + 2]) for i in range(0, len(parts), 2)]
    return parts[0]


def eye(n):
    rows = lax.broadcasted_iota(jnp.int32, (n, n), 0)
    return jnp.where(rows == lax.broadcasted_iota(jnp.int32, (n, n), 1), 1.0, 0.0)


def turned(values):
    return dot_nt(eye(values.shape[1]).astype(BF), values.astype(BF))


def pack_kernel(triple, out_w, up, down, taps, modes, tbias, ubias, *refs):
    vectors, (seg, a_o, b_o, box) = refs[:6], refs[6:]
    _, rows, local = triple.shape
    hidden = up.shape[1]
    for i in range(3):
        a_o[:rows, i * local : (i + 1) * local] = triple[i].astype(BF)
    box[...] = jnp.zeros_like(box)
    box[0 : taps.shape[0], 0:local] = taps[...]
    for i, vector in enumerate(vectors):
        box[8 + i : 9 + i, 0:rows] = vector[...]
    box[14:15, 0:rows] = ubias[...]
    for i in range(3):
        box[8 + i : 9 + i, 2 * TILE : 2 * TILE + tbias.shape[2]] = tbias[i]
    box[8 : 8 + modes.shape[0], 3 * TILE : 3 * TILE + modes.shape[1]] = modes[...]
    lane = lax.broadcasted_iota(jnp.int32, (1, TILE), 1)
    line = jnp.zeros((1, TILE), F32)
    for i in range(2):
        count = jnp.sum((seg[...] < i + 1).astype(F32), axis=1, keepdims=True)
        high = jnp.floor(count * (1.0 / 32))
        line = line + jnp.where(lane == 2 * i, high, 0.0)
        line = line + jnp.where(lane == 2 * i + 1, count - 32 * high, 0.0)
    box[15:16, 0:TILE] = line
    a_o[rows:, :] = box[...].astype(BF)
    b_o[:, :hidden] = up[...].astype(BF)
    b_o[:, hidden : 2 * hidden] = down[...].astype(BF)
    b_o[:, 2 * hidden :] = turned(out_w[...]).astype(BF)


def unpack(meta, order, a_refs, weights, taps_o, vec_o, modes_o, ends_o):
    g, c, h = meta[1], meta[2], meta[3]
    rows = a_refs[0].shape[1] - SMALL
    local = weights[0].shape[1]
    width = weights[0].shape[0]
    n_pieces = 2 * len(a_refs)
    bias_cols, mode_cols = local // n_pieces, TILE // n_pieces

    def spot(n_cols, wide, at):
        i = lax.broadcasted_iota(jnp.int32, (TILE, wide), 0)
        n = lax.broadcasted_iota(jnp.int32, (TILE, wide), 1)
        return jnp.where((n == i + at) & (i < n_cols), 1.0, 0.0).astype(BF)

    vec = jnp.zeros((8, width), F32)
    bias = jnp.zeros((8, local), F32)
    modes = jnp.zeros((8, TILE), F32)
    for k, ref in enumerate(a_refs):
        for j in range(2):
            d = 2 * (g ^ k) + (c ^ j)
            at = pl.multiple_of(d * rows, rows)
            for i, target in enumerate(weights):
                target[pl.ds(at, rows), :] = ref[j, :rows, i * local : (i + 1) * local]
            box = ref[j, rows:, :]
            taps_o[pl.ds(pl.multiple_of(d * 8, 8), 8), :] = box[:, :local].astype(F32)[0:8]
            low = box.astype(F32)[8:16].astype(BF)
            vec = vec + dot(low[:, :TILE], spot(rows, width, d * rows))
            bias = bias + dot(low[:, 2 * TILE : 3 * TILE], spot(bias_cols, local, d * bias_cols))
            modes = modes + dot(low[:, 3 * TILE : 4 * TILE], spot(mode_cols, TILE, d * mode_cols))
    vec_o[...] = vec
    modes_o[...] = modes
    own = 0
    for d in range(n_pieces):
        own = own + jnp.where(order[d] == 2 * g + h, d, 0)
    lane = lax.broadcasted_iota(jnp.int32, (1, width), 1)
    for i in range(2):
        scale = jnp.where(lane == own * rows + 2 * i, 32.0, 0.0)
        scale = scale + jnp.where(lane == own * rows + 2 * i + 1, 1.0, 0.0)
        ends_o[i] = jnp.sum(vec[7:8, :] * scale).astype(jnp.int32)
    return bias


def project_kernel(pieces, meta, *refs):
    if pieces > 1:
        order, refs = refs[0], refs[1:]
    x_refs, refs = refs[:4], refs[4:]
    if pieces > 1:
        a_refs, refs = refs[:pieces], refs[pieces:]
        first_o, q_o, k_o, v_o, mean_o, inv_o = refs[:6]
        weights, (taps_o, vec_ref, modes_o, ends_o) = refs[6:9], refs[9:13]
        bias = unpack(meta, order, a_refs, weights, taps_o, vec_ref, modes_o, ends_o)
        biases = [bias[i : i + 1, :] for i in range(3)]
    else:
        weights, (bias_ref, vec_ref) = refs[:3], refs[3:5]
        first_o, q_o, k_o, v_o, mean_o, inv_o = refs[5:]
        local = weights[0].shape[1]
        biases = [bias_ref[i : i + 1, :] for i in range(3)]
    quarter = x_refs[0].shape[0]
    gain, shift = vec_ref[0:1, :], vec_ref[1:2, :]
    step = 64
    for k, ref in enumerate(x_refs):
        first_o[pl.ds(pl.multiple_of((meta[0] ^ k) * quarter, quarter), quarter), :] = ref[...]

    for k in range(4):
        base = k * quarter
        for i in range(quarter // step):
            to = pl.ds(base + i * step, step)
            values = first_o[to, :].astype(F32)
            mean = jnp.mean(values, axis=-1, keepdims=True)
            centred = values - mean
            inv = lax.rsqrt(jnp.mean(centred * centred, axis=-1, keepdims=True) + EPS)
            mean_o[to, :] = mean
            inv_o[to, :] = inv
            first_o[to, :] = (centred * inv * gain + shift).astype(BF)
        rows = first_o[pl.ds(base, quarter), :]
        for target, weight, bias in zip((q_o, k_o, v_o), weights, biases):
            target[pl.ds(base, quarter), :] = (dot(rows, weight[...]) + bias).astype(target.dtype)


def sequence_of(rows, start, stop):
    return (rows >= start).astype(jnp.int32) + (rows >= stop).astype(jnp.int32)


def spread_rows(source, target, ends, length, channels):
    for i in range(target.shape[0] // GAP):
        total = jnp.zeros((GAP, channels), F32)
        for s in range(SEQUENCES):
            j = i - s - 1
            if 0 <= j < length // GAP:
                rows = lax.broadcasted_iota(jnp.int32, (GAP, channels), 0) + j * GAP
                hit = sequence_of(rows, ends[0], ends[1]) == s
                total = total + jnp.where(hit, source[j * GAP : (j + 1) * GAP, :], 0.0)
        target[i * GAP : (i + 1) * GAP, :] = total


def gather_rows(source, target, ends, length, channels):
    for j in range(length // GAP):
        rows = lax.broadcasted_iota(jnp.int32, (GAP, channels), 0) + j * GAP
        ids = sequence_of(rows, ends[0], ends[1])
        total = jnp.zeros((GAP, channels), F32)
        for s in range(SEQUENCES):
            i = j + s + 1
            total = jnp.where(ids == s, source[i * GAP : (i + 1) * GAP, :], total)
        target[j * GAP : (j + 1) * GAP, :] = total.astype(target.dtype)


def taps_sum(pad, taps, target, sign, blocks):
    channels = target.shape[1]
    n_taps = taps.shape[0]
    reach = n_taps - 8

    def block(i, edges):
        at = pl.multiple_of((i + 1 if sign > 0 else blocks - i) * GAP, GAP)
        if sign > 0:
            window = pad[pl.ds(pl.multiple_of(at - reach, 8), GAP + reach), :]
        else:
            window = pad[pl.ds(at, GAP + reach), :]
        total, fresh = None, []
        for r in range(8):
            part = None
            for m in range(n_taps // 8):
                low = reach - 8 * m if sign > 0 else 8 * m
                term = window[low : low + GAP] * taps[8 * m + r : 8 * m + r + 1, :]
                part = term if part is None else part + term
            if r == 0:
                total = part
            elif sign > 0:
                total = total + jnp.concatenate([edges[r - 1], part], axis=0)[8 - r : 8 - r + GAP]
                fresh.append(part[GAP - 8 :])
            else:
                total = total + jnp.concatenate([part, edges[r - 1]], axis=0)[r : r + GAP]
                fresh.append(part[:8])
        target[pl.ds(at, GAP), :] = total
        return tuple(fresh)

    lax.fori_loop(0, blocks, block, tuple(jnp.zeros((8, channels), F32) for _ in range(7)), unroll=2)


def conv_kernel(ends, k_ref, taps, kb_o, pad_o, made):
    length, channels = k_ref.shape
    spread_rows(k_ref, pad_o, ends, length, channels)
    taps_sum(pad_o, taps, made, 1, length // GAP + SEQUENCES - 1)
    gather_rows(made, kb_o, ends, length, channels)


def conv_back_kernel(ends, gk_ref, taps, graw_o, pad_o, made):
    length, channels = gk_ref.shape
    spread_rows(gk_ref, pad_o, ends, length, channels)
    taps_sum(pad_o, taps, made, -1, length // GAP + SEQUENCES - 1)
    gather_rows(made, graw_o, ends, length, channels)


def taps_grad(grad, keys, sums):
    n_taps = sums.shape[0]
    reach = n_taps - 8
    sums[...] = jnp.zeros_like(sums)

    def block(i, _):
        at = pl.multiple_of((i + 1) * GAP, GAP)
        window = keys[pl.ds(pl.multiple_of(at - reach, 8), GAP + reach), :]
        rows = grad[pl.ds(at, GAP + 8), :]
        for r in range(8):
            turned_rows = pltpu.roll(rows, (GAP + 8 - r) % (GAP + 8), 0)[:GAP]
            for m in range(n_taps // 8):
                low = reach - 8 * m
                sums[8 * m + r, :, :] += folded(turned_rows * window[low : low + GAP])
        return 0

    lax.fori_loop(0, grad.shape[0] // GAP - 2, block, 0, unroll=2)
    return jnp.sum(sums[...], axis=1)


def taps_grad_kernel(grad, keys, gtaps_o, sums):
    gtaps_o[...] = taps_grad(grad, keys, sums)


def late_grad_kernel(meta, grad, keys, first, graw, vec_sums, ubias_a, ubias_b, gbias, modes, *refs):
    targets, (sums, pieces) = refs[:-2], refs[-2:]
    n_pieces, rows, local = pieces.shape
    rows -= SMALL
    made = dot_tn(graw[...], first[...]).T
    pieces[...] = jnp.zeros_like(pieces)
    ubias = jnp.sum(ubias_a[...] + ubias_b[...], axis=0, keepdims=True)
    bias = jnp.concatenate([jnp.sum(gbias[i], axis=0, keepdims=True) for i in range(3)], axis=0)
    heads = modes.shape[0]
    n_bias, n_modes = local // n_pieces, modes.shape[1] // n_pieces
    low = rows + 8
    gtaps = taps_grad(grad, keys, sums)
    for d in range(n_pieces):
        pieces[d, :rows, :] = made[d * rows : (d + 1) * rows, :]
        pieces[d, rows:low, :] = gtaps[8 * d : 8 * d + 8, :]
        wide = slice(d * rows, (d + 1) * rows)
        pieces[d, low : low + 6, :rows] = vec_sums[0:6, wide]
        pieces[d, low + 6 : low + 7, :rows] = ubias[:, wide]
        pieces[d, low : low + 3, TILE : TILE + n_bias] = bias[:, d * n_bias : (d + 1) * n_bias]
        pieces[d, low : low + heads, local - n_modes :] = modes[:, d * n_modes : (d + 1) * n_modes]
    for k, target in enumerate(targets):
        for j in range(2):
            target[j, :, :] = pieces[2 * (meta[1] ^ k) + j].astype(BF)


def make_tiles(lags_ref, tiles, heads):
    for h in range(heads):
        for d in range(LAGS):
            at = TILE * (LAGS - 1 - d)
            row = jnp.broadcast_to(lags_ref[h : h + 1, at : at + 2 * TILE], (TILE, 2 * TILE))
            turned = pltpu.roll(row, TILE + 1, 1, stride=1, stride_axis=0)
            tiles[h, d, :, :] = turned[:, :TILE]


def head_lanes(h, heads, channels):
    size = channels // heads
    lane = lax.broadcasted_iota(jnp.int32, (BLOCK, channels), 1)
    return (lane >= h * size) & (lane < (h + 1) * size)


def head_masked(source, target, heads):
    length, channels = source.shape

    for a in range(length // BLOCK):
        part = source[a * BLOCK : (a + 1) * BLOCK, :]
        for h in range(heads):
            target[a, h * BLOCK : (h + 1) * BLOCK, :] = jnp.where(
                head_lanes(h, heads, channels), part, jnp.zeros_like(part)
            )


def starts_of(ends, target):
    rows = lax.broadcasted_iota(jnp.int32, target.shape, 0)
    first = jnp.where(rows >= ends[0], ends[0], 0)
    target[...] = jnp.where(rows >= ends[1], ends[1], first)


def lives_of(starts, a, lag):
    lives = {}
    for i in range(2):
        for j in range(2):
            if 0 <= 2 * lag + i - j < LAGS:
                lane = lax.broadcasted_iota(jnp.int32, (TILE, TILE), 1)
                lane = lane + ((a - lag) * BLOCK + j * TILE)
                lives[i, j] = lane >= starts[pl.ds(a * BLOCK + i * TILE, TILE), :]
    return lives


def mix_kernel(ends, q_ref, k_ref, v_ref, lags_ref, mixed_o, tiles_o, qm, vmask, starts, weights):
    length, local = q_ref.shape
    heads = tiles_o.shape[0]
    make_tiles(lags_ref, tiles_o, heads)
    head_masked(q_ref, qm, heads)
    head_masked(v_ref, vmask, heads)
    starts_of(ends, starts)
    for a in range(length // BLOCK):
        least = max(0, a - REACH + 1)
        for s in range(least, a + 1):
            lag = a - s
            keys = k_ref[s * BLOCK : (s + 1) * BLOCK, :]
            lives = lives_of(starts, a, lag)
            for h in range(heads):
                scores = dot_nt(qm[a, h * BLOCK : (h + 1) * BLOCK, :], keys)
                at = ((s - least) * heads + h) * BLOCK
                for i in range(2):
                    for j in range(2):
                        spot = (slice(i * TILE, (i + 1) * TILE), slice(j * TILE, (j + 1) * TILE))
                        where = (spot[0], slice(at + j * TILE, at + (j + 1) * TILE))
                        if (i, j) in lives:
                            factor = jnp.where(lives[i, j], tiles_o[h, 2 * lag + i - j], 0.0)
                            weights[where] = (factor * scores[spot]).astype(BF)
                        else:
                            weights[where] = jnp.zeros((TILE, TILE), BF)
        wide = (a - least + 1) * heads * BLOCK
        stack = vmask[least : a + 1].reshape(wide, local)
        mixed_o[a * BLOCK : (a + 1) * BLOCK, :] = dot(weights[:, :wide], stack).astype(BF)


def mix_back_kernel(
    meta, ends, q_ref, k_ref, v_ref, gm0, gm1, gm2, gm3, out_ref, tiles, gq_o, gk_o, gv_o, glag_o,
    gmix, qm, gmask, kmask, qt, gt, starts, grads, gkt, gvt, diag
):
    length, local = q_ref.shape
    heads = tiles.shape[0]
    size = local // heads
    quarter = gm0.shape[0]
    blocks = length // BLOCK
    for k, part in enumerate((gm0, gm1, gm2, gm3)):
        base = pl.multiple_of((meta[0] ^ k) * quarter, quarter)
        gmix[pl.ds(base, quarter), :] = dot(part[...], out_ref[0]).astype(BF)
    head_masked(q_ref, qm, heads)
    head_masked(gmix, gmask, heads)
    head_masked(k_ref, kmask, heads)
    starts_of(ends, starts)

    for a in range(blocks):
        spot = slice(a * BLOCK, (a + 1) * BLOCK)
        qt[a, :, :] = q_ref[spot, :].astype(F32).T.astype(BF)
        gt[a, :, :] = gmix[spot, :].astype(F32).T.astype(BF)
    gkt[...] = jnp.zeros_like(gkt)
    gvt[...] = jnp.zeros_like(gvt)
    diag[...] = jnp.zeros_like(diag)
    for a in range(blocks):
        least = max(0, a - REACH + 1)
        for s in range(least, a + 1):
            lag = a - s
            source = slice(s * BLOCK, (s + 1) * BLOCK)
            keys, vals = k_ref[source, :], v_ref[source, :]
            lives = lives_of(starts, a, lag)
            for h in range(heads):
                own = slice(h * BLOCK, (h + 1) * BLOCK)
                scores = dot_nt(qm[a, own, :], keys)
                wgrad = dot_nt(gmask[a, own, :], vals)
                rows_w, rows_g = [], []
                for i in range(2):
                    line_w, line_g = [], []
                    for j in range(2):
                        if (i, j) in lives:
                            d = 2 * lag + i - j
                            spot = (
                                slice(i * TILE, (i + 1) * TILE),
                                slice(j * TILE, (j + 1) * TILE),
                            )
                            factor = jnp.where(lives[i, j], tiles[h, d], 0.0)
                            line_w.append((factor * scores[spot]).astype(BF))
                            line_g.append((wgrad[spot] * factor).astype(BF))
                            diag[h, d] += jnp.where(lives[i, j], wgrad[spot] * scores[spot], 0.0)
                        else:
                            line_w.append(jnp.zeros((TILE, TILE), BF))
                            line_g.append(jnp.zeros((TILE, TILE), BF))
                    rows_w.append(jnp.concatenate(line_w, axis=1))
                    rows_g.append(jnp.concatenate(line_g, axis=1))
                w = jnp.concatenate(rows_w, axis=0)
                g = jnp.concatenate(rows_g, axis=0)
                at = ((s - least) * heads + h) * BLOCK
                grads[:, at : at + BLOCK] = g
                band = slice(h * size, (h + 1) * size)
                gvt[s, band, :] += dot(gt[a, band, :], w)
                gkt[s, band, :] += dot(qt[a, band, :], g)
        wide = (a - least + 1) * heads * BLOCK
        stack = kmask[least : a + 1].reshape(wide, local)
        gq_o[a * BLOCK : (a + 1) * BLOCK, :] = dot(grads[:, :wide], stack).astype(BF)
    for a in range(blocks):
        gk_o[a * BLOCK : (a + 1) * BLOCK, :] = gkt[a].T
        gv_o[a * BLOCK : (a + 1) * BLOCK, :] = gvt[a].T.astype(BF)
    glag_o[...] = jnp.zeros_like(glag_o)
    for h in range(heads):
        for d in range(LAGS):
            line = jnp.concatenate([diag[h, d], jnp.zeros((TILE, TILE), F32)], axis=1)
            rows = TILE
            while rows > 1:
                rows //= 2
                line = pltpu.roll(line[:rows], rows, 1) + line[rows : 2 * rows]
            at = TILE * (LAGS - 1 - d)
            glag_o[h : h + 1, at : at + 2 * TILE] += line


ROOT_HALF = 0.7071067811865476
PHI_SCALE = 0.3989422804014327


def mlp_kernel(near, meta, x_ref, g_ref, m0, m1, m2, m3, vec, *refs):
    n_out = 9 if near else 10
    ins, refs = refs[:-n_out], refs[-n_out:]
    second_o, act_o, gpre_o, gsec_o, ubias_o = refs[:5]
    pre, agrad, mid = refs[-3:]
    if near:
        out_ref, both = ins
        middle_o = refs[5]
    else:
        out_ref, both = refs[5:7]
        count = len(ins) // 2
        if count == 1:
            out_ref[...] = ins[0][...]
            both[...] = ins[1][...]
        else:
            rows = ins[0].shape[2]
            for k in range(count):
                for j in range(2):
                    to = pl.ds(pl.multiple_of((2 * (meta[1] ^ k) + j) * rows, rows), rows)
                    for i in range(4):
                        out_ref[i, to, :] = ins[k][i, j]
                    both[to, :] = ins[count + k][j]
    quarter = pre.shape[0]
    hidden = both.shape[1] // 2
    step = 64
    ubias_o[...] = jnp.zeros_like(ubias_o)

    for n in range(2):
        k = n if near else n + 2
        base = pl.multiple_of((meta[0] ^ k) * quarter, quarter)
        here = k * quarter
        row = n * quarter
        total = x_ref[pl.ds(here, quarter), :].astype(F32) + vec[2:3, :]
        for i, m in enumerate((m0, m1, m2, m3)):
            total = total + dot_nt(m[pl.ds(base, quarter), :], out_ref[i])
        mid[...] = total
        if near:
            middle_o[pl.ds(row, quarter), :] = total
        for i in range(quarter // step):
            normed, _inv = norm_rows(mid[i * step : (i + 1) * step, :])
            second_o[pl.ds(row + i * step, step), :] = (
                normed * vec[3:4, :] + vec[4:5, :]
            ).astype(BF)
        pre[...] = dot(second_o[pl.ds(row, quarter), :], both[:, :hidden])
        agrad[...] = dot(g_ref[pl.ds(here, quarter), :], both[:, hidden:])
        sums = None
        for i in range(quarter // 32):
            to = pl.ds(row + i * 32, 32)
            v = pre[i * 32 : (i + 1) * 32, :] + vec[6:7, :]
            cdf = 0.5 + 0.5 * lax.erf(v * ROOT_HALF)
            act_o[to, :] = (v * cdf).astype(BF)
            slope = cdf + v * (PHI_SCALE * jnp.exp(-0.5 * v * v))
            grad = (slope * agrad[i * 32 : (i + 1) * 32, :]).astype(BF)
            gpre_o[to, :] = grad
            part = folded(grad.astype(F32))
            sums = part if sums is None else sums + part
        ubias_o[...] += sums
        part = dot_nt(gpre_o[pl.ds(row, quarter), :], both[:, :hidden])
        gsec_o[pl.ds(row, quarter), :] = part.astype(gsec_o.dtype)


def ff_grad_kernel(meta, second_a, second_b, gpre_a, gpre_b, cot, act_a, act_b, *refs):
    targets, made = refs[:-1], refs[-1]
    half = second_a.shape[0]
    made[0, :, :] = dot_tn(second_a[...], gpre_a[...]) + dot_tn(second_b[...], gpre_b[...])
    made[1, :, :] = dot_tn(cot[:half, :], act_a[...]) + dot_tn(cot[half:, :], act_b[...])
    rows = targets[0].shape[2]
    for k, target in enumerate(targets):
        for j in range(2):
            spot = pl.ds(pl.multiple_of((2 * (meta[1] ^ k) + j) * rows, rows), rows)
            for i in range(2):
                target[j, i, :, :] = made[i, spot, :].astype(BF)


def early_grad_kernel(meta, first, gq, gv, gm0, gm1, gm2, gm3, mixed, *refs):
    targets, made = refs[:-1], refs[-1]
    quarter = gm0.shape[0]
    made[0, :, :] = dot_tn(gq[...], first[...]).T
    made[1, :, :] = dot_tn(gv[...], first[...]).T
    total = None
    for k, ref in enumerate((gm0, gm1, gm2, gm3)):
        base = pl.multiple_of((meta[0] ^ k) * quarter, quarter)
        part = dot_tn(mixed[pl.ds(base, quarter), :], ref[...])
        total = part if total is None else total + part
    made[2, :, :] = total.T
    rows = targets[0].shape[2]
    for k, target in enumerate(targets):
        for j in range(2):
            spot = pl.ds(pl.multiple_of((2 * (meta[1] ^ k) + j) * rows, rows), rows)
            for i in range(3):
                target[j, i, :, :] = made[i, spot, :].astype(BF)


def middle_back_kernel(part, near, far, cot, middle, vec, gmid_o, gmb_o, sums_o):
    rows, width = far.shape
    step = 64

    def chunk(i, totals):
        at = pl.multiple_of(i * step, step)
        spot = pl.ds(at, step)
        up = part[spot, :] + near[spot, :].astype(F32) + far[spot, :].astype(F32)
        normed, inv = norm_rows(middle[spot, :])
        cotangent = cot[spot, :].astype(F32)
        e = up * vec[3:4, :]
        mean_e = jnp.mean(e, axis=-1, keepdims=True)
        mean_x = jnp.mean(e * normed, axis=-1, keepdims=True)
        grad = cotangent + inv * (e - mean_e - normed * mean_x)
        gmid_o[spot, :] = grad
        gmb_o[spot, :] = grad.astype(BF)
        terms = (grad, up * normed, up, cotangent)
        return tuple(t + folded(x) for t, x in zip(totals, terms))

    totals = lax.fori_loop(
        0, rows // step, chunk, tuple(jnp.zeros((8, width), F32) for _ in range(4)), unroll=True
    )
    sums_o[...] = jnp.zeros_like(sums_o)
    for i, t in enumerate(totals):
        sums_o[2 + i : 3 + i, :] = jnp.sum(t, axis=0, keepdims=True)


def first_back_kernel(meta, part, near, far, tokens, gmid, vec, mean_ref, inv_ref, grad_o):
    rows, width = tokens.shape
    step = 64
    base = pl.multiple_of(meta[0] * rows, rows)

    def chunk(i, _):
        at = pl.multiple_of(i * step, step)
        spot = pl.ds(at, step)
        stat = pl.ds(pl.multiple_of(base + at, step), step)
        up = part[spot, :] + near[spot, :].astype(F32) + far[spot, :].astype(F32)
        inv = inv_ref[stat, :]
        normed = (tokens[spot, :].astype(F32) - mean_ref[stat, :]) * inv
        e = up * vec[0:1, :]
        mean_e = jnp.mean(e, axis=-1, keepdims=True)
        mean_x = jnp.mean(e * normed, axis=-1, keepdims=True)
        grad_o[spot, :] = (gmid[spot, :] + inv * (e - mean_e - normed * mean_x)).astype(BF)
        return 0

    lax.fori_loop(0, rows // step, chunk, 0, unroll=True)


def first_grad_kernel(
    meta, gq, gk, gv, wq, wk, wv, x_ref, mean_ref, inv_ref, sums_two, near_o, far_o, bias_o, made, sums
):
    length, local = gq.shape
    quarter = length // 4
    step = 64
    for i, ref in enumerate((gq, gk, gv)):
        total = jnp.zeros((8, local), F32)
        for j in range(length // 256):
            total = total + folded(ref[256 * j : 256 * j + 256, :].astype(F32))
        bias_o[i, :, :] = total
    sums[...] = jnp.zeros_like(sums)
    for first, target in ((0, near_o), (2, far_o)):

        for n in range(2):
            base = pl.multiple_of((meta[0] ^ (first + n)) * quarter, quarter)
            here = (first + n) * quarter
            total = None
            for ref, weight in ((gq, wq), (gk, wk), (gv, wv)):
                term = dot_nt(ref[pl.ds(base, quarter), :], weight[...])
                total = term if total is None else total + term
            made[...] = total
            row = n * quarter
            target[pl.ds(row, quarter), :] = total.astype(target.dtype)
            for i in range(quarter // step):
                stat = pl.ds(pl.multiple_of(base + i * step, step), step)
                up = made[i * step : (i + 1) * step, :]
                values = x_ref[pl.ds(here + i * step, step), :].astype(F32)
                normed = (values - mean_ref[stat, :]) * inv_ref[stat, :]
                sums[0, :, :] += folded(up * normed)
                sums[1, :, :] += folded(up)
    ends = jnp.concatenate(
        [
            jnp.sum(sums[0], axis=0, keepdims=True),
            jnp.sum(sums[1], axis=0, keepdims=True),
            sums_two[2:8, :],
            jnp.zeros_like(sums_two),
        ],
        axis=0,
    )
    near_o[2 * quarter :, :] = ends
    far_o[2 * quarter :, :] = ends.astype(BF)


def permute(value, groups, target_of):
    pairs = []
    for g in range(groups):
        for c in range(2):
            for z in range(4):
                to = target_of(g, c, z)
                if to is not None:
                    pairs.append((g * 8 + c * 4 + z, to[0] * 8 + to[1] * 4 + to[2]))
    return lax.ppermute(value, AXES, pairs)


def swap_quarters(value, groups):
    return permute(
        value, groups, lambda g, c, z: (g, c, z) if c == z // 2 else (g, 1 - c, z ^ 2)
    )


def to_core(value, groups):
    return permute(value, groups, lambda g, c, z: (g, 1 - c, z))


def to_chip(value, groups):
    return permute(value, groups, lambda g, c, z: (g, c, z ^ 1))


def gather_group(value, groups):
    chip = to_chip(value, groups)
    core = to_core(value, groups)
    both = to_core(chip, groups)
    return value, chip, core, both


def spread_pieces(piece, groups, same):
    near = permute(
        piece, groups, lambda g, c, z: (g, c, z ^ 2) if c == z // 2 else (g, 1 - c, z)
    )
    far = permute(piece, groups, lambda g, c, z: None if c == z // 2 else (g, 1 - c, z ^ 2))
    return jnp.where(same, piece, near), jnp.where(same, near, far)


def halves_of(pieces, half):
    return tuple(lax.dynamic_index_in_dim(pieces, i, 0, False) for i in (half, 1 - half))


def return_pieces(kept, sent, groups, same):
    near = permute(
        sent, groups, lambda g, c, z: (g, 1 - c, z) if c == z // 2 else (g, c, z ^ 2)
    )
    far = permute(kept, groups, lambda g, c, z: None if c == z // 2 else (g, 1 - c, z ^ 2))
    return near.astype(F32) + jnp.where(same, kept, far).astype(F32)


def after(value, *others):
    return lax.optimization_barrier((value, *others))[0]


def pad_to(value, rows, lanes):
    return jnp.pad(value, ((0, rows - value.shape[0]), (0, lanes - value.shape[1])))


def shift_groups(value, groups, k):
    return permute(value, groups, lambda g, c, z: (g ^ k, c, z))


def send_to_groups(pieces, groups, g):
    if groups != 4:
        shape = pieces.shape
        flat = pieces.reshape(groups * 2 * shape[2], shape[3])
        total = lax.psum_scatter(flat, "g", scatter_dimension=0, tiled=True)
        return (total.reshape(shape[1:]),), ()
    sent = [lax.dynamic_index_in_dim(pieces, g ^ k, 0, False) for k in range(groups)]
    return sent, [shift_groups(sent[k], groups, k) for k in (1, 2, 3)]


def grouped(values, groups):
    n, width, columns = values.shape
    pieces = values.reshape(n, groups, 2, width // groups // 2, columns).transpose(1, 2, 0, 3, 4)
    shape = pieces.shape[1:]
    total = lax.psum_scatter(
        pieces.reshape(-1, columns), "g", scatter_dimension=0, tiled=True
    )
    return total.reshape(shape)


def sum_of(sent, came):
    total = sent[0].astype(F32)
    for value in came:
        total = total + value.astype(F32)
    return total.astype(BF)


def plain_pack(triple, out_w, up, down, taps, modes, tbias, ubias, *rest):
    vectors, seg = rest[:6], rest[6]
    _, rows, local = triple.shape
    first_end = jnp.sum((seg[0] < 1).astype(jnp.int32))
    second_end = jnp.sum((seg[0] < 2).astype(jnp.int32))
    ends = jnp.stack([first_end // 32, first_end % 32, second_end // 32, second_end % 32])
    left = jnp.concatenate(
        [
            pad_to(taps, 8, local),
            pad_to(jnp.concatenate(vectors, axis=0), 6, local),
            pad_to(ubias, 1, local),
            pad_to(ends.astype(F32)[None], 1, local),
        ],
        axis=0,
    )
    low = jnp.concatenate([pad_to(tbias[:, 0, :], 8, TILE), pad_to(modes, 8, TILE)], axis=1)
    right = jnp.concatenate([jnp.zeros_like(low), low], axis=0)
    small = jnp.concatenate([left, jnp.zeros((SMALL, 2 * TILE - local), F32), right], axis=1)
    small = pad_to(small, SMALL, 3 * local)
    main = triple.transpose(1, 0, 2).reshape(rows, 3 * local)
    return (
        jnp.concatenate([main, small], axis=0).astype(BF),
        jnp.concatenate([up, down, out_w.T], axis=1).astype(BF),
    )


def plain_small(gtaps, vec_sums, ubias, bias, modes, n_pieces):
    local, width = gtaps.shape[1], vec_sums.shape[1]
    heads = modes.shape[0]

    def by_piece(value):
        return value.reshape(value.shape[0], n_pieces, -1).transpose(1, 0, 2)

    def block_of(value, n_rows, lanes):
        shape = value.shape
        return jnp.pad(value, ((0, 0), (0, n_rows - shape[1]), (0, lanes - shape[2])))

    left = jnp.concatenate([vec_sums[:6], ubias.reshape(1, width)], axis=0)
    pad = local - TILE - modes.shape[1] // n_pieces
    right = block_of(by_piece(bias), 8, local - TILE)
    right = right + jnp.pad(by_piece(modes), ((0, 0), (0, 8 - heads), (pad, 0)))
    low = jnp.concatenate([block_of(by_piece(left), 8, TILE), right], axis=2)
    high = block_of(gtaps.reshape(n_pieces, -1, local), 8, local)
    return jnp.concatenate([high, low], axis=1)


def on_device(
    groups,
    tokens,
    segments,
    row_order,
    first_gain,
    first_shift,
    triple_weight,
    triple_bias,
    shift_taps,
    kernel_modes,
    out_weight,
    out_bias,
    second_gain,
    second_shift,
    up_weight,
    up_bias,
    down_weight,
    down_bias,
    cotangent,
):
    g = lax.axis_index("g")
    c = lax.axis_index("c")
    h = lax.axis_index("h")
    b = lax.axis_index("b")
    same = c == h
    n_pieces = 2 * groups
    quarter, width = tokens.shape[1:]
    length = 4 * quarter
    rows, _, local = triple_weight.shape
    heads = kernel_modes.shape[0]
    n_modes = kernel_modes.shape[1] * n_pieces // 4
    taps_rows = shift_taps.shape[1]
    n_taps = taps_rows * n_pieces
    mode_cols = kernel_modes.shape[1]
    bias_cols = triple_bias.shape[2]
    hidden = up_weight.shape[1]
    q_at = 2 * c + b
    meta = jnp.stack([q_at, g, c, h]).astype(jnp.int32)

    own_x = swap_quarters(tokens[0], groups)
    vectors = (first_gain, first_shift, out_bias, second_gain, second_shift, down_bias)
    raw = (
        triple_weight.transpose(1, 0, 2), out_weight, up_weight, down_weight.T, shift_taps.T,
        kernel_modes, triple_bias, up_bias, *(v[None] for v in vectors), segments,
    )
    if groups == 4:
        a_piece, b_piece = call(
            pack_kernel, 0, raw,
            [((rows + SMALL, 3 * local), BF), ((rows, 2 * hidden + width // 4), BF)],
            [((SMALL, 3 * local), F32)], name="pack", us=2.2,
        )
    else:
        a_piece, b_piece = plain_pack(*raw)
    a_near, a_other = spread_pieces(a_piece, groups, same)
    a_pair = jnp.stack([a_near, a_other])
    x = gather_group(after(own_x, a_piece), groups)
    if groups == 4:
        a_all = [a_pair] + [shift_groups(a_pair, groups, k) for k in (1, 2, 3)]
    else:
        a_all = lax.all_gather(a_pair, "g", axis=0, tiled=False)
        a_all = jnp.where(c == 0, a_all, a_all[:, ::-1]).reshape(n_pieces, rows + SMALL, 3 * local)

    lo, hi = spread_pieces(after(b_piece, x[1]), groups, same)
    first_b, second_b = jnp.where(c == 0, lo, hi), jnp.where(c == 0, hi, lo)
    b_pair = jnp.stack([first_b[:, : 2 * hidden], second_b[:, : 2 * hidden]])
    out_quad = jnp.stack(gather_group(jnp.stack([first_b, second_b])[:, :, 2 * hidden :], groups))
    if groups == 4:
        b_side, b_next = (shift_groups(b_pair, groups, k) for k in (1, 2))
        b_all = [b_pair, b_side, b_next, shift_groups(b_side, groups, 2)]
        out_all = [out_quad] + [shift_groups(out_quad, groups, k) for k in (1, 2, 3)]
    else:
        b_all = [lax.all_gather(b_pair, "g", axis=0, tiled=False).reshape(width, 2 * hidden)]
        out_all = lax.all_gather(out_quad, "g", axis=0, tiled=False)
        out_all = [out_all.transpose(1, 0, 2, 3, 4).reshape(4, width, local)]

    own_cot = swap_quarters(after(cotangent[0], x[1]), groups)
    cot = gather_group(own_cot, groups)

    made = [((length, width), BF), ((length, local), BF), ((length, local), F32)]
    made += [((length, local), BF), ((length, 1), F32), ((length, 1), F32)]
    if groups == 4:
        unpacked = [((width, local), BF)] * 3
        unpacked += [((n_taps, local), F32), ((8, width), F32), ((8, TILE), F32), ((2,), jnp.int32)]
        first, queries, raw_keys, values, mean, inv, wq, wk, wv, taps, vec, modes, ends = call(
            partial(project_kernel, 4), 2, (meta, row_order, *x, *a_all), made + unpacked,
            name="project", us=6.8,
        )
    else:
        weights = a_all[:, :rows, :].reshape(width, 3 * local)
        wq, wk, wv = (weights[:, i * local : (i + 1) * local] for i in range(3))
        small = a_all[:, rows:, :].astype(F32)
        taps = small[:, :taps_rows, :local].reshape(n_taps, local)
        vec = small[:, 8:16, :rows].transpose(1, 0, 2).reshape(8, width)
        bias = small[:, 8:16, 2 * TILE : 2 * TILE + bias_cols].transpose(1, 0, 2).reshape(8, local)
        modes = small[:, 8:16, 3 * TILE : 3 * TILE + mode_cols].transpose(1, 0, 2).reshape(8, TILE)
        mine = (row_order == 2 * g + h)[:, None]
        found = jnp.sum(jnp.where(mine, small[:, 15, :4], 0), axis=0)
        ends = jnp.stack([32 * found[0] + found[1], 32 * found[2] + found[3]]).astype(jnp.int32)
        first, queries, raw_keys, values, mean, inv = call(
            partial(project_kernel, 1), 1, (meta, *x, wq, wk, wv, bias, vec), made,
            name="project", us=6.8,
        )

    modes = modes[:heads]
    lag = LIMIT + TILE - 1 - jnp.arange(6 * TILE, dtype=jnp.int32)
    held = ((lag >= 0) & (lag < LIMIT)).astype(F32)[None, None, :]
    place = jnp.clip(lag, 0, LIMIT - 1).astype(F32)[None, None, :]
    rate = jnp.exp(modes[:, :n_modes])[:, :, None]
    phase = modes[:, n_modes : 2 * n_modes][:, :, None] * place
    decay = jnp.exp(-rate * place) * held
    wave_c, wave_s = decay * jnp.cos(phase), decay * jnp.sin(phase)
    weight_c = modes[:, 2 * n_modes : 3 * n_modes][:, :, None]
    weight_s = modes[:, 3 * n_modes :][:, :, None]
    lags = jnp.sum(weight_c * wave_c + weight_s * wave_s, axis=1)

    padded = length + (SEQUENCES + 1) * GAP
    n_blocks = length // BLOCK
    keys, key_rows = call(
        conv_kernel, 1, (ends, after(raw_keys, own_cot, b_all[1 % len(b_all)]), taps),
        [((length, local), BF), ((padded, local), F32)], [((padded, local), F32)],
        name="conv", us=8.5,
    )
    per_block = (n_blocks, heads * BLOCK, local)
    mixed, tiles = call(
        mix_kernel, 1, (ends, queries, after(keys, cot[1]), values, lags),
        [((length, local), BF), ((heads, LAGS, TILE, TILE), F32)],
        [
            (per_block, BF), (per_block, BF), ((length, TILE), jnp.int32),
            ((BLOCK, REACH * heads * BLOCK), BF),
        ],
        name="mix", us=4.9,
    )
    mixed = after(mixed, *b_all[1:3], *out_all[1:])
    mixes = gather_group(mixed, groups)

    x_all = jnp.concatenate(x, axis=0)
    cot_all = jnp.concatenate(cot, axis=0)
    half = [((2 * quarter, width), BF), ((2 * quarter, hidden), BF), ((2 * quarter, hidden), BF)]
    scratch = [((quarter, hidden), F32), ((quarter, hidden), F32), ((quarter, width), F32)]
    shared = (meta, x_all, cot_all, *mixes, vec)
    second_b, act_b, gpre_b, gsec_b, ubias_b, outs, both = call(
        partial(mlp_kernel, False), 1, (*shared, *out_all, *b_all),
        half
        + [((2 * quarter, width), BF), ((8, hidden), F32), ((4, width, local), BF)]
        + [((width, 2 * hidden), BF)],
        scratch, name="mlp_far", us=8.9,
    )
    came = to_core(gsec_b, groups)
    second_a, act_a, gpre_a, gsec_a, ubias_a, middle = call(
        partial(mlp_kernel, True), 1, (*shared, outs, both),
        half + [((2 * quarter, width), F32), ((8, hidden), F32), ((2 * quarter, width), F32)],
        scratch, name="mlp_near", us=8.8,
    )
    mid_sent = (gsec_a[quarter:] + came[quarter:].astype(F32)).astype(BF)
    far_own = to_chip(mid_sent, groups)

    if groups == 4:
        b_sent = call(
            ff_grad_kernel, 1,
            (meta, after(second_a, mid_sent), second_b, gpre_a, gpre_b, cot_all, act_a, act_b),
            [((2, 2, rows, hidden), BF)] * 4, [((2, width, hidden), F32)], name="ff_grad", us=5.3,
        )
        b_came = [shift_groups(b_sent[k], groups, k) for k in (1, 2, 3)]
    else:
        up_grad = dot_tn(
            jnp.concatenate([second_a, second_b], axis=0), jnp.concatenate([gpre_a, gpre_b], axis=0)
        )
        down_grad = dot_tn(cot_all, jnp.concatenate([act_a, act_b], axis=0))
        b_sent = [grouped(jnp.stack([up_grad, down_grad]).astype(BF), groups)]
        b_came = []
    down_part = both[:, hidden:]
    share_far = dot_nt(after(act_b, mid_sent), down_part).astype(BF)
    share = dot_nt(after(act_a, mid_sent), down_part)
    gmid, gmb_own, sums_two = call(
        middle_back_kernel, 0, (after(gsec_a, share_far, share, *b_sent), came, far_own, own_cot, middle, vec),
        [((quarter, width), F32), ((quarter, width), BF), ((8, width), F32)],
        name="middle_back", us=3.5,
    )
    gmb = gather_group(gmb_own, groups)

    share_near = to_core(share_far, groups).astype(F32)
    share_chip = to_chip((share[quarter:] + share_near[quarter:]).astype(BF), groups)
    gq, gk, gv, glag = call(
        mix_back_kernel, 2,
        (meta, ends, after(queries, share_far, share, *b_came[:2]), keys, values, *gmb, outs, tiles),
        [
            ((length, local), BF), ((length, local), F32), ((length, local), BF),
            ((8, 6 * TILE), F32),
        ],
        [
            ((length, local), BF), (per_block, BF), (per_block, BF), (per_block, BF),
            ((n_blocks, local, BLOCK), BF), ((n_blocks, local, BLOCK), BF),
            ((length, TILE), jnp.int32), ((BLOCK, REACH * heads * BLOCK), BF),
            ((n_blocks, local, BLOCK), F32), ((n_blocks, local, BLOCK), F32),
            ((heads, LAGS, TILE, TILE), F32),
        ],
        name="mix_back", us=12.3,
    )

    b_kept, b_away = halves_of(sum_of(b_sent, [after(v, gk) for v in b_came]), h)
    b_out = return_pieces(b_kept, b_away, groups, same)
    share_chip = after(share_chip, gk).astype(F32)
    result = middle[:quarter] + share[:quarter] + share_near[:quarter] + share_chip + vec[5:6, :]
    result = result.astype(BF)
    graw, grad_rows = call(
        conv_back_kernel, 1, (ends, after(gk, result, b_kept, b_away), taps),
        [((length, local), BF), ((padded, local), F32)], [((padded, local), F32)],
        name="conv_back", us=8.2,
    )
    result = swap_quarters(result, groups)
    share_rows = 2 * quarter + SMALL
    near_part, far_part, gbias = call(
        first_grad_kernel, 1,
        (meta, gq, after(graw, b_out), gv, wq, wk, wv, x_all, mean, inv, sums_two),
        [((share_rows, width), F32), ((share_rows, width), BF), ((3, 8, local), F32)],
        [((quarter, width), F32), ((2, 8, width), F32)],
        name="first_grad", us=5.3,
    )
    came1 = to_core(far_part, groups)
    far_share = near_part[quarter:] + came1[quarter:].astype(F32)
    far_sent = far_share.astype(BF)
    far_own1 = to_chip(far_sent, groups)
    first_late = after(first, far_sent)
    if groups == 4:
        early_sent = call(
            early_grad_kernel, 1, (meta, first_late, gq, gv, *gmb, mixed),
            [((2, 3, rows, local), BF)] * 4, [((3, width, local), F32)], name="early_grad", us=3.0,
        )
        early_came = [shift_groups(early_sent[k], groups, k) for k in (1, 2, 3)]
    else:
        mixed_rel = jnp.concatenate(
            [lax.dynamic_slice_in_dim(mixed, (q_at ^ k) * quarter, quarter, 0) for k in range(4)],
            axis=0,
        )
        out_grad = dot_tn(jnp.concatenate(gmb, axis=0), mixed_rel)
        early = jnp.stack([dot_tn(first_late, gq), dot_tn(first_late, gv), out_grad])
        early_sent, early_came = [grouped(early.astype(BF), groups)], []

    (back,) = call(
        first_back_kernel, 1,
        (meta, after(near_part, result, *early_sent), came1, far_own1, own_x, gmid, vec)
        + (mean, inv),
        [((quarter, width), BF)], name="first_back", us=3.6,
    )
    input_grad = swap_quarters(back, groups)

    early = sum_of(early_sent, [after(v, back) for v in early_came])
    early = early.reshape(2, 3 * rows, local)
    e_kept, e_away = halves_of(early, h)
    main = return_pieces(e_kept, e_away, groups, same).reshape(3, rows, local)

    glags = glag[:heads][:, None, :]
    grad_c = jnp.sum(glags * wave_c, axis=-1)
    grad_s = jnp.sum(glags * wave_s, axis=-1)
    both_waves = weight_c * wave_c + weight_s * wave_s
    turned_waves = weight_s * wave_c - weight_c * wave_s
    grad_rate = -jnp.sum(glags * place * both_waves, axis=-1) * rate[:, :, 0]
    grad_freq = jnp.sum(glags * place * turned_waves, axis=-1)
    modes_grad = jnp.concatenate([grad_rate, grad_freq, grad_c, grad_s], axis=1)

    vec_sums = far_share[quarter:] + far_own1[quarter:].astype(F32)
    if groups == 4:
        late_sent = call(
            late_grad_kernel, 1,
            (meta, grad_rows, after(key_rows, back, e_kept, e_away), first, graw, vec_sums)
            + (ubias_a, ubias_b, gbias, modes_grad),
            [((2, rows + SMALL, local), BF)] * 4,
            [((n_taps, 8, local), F32), ((n_pieces, rows + SMALL, local), F32)],
            name="late_grad", us=11.0,
        )
        late_came = [shift_groups(after(late_sent[k], input_grad), groups, k) for k in (1, 2, 3)]
    else:
        (gtaps,) = call(
            taps_grad_kernel, 0, (grad_rows, key_rows), [((n_taps, local), F32)],
            [((n_taps, 8, local), F32)], name="taps_grad", us=8.2,
        )
        small = plain_small(
            gtaps, vec_sums, jnp.sum(ubias_a + ubias_b, axis=0), jnp.sum(gbias, axis=1), modes_grad,
            n_pieces,
        )
        key_grad = dot_tn(first, graw).reshape(n_pieces, rows, local)
        late = jnp.concatenate([key_grad, small], axis=1).astype(BF)
        late = late.reshape(1, n_pieces * (rows + SMALL), local)
        late_sent, late_came = [grouped(late, groups)[:, 0]], []
    late_out = return_pieces(*halves_of(sum_of(late_sent, late_came), h), groups, same)
    tail = late_out[rows:]
    return (
        result[None],
        input_grad[None],
        tail[8, :rows],
        tail[9, :rows],
        jnp.stack([main[0], late_out[:rows], main[1]]).transpose(1, 0, 2),
        tail[8:11, TILE : TILE + bias_cols][:, None, :],
        tail[:taps_rows].T,
        tail[8 : 8 + heads, local - mode_cols :],
        main[2].T,
        tail[10, :rows],
        tail[11, :rows],
        tail[12, :rows],
        b_out[0],
        tail[14:15, :rows],
        b_out[1].T,
        tail[13, :rows],
    )


def solution(mesh):
    n_data, _ = mesh.devices.shape
    groups = n_data // 2
    fine = Mesh(mesh.devices.reshape(groups, 2, 2, 2), AXES)
    dp, tensor = ("g", "c"), ("h", "b")
    return jax.shard_map(
        partial(on_device, groups),
        mesh=fine,
        in_specs=(
            P(dp, tensor, None),
            P(dp, None),
            P(),
            P(dp),
            P(dp),
            P(dp, None, tensor),
            P(None, tensor, dp),
            P(tensor, dp),
            P(tensor, dp),
            P(tensor, dp),
            P(dp),
            P(dp),
            P(dp),
            P(dp, tensor),
            P(tensor, dp),
            P(tensor, dp),
            P(dp),
            P(dp, tensor, None),
        ),
        out_specs=(
            P(dp, tensor, None),
            P(dp, tensor, None),
            P(dp),
            P(dp),
            P(dp, None, tensor),
            P(None, tensor, dp),
            P(tensor, dp),
            P(tensor, dp),
            P(tensor, dp),
            P(dp),
            P(dp),
            P(dp),
            P(dp, tensor),
            P(tensor, dp),
            P(tensor, dp),
            P(dp),
        ),
        check_vma=False,
    )
```

```python
from functools import partial

import jax
import jax.numpy as jnp
from jax import lax
from jax.experimental import pallas as pl
from jax.experimental.pallas import tpu as pltpu
from jax.sharding import Mesh
from jax.sharding import PartitionSpec as P

EPS = 1e-05
BF = jnp.bfloat16
F32 = jnp.float32
TILE = 128
BLOCK = 256
LAGS = 5
REACH = 3
LIMIT = 512
SEQUENCES = 3
GAP = 64
SMALL = 16
AXES = ("g", "c", "h", "b")
VMEM_BYTES = 56 * 1024 * 1024


def vm():
    return pl.BlockSpec(memory_space=pltpu.VMEM)


def sm():
    return pl.BlockSpec(memory_space=pltpu.SMEM)


def mult(value, factor):
    return value if isinstance(value, int) else pl.multiple_of(value, factor)


def dot(a, b):
    return jnp.dot(a, b, preferred_element_type=F32)


def dot_nt(a, b):
    return lax.dot_general(a, b, (((1,), (1,)), ((), ())), preferred_element_type=F32)


def dot_tn(a, b):
    return lax.dot_general(a, b, (((0,), (0,)), ((), ())), preferred_element_type=F32)


FLOPS_PER_US = 1_150_000_000


def call(kernel, n_smem, args, outs, scratch=(), name=None, us=1.0):
    return pl.pallas_call(
        kernel,
        out_shape=tuple(jax.ShapeDtypeStruct(s, d) for s, d in outs),
        in_specs=[sm()] * n_smem + [vm()] * (len(args) - n_smem),
        out_specs=tuple(sm() if s == (2,) else vm() for s, _ in outs),
        scratch_shapes=[pltpu.VMEM(s, d) for s, d in scratch],
        compiler_params=pltpu.CompilerParams(vmem_limit_bytes=VMEM_BYTES),
        cost_estimate=pl.CostEstimate(
            flops=int(us * FLOPS_PER_US), bytes_accessed=0, transcendentals=0
        ),
        name=name,
    )(*args)


def norm_rows(values):
    mean = jnp.mean(values, axis=-1, keepdims=True)
    centred = values - mean
    variance = jnp.mean(centred * centred, axis=-1, keepdims=True)
    inv = lax.rsqrt(variance + EPS)
    return centred * inv, inv


def folded(values):
    parts = [values[i : i + 8] for i in range(0, values.shape[0], 8)]
    while len(parts) > 1:
        parts = [sum(parts[i : i + 2]) for i in range(0, len(parts), 2)]
    return parts[0]


def eye(n):
    rows = lax.broadcasted_iota(jnp.int32, (n, n), 0)
    return jnp.where(rows == lax.broadcasted_iota(jnp.int32, (n, n), 1), 1.0, 0.0)


def turned(values):
    return dot_nt(eye(values.shape[1]).astype(BF), values.astype(BF))


def pack_kernel(triple, out_w, up, down, taps, modes, tbias, ubias, *refs):
    vectors, (seg, a_o, b_o, box) = refs[:6], refs[6:]
    _, rows, local = triple.shape
    hidden = up.shape[1]
    for i in range(3):
        a_o[:rows, i * local : (i + 1) * local] = triple[i].astype(BF)
    box[...] = jnp.zeros_like(box)
    box[0 : taps.shape[0], 0:local] = taps[...]
    for i, vector in enumerate(vectors):
        box[8 + i : 9 + i, 0:rows] = vector[...]
    box[14:15, 0:rows] = ubias[...]
    for i in range(3):
        box[8 + i : 9 + i, 2 * TILE : 2 * TILE + tbias.shape[2]] = tbias[i]
    box[8 : 8 + modes.shape[0], 3 * TILE : 3 * TILE + modes.shape[1]] = modes[...]
    lane = lax.broadcasted_iota(jnp.int32, (1, TILE), 1)
    line = jnp.zeros((1, TILE), F32)
    for i in range(2):
        count = jnp.sum((seg[...] < i + 1).astype(F32), axis=1, keepdims=True)
        high = jnp.floor(count * (1.0 / 32))
        line = line + jnp.where(lane == 2 * i, high, 0.0)
        line = line + jnp.where(lane == 2 * i + 1, count - 32 * high, 0.0)
    box[15:16, 0:TILE] = line
    a_o[rows:, :] = box[...].astype(BF)
    b_o[:, :hidden] = up[...].astype(BF)
    b_o[:, hidden : 2 * hidden] = down[...].astype(BF)
    b_o[:, 2 * hidden :] = turned(out_w[...]).astype(BF)


def unpack(meta, order, a_refs, weights, taps_o, vec_o, modes_o, ends_o):
    g, c, h = meta[1], meta[2], meta[3]
    rows = a_refs[0].shape[1] - SMALL
    local = weights[0].shape[1]
    width = weights[0].shape[0]
    n_pieces = 2 * len(a_refs)
    bias_cols, mode_cols = local // n_pieces, TILE // n_pieces

    def spot(n_cols, wide, at):
        i = lax.broadcasted_iota(jnp.int32, (TILE, wide), 0)
        n = lax.broadcasted_iota(jnp.int32, (TILE, wide), 1)
        return jnp.where((n == i + at) & (i < n_cols), 1.0, 0.0).astype(BF)

    vec = jnp.zeros((8, width), F32)
    bias = jnp.zeros((8, local), F32)
    modes = jnp.zeros((8, TILE), F32)
    for k, ref in enumerate(a_refs):
        for j in range(2):
            d = 2 * (g ^ k) + (c ^ j)
            at = pl.multiple_of(d * rows, rows)
            for i, target in enumerate(weights):
                target[pl.ds(at, rows), :] = ref[j, :rows, i * local : (i + 1) * local]
            box = ref[j, rows:, :]
            taps_o[pl.ds(pl.multiple_of(d * 8, 8), 8), :] = box[:, :local].astype(F32)[0:8]
            low = box.astype(F32)[8:16].astype(BF)
            vec = vec + dot(low[:, :TILE], spot(rows, width, d * rows))
            bias = bias + dot(low[:, 2 * TILE : 3 * TILE], spot(bias_cols, local, d * bias_cols))
            modes = modes + dot(low[:, 3 * TILE : 4 * TILE], spot(mode_cols, TILE, d * mode_cols))
    vec_o[...] = vec
    modes_o[...] = modes
    own = 0
    for d in range(n_pieces):
        own = own + jnp.where(order[d] == 2 * g + h, d, 0)
    lane = lax.broadcasted_iota(jnp.int32, (1, width), 1)
    for i in range(2):
        scale = jnp.where(lane == own * rows + 2 * i, 32.0, 0.0)
        scale = scale + jnp.where(lane == own * rows + 2 * i + 1, 1.0, 0.0)
        ends_o[i] = jnp.sum(vec[7:8, :] * scale).astype(jnp.int32)
    return bias


def project_kernel(pieces, meta, *refs):
    if pieces > 1:
        order, refs = refs[0], refs[1:]
    x_refs, refs = refs[:4], refs[4:]
    if pieces > 1:
        a_refs, refs = refs[:pieces], refs[pieces:]
        first_o, q_o, k_o, v_o, mean_o, inv_o = refs[:6]
        weights, (taps_o, vec_ref, modes_o, ends_o) = refs[6:9], refs[9:13]
        bias = unpack(meta, order, a_refs, weights, taps_o, vec_ref, modes_o, ends_o)
        biases = [bias[i : i + 1, :] for i in range(3)]
    else:
        weights, (bias_ref, vec_ref) = refs[:3], refs[3:5]
        first_o, q_o, k_o, v_o, mean_o, inv_o = refs[5:]
        local = weights[0].shape[1]
        biases = [bias_ref[i : i + 1, :] for i in range(3)]
    quarter = x_refs[0].shape[0]
    gain, shift = vec_ref[0:1, :], vec_ref[1:2, :]
    step = 64
    for k, ref in enumerate(x_refs):
        first_o[pl.ds(pl.multiple_of((meta[0] ^ k) * quarter, quarter), quarter), :] = ref[...]

    for k in range(4):
        base = k * quarter
        for i in range(quarter // step):
            to = pl.ds(base + i * step, step)
            values = first_o[to, :].astype(F32)
            mean = jnp.mean(values, axis=-1, keepdims=True)
            centred = values - mean
            inv = lax.rsqrt(jnp.mean(centred * centred, axis=-1, keepdims=True) + EPS)
            mean_o[to, :] = mean
            inv_o[to, :] = inv
            first_o[to, :] = (centred * inv * gain + shift).astype(BF)
        rows = first_o[pl.ds(base, quarter), :]
        for target, weight, bias in zip((q_o, k_o, v_o), weights, biases):
            target[pl.ds(base, quarter), :] = (dot(rows, weight[...]) + bias).astype(target.dtype)


def sequence_of(rows, start, stop):
    return (rows >= start).astype(jnp.int32) + (rows >= stop).astype(jnp.int32)


def spread_rows(source, target, ends, length, channels):
    for i in range(target.shape[0] // GAP):
        total = jnp.zeros((GAP, channels), F32)
        for s in range(SEQUENCES):
            j = i - s - 1
            if 0 <= j < length // GAP:
                rows = lax.broadcasted_iota(jnp.int32, (GAP, channels), 0) + j * GAP
                hit = sequence_of(rows, ends[0], ends[1]) == s
                total = total + jnp.where(hit, source[j * GAP : (j + 1) * GAP, :], 0.0)
        target[i * GAP : (i + 1) * GAP, :] = total


def gather_rows(source, target, ends, length, channels):
    for j in range(length // GAP):
        rows = lax.broadcasted_iota(jnp.int32, (GAP, channels), 0) + j * GAP
        ids = sequence_of(rows, ends[0], ends[1])
        total = jnp.zeros((GAP, channels), F32)
        for s in range(SEQUENCES):
            i = j + s + 1
            total = jnp.where(ids == s, source[i * GAP : (i + 1) * GAP, :], total)
        target[j * GAP : (j + 1) * GAP, :] = total.astype(target.dtype)


def taps_sum(pad, taps, target, sign, blocks):
    n_taps = taps.shape[0]
    reach = n_taps - 8

    def block(i, edges):
        at = pl.multiple_of((i + 1 if sign > 0 else blocks - i) * GAP, GAP)
        if sign > 0:
            window = pad[pl.ds(pl.multiple_of(at - reach, 8), GAP + reach), :TILE]
        else:
            window = pad[pl.ds(at, GAP + reach), :TILE]
        total, fresh = None, []
        for r in range(8):
            part = None
            for m in range(n_taps // 8):
                low = reach - 8 * m if sign > 0 else 8 * m
                term = window[low : low + GAP] * taps[8 * m + r : 8 * m + r + 1, :TILE]
                part = term if part is None else part + term
            if r == 0:
                total = part
            elif sign > 0:
                total = total + jnp.concatenate([edges[r - 1], part], axis=0)[8 - r : 8 - r + GAP]
                fresh.append(part[GAP - 8 :])
            else:
                total = total + jnp.concatenate([part, edges[r - 1]], axis=0)[r : r + GAP]
                fresh.append(part[:8])
        target[pl.ds(at, GAP), :TILE] = total
        return tuple(fresh)

    zero = tuple(jnp.zeros((8, TILE), F32) for _ in range(7))
    lax.fori_loop(0, blocks, block, zero, unroll=2)


def side_sum(side, taps, target, sign, blocks):
    n_taps = taps.shape[0]

    def block(i, _):
        at = pl.multiple_of((i + 1) * GAP, GAP)
        window = side[pl.ds(at - GAP if sign > 0 else at, 2 * GAP), :]
        total = None
        for r in range(8):
            part = None
            for m in range(n_taps // 8):
                low = n_taps - 8 - 8 * m if sign > 0 else 8 * m
                term = window[low : low + GAP + 8] * taps[8 * m + r : 8 * m + r + 1, :]
                part = term if part is None else part + term
            part = part[8 - r : 8 - r + GAP] if sign > 0 else part[r : r + GAP]
            total = part if total is None else total + part
        target[pl.ds(at, GAP), :] = total
        return 0

    lax.fori_loop(0, blocks, block, 0)


def fold_side(source, target, stretch):
    rows = target.shape[0]
    half = source.shape[1] - TILE
    target[:, :half] = source[0:rows, TILE:]
    target[:, half:] = source[stretch : stretch + rows, TILE:]


def all_taps(pad, taps, target, sign, side, side_taps, side_made):
    blocks = pad.shape[0] // GAP - 2
    half = pad.shape[1] - TILE
    stretch = blocks // 2 * GAP
    fold_side(pad, side, stretch)
    side_taps[:, :half] = taps[:, TILE:]
    side_taps[:, half:] = taps[:, TILE:]
    taps_sum(pad, taps, target, sign, blocks)
    side_sum(side, side_taps, side_made, sign, blocks // 2)
    target[GAP : GAP + stretch, TILE:] = side_made[GAP : GAP + stretch, :half]
    target[GAP + stretch : GAP + 2 * stretch, TILE:] = side_made[GAP : GAP + stretch, half:]


def conv_kernel(ends, k_ref, taps, kb_o, pad_o, made, side, side_taps, side_made):
    length, channels = k_ref.shape
    spread_rows(k_ref, pad_o, ends, length, channels)
    all_taps(pad_o, taps, made, 1, side, side_taps, side_made)
    gather_rows(made, kb_o, ends, length, channels)


def conv_back_kernel(ends, gk_ref, taps, graw_o, pad_o, made, side, side_taps, side_made):
    length, channels = gk_ref.shape
    spread_rows(gk_ref, pad_o, ends, length, channels)
    all_taps(pad_o, taps, made, -1, side, side_taps, side_made)
    gather_rows(made, graw_o, ends, length, channels)


def taps_grad(grad, keys, sums, side_grad, side_keys):
    n_taps, _, channels = sums.shape
    reach = n_taps - 8
    blocks = grad.shape[0] // GAP - 2
    half = channels - TILE
    fold_side(grad, side_grad, blocks // 2 * GAP)
    fold_side(keys, side_keys, blocks // 2 * GAP)
    totals = []
    for rows_ref, keys_ref, count in ((grad, keys, blocks), (side_grad, side_keys, blocks // 2)):
        sums[:, :, :TILE] = jnp.zeros((n_taps, 8, TILE), F32)

        def block(i, _, rows_ref=rows_ref, keys_ref=keys_ref):
            at = pl.multiple_of((i + 1) * GAP, GAP)
            window = keys_ref[pl.ds(pl.multiple_of(at - reach, 8), GAP + reach), :TILE]
            rows = rows_ref[pl.ds(at, GAP + 8), :TILE]
            for r in range(8):
                turned_rows = pltpu.roll(rows, (GAP + 8 - r) % (GAP + 8), 0)[:GAP]
                for m in range(n_taps // 8):
                    low = reach - 8 * m
                    sums[8 * m + r, :, :TILE] += folded(turned_rows * window[low : low + GAP])
            return 0

        lax.fori_loop(0, count, block, 0)
        totals.append(jnp.sum(sums[:, :, :TILE], axis=1))
    return jnp.concatenate([totals[0], totals[1][:, :half] + totals[1][:, half:]], axis=1)


def taps_grad_kernel(grad, keys, gtaps_o, sums, side_grad, side_keys):
    gtaps_o[...] = taps_grad(grad, keys, sums, side_grad, side_keys)


def late_grad_kernel(meta, grad, keys, first, graw, vec_sums, ubias_a, ubias_b, gbias, modes, *refs):
    targets, (sums, pieces, side_grad, side_keys) = refs[:-4], refs[-4:]
    n_pieces, rows, local = pieces.shape
    rows -= SMALL
    made = dot_tn(graw[...], first[...]).T
    pieces[...] = jnp.zeros_like(pieces)
    ubias = jnp.sum(ubias_a[...] + ubias_b[...], axis=0, keepdims=True)
    bias = jnp.concatenate([jnp.sum(gbias[i], axis=0, keepdims=True) for i in range(3)], axis=0)
    heads = modes.shape[0]
    n_bias, n_modes = local // n_pieces, modes.shape[1] // n_pieces
    low = rows + 8
    gtaps = taps_grad(grad, keys, sums, side_grad, side_keys)
    for d in range(n_pieces):
        pieces[d, :rows, :] = made[d * rows : (d + 1) * rows, :]
        pieces[d, rows:low, :] = gtaps[8 * d : 8 * d + 8, :]
        wide = slice(d * rows, (d + 1) * rows)
        pieces[d, low : low + 6, :rows] = vec_sums[0:6, wide]
        pieces[d, low + 6 : low + 7, :rows] = ubias[:, wide]
        pieces[d, low : low + 3, TILE : TILE + n_bias] = bias[:, d * n_bias : (d + 1) * n_bias]
        pieces[d, low : low + heads, local - n_modes :] = modes[:, d * n_modes : (d + 1) * n_modes]
    for k, target in enumerate(targets):
        for j in range(2):
            target[j, :, :] = pieces[2 * (meta[1] ^ k) + j].astype(BF)


def make_tiles(lags_ref, tiles, heads):
    for h in range(heads):
        for d in range(LAGS):
            at = TILE * (LAGS - 1 - d)
            row = jnp.broadcast_to(lags_ref[h : h + 1, at : at + 2 * TILE], (TILE, 2 * TILE))
            turned = pltpu.roll(row, TILE + 1, 1, stride=1, stride_axis=0)
            tiles[h, d, :, :] = turned[:, :TILE]


def head_lanes(h, heads, channels):
    size = channels // heads
    lane = lax.broadcasted_iota(jnp.int32, (BLOCK, channels), 1)
    return (lane >= h * size) & (lane < (h + 1) * size)


def head_masked(source, target, heads):
    length, channels = source.shape

    for a in range(length // BLOCK):
        part = source[a * BLOCK : (a + 1) * BLOCK, :]
        for h in range(heads):
            target[a, h * BLOCK : (h + 1) * BLOCK, :] = jnp.where(
                head_lanes(h, heads, channels), part, jnp.zeros_like(part)
            )


def starts_of(ends, target):
    rows = lax.broadcasted_iota(jnp.int32, target.shape, 0)
    first = jnp.where(rows >= ends[0], ends[0], 0)
    target[...] = jnp.where(rows >= ends[1], ends[1], first)


def lives_of(starts, a, lag):
    lives = {}
    for i in range(2):
        for j in range(2):
            if 0 <= 2 * lag + i - j < LAGS:
                lane = lax.broadcasted_iota(jnp.int32, (TILE, TILE), 1)
                lane = lane + ((a - lag) * BLOCK + j * TILE)
                lives[i, j] = lane >= starts[pl.ds(a * BLOCK + i * TILE, TILE), :]
    return lives


def mix_kernel(ends, q_ref, k_ref, v_ref, lags_ref, mixed_o, tiles_o, qm, vmask, starts, weights):
    length, local = q_ref.shape
    heads = tiles_o.shape[0]
    make_tiles(lags_ref, tiles_o, heads)
    head_masked(q_ref, qm, heads)
    head_masked(v_ref, vmask, heads)
    starts_of(ends, starts)
    for a in range(length // BLOCK):
        least = max(0, a - REACH + 1)
        for s in range(least, a + 1):
            lag = a - s
            keys = k_ref[s * BLOCK : (s + 1) * BLOCK, :]
            lives = lives_of(starts, a, lag)
            for h in range(heads):
                scores = dot_nt(qm[a, h * BLOCK : (h + 1) * BLOCK, :], keys)
                at = ((s - least) * heads + h) * BLOCK
                for i in range(2):
                    for j in range(2):
                        spot = (slice(i * TILE, (i + 1) * TILE), slice(j * TILE, (j + 1) * TILE))
                        where = (spot[0], slice(at + j * TILE, at + (j + 1) * TILE))
                        if (i, j) in lives:
                            factor = jnp.where(lives[i, j], tiles_o[h, 2 * lag + i - j], 0.0)
                            weights[where] = (factor * scores[spot]).astype(BF)
                        else:
                            weights[where] = jnp.zeros((TILE, TILE), BF)
        wide = (a - least + 1) * heads * BLOCK
        stack = vmask[least : a + 1].reshape(wide, local)
        mixed_o[a * BLOCK : (a + 1) * BLOCK, :] = dot(weights[:, :wide], stack).astype(BF)


def mix_back_kernel(
    meta, ends, q_ref, k_ref, v_ref, gm0, gm1, gm2, gm3, out_ref, tiles, gq_o, gk_o, gv_o, glag_o,
    gmix, qm, gmask, kmask, qt, gt, starts, grads, gkt, gvt, diag
):
    length, local = q_ref.shape
    heads = tiles.shape[0]
    size = local // heads
    quarter = gm0.shape[0]
    blocks = length // BLOCK
    for k, part in enumerate((gm0, gm1, gm2, gm3)):
        base = pl.multiple_of((meta[0] ^ k) * quarter, quarter)
        gmix[pl.ds(base, quarter), :] = dot(part[...], out_ref[0]).astype(BF)
    head_masked(q_ref, qm, heads)
    head_masked(gmix, gmask, heads)
    head_masked(k_ref, kmask, heads)
    starts_of(ends, starts)

    for a in range(blocks):
        spot = slice(a * BLOCK, (a + 1) * BLOCK)
        qt[a, :, :] = q_ref[spot, :].astype(F32).T.astype(BF)
        gt[a, :, :] = gmix[spot, :].astype(F32).T.astype(BF)
    gkt[...] = jnp.zeros_like(gkt)
    gvt[...] = jnp.zeros_like(gvt)
    diag[...] = jnp.zeros_like(diag)
    for a in range(blocks):
        least = max(0, a - REACH + 1)
        for s in range(least, a + 1):
            lag = a - s
            source = slice(s * BLOCK, (s + 1) * BLOCK)
            keys, vals = k_ref[source, :], v_ref[source, :]
            lives = lives_of(starts, a, lag)
            for h in range(heads):
                own = slice(h * BLOCK, (h + 1) * BLOCK)
                scores = dot_nt(qm[a, own, :], keys)
                wgrad = dot_nt(gmask[a, own, :], vals)
                rows_w, rows_g = [], []
                for i in range(2):
                    line_w, line_g = [], []
                    for j in range(2):
                        if (i, j) in lives:
                            d = 2 * lag + i - j
                            spot = (
                                slice(i * TILE, (i + 1) * TILE),
                                slice(j * TILE, (j + 1) * TILE),
                            )
                            factor = jnp.where(lives[i, j], tiles[h, d], 0.0)
                            line_w.append((factor * scores[spot]).astype(BF))
                            line_g.append((wgrad[spot] * factor).astype(BF))
                            diag[h, d] += jnp.where(lives[i, j], wgrad[spot] * scores[spot], 0.0)
                        else:
                            line_w.append(jnp.zeros((TILE, TILE), BF))
                            line_g.append(jnp.zeros((TILE, TILE), BF))
                    rows_w.append(jnp.concatenate(line_w, axis=1))
                    rows_g.append(jnp.concatenate(line_g, axis=1))
                w = jnp.concatenate(rows_w, axis=0)
                g = jnp.concatenate(rows_g, axis=0)
                at = ((s - least) * heads + h) * BLOCK
                grads[:, at : at + BLOCK] = g
                band = slice(h * size, (h + 1) * size)
                gvt[s, band, :] += dot(gt[a, band, :], w)
                gkt[s, band, :] += dot(qt[a, band, :], g)
        wide = (a - least + 1) * heads * BLOCK
        stack = kmask[least : a + 1].reshape(wide, local)
        gq_o[a * BLOCK : (a + 1) * BLOCK, :] = dot(grads[:, :wide], stack).astype(BF)
    for a in range(blocks):
        gk_o[a * BLOCK : (a + 1) * BLOCK, :] = gkt[a].T
        gv_o[a * BLOCK : (a + 1) * BLOCK, :] = gvt[a].T.astype(BF)
    glag_o[...] = jnp.zeros_like(glag_o)
    for h in range(heads):
        for d in range(LAGS):
            line = jnp.concatenate([diag[h, d], jnp.zeros((TILE, TILE), F32)], axis=1)
            rows = TILE
            while rows > 1:
                rows //= 2
                line = pltpu.roll(line[:rows], rows, 1) + line[rows : 2 * rows]
            at = TILE * (LAGS - 1 - d)
            glag_o[h : h + 1, at : at + 2 * TILE] += line


ROOT_HALF = 0.7071067811865476
PHI_SCALE = 0.3989422804014327


def mlp_kernel(near, meta, x_ref, g_ref, m0, m1, m2, m3, vec, *refs):
    n_out = 9 if near else 10
    ins, refs = refs[:-n_out], refs[-n_out:]
    second_o, act_o, gpre_o, gsec_o, ubias_o = refs[:5]
    pre, agrad, mid = refs[-3:]
    if near:
        out_ref, both = ins
        middle_o = refs[5]
    else:
        out_ref, both = refs[5:7]
        count = len(ins) // 2
        if count == 1:
            out_ref[...] = ins[0][...]
            both[...] = ins[1][...]
        else:
            rows = ins[0].shape[2]
            for k in range(count):
                for j in range(2):
                    to = pl.ds(pl.multiple_of((2 * (meta[1] ^ k) + j) * rows, rows), rows)
                    for i in range(4):
                        out_ref[i, to, :] = ins[k][i, j]
                    both[to, :] = ins[count + k][j]
    quarter = pre.shape[0]
    hidden = both.shape[1] // 2
    step = 64
    ubias_o[...] = jnp.zeros_like(ubias_o)

    for n in range(2):
        k = n if near else n + 2
        base = pl.multiple_of((meta[0] ^ k) * quarter, quarter)
        here = k * quarter
        row = n * quarter
        total = x_ref[pl.ds(here, quarter), :].astype(F32) + vec[2:3, :]
        for i, m in enumerate((m0, m1, m2, m3)):
            total = total + dot_nt(m[pl.ds(base, quarter), :], out_ref[i])
        mid[...] = total
        if near:
            middle_o[pl.ds(row, quarter), :] = total
        for i in range(quarter // step):
            normed, _inv = norm_rows(mid[i * step : (i + 1) * step, :])
            second_o[pl.ds(row + i * step, step), :] = (
                normed * vec[3:4, :] + vec[4:5, :]
            ).astype(BF)
        pre[...] = dot(second_o[pl.ds(row, quarter), :], both[:, :hidden])
        agrad[...] = dot(g_ref[pl.ds(here, quarter), :], both[:, hidden:])
        sums = None
        for i in range(quarter // 32):
            to = pl.ds(row + i * 32, 32)
            v = pre[i * 32 : (i + 1) * 32, :] + vec[6:7, :]
            cdf = 0.5 + 0.5 * lax.erf(v * ROOT_HALF)
            act_o[to, :] = (v * cdf).astype(BF)
            slope = cdf + v * (PHI_SCALE * jnp.exp(-0.5 * v * v))
            grad = (slope * agrad[i * 32 : (i + 1) * 32, :]).astype(BF)
            gpre_o[to, :] = grad
            part = folded(grad.astype(F32))
            sums = part if sums is None else sums + part
        ubias_o[...] += sums
        part = dot_nt(gpre_o[pl.ds(row, quarter), :], both[:, :hidden])
        gsec_o[pl.ds(row, quarter), :] = part.astype(gsec_o.dtype)


def ff_grad_kernel(meta, second_a, second_b, gpre_a, gpre_b, cot, act_a, act_b, *refs):
    targets, made = refs[:-1], refs[-1]
    half = second_a.shape[0]
    made[0, :, :] = dot_tn(second_a[...], gpre_a[...]) + dot_tn(second_b[...], gpre_b[...])
    made[1, :, :] = dot_tn(cot[:half, :], act_a[...]) + dot_tn(cot[half:, :], act_b[...])
    rows = targets[0].shape[2]
    for k, target in enumerate(targets):
        for j in range(2):
            spot = pl.ds(pl.multiple_of((2 * (meta[1] ^ k) + j) * rows, rows), rows)
            for i in range(2):
                target[j, i, :, :] = made[i, spot, :].astype(BF)


def early_grad_kernel(meta, first, gq, gv, gm0, gm1, gm2, gm3, mixed, *refs):
    targets, made = refs[:-1], refs[-1]
    quarter = gm0.shape[0]
    made[0, :, :] = dot_tn(gq[...], first[...]).T
    made[1, :, :] = dot_tn(gv[...], first[...]).T
    total = None
    for k, ref in enumerate((gm0, gm1, gm2, gm3)):
        base = pl.multiple_of((meta[0] ^ k) * quarter, quarter)
        part = dot_tn(mixed[pl.ds(base, quarter), :], ref[...])
        total = part if total is None else total + part
    made[2, :, :] = total.T
    rows = targets[0].shape[2]
    for k, target in enumerate(targets):
        for j in range(2):
            spot = pl.ds(pl.multiple_of((2 * (meta[1] ^ k) + j) * rows, rows), rows)
            for i in range(3):
                target[j, i, :, :] = made[i, spot, :].astype(BF)


def middle_back_kernel(part, near, far, cot, middle, vec, gmid_o, gmb_o, sums_o):
    rows, width = far.shape
    step = 64

    def chunk(i, totals):
        at = pl.multiple_of(i * step, step)
        spot = pl.ds(at, step)
        up = part[spot, :] + near[spot, :].astype(F32) + far[spot, :].astype(F32)
        normed, inv = norm_rows(middle[spot, :])
        cotangent = cot[spot, :].astype(F32)
        e = up * vec[3:4, :]
        mean_e = jnp.mean(e, axis=-1, keepdims=True)
        mean_x = jnp.mean(e * normed, axis=-1, keepdims=True)
        grad = cotangent + inv * (e - mean_e - normed * mean_x)
        gmid_o[spot, :] = grad
        gmb_o[spot, :] = grad.astype(BF)
        terms = (grad, up * normed, up, cotangent)
        return tuple(t + folded(x) for t, x in zip(totals, terms))

    totals = lax.fori_loop(
        0, rows // step, chunk, tuple(jnp.zeros((8, width), F32) for _ in range(4)), unroll=True
    )
    sums_o[...] = jnp.zeros_like(sums_o)
    for i, t in enumerate(totals):
        sums_o[2 + i : 3 + i, :] = jnp.sum(t, axis=0, keepdims=True)


def first_back_kernel(meta, part, near, far, tokens, gmid, vec, mean_ref, inv_ref, grad_o):
    rows, width = tokens.shape
    step = 64
    base = pl.multiple_of(meta[0] * rows, rows)

    def chunk(i, _):
        at = pl.multiple_of(i * step, step)
        spot = pl.ds(at, step)
        stat = pl.ds(pl.multiple_of(base + at, step), step)
        up = part[spot, :] + near[spot, :].astype(F32) + far[spot, :].astype(F32)
        inv = inv_ref[stat, :]
        normed = (tokens[spot, :].astype(F32) - mean_ref[stat, :]) * inv
        e = up * vec[0:1, :]
        mean_e = jnp.mean(e, axis=-1, keepdims=True)
        mean_x = jnp.mean(e * normed, axis=-1, keepdims=True)
        grad_o[spot, :] = (gmid[spot, :] + inv * (e - mean_e - normed * mean_x)).astype(BF)
        return 0

    lax.fori_loop(0, rows // step, chunk, 0, unroll=True)


def first_grad_kernel(
    meta, gq, gk, gv, wq, wk, wv, x_ref, mean_ref, inv_ref, sums_two, near_o, far_o, bias_o, made, sums
):
    length, local = gq.shape
    quarter = length // 4
    step = 64
    for i, ref in enumerate((gq, gk, gv)):
        total = jnp.zeros((8, local), F32)
        for j in range(length // 256):
            total = total + folded(ref[256 * j : 256 * j + 256, :].astype(F32))
        bias_o[i, :, :] = total
    sums[...] = jnp.zeros_like(sums)
    for first, target in ((0, near_o), (2, far_o)):

        for n in range(2):
            base = pl.multiple_of((meta[0] ^ (first + n)) * quarter, quarter)
            here = (first + n) * quarter
            total = None
            for ref, weight in ((gq, wq), (gk, wk), (gv, wv)):
                term = dot_nt(ref[pl.ds(base, quarter), :], weight[...])
                total = term if total is None else total + term
            made[...] = total
            row = n * quarter
            target[pl.ds(row, quarter), :] = total.astype(target.dtype)
            for i in range(quarter // step):
                stat = pl.ds(pl.multiple_of(base + i * step, step), step)
                up = made[i * step : (i + 1) * step, :]
                values = x_ref[pl.ds(here + i * step, step), :].astype(F32)
                normed = (values - mean_ref[stat, :]) * inv_ref[stat, :]
                sums[0, :, :] += folded(up * normed)
                sums[1, :, :] += folded(up)
    ends = jnp.concatenate(
        [
            jnp.sum(sums[0], axis=0, keepdims=True),
            jnp.sum(sums[1], axis=0, keepdims=True),
            sums_two[2:8, :],
            jnp.zeros_like(sums_two),
        ],
        axis=0,
    )
    near_o[2 * quarter :, :] = ends
    far_o[2 * quarter :, :] = ends.astype(BF)


def permute(value, groups, target_of):
    pairs = []
    for g in range(groups):
        for c in range(2):
            for z in range(4):
                to = target_of(g, c, z)
                if to is not None:
                    pairs.append((g * 8 + c * 4 + z, to[0] * 8 + to[1] * 4 + to[2]))
    return lax.ppermute(value, AXES, pairs)


def swap_quarters(value, groups):
    return permute(
        value, groups, lambda g, c, z: (g, c, z) if c == z // 2 else (g, 1 - c, z ^ 2)
    )


def to_core(value, groups):
    return permute(value, groups, lambda g, c, z: (g, 1 - c, z))


def to_chip(value, groups):
    return permute(value, groups, lambda g, c, z: (g, c, z ^ 1))


def gather_group(value, groups):
    chip = to_chip(value, groups)
    core = to_core(value, groups)
    both = to_core(chip, groups)
    return value, chip, core, both


def spread_pieces(piece, groups, same):
    near = permute(
        piece, groups, lambda g, c, z: (g, c, z ^ 2) if c == z // 2 else (g, 1 - c, z)
    )
    far = permute(piece, groups, lambda g, c, z: None if c == z // 2 else (g, 1 - c, z ^ 2))
    return jnp.where(same, piece, near), jnp.where(same, near, far)


def halves_of(pieces, half):
    return tuple(lax.dynamic_index_in_dim(pieces, i, 0, False) for i in (half, 1 - half))


def return_pieces(kept, sent, groups, same):
    near = permute(
        sent, groups, lambda g, c, z: (g, 1 - c, z) if c == z // 2 else (g, c, z ^ 2)
    )
    far = permute(kept, groups, lambda g, c, z: None if c == z // 2 else (g, 1 - c, z ^ 2))
    return near.astype(F32) + jnp.where(same, kept, far).astype(F32)


def after(value, *others):
    return lax.optimization_barrier((value, *others))[0]


def pad_to(value, rows, lanes):
    return jnp.pad(value, ((0, rows - value.shape[0]), (0, lanes - value.shape[1])))


def shift_groups(value, groups, k):
    return permute(value, groups, lambda g, c, z: (g ^ k, c, z))


def send_to_groups(pieces, groups, g):
    if groups != 4:
        shape = pieces.shape
        flat = pieces.reshape(groups * 2 * shape[2], shape[3])
        total = lax.psum_scatter(flat, "g", scatter_dimension=0, tiled=True)
        return (total.reshape(shape[1:]),), ()
    sent = [lax.dynamic_index_in_dim(pieces, g ^ k, 0, False) for k in range(groups)]
    return sent, [shift_groups(sent[k], groups, k) for k in (1, 2, 3)]


def grouped(values, groups):
    n, width, columns = values.shape
    pieces = values.reshape(n, groups, 2, width // groups // 2, columns).transpose(1, 2, 0, 3, 4)
    shape = pieces.shape[1:]
    total = lax.psum_scatter(
        pieces.reshape(-1, columns), "g", scatter_dimension=0, tiled=True
    )
    return total.reshape(shape)


def sum_of(sent, came):
    total = sent[0].astype(F32)
    for value in came:
        total = total + value.astype(F32)
    return total.astype(BF)


def plain_pack(triple, out_w, up, down, taps, modes, tbias, ubias, *rest):
    vectors, seg = rest[:6], rest[6]
    _, rows, local = triple.shape
    first_end = jnp.sum((seg[0] < 1).astype(jnp.int32))
    second_end = jnp.sum((seg[0] < 2).astype(jnp.int32))
    ends = jnp.stack([first_end // 32, first_end % 32, second_end // 32, second_end % 32])
    left = jnp.concatenate(
        [
            pad_to(taps, 8, local),
            pad_to(jnp.concatenate(vectors, axis=0), 6, local),
            pad_to(ubias, 1, local),
            pad_to(ends.astype(F32)[None], 1, local),
        ],
        axis=0,
    )
    low = jnp.concatenate([pad_to(tbias[:, 0, :], 8, TILE), pad_to(modes, 8, TILE)], axis=1)
    right = jnp.concatenate([jnp.zeros_like(low), low], axis=0)
    small = jnp.concatenate([left, jnp.zeros((SMALL, 2 * TILE - local), F32), right], axis=1)
    small = pad_to(small, SMALL, 3 * local)
    main = triple.transpose(1, 0, 2).reshape(rows, 3 * local)
    return (
        jnp.concatenate([main, small], axis=0).astype(BF),
        jnp.concatenate([up, down, out_w.T], axis=1).astype(BF),
    )


def plain_small(gtaps, vec_sums, ubias, bias, modes, n_pieces):
    local, width = gtaps.shape[1], vec_sums.shape[1]
    heads = modes.shape[0]

    def by_piece(value):
        return value.reshape(value.shape[0], n_pieces, -1).transpose(1, 0, 2)

    def block_of(value, n_rows, lanes):
        shape = value.shape
        return jnp.pad(value, ((0, 0), (0, n_rows - shape[1]), (0, lanes - shape[2])))

    left = jnp.concatenate([vec_sums[:6], ubias.reshape(1, width)], axis=0)
    pad = local - TILE - modes.shape[1] // n_pieces
    right = block_of(by_piece(bias), 8, local - TILE)
    right = right + jnp.pad(by_piece(modes), ((0, 0), (0, 8 - heads), (pad, 0)))
    low = jnp.concatenate([block_of(by_piece(left), 8, TILE), right], axis=2)
    high = block_of(gtaps.reshape(n_pieces, -1, local), 8, local)
    return jnp.concatenate([high, low], axis=1)


def on_device(
    groups,
    tokens,
    segments,
    row_order,
    first_gain,
    first_shift,
    triple_weight,
    triple_bias,
    shift_taps,
    kernel_modes,
    out_weight,
    out_bias,
    second_gain,
    second_shift,
    up_weight,
    up_bias,
    down_weight,
    down_bias,
    cotangent,
):
    g = lax.axis_index("g")
    c = lax.axis_index("c")
    h = lax.axis_index("h")
    b = lax.axis_index("b")
    same = c == h
    n_pieces = 2 * groups
    quarter, width = tokens.shape[1:]
    length = 4 * quarter
    rows, _, local = triple_weight.shape
    heads = kernel_modes.shape[0]
    n_modes = kernel_modes.shape[1] * n_pieces // 4
    taps_rows = shift_taps.shape[1]
    n_taps = taps_rows * n_pieces
    mode_cols = kernel_modes.shape[1]
    bias_cols = triple_bias.shape[2]
    hidden = up_weight.shape[1]
    q_at = 2 * c + b
    meta = jnp.stack([q_at, g, c, h]).astype(jnp.int32)

    own_x = swap_quarters(tokens[0], groups)
    vectors = (first_gain, first_shift, out_bias, second_gain, second_shift, down_bias)
    raw = (
        triple_weight.transpose(1, 0, 2), out_weight, up_weight, down_weight.T, shift_taps.T,
        kernel_modes, triple_bias, up_bias, *(v[None] for v in vectors), segments,
    )
    if groups == 4:
        a_piece, b_piece = call(
            pack_kernel, 0, raw,
            [((rows + SMALL, 3 * local), BF), ((rows, 2 * hidden + width // 4), BF)],
            [((SMALL, 3 * local), F32)], name="pack", us=2.2,
        )
    else:
        a_piece, b_piece = plain_pack(*raw)
    a_near, a_other = spread_pieces(a_piece, groups, same)
    a_pair = jnp.stack([a_near, a_other])
    x = gather_group(after(own_x, a_piece), groups)
    if groups == 4:
        a_all = [a_pair] + [shift_groups(a_pair, groups, k) for k in (1, 2, 3)]
    else:
        a_all = lax.all_gather(a_pair, "g", axis=0, tiled=False)
        a_all = jnp.where(c == 0, a_all, a_all[:, ::-1]).reshape(n_pieces, rows + SMALL, 3 * local)

    lo, hi = spread_pieces(after(b_piece, x[1]), groups, same)
    first_b, second_b = jnp.where(c == 0, lo, hi), jnp.where(c == 0, hi, lo)
    b_pair = jnp.stack([first_b[:, : 2 * hidden], second_b[:, : 2 * hidden]])
    out_quad = jnp.stack(gather_group(jnp.stack([first_b, second_b])[:, :, 2 * hidden :], groups))
    if groups == 4:
        b_side, b_next = (shift_groups(b_pair, groups, k) for k in (1, 2))
        b_all = [b_pair, b_side, b_next, shift_groups(b_side, groups, 2)]
        out_all = [out_quad] + [shift_groups(out_quad, groups, k) for k in (1, 2, 3)]
    else:
        b_all = [lax.all_gather(b_pair, "g", axis=0, tiled=False).reshape(width, 2 * hidden)]
        out_all = lax.all_gather(out_quad, "g", axis=0, tiled=False)
        out_all = [out_all.transpose(1, 0, 2, 3, 4).reshape(4, width, local)]

    own_cot = swap_quarters(after(cotangent[0], x[1]), groups)
    cot = gather_group(own_cot, groups)

    made = [((length, width), BF), ((length, local), BF), ((length, local), F32)]
    made += [((length, local), BF), ((length, 1), F32), ((length, 1), F32)]
    if groups == 4:
        unpacked = [((width, local), BF)] * 3
        unpacked += [((n_taps, local), F32), ((8, width), F32), ((8, TILE), F32), ((2,), jnp.int32)]
        first, queries, raw_keys, values, mean, inv, wq, wk, wv, taps, vec, modes, ends = call(
            partial(project_kernel, 4), 2, (meta, row_order, *x, *a_all), made + unpacked,
            name="project", us=6.8,
        )
    else:
        weights = a_all[:, :rows, :].reshape(width, 3 * local)
        wq, wk, wv = (weights[:, i * local : (i + 1) * local] for i in range(3))
        small = a_all[:, rows:, :].astype(F32)
        taps = small[:, :taps_rows, :local].reshape(n_taps, local)
        vec = small[:, 8:16, :rows].transpose(1, 0, 2).reshape(8, width)
        bias = small[:, 8:16, 2 * TILE : 2 * TILE + bias_cols].transpose(1, 0, 2).reshape(8, local)
        modes = small[:, 8:16, 3 * TILE : 3 * TILE + mode_cols].transpose(1, 0, 2).reshape(8, TILE)
        mine = (row_order == 2 * g + h)[:, None]
        found = jnp.sum(jnp.where(mine, small[:, 15, :4], 0), axis=0)
        ends = jnp.stack([32 * found[0] + found[1], 32 * found[2] + found[3]]).astype(jnp.int32)
        first, queries, raw_keys, values, mean, inv = call(
            partial(project_kernel, 1), 1, (meta, *x, wq, wk, wv, bias, vec), made,
            name="project", us=6.8,
        )

    modes = modes[:heads]
    lag = LIMIT + TILE - 1 - jnp.arange(6 * TILE, dtype=jnp.int32)
    held = ((lag >= 0) & (lag < LIMIT)).astype(F32)[None, None, :]
    place = jnp.clip(lag, 0, LIMIT - 1).astype(F32)[None, None, :]
    rate = jnp.exp(modes[:, :n_modes])[:, :, None]
    phase = modes[:, n_modes : 2 * n_modes][:, :, None] * place
    decay = jnp.exp(-rate * place) * held
    wave_c, wave_s = decay * jnp.cos(phase), decay * jnp.sin(phase)
    weight_c = modes[:, 2 * n_modes : 3 * n_modes][:, :, None]
    weight_s = modes[:, 3 * n_modes :][:, :, None]
    lags = jnp.sum(weight_c * wave_c + weight_s * wave_s, axis=1)

    padded = length + (SEQUENCES + 1) * GAP
    sides = [((padded // 2 + GAP, TILE), F32)]
    conv_scratch = [((padded, local), F32), *sides, ((n_taps, TILE), F32), *sides]
    n_blocks = length // BLOCK
    keys, key_rows = call(
        conv_kernel, 1, (ends, after(raw_keys, own_cot, b_all[1 % len(b_all)]), taps),
        [((length, local), BF), ((padded, local), F32)], conv_scratch,
        name="conv", us=7.5,
    )
    per_block = (n_blocks, heads * BLOCK, local)
    mixed, tiles = call(
        mix_kernel, 1, (ends, queries, after(keys, cot[1]), values, lags),
        [((length, local), BF), ((heads, LAGS, TILE, TILE), F32)],
        [
            (per_block, BF), (per_block, BF), ((length, TILE), jnp.int32),
            ((BLOCK, REACH * heads * BLOCK), BF),
        ],
        name="mix", us=4.9,
    )
    mixed = after(mixed, *b_all[1:3], *out_all[1:])
    mixes = gather_group(mixed, groups)

    x_all = jnp.concatenate(x, axis=0)
    cot_all = jnp.concatenate(cot, axis=0)
    half = [((2 * quarter, width), BF), ((2 * quarter, hidden), BF), ((2 * quarter, hidden), BF)]
    scratch = [((quarter, hidden), F32), ((quarter, hidden), F32), ((quarter, width), F32)]
    shared = (meta, x_all, cot_all, *mixes, vec)
    second_b, act_b, gpre_b, gsec_b, ubias_b, outs, both = call(
        partial(mlp_kernel, False), 1, (*shared, *out_all, *b_all),
        half
        + [((2 * quarter, width), BF), ((8, hidden), F32), ((4, width, local), BF)]
        + [((width, 2 * hidden), BF)],
        scratch, name="mlp_far", us=8.9,
    )
    came = to_core(gsec_b, groups)
    second_a, act_a, gpre_a, gsec_a, ubias_a, middle = call(
        partial(mlp_kernel, True), 1, (*shared, outs, both),
        half + [((2 * quarter, width), F32), ((8, hidden), F32), ((2 * quarter, width), F32)],
        scratch, name="mlp_near", us=8.8,
    )
    mid_sent = (gsec_a[quarter:] + came[quarter:].astype(F32)).astype(BF)
    far_own = to_chip(mid_sent, groups)

    if groups == 4:
        b_sent = call(
            ff_grad_kernel, 1,
            (meta, after(second_a, mid_sent), second_b, gpre_a, gpre_b, cot_all, act_a, act_b),
            [((2, 2, rows, hidden), BF)] * 4, [((2, width, hidden), F32)], name="ff_grad", us=5.3,
        )
        b_came = [shift_groups(b_sent[k], groups, k) for k in (1, 2, 3)]
    else:
        up_grad = dot_tn(
            jnp.concatenate([second_a, second_b], axis=0), jnp.concatenate([gpre_a, gpre_b], axis=0)
        )
        down_grad = dot_tn(cot_all, jnp.concatenate([act_a, act_b], axis=0))
        b_sent = [grouped(jnp.stack([up_grad, down_grad]).astype(BF), groups)]
        b_came = []
    down_part = both[:, hidden:]
    share_far = dot_nt(after(act_b, mid_sent), down_part).astype(BF)
    share = dot_nt(after(act_a, mid_sent), down_part)
    gmid, gmb_own, sums_two = call(
        middle_back_kernel, 0, (after(gsec_a, share_far, share, *b_sent), came, far_own, own_cot, middle, vec),
        [((quarter, width), F32), ((quarter, width), BF), ((8, width), F32)],
        name="middle_back", us=3.5,
    )
    gmb = gather_group(gmb_own, groups)

    share_near = to_core(share_far, groups).astype(F32)
    share_chip = to_chip((share[quarter:] + share_near[quarter:]).astype(BF), groups)
    gq, gk, gv, glag = call(
        mix_back_kernel, 2,
        (meta, ends, after(queries, share_far, share, *b_came[:2]), keys, values, *gmb, outs, tiles),
        [
            ((length, local), BF), ((length, local), F32), ((length, local), BF),
            ((8, 6 * TILE), F32),
        ],
        [
            ((length, local), BF), (per_block, BF), (per_block, BF), (per_block, BF),
            ((n_blocks, local, BLOCK), BF), ((n_blocks, local, BLOCK), BF),
            ((length, TILE), jnp.int32), ((BLOCK, REACH * heads * BLOCK), BF),
            ((n_blocks, local, BLOCK), F32), ((n_blocks, local, BLOCK), F32),
            ((heads, LAGS, TILE, TILE), F32),
        ],
        name="mix_back", us=12.3,
    )

    b_kept, b_away = halves_of(sum_of(b_sent, [after(v, gk) for v in b_came]), h)
    b_out = return_pieces(b_kept, b_away, groups, same)
    share_chip = after(share_chip, gk).astype(F32)
    result = middle[:quarter] + share[:quarter] + share_near[:quarter] + share_chip + vec[5:6, :]
    result = result.astype(BF)
    graw, grad_rows = call(
        conv_back_kernel, 1, (ends, after(gk, result, b_kept, b_away), taps),
        [((length, local), BF), ((padded, local), F32)], conv_scratch,
        name="conv_back", us=7.2,
    )
    result = swap_quarters(result, groups)
    share_rows = 2 * quarter + SMALL
    near_part, far_part, gbias = call(
        first_grad_kernel, 1,
        (meta, gq, after(graw, b_out), gv, wq, wk, wv, x_all, mean, inv, sums_two),
        [((share_rows, width), F32), ((share_rows, width), BF), ((3, 8, local), F32)],
        [((quarter, width), F32), ((2, 8, width), F32)],
        name="first_grad", us=5.3,
    )
    came1 = to_core(far_part, groups)
    far_share = near_part[quarter:] + came1[quarter:].astype(F32)
    far_sent = far_share.astype(BF)
    far_own1 = to_chip(far_sent, groups)
    first_late = after(first, far_sent)
    if groups == 4:
        early_sent = call(
            early_grad_kernel, 1, (meta, first_late, gq, gv, *gmb, mixed),
            [((2, 3, rows, local), BF)] * 4, [((3, width, local), F32)], name="early_grad", us=3.0,
        )
        early_came = [shift_groups(early_sent[k], groups, k) for k in (1, 2, 3)]
    else:
        mixed_rel = jnp.concatenate(
            [lax.dynamic_slice_in_dim(mixed, (q_at ^ k) * quarter, quarter, 0) for k in range(4)],
            axis=0,
        )
        out_grad = dot_tn(jnp.concatenate(gmb, axis=0), mixed_rel)
        early = jnp.stack([dot_tn(first_late, gq), dot_tn(first_late, gv), out_grad])
        early_sent, early_came = [grouped(early.astype(BF), groups)], []

    (back,) = call(
        first_back_kernel, 1,
        (meta, after(near_part, result, *early_sent), came1, far_own1, own_x, gmid, vec)
        + (mean, inv),
        [((quarter, width), BF)], name="first_back", us=3.6,
    )
    input_grad = swap_quarters(back, groups)

    early = sum_of(early_sent, [after(v, back) for v in early_came])
    early = early.reshape(2, 3 * rows, local)
    e_kept, e_away = halves_of(early, h)
    main = return_pieces(e_kept, e_away, groups, same).reshape(3, rows, local)

    glags = glag[:heads][:, None, :]
    grad_c = jnp.sum(glags * wave_c, axis=-1)
    grad_s = jnp.sum(glags * wave_s, axis=-1)
    both_waves = weight_c * wave_c + weight_s * wave_s
    turned_waves = weight_s * wave_c - weight_c * wave_s
    grad_rate = -jnp.sum(glags * place * both_waves, axis=-1) * rate[:, :, 0]
    grad_freq = jnp.sum(glags * place * turned_waves, axis=-1)
    modes_grad = jnp.concatenate([grad_rate, grad_freq, grad_c, grad_s], axis=1)

    vec_sums = far_share[quarter:] + far_own1[quarter:].astype(F32)
    if groups == 4:
        late_sent = call(
            late_grad_kernel, 1,
            (meta, grad_rows, after(key_rows, back, e_kept, e_away), first, graw, vec_sums)
            + (ubias_a, ubias_b, gbias, modes_grad),
            [((2, rows + SMALL, local), BF)] * 4,
            [((n_taps, 8, local), F32), ((n_pieces, rows + SMALL, local), F32), *sides, *sides],
            name="late_grad", us=11.0,
        )
        late_came = [shift_groups(after(late_sent[k], input_grad), groups, k) for k in (1, 2, 3)]
    else:
        (gtaps,) = call(
            taps_grad_kernel, 0, (grad_rows, key_rows), [((n_taps, local), F32)],
            [((n_taps, 8, local), F32), *sides, *sides], name="taps_grad", us=8.2,
        )
        small = plain_small(
            gtaps, vec_sums, jnp.sum(ubias_a + ubias_b, axis=0), jnp.sum(gbias, axis=1), modes_grad,
            n_pieces,
        )
        key_grad = dot_tn(first, graw).reshape(n_pieces, rows, local)
        late = jnp.concatenate([key_grad, small], axis=1).astype(BF)
        late = late.reshape(1, n_pieces * (rows + SMALL), local)
        late_sent, late_came = [grouped(late, groups)[:, 0]], []
    late_out = return_pieces(*halves_of(sum_of(late_sent, late_came), h), groups, same)
    tail = late_out[rows:]
    return (
        result[None],
        input_grad[None],
        tail[8, :rows],
        tail[9, :rows],
        jnp.stack([main[0], late_out[:rows], main[1]]).transpose(1, 0, 2),
        tail[8:11, TILE : TILE + bias_cols][:, None, :],
        tail[:taps_rows].T,
        tail[8 : 8 + heads, local - mode_cols :],
        main[2].T,
        tail[10, :rows],
        tail[11, :rows],
        tail[12, :rows],
        b_out[0],
        tail[14:15, :rows],
        b_out[1].T,
        tail[13, :rows],
    )


def solution(mesh):
    n_data, _ = mesh.devices.shape
    groups = n_data // 2
    fine = Mesh(mesh.devices.reshape(groups, 2, 2, 2), AXES)
    dp, tensor = ("g", "c"), ("h", "b")
    return jax.shard_map(
        partial(on_device, groups),
        mesh=fine,
        in_specs=(
            P(dp, tensor, None),
            P(dp, None),
            P(),
            P(dp),
            P(dp),
            P(dp, None, tensor),
            P(None, tensor, dp),
            P(tensor, dp),
            P(tensor, dp),
            P(tensor, dp),
            P(dp),
            P(dp),
            P(dp),
            P(dp, tensor),
            P(tensor, dp),
            P(tensor, dp),
            P(dp),
            P(dp, tensor, None),
        ),
        out_specs=(
            P(dp, tensor, None),
            P(dp, tensor, None),
            P(dp),
            P(dp),
            P(dp, None, tensor),
            P(None, tensor, dp),
            P(tensor, dp),
            P(tensor, dp),
            P(tensor, dp),
            P(dp),
            P(dp),
            P(dp),
            P(dp, tensor),
            P(tensor, dp),
            P(tensor, dp),
            P(dp),
        ),
        check_vma=False,
    )
```

```python
from functools import partial

import jax
import jax.numpy as jnp
from jax import lax
from jax.experimental import pallas as pl
from jax.experimental.pallas import tpu as pltpu
from jax.sharding import Mesh
from jax.sharding import PartitionSpec as P

EPS = 1e-05
BF = jnp.bfloat16
F32 = jnp.float32
TILE = 128
BLOCK = 256
LAGS = 5
REACH = 3
LIMIT = 512
SEQUENCES = 3
GAP = 64
SMALL = 16
AXES = ("g", "c", "h", "b")
VMEM_BYTES = 56 * 1024 * 1024


def vm():
    return pl.BlockSpec(memory_space=pltpu.VMEM)


def sm():
    return pl.BlockSpec(memory_space=pltpu.SMEM)


def mult(value, factor):
    return value if isinstance(value, int) else pl.multiple_of(value, factor)


def dot(a, b):
    return jnp.dot(a, b, preferred_element_type=F32)


def dot_nt(a, b):
    return lax.dot_general(a, b, (((1,), (1,)), ((), ())), preferred_element_type=F32)


def dot_tn(a, b):
    return lax.dot_general(a, b, (((0,), (0,)), ((), ())), preferred_element_type=F32)


FLOPS_PER_US = 1_150_000_000


def call(kernel, n_smem, args, outs, scratch=(), name=None, us=1.0):
    return pl.pallas_call(
        kernel,
        out_shape=tuple(jax.ShapeDtypeStruct(s, d) for s, d in outs),
        in_specs=[sm()] * n_smem + [vm()] * (len(args) - n_smem),
        out_specs=tuple(sm() if s == (2,) else vm() for s, _ in outs),
        scratch_shapes=[pltpu.VMEM(s, d) for s, d in scratch],
        compiler_params=pltpu.CompilerParams(vmem_limit_bytes=VMEM_BYTES),
        cost_estimate=pl.CostEstimate(
            flops=int(us * FLOPS_PER_US), bytes_accessed=0, transcendentals=0
        ),
        name=name,
    )(*args)


def norm_rows(values):
    mean = jnp.mean(values, axis=-1, keepdims=True)
    centred = values - mean
    variance = jnp.mean(centred * centred, axis=-1, keepdims=True)
    inv = lax.rsqrt(variance + EPS)
    return centred * inv, inv


def folded(values):
    parts = [values[i : i + 8] for i in range(0, values.shape[0], 8)]
    while len(parts) > 1:
        parts = [sum(parts[i : i + 2]) for i in range(0, len(parts), 2)]
    return parts[0]


def eye(n):
    rows = lax.broadcasted_iota(jnp.int32, (n, n), 0)
    return jnp.where(rows == lax.broadcasted_iota(jnp.int32, (n, n), 1), 1.0, 0.0)


def turned(values):
    return dot_nt(eye(values.shape[1]).astype(BF), values.astype(BF))


def pack_kernel(triple, out_w, up, down, taps, modes, tbias, ubias, *refs):
    vectors, (seg, a_o, b_o, box) = refs[:6], refs[6:]
    _, rows, local = triple.shape
    hidden = up.shape[1]
    for i in range(3):
        a_o[:rows, i * local : (i + 1) * local] = triple[i].astype(BF)
    box[...] = jnp.zeros_like(box)
    box[0 : taps.shape[0], 0:local] = taps[...]
    for i, vector in enumerate(vectors):
        box[8 + i : 9 + i, 0:rows] = vector[...]
    box[14:15, 0:rows] = ubias[...]
    for i in range(3):
        box[8 + i : 9 + i, 2 * TILE : 2 * TILE + tbias.shape[2]] = tbias[i]
    box[8 : 8 + modes.shape[0], 3 * TILE : 3 * TILE + modes.shape[1]] = modes[...]
    lane = lax.broadcasted_iota(jnp.int32, (1, TILE), 1)
    line = jnp.zeros((1, TILE), F32)
    for i in range(2):
        count = jnp.sum((seg[...] < i + 1).astype(F32), axis=1, keepdims=True)
        high = jnp.floor(count * (1.0 / 32))
        line = line + jnp.where(lane == 2 * i, high, 0.0)
        line = line + jnp.where(lane == 2 * i + 1, count - 32 * high, 0.0)
    box[15:16, 0:TILE] = line
    a_o[rows:, :] = box[...].astype(BF)
    b_o[:, :hidden] = up[...].astype(BF)
    b_o[:, hidden : 2 * hidden] = down[...].astype(BF)
    b_o[:, 2 * hidden :] = turned(out_w[...]).astype(BF)


def unpack(meta, order, a_refs, weights, taps_o, vec_o, modes_o, ends_o):
    g, c, h = meta[1], meta[2], meta[3]
    rows = a_refs[0].shape[1] - SMALL
    local = weights[0].shape[1]
    width = weights[0].shape[0]
    n_pieces = 2 * len(a_refs)
    bias_cols, mode_cols = local // n_pieces, TILE // n_pieces

    def spot(n_cols, wide, at):
        i = lax.broadcasted_iota(jnp.int32, (TILE, wide), 0)
        n = lax.broadcasted_iota(jnp.int32, (TILE, wide), 1)
        return jnp.where((n == i + at) & (i < n_cols), 1.0, 0.0).astype(BF)

    vec = jnp.zeros((8, width), F32)
    bias = jnp.zeros((8, local), F32)
    modes = jnp.zeros((8, TILE), F32)
    for k, ref in enumerate(a_refs):
        for j in range(2):
            d = 2 * (g ^ k) + (c ^ j)
            at = pl.multiple_of(d * rows, rows)
            for i, target in enumerate(weights):
                target[pl.ds(at, rows), :] = ref[j, :rows, i * local : (i + 1) * local]
            box = ref[j, rows:, :]
            taps_o[pl.ds(pl.multiple_of(d * 8, 8), 8), :] = box[:, :local].astype(F32)[0:8]
            low = box.astype(F32)[8:16].astype(BF)
            vec = vec + dot(low[:, :TILE], spot(rows, width, d * rows))
            bias = bias + dot(low[:, 2 * TILE : 3 * TILE], spot(bias_cols, local, d * bias_cols))
            modes = modes + dot(low[:, 3 * TILE : 4 * TILE], spot(mode_cols, TILE, d * mode_cols))
    vec_o[...] = vec
    modes_o[...] = modes
    own = 0
    for d in range(n_pieces):
        own = own + jnp.where(order[d] == 2 * g + h, d, 0)
    lane = lax.broadcasted_iota(jnp.int32, (1, width), 1)
    for i in range(2):
        scale = jnp.where(lane == own * rows + 2 * i, 32.0, 0.0)
        scale = scale + jnp.where(lane == own * rows + 2 * i + 1, 1.0, 0.0)
        ends_o[i] = jnp.sum(vec[7:8, :] * scale).astype(jnp.int32)
    return bias


def project_kernel(pieces, meta, *refs):
    if pieces > 1:
        order, refs = refs[0], refs[1:]
    x_refs, refs = refs[:4], refs[4:]
    if pieces > 1:
        a_refs, refs = refs[:pieces], refs[pieces:]
        first_o, q_o, k_o, v_o, mean_o, inv_o = refs[:6]
        weights, (taps_o, vec_ref, modes_o, ends_o) = refs[6:9], refs[9:13]
        bias = unpack(meta, order, a_refs, weights, taps_o, vec_ref, modes_o, ends_o)
        biases = [bias[i : i + 1, :] for i in range(3)]
    else:
        weights, (bias_ref, vec_ref) = refs[:3], refs[3:5]
        first_o, q_o, k_o, v_o, mean_o, inv_o = refs[5:]
        local = weights[0].shape[1]
        biases = [bias_ref[i : i + 1, :] for i in range(3)]
    quarter = x_refs[0].shape[0]
    gain, shift = vec_ref[0:1, :], vec_ref[1:2, :]
    step = 64
    for k, ref in enumerate(x_refs):
        first_o[pl.ds(pl.multiple_of((meta[0] ^ k) * quarter, quarter), quarter), :] = ref[...]

    for k in range(4):
        base = k * quarter
        for i in range(quarter // step):
            to = pl.ds(base + i * step, step)
            values = first_o[to, :].astype(F32)
            mean = jnp.mean(values, axis=-1, keepdims=True)
            centred = values - mean
            inv = lax.rsqrt(jnp.mean(centred * centred, axis=-1, keepdims=True) + EPS)
            mean_o[to, :] = mean
            inv_o[to, :] = inv
            first_o[to, :] = (centred * inv * gain + shift).astype(BF)
        rows = first_o[pl.ds(base, quarter), :]
        for target, weight, bias in zip((q_o, k_o, v_o), weights, biases):
            target[pl.ds(base, quarter), :] = (dot(rows, weight[...]) + bias).astype(target.dtype)


def sequence_of(rows, start, stop):
    return (rows >= start).astype(jnp.int32) + (rows >= stop).astype(jnp.int32)


def spread_rows(source, target, ends, length, channels):
    for i in range(target.shape[0] // GAP):
        total = jnp.zeros((GAP, channels), F32)
        for s in range(SEQUENCES):
            j = i - s - 1
            if 0 <= j < length // GAP:
                rows = lax.broadcasted_iota(jnp.int32, (GAP, channels), 0) + j * GAP
                hit = sequence_of(rows, ends[0], ends[1]) == s
                total = total + jnp.where(hit, source[j * GAP : (j + 1) * GAP, :], 0.0)
        target[i * GAP : (i + 1) * GAP, :] = total


def gather_rows(source, target, ends, length, channels):
    for j in range(length // GAP):
        rows = lax.broadcasted_iota(jnp.int32, (GAP, channels), 0) + j * GAP
        ids = sequence_of(rows, ends[0], ends[1])
        total = jnp.zeros((GAP, channels), F32)
        for s in range(SEQUENCES):
            i = j + s + 1
            total = jnp.where(ids == s, source[i * GAP : (i + 1) * GAP, :], total)
        target[j * GAP : (j + 1) * GAP, :] = total.astype(target.dtype)


def taps_sum(pad, taps, target, sign, blocks):
    n_taps = taps.shape[0]
    reach = n_taps - 8

    def block(i, edges):
        at = pl.multiple_of((i + 1 if sign > 0 else blocks - i) * GAP, GAP)
        if sign > 0:
            window = pad[pl.ds(pl.multiple_of(at - reach, 8), GAP + reach), :TILE]
        else:
            window = pad[pl.ds(at, GAP + reach), :TILE]
        total, fresh = None, []
        for r in range(8):
            part = None
            for m in range(n_taps // 8):
                low = reach - 8 * m if sign > 0 else 8 * m
                term = window[low : low + GAP] * taps[8 * m + r : 8 * m + r + 1, :TILE]
                part = term if part is None else part + term
            if r == 0:
                total = part
            elif sign > 0:
                total = total + jnp.concatenate([edges[r - 1], part], axis=0)[8 - r : 8 - r + GAP]
                fresh.append(part[GAP - 8 :])
            else:
                total = total + jnp.concatenate([part, edges[r - 1]], axis=0)[r : r + GAP]
                fresh.append(part[:8])
        target[pl.ds(at, GAP), :TILE] = total
        return tuple(fresh)

    zero = tuple(jnp.zeros((8, TILE), F32) for _ in range(7))
    lax.fori_loop(0, blocks, block, zero, unroll=2)


def side_sum(side, taps, target, sign, blocks):
    n_taps = taps.shape[0]

    def block(i, _):
        at = pl.multiple_of((i + 1) * GAP, GAP)
        window = side[pl.ds(at - GAP if sign > 0 else at, 2 * GAP), :]
        total = None
        for r in range(8):
            part = None
            for m in range(n_taps // 8):
                low = n_taps - 8 - 8 * m if sign > 0 else 8 * m
                term = window[low : low + GAP + 8] * taps[8 * m + r : 8 * m + r + 1, :]
                part = term if part is None else part + term
            part = part[8 - r : 8 - r + GAP] if sign > 0 else part[r : r + GAP]
            total = part if total is None else total + part
        target[pl.ds(at, GAP), :] = total
        return 0

    lax.fori_loop(0, blocks, block, 0)


def fold_side(source, target, stretch):
    rows = target.shape[0]
    half = source.shape[1] - TILE
    target[:, :half] = source[0:rows, TILE:]
    target[:, half:] = source[stretch : stretch + rows, TILE:]


def all_taps(pad, taps, target, sign, side, side_taps, side_made):
    blocks = pad.shape[0] // GAP - 2
    half = pad.shape[1] - TILE
    stretch = blocks // 2 * GAP
    fold_side(pad, side, stretch)
    side_taps[:, :half] = taps[:, TILE:]
    side_taps[:, half:] = taps[:, TILE:]
    taps_sum(pad, taps, target, sign, blocks)
    side_sum(side, side_taps, side_made, sign, blocks // 2)
    target[GAP : GAP + stretch, TILE:] = side_made[GAP : GAP + stretch, :half]
    target[GAP + stretch : GAP + 2 * stretch, TILE:] = side_made[GAP : GAP + stretch, half:]


def conv_kernel(ends, k_ref, taps, kb_o, pad_o, made, side, side_taps, side_made):
    length, channels = k_ref.shape
    spread_rows(k_ref, pad_o, ends, length, channels)
    all_taps(pad_o, taps, made, 1, side, side_taps, side_made)
    gather_rows(made, kb_o, ends, length, channels)


def conv_back_kernel(ends, gk_ref, taps, graw_o, pad_o, made, side, side_taps, side_made):
    length, channels = gk_ref.shape
    spread_rows(gk_ref, pad_o, ends, length, channels)
    all_taps(pad_o, taps, made, -1, side, side_taps, side_made)
    gather_rows(made, graw_o, ends, length, channels)


def taps_grad(grad, keys, sums, side_grad, side_keys):
    n_taps, _, channels = sums.shape
    reach = n_taps - 8
    blocks = grad.shape[0] // GAP - 2
    half = channels - TILE
    fold_side(grad, side_grad, blocks // 2 * GAP)
    fold_side(keys, side_keys, blocks // 2 * GAP)
    totals = []
    for rows_ref, keys_ref, count in ((grad, keys, blocks), (side_grad, side_keys, blocks // 2)):
        sums[:, :, :TILE] = jnp.zeros((n_taps, 8, TILE), F32)

        def block(i, _, rows_ref=rows_ref, keys_ref=keys_ref):
            at = pl.multiple_of((i + 1) * GAP, GAP)
            window = keys_ref[pl.ds(pl.multiple_of(at - reach, 8), GAP + reach), :TILE]
            rows = rows_ref[pl.ds(at, GAP + 8), :TILE]
            for r in range(8):
                turned_rows = pltpu.roll(rows, (GAP + 8 - r) % (GAP + 8), 0)[:GAP]
                for m in range(n_taps // 8):
                    low = reach - 8 * m
                    sums[8 * m + r, :, :TILE] += folded(turned_rows * window[low : low + GAP])
            return 0

        lax.fori_loop(0, count, block, 0)
        totals.append(jnp.sum(sums[:, :, :TILE], axis=1))
    return jnp.concatenate([totals[0], totals[1][:, :half] + totals[1][:, half:]], axis=1)


def taps_grad_kernel(grad, keys, gtaps_o, sums, side_grad, side_keys):
    gtaps_o[...] = taps_grad(grad, keys, sums, side_grad, side_keys)


def late_grad_kernel(meta, grad, keys, first, graw, vec_sums, ubias_a, ubias_b, gbias, modes, *refs):
    targets, (sums, pieces, side_grad, side_keys) = refs[:-4], refs[-4:]
    n_pieces, rows, local = pieces.shape
    rows -= SMALL
    made = dot_tn(graw[...], first[...]).T
    pieces[...] = jnp.zeros_like(pieces)
    ubias = jnp.sum(ubias_a[...] + ubias_b[...], axis=0, keepdims=True)
    bias = jnp.concatenate([jnp.sum(gbias[i], axis=0, keepdims=True) for i in range(3)], axis=0)
    heads = modes.shape[0]
    n_bias, n_modes = local // n_pieces, modes.shape[1] // n_pieces
    low = rows + 8
    gtaps = taps_grad(grad, keys, sums, side_grad, side_keys)
    for d in range(n_pieces):
        pieces[d, :rows, :] = made[d * rows : (d + 1) * rows, :]
        pieces[d, rows:low, :] = gtaps[8 * d : 8 * d + 8, :]
        wide = slice(d * rows, (d + 1) * rows)
        pieces[d, low : low + 6, :rows] = vec_sums[0:6, wide]
        pieces[d, low + 6 : low + 7, :rows] = ubias[:, wide]
        pieces[d, low : low + 3, TILE : TILE + n_bias] = bias[:, d * n_bias : (d + 1) * n_bias]
        pieces[d, low : low + heads, local - n_modes :] = modes[:, d * n_modes : (d + 1) * n_modes]
    for k, target in enumerate(targets):
        for j in range(2):
            target[j, :, :] = pieces[2 * (meta[1] ^ k) + j].astype(BF)


def make_tiles(lags_ref, tiles, heads):
    for h in range(heads):
        for d in range(LAGS):
            at = TILE * (LAGS - 1 - d)
            row = jnp.broadcast_to(lags_ref[h : h + 1, at : at + 2 * TILE], (TILE, 2 * TILE))
            turned = pltpu.roll(row, TILE + 1, 1, stride=1, stride_axis=0)
            tiles[h, d, :, :] = turned[:, :TILE]


def head_lanes(h, heads, channels):
    size = channels // heads
    lane = lax.broadcasted_iota(jnp.int32, (BLOCK, channels), 1)
    return (lane >= h * size) & (lane < (h + 1) * size)


def head_masked(source, target, heads):
    length, channels = source.shape

    for a in range(length // BLOCK):
        part = source[a * BLOCK : (a + 1) * BLOCK, :]
        for h in range(heads):
            target[a, h * BLOCK : (h + 1) * BLOCK, :] = jnp.where(
                head_lanes(h, heads, channels), part, jnp.zeros_like(part)
            )


def starts_of(ends, target):
    rows = lax.broadcasted_iota(jnp.int32, target.shape, 0)
    first = jnp.where(rows >= ends[0], ends[0], 0)
    target[...] = jnp.where(rows >= ends[1], ends[1], first)


def lives_of(starts, a, lag):
    lives = {}
    for i in range(2):
        for j in range(2):
            if 0 <= 2 * lag + i - j < LAGS:
                lane = lax.broadcasted_iota(jnp.int32, (TILE, TILE), 1)
                lane = lane + ((a - lag) * BLOCK + j * TILE)
                lives[i, j] = lane >= starts[pl.ds(a * BLOCK + i * TILE, TILE), :]
    return lives


def mix_kernel(ends, q_ref, k_ref, v_ref, lags_ref, mixed_o, tiles_o, qm, vmask, starts, weights):
    length, local = q_ref.shape
    heads = tiles_o.shape[0]
    make_tiles(lags_ref, tiles_o, heads)
    head_masked(q_ref, qm, heads)
    head_masked(v_ref, vmask, heads)
    starts_of(ends, starts)
    for a in range(length // BLOCK):
        least = max(0, a - REACH + 1)
        for s in range(least, a + 1):
            lag = a - s
            keys = k_ref[s * BLOCK : (s + 1) * BLOCK, :]
            lives = lives_of(starts, a, lag)
            for h in range(heads):
                scores = dot_nt(qm[a, h * BLOCK : (h + 1) * BLOCK, :], keys)
                at = ((s - least) * heads + h) * BLOCK
                for i in range(2):
                    for j in range(2):
                        spot = (slice(i * TILE, (i + 1) * TILE), slice(j * TILE, (j + 1) * TILE))
                        where = (spot[0], slice(at + j * TILE, at + (j + 1) * TILE))
                        if (i, j) in lives:
                            factor = jnp.where(lives[i, j], tiles_o[h, 2 * lag + i - j], 0.0)
                            weights[where] = (factor * scores[spot]).astype(BF)
                        else:
                            weights[where] = jnp.zeros((TILE, TILE), BF)
        wide = (a - least + 1) * heads * BLOCK
        stack = vmask[least : a + 1].reshape(wide, local)
        mixed_o[a * BLOCK : (a + 1) * BLOCK, :] = dot(weights[:, :wide], stack).astype(BF)


def mix_back_kernel(
    meta, ends, q_ref, k_ref, v_ref, gm0, gm1, gm2, gm3, out_ref, tiles, gq_o, gk_o, gv_o, glag_o,
    gmix, qm, gmask, kmask, qt, gt, starts, grads, gkt, gvt, diag
):
    length, local = q_ref.shape
    heads = tiles.shape[0]
    size = local // heads
    quarter = gm0.shape[0]
    blocks = length // BLOCK
    for k, part in enumerate((gm0, gm1, gm2, gm3)):
        base = pl.multiple_of((meta[0] ^ k) * quarter, quarter)
        gmix[pl.ds(base, quarter), :] = dot(part[...], out_ref[0]).astype(BF)
    head_masked(q_ref, qm, heads)
    head_masked(gmix, gmask, heads)
    head_masked(k_ref, kmask, heads)
    starts_of(ends, starts)

    for a in range(blocks):
        spot = slice(a * BLOCK, (a + 1) * BLOCK)
        qt[a, :, :] = q_ref[spot, :].astype(F32).T.astype(BF)
        gt[a, :, :] = gmix[spot, :].astype(F32).T.astype(BF)
    gkt[...] = jnp.zeros_like(gkt)
    gvt[...] = jnp.zeros_like(gvt)
    diag[...] = jnp.zeros_like(diag)
    for a in range(blocks):
        least = max(0, a - REACH + 1)
        for s in range(least, a + 1):
            lag = a - s
            source = slice(s * BLOCK, (s + 1) * BLOCK)
            keys, vals = k_ref[source, :], v_ref[source, :]
            lives = lives_of(starts, a, lag)
            for h in range(heads):
                own = slice(h * BLOCK, (h + 1) * BLOCK)
                scores = dot_nt(qm[a, own, :], keys)
                wgrad = dot_nt(gmask[a, own, :], vals)
                rows_w, rows_g = [], []
                for i in range(2):
                    line_w, line_g = [], []
                    for j in range(2):
                        if (i, j) in lives:
                            d = 2 * lag + i - j
                            spot = (
                                slice(i * TILE, (i + 1) * TILE),
                                slice(j * TILE, (j + 1) * TILE),
                            )
                            factor = jnp.where(lives[i, j], tiles[h, d], 0.0)
                            line_w.append((factor * scores[spot]).astype(BF))
                            line_g.append((wgrad[spot] * factor).astype(BF))
                            diag[h, d] += jnp.where(lives[i, j], wgrad[spot] * scores[spot], 0.0)
                        else:
                            line_w.append(jnp.zeros((TILE, TILE), BF))
                            line_g.append(jnp.zeros((TILE, TILE), BF))
                    rows_w.append(jnp.concatenate(line_w, axis=1))
                    rows_g.append(jnp.concatenate(line_g, axis=1))
                w = jnp.concatenate(rows_w, axis=0)
                g = jnp.concatenate(rows_g, axis=0)
                at = ((s - least) * heads + h) * BLOCK
                grads[:, at : at + BLOCK] = g
                band = slice(h * size, (h + 1) * size)
                gvt[s, band, :] += dot(gt[a, band, :], w)
                gkt[s, band, :] += dot(qt[a, band, :], g)
        wide = (a - least + 1) * heads * BLOCK
        stack = kmask[least : a + 1].reshape(wide, local)
        gq_o[a * BLOCK : (a + 1) * BLOCK, :] = dot(grads[:, :wide], stack).astype(BF)
    for a in range(blocks):
        gk_o[a * BLOCK : (a + 1) * BLOCK, :] = gkt[a].T
        gv_o[a * BLOCK : (a + 1) * BLOCK, :] = gvt[a].T.astype(BF)
    glag_o[...] = jnp.zeros_like(glag_o)
    for h in range(heads):
        for d in range(LAGS):
            line = jnp.concatenate([diag[h, d], jnp.zeros((TILE, TILE), F32)], axis=1)
            rows = TILE
            while rows > 1:
                rows //= 2
                line = pltpu.roll(line[:rows], rows, 1) + line[rows : 2 * rows]
            at = TILE * (LAGS - 1 - d)
            glag_o[h : h + 1, at : at + 2 * TILE] += line


ROOT_HALF = 0.7071067811865476
PHI_SCALE = 0.3989422804014327


def mlp_kernel(near, meta, x_ref, g_ref, m0, m1, m2, m3, vec, *refs):
    n_out = 9 if near else 10
    ins, refs = refs[:-n_out], refs[-n_out:]
    second_o, act_o, gpre_o, gsec_o, ubias_o = refs[:5]
    pre, agrad, mid = refs[-3:]
    if near:
        out_ref, both = ins
        middle_o = refs[5]
    else:
        out_ref, both = refs[5:7]
        count = len(ins) // 2
        if count == 1:
            out_ref[...] = ins[0][...]
            both[...] = ins[1][...]
        else:
            rows = ins[0].shape[2]
            for k in range(count):
                for j in range(2):
                    to = pl.ds(pl.multiple_of((2 * (meta[1] ^ k) + j) * rows, rows), rows)
                    for i in range(4):
                        out_ref[i, to, :] = ins[k][i, j]
                    both[to, :] = ins[count + k][j]
    quarter = pre.shape[0]
    hidden = both.shape[1] // 2
    step = 64
    ubias_o[...] = jnp.zeros_like(ubias_o)

    for n in range(2):
        k = n if near else n + 2
        base = pl.multiple_of((meta[0] ^ k) * quarter, quarter)
        here = k * quarter
        row = n * quarter
        total = x_ref[pl.ds(here, quarter), :].astype(F32) + vec[2:3, :]
        for i, m in enumerate((m0, m1, m2, m3)):
            total = total + dot_nt(m[pl.ds(base, quarter), :], out_ref[i])
        mid[...] = total
        if near:
            middle_o[pl.ds(row, quarter), :] = total
        for i in range(quarter // step):
            normed, _inv = norm_rows(mid[i * step : (i + 1) * step, :])
            second_o[pl.ds(row + i * step, step), :] = (
                normed * vec[3:4, :] + vec[4:5, :]
            ).astype(BF)
        pre[...] = dot(second_o[pl.ds(row, quarter), :], both[:, :hidden])
        agrad[...] = dot(g_ref[pl.ds(here, quarter), :], both[:, hidden:])
        sums = None
        for i in range(quarter // 32):
            to = pl.ds(row + i * 32, 32)
            v = pre[i * 32 : (i + 1) * 32, :] + vec[6:7, :]
            cdf = 0.5 + 0.5 * lax.erf(v * ROOT_HALF)
            act_o[to, :] = (v * cdf).astype(BF)
            slope = cdf + v * (PHI_SCALE * jnp.exp(-0.5 * v * v))
            grad = (slope * agrad[i * 32 : (i + 1) * 32, :]).astype(BF)
            gpre_o[to, :] = grad
            part = folded(grad.astype(F32))
            sums = part if sums is None else sums + part
        ubias_o[...] += sums
        part = dot_nt(gpre_o[pl.ds(row, quarter), :], both[:, :hidden])
        gsec_o[pl.ds(row, quarter), :] = part.astype(gsec_o.dtype)


def ff_grad_kernel(meta, second_a, second_b, gpre_a, gpre_b, cot, act_a, act_b, *refs):
    targets, made = refs[:-1], refs[-1]
    half = second_a.shape[0]
    made[0, :, :] = dot_tn(second_a[...], gpre_a[...]) + dot_tn(second_b[...], gpre_b[...])
    made[1, :, :] = dot_tn(cot[:half, :], act_a[...]) + dot_tn(cot[half:, :], act_b[...])
    rows = targets[0].shape[2]
    for k, target in enumerate(targets):
        for j in range(2):
            spot = pl.ds(pl.multiple_of((2 * (meta[1] ^ k) + j) * rows, rows), rows)
            for i in range(2):
                target[j, i, :, :] = made[i, spot, :].astype(BF)


def early_grad_kernel(meta, first, gq, gv, gm0, gm1, gm2, gm3, mixed, *refs):
    targets, made = refs[:-1], refs[-1]
    quarter = gm0.shape[0]
    made[0, :, :] = dot_tn(gq[...], first[...]).T
    made[1, :, :] = dot_tn(gv[...], first[...]).T
    total = None
    for k, ref in enumerate((gm0, gm1, gm2, gm3)):
        base = pl.multiple_of((meta[0] ^ k) * quarter, quarter)
        part = dot_tn(mixed[pl.ds(base, quarter), :], ref[...])
        total = part if total is None else total + part
    made[2, :, :] = total.T
    rows = targets[0].shape[2]
    for k, target in enumerate(targets):
        for j in range(2):
            spot = pl.ds(pl.multiple_of((2 * (meta[1] ^ k) + j) * rows, rows), rows)
            for i in range(3):
                target[j, i, :, :] = made[i, spot, :].astype(BF)


def middle_back_kernel(part, near, far, cot, middle, vec, gmid_o, gmb_o, sums_o):
    rows, width = far.shape
    step = 64

    def chunk(i, totals):
        at = pl.multiple_of(i * step, step)
        spot = pl.ds(at, step)
        up = part[spot, :] + near[spot, :].astype(F32) + far[spot, :].astype(F32)
        normed, inv = norm_rows(middle[spot, :])
        cotangent = cot[spot, :].astype(F32)
        e = up * vec[3:4, :]
        mean_e = jnp.mean(e, axis=-1, keepdims=True)
        mean_x = jnp.mean(e * normed, axis=-1, keepdims=True)
        grad = cotangent + inv * (e - mean_e - normed * mean_x)
        gmid_o[spot, :] = grad
        gmb_o[spot, :] = grad.astype(BF)
        terms = (grad, up * normed, up, cotangent)
        return tuple(t + folded(x) for t, x in zip(totals, terms))

    totals = lax.fori_loop(
        0, rows // step, chunk, tuple(jnp.zeros((8, width), F32) for _ in range(4)), unroll=True
    )
    sums_o[...] = jnp.zeros_like(sums_o)
    for i, t in enumerate(totals):
        sums_o[2 + i : 3 + i, :] = jnp.sum(t, axis=0, keepdims=True)


def first_back_kernel(meta, part, near, far, tokens, gmid, vec, mean_ref, inv_ref, grad_o):
    rows, width = tokens.shape
    step = 64
    base = pl.multiple_of(meta[0] * rows, rows)

    def chunk(i, _):
        at = pl.multiple_of(i * step, step)
        spot = pl.ds(at, step)
        stat = pl.ds(pl.multiple_of(base + at, step), step)
        up = part[spot, :] + near[spot, :].astype(F32) + far[spot, :].astype(F32)
        inv = inv_ref[stat, :]
        normed = (tokens[spot, :].astype(F32) - mean_ref[stat, :]) * inv
        e = up * vec[0:1, :]
        mean_e = jnp.mean(e, axis=-1, keepdims=True)
        mean_x = jnp.mean(e * normed, axis=-1, keepdims=True)
        grad_o[spot, :] = (gmid[spot, :] + inv * (e - mean_e - normed * mean_x)).astype(BF)
        return 0

    lax.fori_loop(0, rows // step, chunk, 0, unroll=True)


def first_grad_kernel(
    meta, gq, gk, gv, wq, wk, wv, x_ref, mean_ref, inv_ref, sums_two, near_o, far_o, bias_o, made, sums
):
    length, local = gq.shape
    quarter = length // 4
    step = 64
    for i, ref in enumerate((gq, gk, gv)):
        total = jnp.zeros((8, local), F32)
        for j in range(length // 256):
            total = total + folded(ref[256 * j : 256 * j + 256, :].astype(F32))
        bias_o[i, :, :] = total
    sums[...] = jnp.zeros_like(sums)
    for first, target in ((0, near_o), (2, far_o)):

        for n in range(2):
            base = pl.multiple_of((meta[0] ^ (first + n)) * quarter, quarter)
            here = (first + n) * quarter
            total = None
            for ref, weight in ((gq, wq), (gk, wk), (gv, wv)):
                term = dot_nt(ref[pl.ds(base, quarter), :], weight[...])
                total = term if total is None else total + term
            made[...] = total
            row = n * quarter
            target[pl.ds(row, quarter), :] = total.astype(target.dtype)
            for i in range(quarter // step):
                stat = pl.ds(pl.multiple_of(base + i * step, step), step)
                up = made[i * step : (i + 1) * step, :]
                values = x_ref[pl.ds(here + i * step, step), :].astype(F32)
                normed = (values - mean_ref[stat, :]) * inv_ref[stat, :]
                sums[0, :, :] += folded(up * normed)
                sums[1, :, :] += folded(up)
    ends = jnp.concatenate(
        [
            jnp.sum(sums[0], axis=0, keepdims=True),
            jnp.sum(sums[1], axis=0, keepdims=True),
            sums_two[2:8, :],
            jnp.zeros_like(sums_two),
        ],
        axis=0,
    )
    near_o[2 * quarter :, :] = ends
    far_o[2 * quarter :, :] = ends.astype(BF)


def permute(value, groups, target_of):
    pairs = []
    for g in range(groups):
        for c in range(2):
            for z in range(4):
                to = target_of(g, c, z)
                if to is not None:
                    pairs.append((g * 8 + c * 4 + z, to[0] * 8 + to[1] * 4 + to[2]))
    return lax.ppermute(value, AXES, pairs)


def swap_quarters(value, groups):
    return permute(
        value, groups, lambda g, c, z: (g, c, z) if c == z // 2 else (g, 1 - c, z ^ 2)
    )


def to_core(value, groups):
    return permute(value, groups, lambda g, c, z: (g, 1 - c, z))


def to_chip(value, groups):
    return permute(value, groups, lambda g, c, z: (g, c, z ^ 1))


def gather_group(value, groups):
    chip = to_chip(value, groups)
    core = to_core(value, groups)
    both = to_core(chip, groups)
    return value, chip, core, both


def spread_pieces(piece, groups, same):
    near = permute(
        piece, groups, lambda g, c, z: (g, c, z ^ 2) if c == z // 2 else (g, 1 - c, z)
    )
    far = permute(piece, groups, lambda g, c, z: None if c == z // 2 else (g, 1 - c, z ^ 2))
    return jnp.where(same, piece, near), jnp.where(same, near, far)


def halves_of(pieces, half):
    return tuple(lax.dynamic_index_in_dim(pieces, i, 0, False) for i in (half, 1 - half))


def return_pieces(kept, sent, groups, same):
    near = permute(
        sent, groups, lambda g, c, z: (g, 1 - c, z) if c == z // 2 else (g, c, z ^ 2)
    )
    far = permute(kept, groups, lambda g, c, z: None if c == z // 2 else (g, 1 - c, z ^ 2))
    return near.astype(F32) + jnp.where(same, kept, far).astype(F32)


def after(value, *others):
    return lax.optimization_barrier((value, *others))[0]


def pad_to(value, rows, lanes):
    return jnp.pad(value, ((0, rows - value.shape[0]), (0, lanes - value.shape[1])))


def shift_groups(value, groups, k):
    return permute(value, groups, lambda g, c, z: (g ^ k, c, z))


def send_to_groups(pieces, groups, g):
    if groups != 4:
        shape = pieces.shape
        flat = pieces.reshape(groups * 2 * shape[2], shape[3])
        total = lax.psum_scatter(flat, "g", scatter_dimension=0, tiled=True)
        return (total.reshape(shape[1:]),), ()
    sent = [lax.dynamic_index_in_dim(pieces, g ^ k, 0, False) for k in range(groups)]
    return sent, [shift_groups(sent[k], groups, k) for k in (1, 2, 3)]


def grouped(values, groups):
    n, width, columns = values.shape
    pieces = values.reshape(n, groups, 2, width // groups // 2, columns).transpose(1, 2, 0, 3, 4)
    shape = pieces.shape[1:]
    total = lax.psum_scatter(
        pieces.reshape(-1, columns), "g", scatter_dimension=0, tiled=True
    )
    return total.reshape(shape)


def sum_of(sent, came):
    total = sent[0].astype(F32)
    for value in came:
        total = total + value.astype(F32)
    return total.astype(BF)


def plain_pack(triple, out_w, up, down, taps, modes, tbias, ubias, *rest):
    vectors, seg = rest[:6], rest[6]
    _, rows, local = triple.shape
    first_end = jnp.sum((seg[0] < 1).astype(jnp.int32))
    second_end = jnp.sum((seg[0] < 2).astype(jnp.int32))
    ends = jnp.stack([first_end // 32, first_end % 32, second_end // 32, second_end % 32])
    left = jnp.concatenate(
        [
            pad_to(taps, 8, local),
            pad_to(jnp.concatenate(vectors, axis=0), 6, local),
            pad_to(ubias, 1, local),
            pad_to(ends.astype(F32)[None], 1, local),
        ],
        axis=0,
    )
    low = jnp.concatenate([pad_to(tbias[:, 0, :], 8, TILE), pad_to(modes, 8, TILE)], axis=1)
    right = jnp.concatenate([jnp.zeros_like(low), low], axis=0)
    small = jnp.concatenate([left, jnp.zeros((SMALL, 2 * TILE - local), F32), right], axis=1)
    small = pad_to(small, SMALL, 3 * local)
    main = triple.transpose(1, 0, 2).reshape(rows, 3 * local)
    return (
        jnp.concatenate([main, small], axis=0).astype(BF),
        jnp.concatenate([up, down, out_w.T], axis=1).astype(BF),
    )


def plain_small(gtaps, vec_sums, ubias, bias, modes, n_pieces):
    local, width = gtaps.shape[1], vec_sums.shape[1]
    heads = modes.shape[0]

    def by_piece(value):
        return value.reshape(value.shape[0], n_pieces, -1).transpose(1, 0, 2)

    def block_of(value, n_rows, lanes):
        shape = value.shape
        return jnp.pad(value, ((0, 0), (0, n_rows - shape[1]), (0, lanes - shape[2])))

    left = jnp.concatenate([vec_sums[:6], ubias.reshape(1, width)], axis=0)
    pad = local - TILE - modes.shape[1] // n_pieces
    right = block_of(by_piece(bias), 8, local - TILE)
    right = right + jnp.pad(by_piece(modes), ((0, 0), (0, 8 - heads), (pad, 0)))
    low = jnp.concatenate([block_of(by_piece(left), 8, TILE), right], axis=2)
    high = block_of(gtaps.reshape(n_pieces, -1, local), 8, local)
    return jnp.concatenate([high, low], axis=1)


def on_device(
    groups,
    tokens,
    segments,
    row_order,
    first_gain,
    first_shift,
    triple_weight,
    triple_bias,
    shift_taps,
    kernel_modes,
    out_weight,
    out_bias,
    second_gain,
    second_shift,
    up_weight,
    up_bias,
    down_weight,
    down_bias,
    cotangent,
):
    g = lax.axis_index("g")
    c = lax.axis_index("c")
    h = lax.axis_index("h")
    b = lax.axis_index("b")
    same = c == h
    n_pieces = 2 * groups
    quarter, width = tokens.shape[1:]
    length = 4 * quarter
    rows, _, local = triple_weight.shape
    heads = kernel_modes.shape[0]
    n_modes = kernel_modes.shape[1] * n_pieces // 4
    taps_rows = shift_taps.shape[1]
    n_taps = taps_rows * n_pieces
    mode_cols = kernel_modes.shape[1]
    bias_cols = triple_bias.shape[2]
    hidden = up_weight.shape[1]
    q_at = 2 * c + b
    meta = jnp.stack([q_at, g, c, h]).astype(jnp.int32)

    own_x = swap_quarters(tokens[0], groups)
    vectors = (first_gain, first_shift, out_bias, second_gain, second_shift, down_bias)
    raw = (
        triple_weight.transpose(1, 0, 2), out_weight, up_weight, down_weight.T, shift_taps.T,
        kernel_modes, triple_bias, up_bias, *(v[None] for v in vectors), segments,
    )
    if groups == 4:
        a_piece, b_piece = call(
            pack_kernel, 0, raw,
            [((rows + SMALL, 3 * local), BF), ((rows, 2 * hidden + width // 4), BF)],
            [((SMALL, 3 * local), F32)], name="pack", us=2.2,
        )
    else:
        a_piece, b_piece = plain_pack(*raw)
    a_near, a_other = spread_pieces(a_piece, groups, same)
    a_pair = jnp.stack([a_near, a_other])
    x = gather_group(after(own_x, a_piece), groups)
    if groups == 4:
        a_all = [a_pair] + [shift_groups(a_pair, groups, k) for k in (1, 2, 3)]
    else:
        a_all = lax.all_gather(a_pair, "g", axis=0, tiled=False)
        a_all = jnp.where(c == 0, a_all, a_all[:, ::-1]).reshape(n_pieces, rows + SMALL, 3 * local)

    lo, hi = spread_pieces(after(b_piece, x[1]), groups, same)
    first_b, second_b = jnp.where(c == 0, lo, hi), jnp.where(c == 0, hi, lo)
    b_pair = jnp.stack([first_b[:, : 2 * hidden], second_b[:, : 2 * hidden]])
    out_quad = jnp.stack(gather_group(jnp.stack([first_b, second_b])[:, :, 2 * hidden :], groups))
    if groups == 4:
        b_side, b_next = (shift_groups(b_pair, groups, k) for k in (1, 2))
        b_all = [b_pair, b_side, b_next, shift_groups(b_side, groups, 2)]
        out_all = [out_quad] + [shift_groups(out_quad, groups, k) for k in (1, 2, 3)]
    else:
        b_all = [lax.all_gather(b_pair, "g", axis=0, tiled=False).reshape(width, 2 * hidden)]
        out_all = lax.all_gather(out_quad, "g", axis=0, tiled=False)
        out_all = [out_all.transpose(1, 0, 2, 3, 4).reshape(4, width, local)]

    own_cot = swap_quarters(after(cotangent[0], x[1]), groups)
    cot = gather_group(own_cot, groups)

    made = [((length, width), BF), ((length, local), BF), ((length, local), F32)]
    made += [((length, local), BF), ((length, 1), F32), ((length, 1), F32)]
    if groups == 4:
        unpacked = [((width, local), BF)] * 3
        unpacked += [((n_taps, local), F32), ((8, width), F32), ((8, TILE), F32), ((2,), jnp.int32)]
        first, queries, raw_keys, values, mean, inv, wq, wk, wv, taps, vec, modes, ends = call(
            partial(project_kernel, 4), 2, (meta, row_order, *x, *a_all), made + unpacked,
            name="project", us=6.8,
        )
    else:
        weights = a_all[:, :rows, :].reshape(width, 3 * local)
        wq, wk, wv = (weights[:, i * local : (i + 1) * local] for i in range(3))
        small = a_all[:, rows:, :].astype(F32)
        taps = small[:, :taps_rows, :local].reshape(n_taps, local)
        vec = small[:, 8:16, :rows].transpose(1, 0, 2).reshape(8, width)
        bias = small[:, 8:16, 2 * TILE : 2 * TILE + bias_cols].transpose(1, 0, 2).reshape(8, local)
        modes = small[:, 8:16, 3 * TILE : 3 * TILE + mode_cols].transpose(1, 0, 2).reshape(8, TILE)
        mine = (row_order == 2 * g + h)[:, None]
        found = jnp.sum(jnp.where(mine, small[:, 15, :4], 0), axis=0)
        ends = jnp.stack([32 * found[0] + found[1], 32 * found[2] + found[3]]).astype(jnp.int32)
        first, queries, raw_keys, values, mean, inv = call(
            partial(project_kernel, 1), 1, (meta, *x, wq, wk, wv, bias, vec), made,
            name="project", us=6.8,
        )

    modes = modes[:heads]
    lag = LIMIT + TILE - 1 - jnp.arange(6 * TILE, dtype=jnp.int32)
    held = ((lag >= 0) & (lag < LIMIT)).astype(F32)[None, None, :]
    place = jnp.clip(lag, 0, LIMIT - 1).astype(F32)[None, None, :]
    rate = jnp.exp(modes[:, :n_modes])[:, :, None]
    phase = modes[:, n_modes : 2 * n_modes][:, :, None] * place
    decay = jnp.exp(-rate * place) * held
    wave_c, wave_s = decay * jnp.cos(phase), decay * jnp.sin(phase)
    weight_c = modes[:, 2 * n_modes : 3 * n_modes][:, :, None]
    weight_s = modes[:, 3 * n_modes :][:, :, None]
    lags = jnp.sum(weight_c * wave_c + weight_s * wave_s, axis=1)

    padded = length + (SEQUENCES + 1) * GAP
    sides = [((padded // 2 + GAP, TILE), F32)]
    conv_scratch = [((padded, local), F32), *sides, ((n_taps, TILE), F32), *sides]
    n_blocks = length // BLOCK
    keys, key_rows = call(
        conv_kernel, 1, (ends, after(raw_keys, own_cot, b_all[1 % len(b_all)]), taps),
        [((length, local), BF), ((padded, local), F32)], conv_scratch,
        name="conv", us=7.5,
    )
    per_block = (n_blocks, heads * BLOCK, local)
    mixed, tiles = call(
        mix_kernel, 1, (ends, queries, after(keys, cot[1]), values, lags),
        [((length, local), BF), ((heads, LAGS, TILE, TILE), F32)],
        [
            (per_block, BF), (per_block, BF), ((length, TILE), jnp.int32),
            ((BLOCK, REACH * heads * BLOCK), BF),
        ],
        name="mix", us=4.9,
    )
    mixed = after(mixed, *b_all[1:3], *out_all[1:])
    mixes = gather_group(mixed, groups)

    x_all = jnp.concatenate(x, axis=0)
    cot_all = jnp.concatenate(cot, axis=0)
    half = [((2 * quarter, width), BF), ((2 * quarter, hidden), BF), ((2 * quarter, hidden), BF)]
    scratch = [((quarter, hidden), F32), ((quarter, hidden), F32), ((quarter, width), F32)]
    shared = (meta, x_all, cot_all, *mixes, vec)
    second_b, act_b, gpre_b, gsec_b, ubias_b, outs, both = call(
        partial(mlp_kernel, False), 1, (*shared, *out_all, *b_all),
        half
        + [((2 * quarter, width), BF), ((8, hidden), F32), ((4, width, local), BF)]
        + [((width, 2 * hidden), BF)],
        scratch, name="mlp_far", us=8.9,
    )
    came = to_core(gsec_b, groups)
    second_a, act_a, gpre_a, gsec_a, ubias_a, middle = call(
        partial(mlp_kernel, True), 1, (*shared, outs, both),
        half + [((2 * quarter, width), F32), ((8, hidden), F32), ((2 * quarter, width), F32)],
        scratch, name="mlp_near", us=8.8,
    )
    mid_sent = (gsec_a[quarter:] + came[quarter:].astype(F32)).astype(BF)
    far_own = to_chip(mid_sent, groups)

    if groups == 4:
        b_sent = call(
            ff_grad_kernel, 1,
            (meta, after(second_a, mid_sent), second_b, gpre_a, gpre_b, cot_all, act_a, act_b),
            [((2, 2, rows, hidden), BF)] * 4, [((2, width, hidden), F32)], name="ff_grad", us=5.3,
        )
        b_came = [shift_groups(b_sent[k], groups, k) for k in (1, 2, 3)]
    else:
        up_grad = dot_tn(
            jnp.concatenate([second_a, second_b], axis=0), jnp.concatenate([gpre_a, gpre_b], axis=0)
        )
        down_grad = dot_tn(cot_all, jnp.concatenate([act_a, act_b], axis=0))
        b_sent = [grouped(jnp.stack([up_grad, down_grad]).astype(BF), groups)]
        b_came = []
    down_part = both[:, hidden:]
    share_far = dot_nt(after(act_b, mid_sent), down_part).astype(BF)
    share = dot_nt(after(act_a, mid_sent), down_part)
    gmid, gmb_own, sums_two = call(
        middle_back_kernel, 0, (after(gsec_a, share_far, share, *b_sent), came, far_own, own_cot, middle, vec),
        [((quarter, width), F32), ((quarter, width), BF), ((8, width), F32)],
        name="middle_back", us=3.5,
    )
    gmb = gather_group(gmb_own, groups)

    share_near = to_core(share_far, groups).astype(F32)
    share_chip = to_chip((share[quarter:] + share_near[quarter:]).astype(BF), groups)
    gq, gk, gv, glag = call(
        mix_back_kernel, 2,
        (meta, ends, after(queries, share_far, share, *b_came[:2]), keys, values, *gmb, outs, tiles),
        [
            ((length, local), BF), ((length, local), F32), ((length, local), BF),
            ((8, 6 * TILE), F32),
        ],
        [
            ((length, local), BF), (per_block, BF), (per_block, BF), (per_block, BF),
            ((n_blocks, local, BLOCK), BF), ((n_blocks, local, BLOCK), BF),
            ((length, TILE), jnp.int32), ((BLOCK, REACH * heads * BLOCK), BF),
            ((n_blocks, local, BLOCK), F32), ((n_blocks, local, BLOCK), F32),
            ((heads, LAGS, TILE, TILE), F32),
        ],
        name="mix_back", us=12.3,
    )

    b_kept, b_away = halves_of(sum_of(b_sent, [after(v, gk) for v in b_came]), h)
    b_out = return_pieces(b_kept, b_away, groups, same)
    share_chip = after(share_chip, gk).astype(F32)
    result = middle[:quarter] + share[:quarter] + share_near[:quarter] + share_chip + vec[5:6, :]
    result = result.astype(BF)
    graw, grad_rows = call(
        conv_back_kernel, 1, (ends, after(gk, result, b_kept, b_away), taps),
        [((length, local), BF), ((padded, local), F32)], conv_scratch,
        name="conv_back", us=7.2,
    )
    result = swap_quarters(result, groups)
    share_rows = 2 * quarter + SMALL
    near_part, far_part, gbias = call(
        first_grad_kernel, 1,
        (meta, gq, graw, gv, wq, wk, wv, x_all, mean, inv, sums_two),
        [((share_rows, width), F32), ((share_rows, width), BF), ((3, 8, local), F32)],
        [((quarter, width), F32), ((2, 8, width), F32)],
        name="first_grad", us=5.3,
    )
    came1 = to_core(far_part, groups)
    far_share = near_part[quarter:] + came1[quarter:].astype(F32)
    far_sent = far_share.astype(BF)
    far_own1 = to_chip(far_sent, groups)
    first_late = after(first, far_sent, b_out)
    if groups == 4:
        early_sent = call(
            early_grad_kernel, 1, (meta, first_late, gq, gv, *gmb, mixed),
            [((2, 3, rows, local), BF)] * 4, [((3, width, local), F32)], name="early_grad", us=3.0,
        )
        early_came = [shift_groups(early_sent[k], groups, k) for k in (1, 2, 3)]
    else:
        mixed_rel = jnp.concatenate(
            [lax.dynamic_slice_in_dim(mixed, (q_at ^ k) * quarter, quarter, 0) for k in range(4)],
            axis=0,
        )
        out_grad = dot_tn(jnp.concatenate(gmb, axis=0), mixed_rel)
        early = jnp.stack([dot_tn(first_late, gq), dot_tn(first_late, gv), out_grad])
        early_sent, early_came = [grouped(early.astype(BF), groups)], []

    (back,) = call(
        first_back_kernel, 1,
        (meta, after(near_part, result, *early_sent), came1, far_own1, own_x, gmid, vec)
        + (mean, inv),
        [((quarter, width), BF)], name="first_back", us=3.6,
    )
    input_grad = swap_quarters(back, groups)

    early = sum_of(early_sent, [after(v, back) for v in early_came])
    early = early.reshape(2, 3 * rows, local)
    e_kept, e_away = halves_of(early, h)
    main = return_pieces(e_kept, e_away, groups, same).reshape(3, rows, local)

    glags = glag[:heads][:, None, :]
    grad_c = jnp.sum(glags * wave_c, axis=-1)
    grad_s = jnp.sum(glags * wave_s, axis=-1)
    both_waves = weight_c * wave_c + weight_s * wave_s
    turned_waves = weight_s * wave_c - weight_c * wave_s
    grad_rate = -jnp.sum(glags * place * both_waves, axis=-1) * rate[:, :, 0]
    grad_freq = jnp.sum(glags * place * turned_waves, axis=-1)
    modes_grad = jnp.concatenate([grad_rate, grad_freq, grad_c, grad_s], axis=1)

    vec_sums = far_share[quarter:] + far_own1[quarter:].astype(F32)
    if groups == 4:
        late_sent = call(
            late_grad_kernel, 1,
            (meta, grad_rows, after(key_rows, back, e_kept, e_away), first, graw, vec_sums)
            + (ubias_a, ubias_b, gbias, modes_grad),
            [((2, rows + SMALL, local), BF)] * 4,
            [((n_taps, 8, local), F32), ((n_pieces, rows + SMALL, local), F32), *sides, *sides],
            name="late_grad", us=11.0,
        )
        late_came = [shift_groups(after(late_sent[k], input_grad), groups, k) for k in (1, 2, 3)]
    else:
        (gtaps,) = call(
            taps_grad_kernel, 0, (grad_rows, key_rows), [((n_taps, local), F32)],
            [((n_taps, 8, local), F32), *sides, *sides], name="taps_grad", us=8.2,
        )
        small = plain_small(
            gtaps, vec_sums, jnp.sum(ubias_a + ubias_b, axis=0), jnp.sum(gbias, axis=1), modes_grad,
            n_pieces,
        )
        key_grad = dot_tn(first, graw).reshape(n_pieces, rows, local)
        late = jnp.concatenate([key_grad, small], axis=1).astype(BF)
        late = late.reshape(1, n_pieces * (rows + SMALL), local)
        late_sent, late_came = [grouped(late, groups)[:, 0]], []
    late_out = return_pieces(*halves_of(sum_of(late_sent, late_came), h), groups, same)
    tail = late_out[rows:]
    return (
        result[None],
        input_grad[None],
        tail[8, :rows],
        tail[9, :rows],
        jnp.stack([main[0], late_out[:rows], main[1]]).transpose(1, 0, 2),
        tail[8:11, TILE : TILE + bias_cols][:, None, :],
        tail[:taps_rows].T,
        tail[8 : 8 + heads, local - mode_cols :],
        main[2].T,
        tail[10, :rows],
        tail[11, :rows],
        tail[12, :rows],
        b_out[0],
        tail[14:15, :rows],
        b_out[1].T,
        tail[13, :rows],
    )


def solution(mesh):
    n_data, _ = mesh.devices.shape
    groups = n_data // 2
    fine = Mesh(mesh.devices.reshape(groups, 2, 2, 2), AXES)
    dp, tensor = ("g", "c"), ("h", "b")
    return jax.shard_map(
        partial(on_device, groups),
        mesh=fine,
        in_specs=(
            P(dp, tensor, None),
            P(dp, None),
            P(),
            P(dp),
            P(dp),
            P(dp, None, tensor),
            P(None, tensor, dp),
            P(tensor, dp),
            P(tensor, dp),
            P(tensor, dp),
            P(dp),
            P(dp),
            P(dp),
            P(dp, tensor),
            P(tensor, dp),
            P(tensor, dp),
            P(dp),
            P(dp, tensor, None),
        ),
        out_specs=(
            P(dp, tensor, None),
            P(dp, tensor, None),
            P(dp),
            P(dp),
            P(dp, None, tensor),
            P(None, tensor, dp),
            P(tensor, dp),
            P(tensor, dp),
            P(tensor, dp),
            P(dp),
            P(dp),
            P(dp),
            P(dp, tensor),
            P(tensor, dp),
            P(tensor, dp),
            P(dp),
        ),
        check_vma=False,
    )
```

```python
from functools import partial

import jax
import jax.numpy as jnp
from jax import lax
from jax.experimental import pallas as pl
from jax.experimental.pallas import tpu as pltpu
from jax.sharding import Mesh
from jax.sharding import PartitionSpec as P

EPS = 1e-05
BF = jnp.bfloat16
F32 = jnp.float32
TILE = 128
BLOCK = 256
LAGS = 5
REACH = 3
LIMIT = 512
SEQUENCES = 3
GAP = 64
SMALL = 16
AXES = ("g", "c", "h", "b")
VMEM_BYTES = 56 * 1024 * 1024


def vm():
    return pl.BlockSpec(memory_space=pltpu.VMEM)


def sm():
    return pl.BlockSpec(memory_space=pltpu.SMEM)


def mult(value, factor):
    return value if isinstance(value, int) else pl.multiple_of(value, factor)


def dot(a, b):
    return jnp.dot(a, b, preferred_element_type=F32)


def dot_nt(a, b):
    return lax.dot_general(a, b, (((1,), (1,)), ((), ())), preferred_element_type=F32)


def dot_tn(a, b):
    return lax.dot_general(a, b, (((0,), (0,)), ((), ())), preferred_element_type=F32)


FLOPS_PER_US = 1_150_000_000


def call(kernel, n_smem, args, outs, scratch=(), name=None, us=1.0):
    return pl.pallas_call(
        kernel,
        out_shape=tuple(jax.ShapeDtypeStruct(s, d) for s, d in outs),
        in_specs=[sm()] * n_smem + [vm()] * (len(args) - n_smem),
        out_specs=tuple(sm() if s == (2,) else vm() for s, _ in outs),
        scratch_shapes=[pltpu.VMEM(s, d) for s, d in scratch],
        compiler_params=pltpu.CompilerParams(vmem_limit_bytes=VMEM_BYTES),
        cost_estimate=pl.CostEstimate(
            flops=int(us * FLOPS_PER_US), bytes_accessed=0, transcendentals=0
        ),
        name=name,
    )(*args)


def norm_rows(values):
    mean = jnp.mean(values, axis=-1, keepdims=True)
    centred = values - mean
    variance = jnp.mean(centred * centred, axis=-1, keepdims=True)
    inv = lax.rsqrt(variance + EPS)
    return centred * inv, inv


def folded(values):
    parts = [values[i : i + 8] for i in range(0, values.shape[0], 8)]
    while len(parts) > 1:
        parts = [sum(parts[i : i + 2]) for i in range(0, len(parts), 2)]
    return parts[0]


def eye(n):
    rows = lax.broadcasted_iota(jnp.int32, (n, n), 0)
    return jnp.where(rows == lax.broadcasted_iota(jnp.int32, (n, n), 1), 1.0, 0.0)


def turned(values):
    return dot_nt(eye(values.shape[1]).astype(BF), values.astype(BF))


def pack_kernel(triple, out_w, up, down, taps, modes, tbias, ubias, *refs):
    vectors, (seg, a_o, b_o, box) = refs[:6], refs[6:]
    _, rows, local = triple.shape
    hidden = up.shape[1]
    for i in range(3):
        a_o[:rows, i * local : (i + 1) * local] = triple[i].astype(BF)
    box[...] = jnp.zeros_like(box)
    box[0 : taps.shape[0], 0:local] = taps[...]
    for i, vector in enumerate(vectors):
        box[8 + i : 9 + i, 0:rows] = vector[...]
    box[14:15, 0:rows] = ubias[...]
    for i in range(3):
        box[8 + i : 9 + i, 2 * TILE : 2 * TILE + tbias.shape[2]] = tbias[i]
    box[8 : 8 + modes.shape[0], 3 * TILE : 3 * TILE + modes.shape[1]] = modes[...]
    lane = lax.broadcasted_iota(jnp.int32, (1, TILE), 1)
    line = jnp.zeros((1, TILE), F32)
    for i in range(2):
        count = jnp.sum((seg[...] < i + 1).astype(F32), axis=1, keepdims=True)
        high = jnp.floor(count * (1.0 / 32))
        line = line + jnp.where(lane == 2 * i, high, 0.0)
        line = line + jnp.where(lane == 2 * i + 1, count - 32 * high, 0.0)
    box[15:16, 0:TILE] = line
    a_o[rows:, :] = box[...].astype(BF)
    b_o[:, :hidden] = up[...].astype(BF)
    b_o[:, hidden : 2 * hidden] = down[...].astype(BF)
    b_o[:, 2 * hidden :] = turned(out_w[...]).astype(BF)


def unpack(meta, order, a_refs, weights, taps_o, vec_o, modes_o, ends_o):
    g, c, h = meta[1], meta[2], meta[3]
    rows = a_refs[0].shape[1] - SMALL
    local = weights[0].shape[1]
    width = weights[0].shape[0]
    n_pieces = 2 * len(a_refs)
    bias_cols, mode_cols = local // n_pieces, TILE // n_pieces

    def spot(n_cols, wide, at):
        i = lax.broadcasted_iota(jnp.int32, (TILE, wide), 0)
        n = lax.broadcasted_iota(jnp.int32, (TILE, wide), 1)
        return jnp.where((n == i + at) & (i < n_cols), 1.0, 0.0).astype(BF)

    vec = jnp.zeros((8, width), F32)
    bias = jnp.zeros((8, local), F32)
    modes = jnp.zeros((8, TILE), F32)
    for k, ref in enumerate(a_refs):
        for j in range(2):
            d = 2 * (g ^ k) + (c ^ j)
            at = pl.multiple_of(d * rows, rows)
            for i, target in enumerate(weights):
                target[pl.ds(at, rows), :] = ref[j, :rows, i * local : (i + 1) * local]
            box = ref[j, rows:, :]
            taps_o[pl.ds(pl.multiple_of(d * 8, 8), 8), :] = box[:, :local].astype(F32)[0:8]
            low = box.astype(F32)[8:16].astype(BF)
            vec = vec + dot(low[:, :TILE], spot(rows, width, d * rows))
            bias = bias + dot(low[:, 2 * TILE : 3 * TILE], spot(bias_cols, local, d * bias_cols))
            modes = modes + dot(low[:, 3 * TILE : 4 * TILE], spot(mode_cols, TILE, d * mode_cols))
    vec_o[...] = vec
    modes_o[...] = modes
    own = 0
    for d in range(n_pieces):
        own = own + jnp.where(order[d] == 2 * g + h, d, 0)
    lane = lax.broadcasted_iota(jnp.int32, (1, width), 1)
    for i in range(2):
        scale = jnp.where(lane == own * rows + 2 * i, 32.0, 0.0)
        scale = scale + jnp.where(lane == own * rows + 2 * i + 1, 1.0, 0.0)
        ends_o[i] = jnp.sum(vec[7:8, :] * scale).astype(jnp.int32)
    return bias


def project_kernel(pieces, meta, *refs):
    if pieces > 1:
        order, refs = refs[0], refs[1:]
    x_refs, refs = refs[:4], refs[4:]
    if pieces > 1:
        a_refs, refs = refs[:pieces], refs[pieces:]
        first_o, q_o, k_o, v_o, mean_o, inv_o = refs[:6]
        weights, (taps_o, vec_ref, modes_o, ends_o) = refs[6:9], refs[9:13]
        bias = unpack(meta, order, a_refs, weights, taps_o, vec_ref, modes_o, ends_o)
        biases = [bias[i : i + 1, :] for i in range(3)]
    else:
        weights, (bias_ref, vec_ref) = refs[:3], refs[3:5]
        first_o, q_o, k_o, v_o, mean_o, inv_o = refs[5:]
        local = weights[0].shape[1]
        biases = [bias_ref[i : i + 1, :] for i in range(3)]
    quarter = x_refs[0].shape[0]
    gain, shift = vec_ref[0:1, :], vec_ref[1:2, :]
    step = 64
    for k, ref in enumerate(x_refs):
        first_o[pl.ds(pl.multiple_of((meta[0] ^ k) * quarter, quarter), quarter), :] = ref[...]

    for k in range(4):
        base = k * quarter
        for i in range(quarter // step):
            to = pl.ds(base + i * step, step)
            values = first_o[to, :].astype(F32)
            mean = jnp.mean(values, axis=-1, keepdims=True)
            centred = values - mean
            inv = lax.rsqrt(jnp.mean(centred * centred, axis=-1, keepdims=True) + EPS)
            mean_o[to, :] = mean
            inv_o[to, :] = inv
            first_o[to, :] = (centred * inv * gain + shift).astype(BF)
        rows = first_o[pl.ds(base, quarter), :]
        for target, weight, bias in zip((q_o, k_o, v_o), weights, biases):
            target[pl.ds(base, quarter), :] = (dot(rows, weight[...]) + bias).astype(target.dtype)


def sequence_of(rows, start, stop):
    return (rows >= start).astype(jnp.int32) + (rows >= stop).astype(jnp.int32)


def spread_rows(source, target, ends, length, channels):
    for i in range(target.shape[0] // GAP):
        total = jnp.zeros((GAP, channels), F32)
        for s in range(SEQUENCES):
            j = i - s - 1
            if 0 <= j < length // GAP:
                rows = lax.broadcasted_iota(jnp.int32, (GAP, channels), 0) + j * GAP
                hit = sequence_of(rows, ends[0], ends[1]) == s
                total = total + jnp.where(hit, source[j * GAP : (j + 1) * GAP, :], 0.0)
        target[i * GAP : (i + 1) * GAP, :] = total


def gather_rows(source, target, ends, length, channels):
    for j in range(length // GAP):
        rows = lax.broadcasted_iota(jnp.int32, (GAP, channels), 0) + j * GAP
        ids = sequence_of(rows, ends[0], ends[1])
        total = jnp.zeros((GAP, channels), F32)
        for s in range(SEQUENCES):
            i = j + s + 1
            total = jnp.where(ids == s, source[i * GAP : (i + 1) * GAP, :], total)
        target[j * GAP : (j + 1) * GAP, :] = total.astype(target.dtype)


def taps_sum(pad, taps, target, sign, blocks):
    n_taps = taps.shape[0]
    reach = n_taps - 8

    def block(i, edges):
        at = pl.multiple_of((i + 1 if sign > 0 else blocks - i) * GAP, GAP)
        if sign > 0:
            window = pad[pl.ds(pl.multiple_of(at - reach, 8), GAP + reach), :TILE]
        else:
            window = pad[pl.ds(at, GAP + reach), :TILE]
        total, fresh = None, []
        for r in range(8):
            part = None
            for m in range(n_taps // 8):
                low = reach - 8 * m if sign > 0 else 8 * m
                term = window[low : low + GAP] * taps[8 * m + r : 8 * m + r + 1, :TILE]
                part = term if part is None else part + term
            if r == 0:
                total = part
            elif sign > 0:
                total = total + jnp.concatenate([edges[r - 1], part], axis=0)[8 - r : 8 - r + GAP]
                fresh.append(part[GAP - 8 :])
            else:
                total = total + jnp.concatenate([part, edges[r - 1]], axis=0)[r : r + GAP]
                fresh.append(part[:8])
        target[pl.ds(at, GAP), :TILE] = total
        return tuple(fresh)

    zero = tuple(jnp.zeros((8, TILE), F32) for _ in range(7))
    lax.fori_loop(0, blocks, block, zero, unroll=2)


def side_sum(side, taps, target, sign, blocks):
    n_taps = taps.shape[0]

    def block(i, _):
        at = pl.multiple_of((i + 1) * GAP, GAP)
        window = side[pl.ds(at - GAP if sign > 0 else at, 2 * GAP), :]
        total = None
        for r in range(8):
            part = None
            for m in range(n_taps // 8):
                low = n_taps - 8 - 8 * m if sign > 0 else 8 * m
                term = window[low : low + GAP + 8] * taps[8 * m + r : 8 * m + r + 1, :]
                part = term if part is None else part + term
            part = part[8 - r : 8 - r + GAP] if sign > 0 else part[r : r + GAP]
            total = part if total is None else total + part
        target[pl.ds(at, GAP), :] = total
        return 0

    lax.fori_loop(0, blocks, block, 0)


def fold_side(source, target, stretch):
    rows = target.shape[0]
    half = source.shape[1] - TILE
    target[:, :half] = source[0:rows, TILE:]
    target[:, half:] = source[stretch : stretch + rows, TILE:]


def all_taps(pad, taps, target, sign, side, side_taps, side_made):
    blocks = pad.shape[0] // GAP - 2
    half = pad.shape[1] - TILE
    stretch = blocks // 2 * GAP
    fold_side(pad, side, stretch)
    side_taps[:, :half] = taps[:, TILE:]
    side_taps[:, half:] = taps[:, TILE:]
    taps_sum(pad, taps, target, sign, blocks)
    side_sum(side, side_taps, side_made, sign, blocks // 2)
    target[GAP : GAP + stretch, TILE:] = side_made[GAP : GAP + stretch, :half]
    target[GAP + stretch : GAP + 2 * stretch, TILE:] = side_made[GAP : GAP + stretch, half:]


def conv_kernel(ends, k_ref, taps, kb_o, pad_o, made, side, side_taps, side_made):
    length, channels = k_ref.shape
    spread_rows(k_ref, pad_o, ends, length, channels)
    all_taps(pad_o, taps, made, 1, side, side_taps, side_made)
    gather_rows(made, kb_o, ends, length, channels)


def conv_back_kernel(ends, gk_ref, taps, graw_o, pad_o, made, side, side_taps, side_made):
    length, channels = gk_ref.shape
    spread_rows(gk_ref, pad_o, ends, length, channels)
    all_taps(pad_o, taps, made, -1, side, side_taps, side_made)
    gather_rows(made, graw_o, ends, length, channels)


def taps_grad(grad, keys, sums, side_grad, side_keys):
    n_taps, _, channels = sums.shape
    reach = n_taps - 8
    blocks = grad.shape[0] // GAP - 2
    half = channels - TILE
    fold_side(grad, side_grad, blocks // 2 * GAP)
    fold_side(keys, side_keys, blocks // 2 * GAP)
    totals = []
    for rows_ref, keys_ref, count in ((grad, keys, blocks), (side_grad, side_keys, blocks // 2)):
        sums[:, :, :TILE] = jnp.zeros((n_taps, 8, TILE), F32)

        def block(i, _, rows_ref=rows_ref, keys_ref=keys_ref):
            at = pl.multiple_of((i + 1) * GAP, GAP)
            window = keys_ref[pl.ds(pl.multiple_of(at - reach, 8), GAP + reach), :TILE]
            rows = rows_ref[pl.ds(at, GAP + 8), :TILE]
            for r in range(8):
                turned_rows = pltpu.roll(rows, (GAP + 8 - r) % (GAP + 8), 0)[:GAP]
                for m in range(n_taps // 8):
                    low = reach - 8 * m
                    sums[8 * m + r, :, :TILE] += folded(turned_rows * window[low : low + GAP])
            return 0

        lax.fori_loop(0, count, block, 0)
        totals.append(jnp.sum(sums[:, :, :TILE], axis=1))
    return jnp.concatenate([totals[0], totals[1][:, :half] + totals[1][:, half:]], axis=1)


def taps_grad_kernel(grad, keys, gtaps_o, sums, side_grad, side_keys):
    gtaps_o[...] = taps_grad(grad, keys, sums, side_grad, side_keys)


def late_grad_kernel(meta, grad, keys, first, graw, vec_sums, ubias_a, ubias_b, gbias, modes, *refs):
    targets, (sums, pieces, side_grad, side_keys) = refs[:-4], refs[-4:]
    n_pieces, rows, local = pieces.shape
    rows -= SMALL
    made = dot_tn(graw[...], first[...]).T
    pieces[...] = jnp.zeros_like(pieces)
    ubias = jnp.sum(ubias_a[...] + ubias_b[...], axis=0, keepdims=True)
    bias = jnp.concatenate([jnp.sum(gbias[i], axis=0, keepdims=True) for i in range(3)], axis=0)
    heads = modes.shape[0]
    n_bias, n_modes = local // n_pieces, modes.shape[1] // n_pieces
    low = rows + 8
    gtaps = taps_grad(grad, keys, sums, side_grad, side_keys)
    for d in range(n_pieces):
        pieces[d, :rows, :] = made[d * rows : (d + 1) * rows, :]
        pieces[d, rows:low, :] = gtaps[8 * d : 8 * d + 8, :]
        wide = slice(d * rows, (d + 1) * rows)
        pieces[d, low : low + 6, :rows] = vec_sums[0:6, wide]
        pieces[d, low + 6 : low + 7, :rows] = ubias[:, wide]
        pieces[d, low : low + 3, TILE : TILE + n_bias] = bias[:, d * n_bias : (d + 1) * n_bias]
        pieces[d, low : low + heads, local - n_modes :] = modes[:, d * n_modes : (d + 1) * n_modes]
    for k, target in enumerate(targets):
        for j in range(2):
            target[j, :, :] = pieces[2 * (meta[1] ^ k) + j].astype(BF)


def make_tiles(lags_ref, tiles, heads):
    for h in range(heads):
        for d in range(LAGS):
            at = TILE * (LAGS - 1 - d)
            row = jnp.broadcast_to(lags_ref[h : h + 1, at : at + 2 * TILE], (TILE, 2 * TILE))
            turned = pltpu.roll(row, TILE + 1, 1, stride=1, stride_axis=0)
            tiles[h, d, :, :] = turned[:, :TILE]


def head_lanes(h, heads, channels):
    size = channels // heads
    lane = lax.broadcasted_iota(jnp.int32, (BLOCK, channels), 1)
    return (lane >= h * size) & (lane < (h + 1) * size)


def head_masked(source, target, heads):
    length, channels = source.shape

    for a in range(length // BLOCK):
        part = source[a * BLOCK : (a + 1) * BLOCK, :]
        for h in range(heads):
            target[a, h * BLOCK : (h + 1) * BLOCK, :] = jnp.where(
                head_lanes(h, heads, channels), part, jnp.zeros_like(part)
            )


def starts_of(ends, target):
    rows = lax.broadcasted_iota(jnp.int32, target.shape, 0)
    first = jnp.where(rows >= ends[0], ends[0], 0)
    target[...] = jnp.where(rows >= ends[1], ends[1], first)


def lives_of(starts, a, lag):
    lives = {}
    for i in range(2):
        for j in range(2):
            if 0 <= 2 * lag + i - j < LAGS:
                lane = lax.broadcasted_iota(jnp.int32, (TILE, TILE), 1)
                lane = lane + ((a - lag) * BLOCK + j * TILE)
                lives[i, j] = lane >= starts[pl.ds(a * BLOCK + i * TILE, TILE), :]
    return lives


def mix_kernel(ends, q_ref, k_ref, v_ref, lags_ref, mixed_o, tiles_o, qm, vmask, starts, weights):
    length, local = q_ref.shape
    heads = tiles_o.shape[0]
    make_tiles(lags_ref, tiles_o, heads)
    head_masked(q_ref, qm, heads)
    head_masked(v_ref, vmask, heads)
    starts_of(ends, starts)
    for a in range(length // BLOCK):
        least = max(0, a - REACH + 1)
        for s in range(least, a + 1):
            lag = a - s
            keys = k_ref[s * BLOCK : (s + 1) * BLOCK, :]
            lives = lives_of(starts, a, lag)
            for h in range(heads):
                scores = dot_nt(qm[a, h * BLOCK : (h + 1) * BLOCK, :], keys)
                at = ((s - least) * heads + h) * BLOCK
                for i in range(2):
                    for j in range(2):
                        spot = (slice(i * TILE, (i + 1) * TILE), slice(j * TILE, (j + 1) * TILE))
                        where = (spot[0], slice(at + j * TILE, at + (j + 1) * TILE))
                        if (i, j) in lives:
                            factor = jnp.where(lives[i, j], tiles_o[h, 2 * lag + i - j], 0.0)
                            weights[where] = (factor * scores[spot]).astype(BF)
                        else:
                            weights[where] = jnp.zeros((TILE, TILE), BF)
        wide = (a - least + 1) * heads * BLOCK
        stack = vmask[least : a + 1].reshape(wide, local)
        mixed_o[a * BLOCK : (a + 1) * BLOCK, :] = dot(weights[:, :wide], stack).astype(BF)


def mix_back_kernel(
    meta, ends, q_ref, k_ref, v_ref, gm0, gm1, gm2, gm3, out_ref, tiles, gq_o, gk_o, gv_o, glag_o,
    gmix, qm, gmask, kmask, qt, gt, starts, grads, gkt, gvt, diag
):
    length, local = q_ref.shape
    heads = tiles.shape[0]
    size = local // heads
    quarter = gm0.shape[0]
    blocks = length // BLOCK
    for k, part in enumerate((gm0, gm1, gm2, gm3)):
        base = pl.multiple_of((meta[0] ^ k) * quarter, quarter)
        gmix[pl.ds(base, quarter), :] = dot(part[...], out_ref[0]).astype(BF)
    head_masked(q_ref, qm, heads)
    head_masked(gmix, gmask, heads)
    head_masked(k_ref, kmask, heads)
    starts_of(ends, starts)

    for a in range(blocks):
        spot = slice(a * BLOCK, (a + 1) * BLOCK)
        qt[a, :, :] = q_ref[spot, :].astype(F32).T.astype(BF)
        gt[a, :, :] = gmix[spot, :].astype(F32).T.astype(BF)
    gkt[...] = jnp.zeros_like(gkt)
    gvt[...] = jnp.zeros_like(gvt)
    diag[...] = jnp.zeros_like(diag)
    for a in range(blocks):
        least = max(0, a - REACH + 1)
        for s in range(least, a + 1):
            lag = a - s
            source = slice(s * BLOCK, (s + 1) * BLOCK)
            keys, vals = k_ref[source, :], v_ref[source, :]
            lives = lives_of(starts, a, lag)
            for h in range(heads):
                own = slice(h * BLOCK, (h + 1) * BLOCK)
                scores = dot_nt(qm[a, own, :], keys)
                wgrad = dot_nt(gmask[a, own, :], vals)
                rows_w, rows_g = [], []
                for i in range(2):
                    line_w, line_g = [], []
                    for j in range(2):
                        if (i, j) in lives:
                            d = 2 * lag + i - j
                            spot = (
                                slice(i * TILE, (i + 1) * TILE),
                                slice(j * TILE, (j + 1) * TILE),
                            )
                            factor = jnp.where(lives[i, j], tiles[h, d], 0.0)
                            line_w.append((factor * scores[spot]).astype(BF))
                            line_g.append((wgrad[spot] * factor).astype(BF))
                            diag[h, d] += jnp.where(lives[i, j], wgrad[spot] * scores[spot], 0.0)
                        else:
                            line_w.append(jnp.zeros((TILE, TILE), BF))
                            line_g.append(jnp.zeros((TILE, TILE), BF))
                    rows_w.append(jnp.concatenate(line_w, axis=1))
                    rows_g.append(jnp.concatenate(line_g, axis=1))
                w = jnp.concatenate(rows_w, axis=0)
                g = jnp.concatenate(rows_g, axis=0)
                at = ((s - least) * heads + h) * BLOCK
                grads[:, at : at + BLOCK] = g
                band = slice(h * size, (h + 1) * size)
                gvt[s, band, :] += dot(gt[a, band, :], w)
                gkt[s, band, :] += dot(qt[a, band, :], g)
        wide = (a - least + 1) * heads * BLOCK
        stack = kmask[least : a + 1].reshape(wide, local)
        gq_o[a * BLOCK : (a + 1) * BLOCK, :] = dot(grads[:, :wide], stack).astype(BF)
    for a in range(blocks):
        gk_o[a * BLOCK : (a + 1) * BLOCK, :] = gkt[a].T
        gv_o[a * BLOCK : (a + 1) * BLOCK, :] = gvt[a].T.astype(BF)
    glag_o[...] = jnp.zeros_like(glag_o)
    for h in range(heads):
        for d in range(LAGS):
            line = jnp.concatenate([diag[h, d], jnp.zeros((TILE, TILE), F32)], axis=1)
            rows = TILE
            while rows > 1:
                rows //= 2
                line = pltpu.roll(line[:rows], rows, 1) + line[rows : 2 * rows]
            at = TILE * (LAGS - 1 - d)
            glag_o[h : h + 1, at : at + 2 * TILE] += line


ROOT_HALF = 0.7071067811865476
PHI_SCALE = 0.3989422804014327


def mlp_kernel(near, meta, x_ref, g_ref, m0, m1, m2, m3, vec, *refs):
    n_out = 9 if near else 10
    ins, refs = refs[:-n_out], refs[-n_out:]
    second_o, act_o, gpre_o, gsec_o, ubias_o = refs[:5]
    pre, agrad, mid = refs[-3:]
    if near:
        out_ref, both = ins
        middle_o = refs[5]
    else:
        out_ref, both = refs[5:7]
        count = len(ins) // 2
        if count == 1:
            out_ref[...] = ins[0][...]
            both[...] = ins[1][...]
        else:
            rows = ins[0].shape[2]
            for k in range(count):
                for j in range(2):
                    to = pl.ds(pl.multiple_of((2 * (meta[1] ^ k) + j) * rows, rows), rows)
                    for i in range(4):
                        out_ref[i, to, :] = ins[k][i, j]
                    both[to, :] = ins[count + k][j]
    quarter = pre.shape[0]
    hidden = both.shape[1] // 2
    step = 64
    ubias_o[...] = jnp.zeros_like(ubias_o)

    for n in range(2):
        k = n if near else n + 2
        base = pl.multiple_of((meta[0] ^ k) * quarter, quarter)
        here = k * quarter
        row = n * quarter
        total = x_ref[pl.ds(here, quarter), :].astype(F32) + vec[2:3, :]
        for i, m in enumerate((m0, m1, m2, m3)):
            total = total + dot_nt(m[pl.ds(base, quarter), :], out_ref[i])
        mid[...] = total
        if near:
            middle_o[pl.ds(row, quarter), :] = total
        for i in range(quarter // step):
            normed, _inv = norm_rows(mid[i * step : (i + 1) * step, :])
            second_o[pl.ds(row + i * step, step), :] = (
                normed * vec[3:4, :] + vec[4:5, :]
            ).astype(BF)
        pre[...] = dot(second_o[pl.ds(row, quarter), :], both[:, :hidden])
        agrad[...] = dot(g_ref[pl.ds(here, quarter), :], both[:, hidden:])
        sums = None
        for i in range(quarter // 32):
            to = pl.ds(row + i * 32, 32)
            v = pre[i * 32 : (i + 1) * 32, :] + vec[6:7, :]
            cdf = 0.5 + 0.5 * lax.erf(v * ROOT_HALF)
            act_o[to, :] = (v * cdf).astype(BF)
            slope = cdf + v * (PHI_SCALE * jnp.exp(-0.5 * v * v))
            grad = (slope * agrad[i * 32 : (i + 1) * 32, :]).astype(BF)
            gpre_o[to, :] = grad
            part = folded(grad.astype(F32))
            sums = part if sums is None else sums + part
        ubias_o[...] += sums
        part = dot_nt(gpre_o[pl.ds(row, quarter), :], both[:, :hidden])
        gsec_o[pl.ds(row, quarter), :] = part.astype(gsec_o.dtype)


def ff_grad_kernel(meta, second_a, second_b, gpre_a, gpre_b, cot, act_a, act_b, *refs):
    targets, made = refs[:-1], refs[-1]
    half = second_a.shape[0]
    made[0, :, :] = dot_tn(second_a[...], gpre_a[...]) + dot_tn(second_b[...], gpre_b[...])
    made[1, :, :] = dot_tn(cot[:half, :], act_a[...]) + dot_tn(cot[half:, :], act_b[...])
    rows = targets[0].shape[2]
    for k, target in enumerate(targets):
        for j in range(2):
            spot = pl.ds(pl.multiple_of((2 * (meta[1] ^ k) + j) * rows, rows), rows)
            for i in range(2):
                target[j, i, :, :] = made[i, spot, :].astype(BF)


def early_grad_kernel(meta, first, gq, gv, gm0, gm1, gm2, gm3, mixed, *refs):
    targets, made = refs[:-1], refs[-1]
    quarter = gm0.shape[0]
    made[0, :, :] = dot_tn(gq[...], first[...]).T
    made[1, :, :] = dot_tn(gv[...], first[...]).T
    total = None
    for k, ref in enumerate((gm0, gm1, gm2, gm3)):
        base = pl.multiple_of((meta[0] ^ k) * quarter, quarter)
        part = dot_tn(mixed[pl.ds(base, quarter), :], ref[...])
        total = part if total is None else total + part
    made[2, :, :] = total.T
    rows = targets[0].shape[2]
    for k, target in enumerate(targets):
        for j in range(2):
            spot = pl.ds(pl.multiple_of((2 * (meta[1] ^ k) + j) * rows, rows), rows)
            for i in range(3):
                target[j, i, :, :] = made[i, spot, :].astype(BF)


def middle_back_kernel(part, near, far, cot, middle, vec, gmid_o, gmb_o, sums_o):
    rows, width = far.shape
    step = 64

    def chunk(i, totals):
        at = pl.multiple_of(i * step, step)
        spot = pl.ds(at, step)
        up = part[spot, :] + near[spot, :].astype(F32) + far[spot, :].astype(F32)
        normed, inv = norm_rows(middle[spot, :])
        cotangent = cot[spot, :].astype(F32)
        e = up * vec[3:4, :]
        mean_e = jnp.mean(e, axis=-1, keepdims=True)
        mean_x = jnp.mean(e * normed, axis=-1, keepdims=True)
        grad = cotangent + inv * (e - mean_e - normed * mean_x)
        gmid_o[spot, :] = grad
        gmb_o[spot, :] = grad.astype(BF)
        terms = (grad, up * normed, up, cotangent)
        return tuple(t + folded(x) for t, x in zip(totals, terms))

    totals = lax.fori_loop(
        0, rows // step, chunk, tuple(jnp.zeros((8, width), F32) for _ in range(4)), unroll=True
    )
    sums_o[...] = jnp.zeros_like(sums_o)
    for i, t in enumerate(totals):
        sums_o[2 + i : 3 + i, :] = jnp.sum(t, axis=0, keepdims=True)


def first_back_kernel(meta, part, near, far, tokens, gmid, vec, mean_ref, inv_ref, grad_o):
    rows, width = tokens.shape
    step = 64
    base = pl.multiple_of(meta[0] * rows, rows)

    def chunk(i, _):
        at = pl.multiple_of(i * step, step)
        spot = pl.ds(at, step)
        stat = pl.ds(pl.multiple_of(base + at, step), step)
        up = part[spot, :] + near[spot, :].astype(F32) + far[spot, :].astype(F32)
        inv = inv_ref[stat, :]
        normed = (tokens[spot, :].astype(F32) - mean_ref[stat, :]) * inv
        e = up * vec[0:1, :]
        mean_e = jnp.mean(e, axis=-1, keepdims=True)
        mean_x = jnp.mean(e * normed, axis=-1, keepdims=True)
        grad_o[spot, :] = (gmid[spot, :] + inv * (e - mean_e - normed * mean_x)).astype(BF)
        return 0

    lax.fori_loop(0, rows // step, chunk, 0, unroll=True)


def first_grad_kernel(
    meta, gq, gk, gv, wq, wk, wv, x_ref, mean_ref, inv_ref, sums_two, near_o, far_o, bias_o, made, sums
):
    length, local = gq.shape
    quarter = length // 4
    step = 64
    for i, ref in enumerate((gq, gk, gv)):
        total = jnp.zeros((8, local), F32)
        for j in range(length // 256):
            total = total + folded(ref[256 * j : 256 * j + 256, :].astype(F32))
        bias_o[i, :, :] = total
    sums[...] = jnp.zeros_like(sums)
    for first, target in ((0, near_o), (2, far_o)):

        for n in range(2):
            base = pl.multiple_of((meta[0] ^ (first + n)) * quarter, quarter)
            here = (first + n) * quarter
            total = None
            for ref, weight in ((gq, wq), (gk, wk), (gv, wv)):
                term = dot_nt(ref[pl.ds(base, quarter), :], weight[...])
                total = term if total is None else total + term
            made[...] = total
            row = n * quarter
            target[pl.ds(row, quarter), :] = total.astype(target.dtype)
            for i in range(quarter // step):
                stat = pl.ds(pl.multiple_of(base + i * step, step), step)
                up = made[i * step : (i + 1) * step, :]
                values = x_ref[pl.ds(here + i * step, step), :].astype(F32)
                normed = (values - mean_ref[stat, :]) * inv_ref[stat, :]
                sums[0, :, :] += folded(up * normed)
                sums[1, :, :] += folded(up)
    ends = jnp.concatenate(
        [
            jnp.sum(sums[0], axis=0, keepdims=True),
            jnp.sum(sums[1], axis=0, keepdims=True),
            sums_two[2:8, :],
            jnp.zeros_like(sums_two),
        ],
        axis=0,
    )
    near_o[2 * quarter :, :] = ends
    far_o[2 * quarter :, :] = ends.astype(BF)


def permute(value, groups, target_of):
    pairs = []
    for g in range(groups):
        for c in range(2):
            for z in range(4):
                to = target_of(g, c, z)
                if to is not None:
                    pairs.append((g * 8 + c * 4 + z, to[0] * 8 + to[1] * 4 + to[2]))
    return lax.ppermute(value, AXES, pairs)


def swap_quarters(value, groups):
    return permute(
        value, groups, lambda g, c, z: (g, c, z) if c == z // 2 else (g, 1 - c, z ^ 2)
    )


def to_core(value, groups):
    return permute(value, groups, lambda g, c, z: (g, 1 - c, z))


def to_chip(value, groups):
    return permute(value, groups, lambda g, c, z: (g, c, z ^ 1))


def gather_group(value, groups):
    chip = to_chip(value, groups)
    core = to_core(value, groups)
    both = to_core(chip, groups)
    return value, chip, core, both


def spread_pieces(piece, groups, same):
    near = permute(
        piece, groups, lambda g, c, z: (g, c, z ^ 2) if c == z // 2 else (g, 1 - c, z)
    )
    far = permute(piece, groups, lambda g, c, z: None if c == z // 2 else (g, 1 - c, z ^ 2))
    return jnp.where(same, piece, near), jnp.where(same, near, far)


def halves_of(pieces, half):
    return tuple(lax.dynamic_index_in_dim(pieces, i, 0, False) for i in (half, 1 - half))


def return_pieces(kept, sent, groups, same):
    near = permute(
        sent, groups, lambda g, c, z: (g, 1 - c, z) if c == z // 2 else (g, c, z ^ 2)
    )
    far = permute(kept, groups, lambda g, c, z: None if c == z // 2 else (g, 1 - c, z ^ 2))
    return near.astype(F32) + jnp.where(same, kept, far).astype(F32)


def after(value, *others):
    return lax.optimization_barrier((value, *others))[0]


def pad_to(value, rows, lanes):
    return jnp.pad(value, ((0, rows - value.shape[0]), (0, lanes - value.shape[1])))


def shift_groups(value, groups, k):
    return permute(value, groups, lambda g, c, z: (g ^ k, c, z))


def send_to_groups(pieces, groups, g):
    if groups != 4:
        shape = pieces.shape
        flat = pieces.reshape(groups * 2 * shape[2], shape[3])
        total = lax.psum_scatter(flat, "g", scatter_dimension=0, tiled=True)
        return (total.reshape(shape[1:]),), ()
    sent = [lax.dynamic_index_in_dim(pieces, g ^ k, 0, False) for k in range(groups)]
    return sent, [shift_groups(sent[k], groups, k) for k in (1, 2, 3)]


def grouped(values, groups):
    n, width, columns = values.shape
    pieces = values.reshape(n, groups, 2, width // groups // 2, columns).transpose(1, 2, 0, 3, 4)
    shape = pieces.shape[1:]
    total = lax.psum_scatter(
        pieces.reshape(-1, columns), "g", scatter_dimension=0, tiled=True
    )
    return total.reshape(shape)


def sum_of(sent, came):
    total = sent[0].astype(F32)
    for value in came:
        total = total + value.astype(F32)
    return total.astype(BF)


def plain_pack(triple, out_w, up, down, taps, modes, tbias, ubias, *rest):
    vectors, seg = rest[:6], rest[6]
    _, rows, local = triple.shape
    first_end = jnp.sum((seg[0] < 1).astype(jnp.int32))
    second_end = jnp.sum((seg[0] < 2).astype(jnp.int32))
    ends = jnp.stack([first_end // 32, first_end % 32, second_end // 32, second_end % 32])
    left = jnp.concatenate(
        [
            pad_to(taps, 8, local),
            pad_to(jnp.concatenate(vectors, axis=0), 6, local),
            pad_to(ubias, 1, local),
            pad_to(ends.astype(F32)[None], 1, local),
        ],
        axis=0,
    )
    low = jnp.concatenate([pad_to(tbias[:, 0, :], 8, TILE), pad_to(modes, 8, TILE)], axis=1)
    right = jnp.concatenate([jnp.zeros_like(low), low], axis=0)
    small = jnp.concatenate([left, jnp.zeros((SMALL, 2 * TILE - local), F32), right], axis=1)
    small = pad_to(small, SMALL, 3 * local)
    main = triple.transpose(1, 0, 2).reshape(rows, 3 * local)
    return (
        jnp.concatenate([main, small], axis=0).astype(BF),
        jnp.concatenate([up, down, out_w.T], axis=1).astype(BF),
    )


def plain_small(gtaps, vec_sums, ubias, bias, modes, n_pieces):
    local, width = gtaps.shape[1], vec_sums.shape[1]
    heads = modes.shape[0]

    def by_piece(value):
        return value.reshape(value.shape[0], n_pieces, -1).transpose(1, 0, 2)

    def block_of(value, n_rows, lanes):
        shape = value.shape
        return jnp.pad(value, ((0, 0), (0, n_rows - shape[1]), (0, lanes - shape[2])))

    left = jnp.concatenate([vec_sums[:6], ubias.reshape(1, width)], axis=0)
    pad = local - TILE - modes.shape[1] // n_pieces
    right = block_of(by_piece(bias), 8, local - TILE)
    right = right + jnp.pad(by_piece(modes), ((0, 0), (0, 8 - heads), (pad, 0)))
    low = jnp.concatenate([block_of(by_piece(left), 8, TILE), right], axis=2)
    high = block_of(gtaps.reshape(n_pieces, -1, local), 8, local)
    return jnp.concatenate([high, low], axis=1)


def on_device(
    groups,
    tokens,
    segments,
    row_order,
    first_gain,
    first_shift,
    triple_weight,
    triple_bias,
    shift_taps,
    kernel_modes,
    out_weight,
    out_bias,
    second_gain,
    second_shift,
    up_weight,
    up_bias,
    down_weight,
    down_bias,
    cotangent,
):
    g = lax.axis_index("g")
    c = lax.axis_index("c")
    h = lax.axis_index("h")
    b = lax.axis_index("b")
    same = c == h
    n_pieces = 2 * groups
    quarter, width = tokens.shape[1:]
    length = 4 * quarter
    rows, _, local = triple_weight.shape
    heads = kernel_modes.shape[0]
    n_modes = kernel_modes.shape[1] * n_pieces // 4
    taps_rows = shift_taps.shape[1]
    n_taps = taps_rows * n_pieces
    mode_cols = kernel_modes.shape[1]
    bias_cols = triple_bias.shape[2]
    hidden = up_weight.shape[1]
    q_at = 2 * c + b
    meta = jnp.stack([q_at, g, c, h]).astype(jnp.int32)

    own_x = swap_quarters(tokens[0], groups)
    vectors = (first_gain, first_shift, out_bias, second_gain, second_shift, down_bias)
    raw = (
        triple_weight.transpose(1, 0, 2), out_weight, up_weight, down_weight.T, shift_taps.T,
        kernel_modes, triple_bias, up_bias, *(v[None] for v in vectors), segments,
    )
    if groups == 4:
        a_piece, b_piece = call(
            pack_kernel, 0, raw,
            [((rows + SMALL, 3 * local), BF), ((rows, 2 * hidden + width // 4), BF)],
            [((SMALL, 3 * local), F32)], name="pack", us=2.2,
        )
    else:
        a_piece, b_piece = plain_pack(*raw)
    a_near, a_other = spread_pieces(a_piece, groups, same)
    a_pair = jnp.stack([a_near, a_other])
    x = gather_group(after(own_x, a_piece), groups)
    if groups == 4:
        a_all = [a_pair] + [shift_groups(a_pair, groups, k) for k in (1, 2, 3)]
    else:
        a_all = lax.all_gather(a_pair, "g", axis=0, tiled=False)
        a_all = jnp.where(c == 0, a_all, a_all[:, ::-1]).reshape(n_pieces, rows + SMALL, 3 * local)

    lo, hi = spread_pieces(after(b_piece, x[1]), groups, same)
    first_b, second_b = jnp.where(c == 0, lo, hi), jnp.where(c == 0, hi, lo)
    b_pair = jnp.stack([first_b[:, : 2 * hidden], second_b[:, : 2 * hidden]])
    out_quad = jnp.stack(gather_group(jnp.stack([first_b, second_b])[:, :, 2 * hidden :], groups))
    if groups == 4:
        b_side, b_next = (shift_groups(b_pair, groups, k) for k in (1, 2))
        b_all = [b_pair, b_side, b_next, shift_groups(b_side, groups, 2)]
        out_all = [out_quad] + [shift_groups(out_quad, groups, k) for k in (1, 2, 3)]
    else:
        b_all = [lax.all_gather(b_pair, "g", axis=0, tiled=False).reshape(width, 2 * hidden)]
        out_all = lax.all_gather(out_quad, "g", axis=0, tiled=False)
        out_all = [out_all.transpose(1, 0, 2, 3, 4).reshape(4, width, local)]

    own_cot = swap_quarters(after(cotangent[0], x[1]), groups)
    cot = gather_group(own_cot, groups)

    made = [((length, width), BF), ((length, local), BF), ((length, local), F32)]
    made += [((length, local), BF), ((length, 1), F32), ((length, 1), F32)]
    if groups == 4:
        unpacked = [((width, local), BF)] * 3
        unpacked += [((n_taps, local), F32), ((8, width), F32), ((8, TILE), F32), ((2,), jnp.int32)]
        first, queries, raw_keys, values, mean, inv, wq, wk, wv, taps, vec, modes, ends = call(
            partial(project_kernel, 4), 2, (meta, row_order, *x, *a_all), made + unpacked,
            name="project", us=6.8,
        )
    else:
        weights = a_all[:, :rows, :].reshape(width, 3 * local)
        wq, wk, wv = (weights[:, i * local : (i + 1) * local] for i in range(3))
        small = a_all[:, rows:, :].astype(F32)
        taps = small[:, :taps_rows, :local].reshape(n_taps, local)
        vec = small[:, 8:16, :rows].transpose(1, 0, 2).reshape(8, width)
        bias = small[:, 8:16, 2 * TILE : 2 * TILE + bias_cols].transpose(1, 0, 2).reshape(8, local)
        modes = small[:, 8:16, 3 * TILE : 3 * TILE + mode_cols].transpose(1, 0, 2).reshape(8, TILE)
        mine = (row_order == 2 * g + h)[:, None]
        found = jnp.sum(jnp.where(mine, small[:, 15, :4], 0), axis=0)
        ends = jnp.stack([32 * found[0] + found[1], 32 * found[2] + found[3]]).astype(jnp.int32)
        first, queries, raw_keys, values, mean, inv = call(
            partial(project_kernel, 1), 1, (meta, *x, wq, wk, wv, bias, vec), made,
            name="project", us=6.8,
        )

    modes = modes[:heads]
    lag = LIMIT + TILE - 1 - jnp.arange(6 * TILE, dtype=jnp.int32)
    held = ((lag >= 0) & (lag < LIMIT)).astype(F32)[None, None, :]
    place = jnp.clip(lag, 0, LIMIT - 1).astype(F32)[None, None, :]
    rate = jnp.exp(modes[:, :n_modes])[:, :, None]
    phase = modes[:, n_modes : 2 * n_modes][:, :, None] * place
    decay = jnp.exp(-rate * place) * held
    wave_c, wave_s = decay * jnp.cos(phase), decay * jnp.sin(phase)
    weight_c = modes[:, 2 * n_modes : 3 * n_modes][:, :, None]
    weight_s = modes[:, 3 * n_modes :][:, :, None]
    lags = jnp.sum(weight_c * wave_c + weight_s * wave_s, axis=1)

    padded = length + (SEQUENCES + 1) * GAP
    sides = [((padded // 2 + GAP, TILE), F32)]
    conv_scratch = [((padded, local), F32), *sides, ((n_taps, TILE), F32), *sides]
    n_blocks = length // BLOCK
    keys, key_rows = call(
        conv_kernel, 1, (ends, after(raw_keys, own_cot, b_all[1 % len(b_all)]), taps),
        [((length, local), BF), ((padded, local), F32)], conv_scratch,
        name="conv", us=7.5,
    )
    per_block = (n_blocks, heads * BLOCK, local)
    mixed, tiles = call(
        mix_kernel, 1, (ends, queries, after(keys, cot[1]), values, lags),
        [((length, local), BF), ((heads, LAGS, TILE, TILE), F32)],
        [
            (per_block, BF), (per_block, BF), ((length, TILE), jnp.int32),
            ((BLOCK, REACH * heads * BLOCK), BF),
        ],
        name="mix", us=4.9,
    )
    mixed = after(mixed, *b_all[1:3], *out_all[1:])
    mixes = gather_group(mixed, groups)

    x_all = jnp.concatenate(x, axis=0)
    cot_all = jnp.concatenate(cot, axis=0)
    half = [((2 * quarter, width), BF), ((2 * quarter, hidden), BF), ((2 * quarter, hidden), BF)]
    scratch = [((quarter, hidden), F32), ((quarter, hidden), F32), ((quarter, width), F32)]
    shared = (meta, x_all, cot_all, *mixes, vec)
    second_b, act_b, gpre_b, gsec_b, ubias_b, outs, both = call(
        partial(mlp_kernel, False), 1, (*shared, *out_all, *b_all),
        half
        + [((2 * quarter, width), BF), ((8, hidden), F32), ((4, width, local), BF)]
        + [((width, 2 * hidden), BF)],
        scratch, name="mlp_far", us=8.9,
    )
    came = to_core(gsec_b, groups)
    second_a, act_a, gpre_a, gsec_a, ubias_a, middle = call(
        partial(mlp_kernel, True), 1, (*shared, outs, both),
        half + [((2 * quarter, width), F32), ((8, hidden), F32), ((2 * quarter, width), F32)],
        scratch, name="mlp_near", us=8.8,
    )
    mid_sent = (gsec_a[quarter:] + came[quarter:].astype(F32)).astype(BF)
    far_own = to_chip(mid_sent, groups)

    if groups == 4:
        b_sent = call(
            ff_grad_kernel, 1,
            (meta, after(second_a, mid_sent), second_b, gpre_a, gpre_b, cot_all, act_a, act_b),
            [((2, 2, rows, hidden), BF)] * 4, [((2, width, hidden), F32)], name="ff_grad", us=5.3,
        )
        b_came = [shift_groups(b_sent[k], groups, k) for k in (1, 2, 3)]
    else:
        up_grad = dot_tn(
            jnp.concatenate([second_a, second_b], axis=0), jnp.concatenate([gpre_a, gpre_b], axis=0)
        )
        down_grad = dot_tn(cot_all, jnp.concatenate([act_a, act_b], axis=0))
        b_sent = [grouped(jnp.stack([up_grad, down_grad]).astype(BF), groups)]
        b_came = []
    down_part = both[:, hidden:]
    share_far = dot_nt(after(act_b, mid_sent), down_part).astype(BF)
    share = dot_nt(after(act_a, mid_sent), down_part)
    gmid, gmb_own, sums_two = call(
        middle_back_kernel, 0, (after(gsec_a, share_far, share, *b_sent), came, far_own, own_cot, middle, vec),
        [((quarter, width), F32), ((quarter, width), BF), ((8, width), F32)],
        name="middle_back", us=3.5,
    )
    gmb = gather_group(gmb_own, groups)

    share_near = to_core(share_far, groups).astype(F32)
    share_chip = to_chip((share[quarter:] + share_near[quarter:]).astype(BF), groups)
    gq, gk, gv, glag = call(
        mix_back_kernel, 2,
        (meta, ends, after(queries, share_far, share, *b_came[:2]), keys, values, *gmb, outs, tiles),
        [
            ((length, local), BF), ((length, local), F32), ((length, local), BF),
            ((8, 6 * TILE), F32),
        ],
        [
            ((length, local), BF), (per_block, BF), (per_block, BF), (per_block, BF),
            ((n_blocks, local, BLOCK), BF), ((n_blocks, local, BLOCK), BF),
            ((length, TILE), jnp.int32), ((BLOCK, REACH * heads * BLOCK), BF),
            ((n_blocks, local, BLOCK), F32), ((n_blocks, local, BLOCK), F32),
            ((heads, LAGS, TILE, TILE), F32),
        ],
        name="mix_back", us=12.3,
    )

    b_kept, b_away = halves_of(sum_of(b_sent, [after(v, gk) for v in b_came]), h)
    b_out = return_pieces(b_kept, b_away, groups, same)
    graw, grad_rows = call(
        conv_back_kernel, 1, (ends, after(gk, b_kept, b_away), taps),
        [((length, local), BF), ((padded, local), F32)], conv_scratch,
        name="conv_back", us=7.2,
    )
    share_chip = after(share_chip, graw).astype(F32)
    result = middle[:quarter] + share[:quarter] + share_near[:quarter] + share_chip + vec[5:6, :]
    result = result.astype(BF)
    result = swap_quarters(result, groups)
    share_rows = 2 * quarter + SMALL
    near_part, far_part, gbias = call(
        first_grad_kernel, 1,
        (meta, gq, graw, gv, wq, wk, wv, x_all, mean, inv, sums_two),
        [((share_rows, width), F32), ((share_rows, width), BF), ((3, 8, local), F32)],
        [((quarter, width), F32), ((2, 8, width), F32)],
        name="first_grad", us=5.3,
    )
    came1 = to_core(far_part, groups)
    far_share = near_part[quarter:] + came1[quarter:].astype(F32)
    far_sent = far_share.astype(BF)
    far_own1 = to_chip(far_sent, groups)
    first_late = after(first, far_sent, b_out)
    if groups == 4:
        early_sent = call(
            early_grad_kernel, 1, (meta, first_late, gq, gv, *gmb, mixed),
            [((2, 3, rows, local), BF)] * 4, [((3, width, local), F32)], name="early_grad", us=3.0,
        )
        early_came = [shift_groups(early_sent[k], groups, k) for k in (1, 2, 3)]
    else:
        mixed_rel = jnp.concatenate(
            [lax.dynamic_slice_in_dim(mixed, (q_at ^ k) * quarter, quarter, 0) for k in range(4)],
            axis=0,
        )
        out_grad = dot_tn(jnp.concatenate(gmb, axis=0), mixed_rel)
        early = jnp.stack([dot_tn(first_late, gq), dot_tn(first_late, gv), out_grad])
        early_sent, early_came = [grouped(early.astype(BF), groups)], []

    (back,) = call(
        first_back_kernel, 1,
        (meta, after(near_part, result, *early_sent), came1, far_own1, own_x, gmid, vec)
        + (mean, inv),
        [((quarter, width), BF)], name="first_back", us=3.6,
    )
    input_grad = swap_quarters(back, groups)

    early = sum_of(early_sent, [after(v, back) for v in early_came])
    early = early.reshape(2, 3 * rows, local)
    e_kept, e_away = halves_of(early, h)
    main = return_pieces(e_kept, e_away, groups, same).reshape(3, rows, local)

    glags = glag[:heads][:, None, :]
    grad_c = jnp.sum(glags * wave_c, axis=-1)
    grad_s = jnp.sum(glags * wave_s, axis=-1)
    both_waves = weight_c * wave_c + weight_s * wave_s
    turned_waves = weight_s * wave_c - weight_c * wave_s
    grad_rate = -jnp.sum(glags * place * both_waves, axis=-1) * rate[:, :, 0]
    grad_freq = jnp.sum(glags * place * turned_waves, axis=-1)
    modes_grad = jnp.concatenate([grad_rate, grad_freq, grad_c, grad_s], axis=1)

    vec_sums = far_share[quarter:] + far_own1[quarter:].astype(F32)
    if groups == 4:
        late_sent = call(
            late_grad_kernel, 1,
            (meta, grad_rows, after(key_rows, back, e_kept, e_away), first, graw, vec_sums)
            + (ubias_a, ubias_b, gbias, modes_grad),
            [((2, rows + SMALL, local), BF)] * 4,
            [((n_taps, 8, local), F32), ((n_pieces, rows + SMALL, local), F32), *sides, *sides],
            name="late_grad", us=11.0,
        )
        late_came = [shift_groups(after(late_sent[k], input_grad), groups, k) for k in (1, 2, 3)]
    else:
        (gtaps,) = call(
            taps_grad_kernel, 0, (grad_rows, key_rows), [((n_taps, local), F32)],
            [((n_taps, 8, local), F32), *sides, *sides], name="taps_grad", us=8.2,
        )
        small = plain_small(
            gtaps, vec_sums, jnp.sum(ubias_a + ubias_b, axis=0), jnp.sum(gbias, axis=1), modes_grad,
            n_pieces,
        )
        key_grad = dot_tn(first, graw).reshape(n_pieces, rows, local)
        late = jnp.concatenate([key_grad, small], axis=1).astype(BF)
        late = late.reshape(1, n_pieces * (rows + SMALL), local)
        late_sent, late_came = [grouped(late, groups)[:, 0]], []
    late_out = return_pieces(*halves_of(sum_of(late_sent, late_came), h), groups, same)
    tail = late_out[rows:]
    return (
        result[None],
        input_grad[None],
        tail[8, :rows],
        tail[9, :rows],
        jnp.stack([main[0], late_out[:rows], main[1]]).transpose(1, 0, 2),
        tail[8:11, TILE : TILE + bias_cols][:, None, :],
        tail[:taps_rows].T,
        tail[8 : 8 + heads, local - mode_cols :],
        main[2].T,
        tail[10, :rows],
        tail[11, :rows],
        tail[12, :rows],
        b_out[0],
        tail[14:15, :rows],
        b_out[1].T,
        tail[13, :rows],
    )


def solution(mesh):
    n_data, _ = mesh.devices.shape
    groups = n_data // 2
    fine = Mesh(mesh.devices.reshape(groups, 2, 2, 2), AXES)
    dp, tensor = ("g", "c"), ("h", "b")
    return jax.shard_map(
        partial(on_device, groups),
        mesh=fine,
        in_specs=(
            P(dp, tensor, None),
            P(dp, None),
            P(),
            P(dp),
            P(dp),
            P(dp, None, tensor),
            P(None, tensor, dp),
            P(tensor, dp),
            P(tensor, dp),
            P(tensor, dp),
            P(dp),
            P(dp),
            P(dp),
            P(dp, tensor),
            P(tensor, dp),
            P(tensor, dp),
            P(dp),
            P(dp, tensor, None),
        ),
        out_specs=(
            P(dp, tensor, None),
            P(dp, tensor, None),
            P(dp),
            P(dp),
            P(dp, None, tensor),
            P(None, tensor, dp),
            P(tensor, dp),
            P(tensor, dp),
            P(tensor, dp),
            P(dp),
            P(dp),
            P(dp),
            P(dp, tensor),
            P(tensor, dp),
            P(tensor, dp),
            P(dp),
        ),
        check_vma=False,
    )
```
